32 devices in a mesh: wide: 8 (over z, x), narrow: 4 (over y, core).
Axes of the slice: x: 2, y: 2, z: 4, core: 2. Of those that a mesh axis runs over, the one named last changes fastest.
Arguments:
- tokens: bfloat16 [64, 512, 768], P(('wide', 'narrow')), may hold values from -6 to 6
- doc_lengths: int32 [64], P(('wide', 'narrow')), may hold values from 30 to 512
- qkv_weight: bfloat16 [768, 2304], replicated, may hold values from -0.21875 to 0.21875
- query_bias: bfloat16 [768], replicated, may hold values from -3 to 3
- value_bias: bfloat16 [768], replicated, may hold values from -3 to 3
- out_weight: bfloat16 [768, 768], replicated, may hold values from -0.625 to 0.625
- out_bias: bfloat16 [768], replicated, may hold values from -1.75 to 1.75
- first_gain: bfloat16 [768], replicated, may hold values from 0.5 to 1.5
- first_shift: bfloat16 [768], replicated, may hold values from -1.75 to 1.75
- up_weight: bfloat16 [768, 3072], replicated, may hold values from -0.21875 to 0.21875
- up_bias: bfloat16 [3072], replicated, may hold values from -3 to 3
- down_weight: bfloat16 [3072, 768], replicated, may hold values from -0.15625 to 0.15625
- down_bias: bfloat16 [768], replicated, may hold values from -1.75 to 1.75
- second_gain: bfloat16 [768], replicated, may hold values from 0.5 to 1.5
- second_shift: bfloat16 [768], replicated, may hold values from -1.75 to 1.75
- dir_weight: bfloat16 [1536, 8], replicated, may hold values from -0.375 to 0.375
- dir_bias: bfloat16 [8], replicated, may hold values from -1 to 1
- segment_rows: int32 [64, 128], P(('wide', 'narrow')), may hold values from 0 to 511, as said below
- segment_slots: int32 [32, 256], P(('wide', 'narrow')), may hold values from 0 to 255, each once within a row
- pair_rows: int32 [32, 256, 2], P(('wide', 'narrow')), may hold values from 0 to 255
- pair_labels: int32 [32, 256], P(('wide', 'narrow')), may hold values from 0 to 7
- out_cotangent: bfloat16 [64, 512, 768], P(('wide', 'narrow')), may hold values from -6 to 6
Outputs:
- encoded: bfloat16 [64, 512, 768], P(('wide', 'narrow'))
- grad_tokens: bfloat16 [64, 512, 768], P(('wide', 'narrow'))
- grad_qkv_weight: float32 [768, 2304], P('narrow', 'wide')
- grad_query_bias: float32 [768], replicated
- grad_value_bias: float32 [768], replicated
- grad_out_weight: float32 [768, 768], P('narrow', 'wide')
- grad_out_bias: float32 [768], replicated
- grad_first_gain: float32 [768], replicated
- grad_first_shift: float32 [768], replicated
- grad_up_weight: float32 [768, 3072], P('narrow', 'wide')
- grad_up_bias: float32 [3072], replicated
- grad_down_weight: float32 [3072, 768], P('narrow', 'wide')
- grad_down_bias: float32 [768], replicated
- grad_second_gain: float32 [768], replicated
- grad_second_shift: float32 [768], replicated
- grad_dir_weight: float32 [1536, 8], replicated
- grad_dir_bias: float32 [8], replicated
The draws below stay inside these ranges and needn't reach their ends.
Inputs may be any that keep to these rules, and one draw needn't show every extreme that they name: `segment_rows`: each value is below the token count of its document. `segment_slots`: each device's row holds every slot once.
All inputs are finite; a program needn't handle non-finite values.
Results may differ from the reference program's by a relative error of at most 0.02.
Values may be sent and summed in bfloat16 or wider, within the bound.
A program may use at most 192 MiB of HBM per device.

```python
import jax
import jax.numpy as jnp
from jax import lax

D = 768
HEADS = 12
HEAD_DIM = 64
FF = 3072
L = 512
MIN_TOK = 30
DIRS = 8
DOC_DEV = 2
SEG_DOC = 128
PAIR_DEV = 256
GROUPS = 32
DOCS = 64
SEG_DEV = 256
CAP = 32
N_NARROW = 4


def token_counts(key):
    counts = jax.random.randint(jax.random.fold_in(key, 11), (DOCS,), MIN_TOK, L + 1)
    longest = jax.random.randint(jax.random.fold_in(key, 12), (), 0, DOCS)
    offset = jax.random.randint(jax.random.fold_in(key, 13), (), 1, DOCS)
    shortest = (longest + offset) % DOCS
    places = jnp.arange(DOCS)
    counts = jnp.where(places == longest, L, counts)
    counts = jnp.where(places == shortest, MIN_TOK, counts)
    return counts.astype(jnp.int32)


def draw_doc_lengths(key, part):
    return token_counts(key)


def draw_segment_rows(key, part):
    counts = token_counts(key)
    raw = jax.random.randint(jax.random.fold_in(key, 14), (DOCS, SEG_DOC), 0, 1 << 20)
    rows = raw % counts[:, None]
    columns = jnp.arange(SEG_DOC)[None, :]
    rows = jnp.where(columns == 0, counts[:, None] - 1, rows)
    rows = jnp.where(columns == 1, 0, rows)
    return rows.astype(jnp.int32)


def touch_ends(drawn, own_key, smallest, high):
    place = [jax.random.randint(jax.random.fold_in(own_key, axis), (), 0, length) for axis, length in enumerate(drawn.shape)]
    widest = drawn.shape.index(max(drawn.shape))
    next_to = place[:widest] + [(place[widest] + 1) % drawn.shape[widest]] + place[widest + 1:]
    return drawn.at[tuple(place)].set(smallest).at[tuple(next_to)].set(high)


def block_scale(key, dims, pieces, low, largest):
    level, own = 1.0, jax.random.fold_in(key, 6)
    for axis_at, parts in pieces:
        heights = jnp.exp(jax.random.uniform(jax.random.fold_in(own, axis_at), (parts,), jnp.float32, low / len(pieces), largest / len(pieces)))
        level = level * jnp.repeat(heights, dims[axis_at] // parts).reshape([-1 if axis == axis_at else 1 for axis in range(len(dims))])
    return level


def scatter_about(key, shape, deviation, most, cuts=(), kind=jnp.bfloat16):
    values = jax.random.normal(key, shape, jnp.float32) * deviation
    if len(cuts) > 0:
        values = block_scale(key, shape, cuts, -0.22, 0.18) * values
    return jnp.clip(values, min=-most, max=most).astype(kind)


def setup_inputs(seed: int = 0) -> dict:
    keys = jax.random.split(jax.random.key(seed), 23)
    return {
        "tokens": scatter_about(keys[0], (DOCS, L, D), 1.0, 6.0, ((0, 32),)),
        "doc_lengths": draw_doc_lengths(jax.random.fold_in(keys[22], 71), 0),
        "qkv_weight": scatter_about(keys[2], (D, 3 * D), D ** -0.5, 0.21875),
        "query_bias": scatter_about(keys[3], (D,), 0.5, 3.0),
        "value_bias": scatter_about(keys[4], (D,), 0.5, 3.0),
        "out_weight": scatter_about(keys[5], (D, D), (D // 8) ** -0.5, 0.625),
        "out_bias": scatter_about(keys[6], (D,), 0.3, 1.75),
        "first_gain": jnp.clip(1.0 + 0.1 * jax.random.normal(keys[7], (D,), jnp.float32), 0.5, 1.5).astype(jnp.bfloat16),
        "first_shift": scatter_about(keys[8], (D,), 0.3, 1.75),
        "up_weight": scatter_about(keys[9], (D, FF), D ** -0.5, 0.21875),
        "up_bias": scatter_about(keys[10], (FF,), 0.5, 3.0),
        "down_weight": scatter_about(keys[11], (FF, D), (FF // 2) ** -0.5, 0.15625),
        "down_bias": scatter_about(keys[12], (D,), 0.3, 1.75),
        "second_gain": jnp.clip(1.0 + 0.1 * jax.random.normal(keys[13], (D,), jnp.float32), 0.5, 1.5).astype(jnp.bfloat16),
        "second_shift": scatter_about(keys[14], (D,), 0.3, 1.75),
        "dir_weight": scatter_about(keys[15], (2 * D, DIRS), 0.06, 0.375),
        "dir_bias": jnp.clip(jax.random.uniform(keys[16], (DIRS,), jnp.float32, -1.0, 1.0), -1.0, 1.0).astype(jnp.bfloat16),
        "segment_rows": draw_segment_rows(jax.random.fold_in(keys[22], 71), 0),
        "segment_slots": jax.vmap(lambda own: jax.random.permutation(own, SEG_DEV))(jax.random.split(keys[18], GROUPS)).reshape((GROUPS, SEG_DEV)).astype(jnp.int32),
        "pair_rows": touch_ends(jax.random.randint(keys[19], (GROUPS, PAIR_DEV, 2), 0, SEG_DEV), jax.random.fold_in(keys[19], 1), 0, SEG_DEV - 1).astype(jnp.int32),
        "pair_labels": touch_ends(jax.random.randint(keys[20], (GROUPS, PAIR_DEV), 0, DIRS), jax.random.fold_in(keys[20], 1), 0, DIRS - 1).astype(jnp.int32),
        "out_cotangent": scatter_about(keys[21], (DOCS, L, D), 1.0, 6.0, ((0, 32),)),
    }


@jax.custom_vjp
def low(v):
    return lax.optimization_barrier(v.astype(jnp.bfloat16)).astype(jnp.float32)

@jax.custom_vjp
def low_back(v):
    return v

def low_keep(v):
    return (low(v), None)

def low_pass(kept, grad):
    return (grad,)

def back_keep(v):
    return (v, None)

def back_low(kept, grad):
    return (low(grad),)
low.defvjp(low_keep, low_pass)
low_back.defvjp(back_keep, back_low)
EXACT = lax.Precision.HIGHEST
MASKED = -1e+30
EPSILON = 1e-05

def matmul(left, right):
    return jnp.dot(left, right, precision=EXACT, preferred_element_type=jnp.float32)

def layer_norm(values, gain, shift):
    center = lax.optimization_barrier(jnp.mean(values, -1, keepdims=True))
    centered = values - center
    variance = lax.optimization_barrier(jnp.mean(centered * centered, -1, keepdims=True))
    return centered * lax.rsqrt(variance + EPSILON) * gain + shift

def encode_group(group_tokens, lengths, params):
    qkv_weight, query_bias, value_bias, out_weight, out_bias, first_gain, first_shift, up_weight, up_bias, down_weight, down_bias, second_gain, second_shift = params
    token_rows = group_tokens.reshape(-1, D)
    bias_row = jnp.concatenate([query_bias, jnp.zeros_like(query_bias), value_bias])
    qkv = low_back(low(matmul(token_rows, qkv_weight) + bias_row))
    qkv = qkv.reshape(DOC_DEV, L, 3, HEADS, HEAD_DIM)
    queries = qkv[:, :, 0]
    key_rows = qkv[:, :, 1]
    value_rows = qkv[:, :, 2]
    scores = jnp.einsum('bqhd,bkhd->bhqk', queries, key_rows, precision=EXACT) * HEAD_DIM ** (-0.5)
    scores = low_back(scores)
    allowed = jnp.arange(L, dtype=jnp.int32)[None, :] < lengths[:, None]
    scores = jnp.where(allowed[:, None, None, :], scores, MASKED)
    attention = jax.nn.softmax(scores, axis=-1)
    mixed = jnp.einsum('bhqk,bkhd->bqhd', low(attention), value_rows, precision=EXACT).reshape(-1, D)
    mixed = low_back(low(mixed))
    attended = low_back(matmul(mixed, out_weight) + out_bias)
    hidden_one = layer_norm(token_rows + attended, first_gain, first_shift)
    upper_pre = low_back(matmul(low(hidden_one), up_weight) + up_bias)
    active = low(jax.nn.gelu(upper_pre, approximate=False))
    lowered = low_back(matmul(active, down_weight) + down_bias)
    row_mask = allowed.reshape(-1, 1).astype(jnp.float32)
    encoded = layer_norm(hidden_one + lowered, second_gain, second_shift) * row_mask
    return encoded.reshape(DOC_DEV, L, D)

def pick_rows(table, indices):
    return table[indices]

def forward(tokens_f, params, dir_f, dir_bias_f, doc_lengths, segment_rows, segment_slots, pair_rows, pair_labels):

    def step(carry, item):
        return (carry, jax.checkpoint(encode_group)(item[0], item[1], params))
    unused, encoded = lax.scan(step, jnp.zeros((), jnp.int32), (tokens_f.reshape(GROUPS, DOC_DEV, L, D), doc_lengths.reshape(GROUPS, DOC_DEV)))
    group_rows = encoded.reshape(GROUPS, DOC_DEV * L, D)
    starts = (jnp.arange(DOC_DEV, dtype=jnp.int32) * L)[None, :, None]
    local_rows = (segment_rows.reshape(GROUPS, DOC_DEV, SEG_DOC) + starts).reshape(GROUPS, SEG_DEV).astype(jnp.int32)
    picked = jax.vmap(pick_rows)(group_rows, local_rows)
    picked = low_back(low(picked))
    group_ids = jnp.arange(GROUPS, dtype=jnp.int32)[:, None]
    target = ((segment_slots // CAP * N_NARROW + group_ids % N_NARROW) * SEG_DEV + group_ids // N_NARROW * CAP + segment_slots % CAP).astype(jnp.int32)
    arrived = jnp.zeros((GROUPS * SEG_DEV, D), jnp.float32).at[target.reshape(-1)].set(picked.reshape(-1, D))
    chosen = (pair_rows + group_ids[:, :, None] * SEG_DEV).astype(jnp.int32)
    first_rows = arrived[chosen[:, :, 0].reshape(-1)]
    second_rows = arrived[chosen[:, :, 1].reshape(-1)]
    logits = matmul(first_rows, dir_f[:D]) + matmul(second_rows, dir_f[D:]) + dir_bias_f
    totals = jax.nn.logsumexp(logits, axis=-1)
    labelled = jnp.take_along_axis(logits, pair_labels.reshape(-1, 1).astype(jnp.int32), axis=1)[:, 0]
    return (encoded.reshape(DOCS, L, D), jnp.sum(totals - labelled))

def reference(tokens, doc_lengths, qkv_weight, query_bias, value_bias, out_weight, out_bias, first_gain, first_shift, up_weight, up_bias, down_weight, down_bias, second_gain, second_shift, dir_weight, dir_bias, segment_rows, segment_slots, pair_rows, pair_labels, out_cotangent):
    params = tuple((item.astype(jnp.float32) for item in (qkv_weight, query_bias, value_bias, out_weight, out_bias, first_gain, first_shift, up_weight, up_bias, down_weight, down_bias, second_gain, second_shift)))

    def objective(tokens_f, params_f, dir_f, dir_bias_f):
        return forward(tokens_f, params_f, dir_f, dir_bias_f, doc_lengths, segment_rows, segment_slots, pair_rows, pair_labels)
    (encoded, loss), pull = jax.vjp(objective, tokens.astype(jnp.float32), params, dir_weight.astype(jnp.float32), dir_bias.astype(jnp.float32))
    grad_input, grad_params, grad_dir, grad_dir_shift = pull((out_cotangent.astype(jnp.float32), jnp.ones_like(loss)))
    return (encoded.astype(jnp.bfloat16), grad_input.astype(jnp.bfloat16), grad_params[0], grad_params[1], grad_params[2], grad_params[3], grad_params[4], grad_params[5], grad_params[6], grad_params[7], grad_params[8], grad_params[9], grad_params[10], grad_params[11], grad_params[12], grad_dir, grad_dir_shift)
```

```python
import jax
import jax.numpy as jnp
from jax import lax
from jax.experimental import pallas as pl
from jax.experimental.pallas import tpu as pltpu
from jax.sharding import PartitionSpec as P

HEADS = 12
HEAD_DIM = 64


EXACT = lax.Precision.HIGHEST
MASKED = -1e30
EPSILON = 1e-05


def norm_forward(values, gain, shift):
    center = jnp.mean(values, -1, keepdims=True)
    centered = values - center
    inverse = lax.rsqrt(jnp.mean(centered * centered, -1, keepdims=True) + EPSILON)
    normed = centered * inverse
    return (normed * gain + shift, normed, inverse)


def norm_backward(grad, normed, inverse, gain):
    scaled = grad * gain
    first_mean = jnp.mean(scaled, -1, keepdims=True)
    second_mean = jnp.mean(scaled * normed, -1, keepdims=True)
    return (
        (scaled - first_mean - normed * second_mean) * inverse,
        jnp.sum(grad * normed, 0),
        jnp.sum(grad, 0),
    )


def normal_cdf(values):
    return 0.5 * (1.0 + lax.erf(values * 0.7071067811865476))


MESH_ID = pl.DeviceIdType.MESH


def axis_bits():
    names = []
    for axis in ("wide", "narrow"):
        count = lax.axis_size(axis).bit_length() - 1
        names += [(axis, bit) for bit in reversed(range(count))]
    return names


class Place:
    def __init__(self):
        self.index = {axis: lax.axis_index(axis) for axis in ("wide", "narrow")}
        self.names = axis_bits()
        self.bit = {name: (self.index[name[0]] // (1 << name[1])) % 2 for name in self.names}

    def across(self, name):
        axis, bit = name
        target = dict(self.index)
        target[axis] = target[axis] + (1 << bit) - (2 << bit) * self.bit[name]
        return target

    def greet(self):
        barrier = pltpu.get_barrier_semaphore()
        for name in self.names:
            pl.semaphore_signal(barrier, inc=1, device_id=self.across(name), device_id_type=MESH_ID)
        pl.semaphore_wait(barrier, len(self.names))


class Halving:
    def __init__(self, place, order, source, own, received, send_sems, recv_sems, first_sem):
        self.place, self.order = place, order
        self.source, self.own, self.received = source, own, received
        self.send_sems, self.recv_sems, self.first_sem = send_sems, recv_sems, first_sem
        self.copies = {}

    def region(self, step, mine):
        index = []
        for name in self.place.names:
            if name in self.order[:step]:
                index.append(self.place.bit[name])
            elif name == self.order[step]:
                index.append(self.place.bit[name] if mine else 1 - self.place.bit[name])
            else:
                index.append(slice(None))
        return tuple(index)

    def send(self, step):
        held = self.source if step == 0 else self.own
        self.copies[step] = pltpu.make_async_remote_copy(
            src_ref=held.at[self.region(step, False)],
            dst_ref=self.received[step],
            send_sem=self.send_sems.at[self.first_sem + step],
            recv_sem=self.recv_sems.at[self.first_sem + step],
            device_id=self.place.across(self.order[step]),
            device_id_type=MESH_ID,
        )
        self.copies[step].start()

    def add(self, step):
        self.copies[step].wait_recv()
        mine = self.region(step, True)
        if step + 1 < len(self.order):
            self.own[mine] = self.own[mine] + self.received[step][...]
            return None
        return self.own[mine].astype(jnp.float32) + self.received[step][...].astype(jnp.float32)

    def close(self):
        for copy in self.copies.values():
            copy.wait_send()


def received_shapes(names, order, block):
    left = len(names)
    shapes = []
    for _ in order:
        left -= 1
        shapes.append((2,) * left + block)
    return shapes


def link_orders():
    wide = [("wide", bit) for bit in range(lax.axis_size("wide").bit_length() - 1)]
    narrow = [("narrow", bit) for bit in range(1, lax.axis_size("narrow").bit_length() - 1)]
    core = [("narrow", 0)]
    return {
        "y_x_z": core + narrow + wide,
        "x_y_z": core + wide[:1] + narrow + wide[1:],
        "x_z_y": core + wide + narrow,
        "y_z_x": core + narrow + wide[1:] + wide[:1],
    }


def reduce_all(*operands):
    arrays, flat = operands[:-1], operands[-1]
    names = axis_bits()
    steps = len(names)
    orders = link_orders()
    pieces = [(0, orders["y_x_z"]), (1, orders["x_y_z"]), (2, orders["x_z_y"]), (3, orders["y_z_x"])]
    count = len(pieces)
    blocks = [array.shape[-2:] for array in arrays]

    def kernel(*refs):
        sources, small = refs[:count], refs[count]
        outs, small_out = refs[count + 1 : 2 * count + 1], refs[2 * count + 1]
        rest = list(refs[2 * count + 2 :])
        owns = [rest.pop(0) for _ in range(count)]
        received = [[rest.pop(0) for _ in range(steps)] for _ in range(count)]
        small_sent, small_received = rest.pop(0), rest.pop(0)
        send_sems, recv_sems, local_sems = rest
        place = Place()
        place.greet()
        running = []
        local = []
        for number, (array, order) in enumerate(pieces):
            item = Halving(
                place, order, sources[array], owns[array], received[array], send_sems, recv_sems, number * steps
            )
            item.send(0)
            keep = item.region(0, True)
            copy = pltpu.make_async_copy(
                sources[array].at[keep], owns[array].at[keep], local_sems.at[number]
            )
            copy.start()
            running.append(item)
            local.append(copy)
        small_sent[0] = small[...]
        small_copies = []
        last_sem = count * steps
        for step in range(steps):
            copy = pltpu.make_async_remote_copy(
                src_ref=small_sent.at[step],
                dst_ref=small_received.at[step],
                send_sem=send_sems.at[last_sem + step],
                recv_sem=recv_sems.at[last_sem + step],
                device_id=place.across(orders["x_y_z"][step]),
                device_id_type=MESH_ID,
            )
            copy.start()
            small_copies.append(copy)
            for number, item in enumerate(running):
                if step == 0:
                    local[number].wait()
                total = item.add(step)
                if total is None:
                    item.send(step + 1)
                elif number < 2:
                    outs[number][...] = total
                else:
                    outs[number][place.bit["narrow", 0]] = total
            copy.wait_recv()
            if step + 1 < steps:
                small_sent[step + 1] = small_sent[step] + small_received[step]
            else:
                small_out[...] = small_sent[step] + small_received[step]
        swaps = []
        for slot, number in enumerate((2, 3)):
            mine = outs[number].at[place.bit["narrow", 0]]
            copy = pltpu.make_async_remote_copy(
                src_ref=mine,
                dst_ref=mine,
                send_sem=send_sems.at[last_sem + steps + slot],
                recv_sem=recv_sems.at[last_sem + steps + slot],
                device_id=place.across(("narrow", 0)),
                device_id_type=MESH_ID,
            )
            copy.start()
            swaps.append(copy)
        for copy in swaps:
            copy.wait()
        for item in running:
            item.close()
        for copy in small_copies:
            copy.wait_send()

    scratch = [pltpu.VMEM(array.shape, jnp.bfloat16) for array in arrays]
    for number, (array, order) in enumerate(pieces):
        scratch += [pltpu.VMEM(shape, jnp.bfloat16) for shape in received_shapes(names, order, blocks[array])]
    scratch += [pltpu.VMEM((steps,) + flat.shape, jnp.float32)] * 2
    sems = count * steps + steps + 2
    scratch += [pltpu.SemaphoreType.DMA((sems,)), pltpu.SemaphoreType.DMA((sems,)), pltpu.SemaphoreType.DMA((count,))]
    out_shape = [jax.ShapeDtypeStruct(blocks[0], jnp.float32), jax.ShapeDtypeStruct(blocks[1], jnp.float32)]
    out_shape += [jax.ShapeDtypeStruct((2,) + blocks[number], jnp.float32) for number in (2, 3)]
    out_shape += [jax.ShapeDtypeStruct(flat.shape, jnp.float32)]
    return pl.pallas_call(
        kernel,
        out_shape=out_shape,
        in_specs=[pl.BlockSpec(memory_space=pl.ANY)] * count + [pl.BlockSpec(memory_space=pltpu.VMEM)],
        out_specs=[pl.BlockSpec(memory_space=pltpu.VMEM)] * (count + 1),
        scratch_shapes=scratch,
        compiler_params=pltpu.CompilerParams(
            collective_id=0, has_side_effects=True, vmem_limit_bytes=60 << 20
        ),
        name="reduce_all",
    )(*operands)


def on_device_fast(
    tokens,
    doc_lengths,
    qkv_weight,
    query_bias,
    value_bias,
    out_weight,
    out_bias,
    first_gain,
    first_shift,
    up_weight,
    up_bias,
    down_weight,
    down_bias,
    second_gain,
    second_shift,
    dir_weight,
    dir_bias,
    segment_rows,
    segment_slots,
    pair_rows,
    pair_labels,
    out_cotangent,
):
    doc_count, length, model_width = tokens.shape
    score_scale = HEAD_DIM ** (-0.5)
    token_rows = tokens.reshape(doc_count * length, model_width)
    allowed = lax.broadcasted_iota(jnp.int32, (doc_count, length), 1) < doc_lengths[:, None]
    allowed_rows = allowed.reshape(-1, 1).astype(jnp.float32)
    bias_row = jnp.concatenate([query_bias, jnp.zeros_like(query_bias), value_bias]).astype(
        jnp.float32
    )
    qkv = (jnp.dot(token_rows, qkv_weight, preferred_element_type=jnp.float32) + bias_row).astype(
        jnp.bfloat16
    )

    def split_heads(doc_block, which):
        return doc_block[:, which * model_width : (which + 1) * model_width].reshape(
            length, HEADS, HEAD_DIM
        )

    def scores_of(queries, key_rows, doc_mask):
        scores = (
            jnp.einsum("qhd,khd->hqk", queries, key_rows, preferred_element_type=jnp.float32)
            * score_scale
        )
        return jnp.where(doc_mask[None, None, :], scores, MASKED)

    mixed_parts = []
    log_totals = []
    for doc_index in range(doc_count):
        doc_block = qkv[doc_index * length : (doc_index + 1) * length]
        queries = split_heads(doc_block, 0)
        key_rows = split_heads(doc_block, 1)
        value_rows = split_heads(doc_block, 2)
        scores = scores_of(queries, key_rows, allowed[doc_index])
        highest = jnp.max(scores, -1, keepdims=True)
        powers = jnp.exp(scores - highest)
        summed = jnp.sum(powers, -1, keepdims=True)
        attention = (powers / summed).astype(jnp.bfloat16)
        log_totals.append(highest + jnp.log(summed))
        mixed_parts.append(
            jnp.einsum(
                "hqk,khd->qhd", attention, value_rows, preferred_element_type=jnp.float32
            ).reshape(length, model_width)
        )
    mixed = jnp.concatenate(mixed_parts).astype(jnp.bfloat16)
    attended = jnp.dot(mixed, out_weight, preferred_element_type=jnp.float32) + out_bias.astype(
        jnp.float32
    )
    resid_one = token_rows.astype(jnp.float32) + attended
    hidden_one, normed_one, inverse_one = norm_forward(
        resid_one, first_gain.astype(jnp.float32), first_shift.astype(jnp.float32)
    )
    hidden_low = hidden_one.astype(jnp.bfloat16)
    upper_pre = jnp.dot(hidden_low, up_weight, preferred_element_type=jnp.float32) + up_bias.astype(
        jnp.float32
    )
    cumulative = normal_cdf(upper_pre)
    active = (upper_pre * cumulative).astype(jnp.bfloat16)
    lowered = jnp.dot(active, down_weight, preferred_element_type=jnp.float32) + down_bias.astype(
        jnp.float32
    )
    resid_two = hidden_one + lowered
    second_float = second_gain.astype(jnp.float32)
    normed_out, normed_two, inverse_two = norm_forward(
        resid_two, second_float, second_shift.astype(jnp.float32)
    )
    encoded_rows = (normed_out * allowed_rows).astype(jnp.bfloat16)
    doc_starts = lax.broadcasted_iota(jnp.int32, (doc_count, 1), 0) * length
    picked_rows = (segment_rows + doc_starts).reshape(-1)
    picked = encoded_rows[picked_rows]
    slots = segment_slots.reshape(-1)
    outgoing = jnp.zeros_like(picked).at[slots].set(picked)
    arrived = lax.all_to_all(outgoing, "wide", split_axis=0, concat_axis=0, tiled=True)
    pairs = pair_rows.reshape(-1, 2)
    labels = pair_labels.reshape(-1)
    first_rows = arrived[pairs[:, 0]]
    second_rows = arrived[pairs[:, 1]]
    logits = (
        jnp.dot(first_rows, dir_weight[:model_width], preferred_element_type=jnp.float32)
        + jnp.dot(second_rows, dir_weight[model_width:], preferred_element_type=jnp.float32)
        + dir_bias.astype(jnp.float32)
    )
    powers_head = jnp.exp(logits - jnp.max(logits, -1, keepdims=True))
    chance = powers_head / jnp.sum(powers_head, -1, keepdims=True)
    classes = lax.broadcasted_iota(jnp.int32, logits.shape, 1)
    delta = chance - (labels[:, None] == classes).astype(jnp.float32)
    first_float = first_rows.astype(jnp.float32)
    second_rows_float = second_rows.astype(jnp.float32)
    grad_dir_weight = jnp.concatenate(
        [
            jnp.dot(first_float.T, delta, precision=EXACT, preferred_element_type=jnp.float32),
            jnp.dot(
                second_rows_float.T, delta, precision=EXACT, preferred_element_type=jnp.float32
            ),
        ]
    )
    grad_dir_bias = jnp.sum(delta, 0)
    dir_float = dir_weight.astype(jnp.float32)
    grad_first = jnp.dot(
        delta, dir_float[:model_width].T, precision=EXACT, preferred_element_type=jnp.float32
    )
    grad_second = jnp.dot(
        delta, dir_float[model_width:].T, precision=EXACT, preferred_element_type=jnp.float32
    )
    grad_arrived = jnp.zeros((arrived.shape[0], model_width), jnp.float32)
    grad_arrived = grad_arrived.at[pairs[:, 0]].add(grad_first).at[pairs[:, 1]].add(grad_second)
    returned = lax.all_to_all(
        grad_arrived.astype(jnp.bfloat16), "wide", split_axis=0, concat_axis=0, tiled=True
    )
    grad_picked = returned[slots].astype(jnp.float32)
    grad_encoded = (
        out_cotangent.reshape(-1, model_width).astype(jnp.float32).at[picked_rows].add(grad_picked)
    )
    grad_encoded = grad_encoded * allowed_rows
    grad_two, grad_second_gain, grad_second_shift = norm_backward(
        grad_encoded, normed_two, inverse_two, second_float
    )
    grad_lowered = grad_two.astype(jnp.bfloat16)
    grad_down_weight = jnp.einsum(
        "rd,rf->df", grad_lowered, active, preferred_element_type=jnp.float32
    )
    grad_down_bias = jnp.sum(grad_lowered.astype(jnp.float32), 0)
    grad_active = jnp.einsum(
        "rd,fd->rf", grad_lowered, down_weight, preferred_element_type=jnp.float32
    )
    density = jnp.exp(-0.5 * upper_pre * upper_pre) * 0.3989422804014327
    grad_upper = (grad_active * (cumulative + upper_pre * density)).astype(jnp.bfloat16)
    grad_up_weight = jnp.einsum(
        "rd,rf->df", hidden_low, grad_upper, preferred_element_type=jnp.float32
    )
    grad_up_bias = jnp.sum(grad_upper.astype(jnp.float32), 0)
    grad_hidden = grad_two + jnp.einsum(
        "rf,df->rd", grad_upper, up_weight, preferred_element_type=jnp.float32
    )
    grad_one, grad_first_gain, grad_first_shift = norm_backward(
        grad_hidden, normed_one, inverse_one, first_gain.astype(jnp.float32)
    )
    grad_attended = grad_one.astype(jnp.bfloat16)
    grad_out_weight = jnp.einsum(
        "re,rd->ed", grad_attended, mixed, preferred_element_type=jnp.float32
    )
    grad_out_bias = jnp.sum(grad_attended.astype(jnp.float32), 0)
    grad_mixed = jnp.einsum(
        "re,de->rd", grad_attended, out_weight, preferred_element_type=jnp.float32
    ).astype(jnp.bfloat16)
    grad_parts = []
    for doc_index in range(doc_count):
        doc_block = qkv[doc_index * length : (doc_index + 1) * length]
        queries = split_heads(doc_block, 0)
        key_rows = split_heads(doc_block, 1)
        value_rows = split_heads(doc_block, 2)
        scores = scores_of(queries, key_rows, allowed[doc_index])
        attention = jnp.exp(scores - log_totals[doc_index])
        grad_doc = grad_mixed[doc_index * length : (doc_index + 1) * length].reshape(
            length, HEADS, HEAD_DIM
        )
        grad_chance = jnp.einsum(
            "qhd,khd->hqk", grad_doc, value_rows, preferred_element_type=jnp.float32
        )
        inner = jnp.sum(grad_chance * attention, -1, keepdims=True)
        grad_scores = (attention * (grad_chance - inner)).astype(jnp.bfloat16)
        grad_query = (
            jnp.einsum("hqk,khd->qhd", grad_scores, key_rows, preferred_element_type=jnp.float32)
            * score_scale
        )
        grad_key = (
            jnp.einsum("hqk,qhd->khd", grad_scores, queries, preferred_element_type=jnp.float32)
            * score_scale
        )
        grad_value = jnp.einsum(
            "hqk,qhd->khd",
            attention.astype(jnp.bfloat16),
            grad_doc,
            preferred_element_type=jnp.float32,
        )
        grad_parts.append(
            jnp.concatenate(
                [
                    grad_query.reshape(length, model_width),
                    grad_key.reshape(length, model_width),
                    grad_value.reshape(length, model_width),
                ],
                axis=1,
            )
        )
    grad_qkv = jnp.concatenate(grad_parts).astype(jnp.bfloat16)
    grad_qkv_float = grad_qkv.astype(jnp.float32)
    grad_query_bias = jnp.sum(grad_qkv_float[:, :model_width], 0)
    grad_value_bias = jnp.sum(grad_qkv_float[:, 2 * model_width :], 0)
    grad_qkv_weight = jnp.einsum(
        "re,rd->ed", grad_qkv, token_rows, preferred_element_type=jnp.float32
    )
    grad_tokens = (
        jnp.einsum("re,de->rd", grad_qkv, qkv_weight, preferred_element_type=jnp.float32) + grad_one
    ).astype(jnp.bfloat16)
    wide, narrow = lax.axis_size("wide"), lax.axis_size("narrow")
    ff = up_weight.shape[1]
    bits = (2,) * (wide.bit_length() - 1 + narrow.bit_length() - 1)
    half = narrow // 2

    def low(values):
        return values.astype(jnp.bfloat16)

    blocks_down = low(grad_down_weight).reshape(wide, model_width // wide, narrow, ff // narrow)
    blocks_down = blocks_down.transpose(0, 2, 1, 3).reshape(bits + (model_width // wide, ff // narrow))
    blocks_up = low(grad_up_weight).reshape(narrow, model_width // narrow, wide, ff // wide)
    blocks_up = blocks_up.transpose(2, 0, 1, 3).reshape(bits + (model_width // narrow, ff // wide))

    def by_row_half(matrix):
        rows = matrix.shape[0] // wide // 2
        blocks = low(matrix).reshape(wide, 2, rows, half, model_width // half)
        return blocks.transpose(0, 3, 1, 2, 4).reshape(bits + (rows, model_width // half))

    smalls_in = (
        grad_query_bias,
        grad_value_bias,
        grad_out_bias,
        grad_first_gain,
        grad_first_shift,
        grad_up_bias,
        grad_down_bias,
        grad_second_gain,
        grad_second_shift,
        grad_dir_weight,
        grad_dir_bias,
    )
    sizes = [item.size for item in smalls_in]
    flat = jnp.concatenate([item.reshape(-1) for item in smalls_in])
    flat = jnp.pad(flat, (0, -flat.size % 1024)).reshape(-1, 128)
    out_down, out_up, out_qkv, out_out, flat = reduce_all(
        blocks_down, blocks_up, by_row_half(grad_qkv_weight), by_row_half(grad_out_weight), flat
    )
    flat = flat.reshape(-1)
    smalls = []
    start = 0
    for item, size in zip(smalls_in, sizes):
        smalls.append(flat[start : start + size].reshape(item.shape))
        start += size
    core = lax.axis_index("narrow") % 2
    width = model_width // narrow

    def own_lanes(halves):
        rows = halves.reshape(-1, halves.shape[-1])
        return lax.dynamic_slice_in_dim(rows, core * width, width, 1).T

    return (
        encoded_rows.reshape(tokens.shape),
        grad_tokens.reshape(tokens.shape),
        own_lanes(out_qkv),
        smalls[0],
        smalls[1],
        own_lanes(out_out),
        smalls[2],
        smalls[3],
        smalls[4],
        out_up,
        smalls[5],
        out_down.T,
        smalls[6],
        smalls[7],
        smalls[8],
        smalls[9],
        smalls[10],
    )


def on_device(
    tokens,
    doc_lengths,
    qkv_weight,
    query_bias,
    value_bias,
    out_weight,
    out_bias,
    first_gain,
    first_shift,
    up_weight,
    up_bias,
    down_weight,
    down_bias,
    second_gain,
    second_shift,
    dir_weight,
    dir_bias,
    segment_rows,
    segment_slots,
    pair_rows,
    pair_labels,
    out_cotangent,
):
    doc_count, length, model_width = tokens.shape
    score_scale = HEAD_DIM ** (-0.5)
    token_rows = tokens.reshape(doc_count * length, model_width)
    allowed = lax.broadcasted_iota(jnp.int32, (doc_count, length), 1) < doc_lengths[:, None]
    allowed_rows = allowed.reshape(-1, 1).astype(jnp.float32)
    bias_row = jnp.concatenate([query_bias, jnp.zeros_like(query_bias), value_bias]).astype(
        jnp.float32
    )
    qkv = (jnp.dot(token_rows, qkv_weight, preferred_element_type=jnp.float32) + bias_row).astype(
        jnp.bfloat16
    )

    def split_heads(doc_block, which):
        return doc_block[:, which * model_width : (which + 1) * model_width].reshape(
            length, HEADS, HEAD_DIM
        )

    def scores_of(queries, key_rows, doc_mask):
        scores = (
            jnp.einsum("qhd,khd->hqk", queries, key_rows, preferred_element_type=jnp.float32)
            * score_scale
        )
        return jnp.where(doc_mask[None, None, :], scores, MASKED)

    mixed_parts = []
    log_totals = []
    for doc_index in range(doc_count):
        doc_block = qkv[doc_index * length : (doc_index + 1) * length]
        queries = split_heads(doc_block, 0)
        key_rows = split_heads(doc_block, 1)
        value_rows = split_heads(doc_block, 2)
        scores = scores_of(queries, key_rows, allowed[doc_index])
        highest = jnp.max(scores, -1, keepdims=True)
        powers = jnp.exp(scores - highest)
        summed = jnp.sum(powers, -1, keepdims=True)
        attention = (powers / summed).astype(jnp.bfloat16)
        log_totals.append(highest + jnp.log(summed))
        mixed_parts.append(
            jnp.einsum(
                "hqk,khd->qhd", attention, value_rows, preferred_element_type=jnp.float32
            ).reshape(length, model_width)
        )
    mixed = jnp.concatenate(mixed_parts).astype(jnp.bfloat16)
    attended = jnp.dot(mixed, out_weight, preferred_element_type=jnp.float32) + out_bias.astype(
        jnp.float32
    )
    resid_one = token_rows.astype(jnp.float32) + attended
    hidden_one, normed_one, inverse_one = norm_forward(
        resid_one, first_gain.astype(jnp.float32), first_shift.astype(jnp.float32)
    )
    hidden_low = hidden_one.astype(jnp.bfloat16)
    upper_pre = jnp.dot(hidden_low, up_weight, preferred_element_type=jnp.float32) + up_bias.astype(
        jnp.float32
    )
    cumulative = normal_cdf(upper_pre)
    active = (upper_pre * cumulative).astype(jnp.bfloat16)
    lowered = jnp.dot(active, down_weight, preferred_element_type=jnp.float32) + down_bias.astype(
        jnp.float32
    )
    resid_two = hidden_one + lowered
    second_float = second_gain.astype(jnp.float32)
    normed_out, normed_two, inverse_two = norm_forward(
        resid_two, second_float, second_shift.astype(jnp.float32)
    )
    encoded_rows = (normed_out * allowed_rows).astype(jnp.bfloat16)
    doc_starts = lax.broadcasted_iota(jnp.int32, (doc_count, 1), 0) * length
    picked_rows = (segment_rows + doc_starts).reshape(-1)
    picked = encoded_rows[picked_rows]
    slots = segment_slots.reshape(-1)
    outgoing = jnp.zeros_like(picked).at[slots].set(picked)
    arrived = lax.all_to_all(outgoing, "wide", split_axis=0, concat_axis=0, tiled=True)
    pairs = pair_rows.reshape(-1, 2)
    labels = pair_labels.reshape(-1)
    first_rows = arrived[pairs[:, 0]]
    second_rows = arrived[pairs[:, 1]]
    logits = (
        jnp.dot(first_rows, dir_weight[:model_width], preferred_element_type=jnp.float32)
        + jnp.dot(second_rows, dir_weight[model_width:], preferred_element_type=jnp.float32)
        + dir_bias.astype(jnp.float32)
    )
    powers_head = jnp.exp(logits - jnp.max(logits, -1, keepdims=True))
    chance = powers_head / jnp.sum(powers_head, -1, keepdims=True)
    classes = lax.broadcasted_iota(jnp.int32, logits.shape, 1)
    delta = chance - (labels[:, None] == classes).astype(jnp.float32)
    first_float = first_rows.astype(jnp.float32)
    second_rows_float = second_rows.astype(jnp.float32)
    grad_dir_weight = jnp.concatenate(
        [
            jnp.dot(first_float.T, delta, precision=EXACT, preferred_element_type=jnp.float32),
            jnp.dot(
                second_rows_float.T, delta, precision=EXACT, preferred_element_type=jnp.float32
            ),
        ]
    )
    grad_dir_bias = jnp.sum(delta, 0)
    dir_float = dir_weight.astype(jnp.float32)
    grad_first = jnp.dot(
        delta, dir_float[:model_width].T, precision=EXACT, preferred_element_type=jnp.float32
    )
    grad_second = jnp.dot(
        delta, dir_float[model_width:].T, precision=EXACT, preferred_element_type=jnp.float32
    )
    grad_arrived = jnp.zeros((arrived.shape[0], model_width), jnp.float32)
    grad_arrived = grad_arrived.at[pairs[:, 0]].add(grad_first).at[pairs[:, 1]].add(grad_second)
    returned = lax.all_to_all(
        grad_arrived.astype(jnp.bfloat16), "wide", split_axis=0, concat_axis=0, tiled=True
    )
    grad_picked = returned[slots].astype(jnp.float32)
    grad_encoded = (
        out_cotangent.reshape(-1, model_width).astype(jnp.float32).at[picked_rows].add(grad_picked)
    )
    grad_encoded = grad_encoded * allowed_rows
    grad_two, grad_second_gain, grad_second_shift = norm_backward(
        grad_encoded, normed_two, inverse_two, second_float
    )
    grad_lowered = grad_two.astype(jnp.bfloat16)
    grad_down_weight = jnp.einsum(
        "rf,rd->fd", active, grad_lowered, preferred_element_type=jnp.float32
    )
    grad_down_bias = jnp.sum(grad_lowered.astype(jnp.float32), 0)
    grad_active = jnp.einsum(
        "rd,fd->rf", grad_lowered, down_weight, preferred_element_type=jnp.float32
    )
    density = jnp.exp(-0.5 * upper_pre * upper_pre) * 0.3989422804014327
    grad_upper = (grad_active * (cumulative + upper_pre * density)).astype(jnp.bfloat16)
    grad_up_weight = jnp.einsum(
        "rd,rf->df", hidden_low, grad_upper, preferred_element_type=jnp.float32
    )
    grad_up_bias = jnp.sum(grad_upper.astype(jnp.float32), 0)
    grad_hidden = grad_two + jnp.einsum(
        "rf,df->rd", grad_upper, up_weight, preferred_element_type=jnp.float32
    )
    grad_one, grad_first_gain, grad_first_shift = norm_backward(
        grad_hidden, normed_one, inverse_one, first_gain.astype(jnp.float32)
    )
    grad_attended = grad_one.astype(jnp.bfloat16)
    grad_out_weight = jnp.einsum(
        "rd,re->de", mixed, grad_attended, preferred_element_type=jnp.float32
    )
    grad_out_bias = jnp.sum(grad_attended.astype(jnp.float32), 0)
    grad_mixed = jnp.einsum(
        "re,de->rd", grad_attended, out_weight, preferred_element_type=jnp.float32
    ).astype(jnp.bfloat16)
    grad_parts = []
    for doc_index in range(doc_count):
        doc_block = qkv[doc_index * length : (doc_index + 1) * length]
        queries = split_heads(doc_block, 0)
        key_rows = split_heads(doc_block, 1)
        value_rows = split_heads(doc_block, 2)
        scores = scores_of(queries, key_rows, allowed[doc_index])
        attention = jnp.exp(scores - log_totals[doc_index])
        grad_doc = grad_mixed[doc_index * length : (doc_index + 1) * length].reshape(
            length, HEADS, HEAD_DIM
        )
        grad_chance = jnp.einsum(
            "qhd,khd->hqk", grad_doc, value_rows, preferred_element_type=jnp.float32
        )
        inner = jnp.sum(grad_chance * attention, -1, keepdims=True)
        grad_scores = (attention * (grad_chance - inner)).astype(jnp.bfloat16)
        grad_query = (
            jnp.einsum("hqk,khd->qhd", grad_scores, key_rows, preferred_element_type=jnp.float32)
            * score_scale
        )
        grad_key = (
            jnp.einsum("hqk,qhd->khd", grad_scores, queries, preferred_element_type=jnp.float32)
            * score_scale
        )
        grad_value = jnp.einsum(
            "hqk,qhd->khd",
            attention.astype(jnp.bfloat16),
            grad_doc,
            preferred_element_type=jnp.float32,
        )
        grad_parts.append(
            jnp.concatenate(
                [
                    grad_query.reshape(length, model_width),
                    grad_key.reshape(length, model_width),
                    grad_value.reshape(length, model_width),
                ],
                axis=1,
            )
        )
    grad_qkv = jnp.concatenate(grad_parts).astype(jnp.bfloat16)
    grad_qkv_float = grad_qkv.astype(jnp.float32)
    grad_query_bias = jnp.sum(grad_qkv_float[:, :model_width], 0)
    grad_value_bias = jnp.sum(grad_qkv_float[:, 2 * model_width :], 0)
    grad_qkv_weight = jnp.einsum(
        "rd,re->de", token_rows, grad_qkv, preferred_element_type=jnp.float32
    )
    grad_tokens = (
        jnp.einsum("re,de->rd", grad_qkv, qkv_weight, preferred_element_type=jnp.float32) + grad_one
    ).astype(jnp.bfloat16)
    matrices = (grad_qkv_weight, grad_out_weight, grad_up_weight, grad_down_weight)
    partial_sums = (
        lax.psum_scatter(
            matrices[0].astype(jnp.bfloat16), "wide", scatter_dimension=1, tiled=True
        ).astype(jnp.float32),
        lax.psum_scatter(
            matrices[1].astype(jnp.bfloat16), "wide", scatter_dimension=1, tiled=True
        ).astype(jnp.float32),
        lax.psum_scatter(
            matrices[2].astype(jnp.bfloat16), "wide", scatter_dimension=1, tiled=True
        ).astype(jnp.float32),
        lax.psum_scatter(
            matrices[3].astype(jnp.bfloat16), "wide", scatter_dimension=1, tiled=True
        ).astype(jnp.float32),
    )
    summed_mats = (
        lax.psum_scatter(
            partial_sums[0].astype(jnp.bfloat16), "narrow", scatter_dimension=0, tiled=True
        ).astype(jnp.float32),
        lax.psum_scatter(
            partial_sums[1].astype(jnp.bfloat16), "narrow", scatter_dimension=0, tiled=True
        ).astype(jnp.float32),
        lax.psum_scatter(
            partial_sums[2].astype(jnp.bfloat16), "narrow", scatter_dimension=0, tiled=True
        ).astype(jnp.float32),
        lax.psum_scatter(
            partial_sums[3].astype(jnp.bfloat16), "narrow", scatter_dimension=0, tiled=True
        ).astype(jnp.float32),
    )
    smalls = lax.psum(
        (
            grad_query_bias,
            grad_value_bias,
            grad_out_bias,
            grad_first_gain,
            grad_first_shift,
            grad_up_bias,
            grad_down_bias,
            grad_second_gain,
            grad_second_shift,
            grad_dir_weight,
            grad_dir_bias,
        ),
        ("wide", "narrow"),
    )
    return (
        encoded_rows.reshape(tokens.shape),
        grad_tokens.reshape(tokens.shape),
        summed_mats[0],
        smalls[0],
        smalls[1],
        summed_mats[1],
        smalls[2],
        smalls[3],
        smalls[4],
        summed_mats[2],
        smalls[5],
        summed_mats[3],
        smalls[6],
        smalls[7],
        smalls[8],
        smalls[9],
        smalls[10],
    )


def fits_blocks(mesh):
    wide, narrow = mesh.shape["wide"], mesh.shape["narrow"]
    width, ff = HEADS * HEAD_DIM, 4 * HEADS * HEAD_DIM
    if narrow % 2 or wide & (wide - 1) or narrow & (narrow - 1):
        return False
    lanes = (ff // narrow, ff // wide, 2 * width // narrow)
    rows = (width // wide, width // narrow, width // wide // 2, 3 * width // wide // 2)
    return all(size % 128 == 0 for size in lanes) and all(size % 16 == 0 for size in rows)


def solution(mesh):
    placed = (
        P(("wide", "narrow"), None, None),
        P(("wide", "narrow")),
        P(),
        P(),
        P(),
        P(),
        P(),
        P(),
        P(),
        P(),
        P(),
        P(),
        P(),
        P(),
        P(),
        P(),
        P(),
        P(("wide", "narrow"), None),
        P(("wide", "narrow"), None),
        P(("wide", "narrow"), None, None),
        P(("wide", "narrow"), None),
        P(("wide", "narrow"), None, None),
    )
    return jax.shard_map(
        on_device_fast if fits_blocks(mesh) else on_device,
        mesh=mesh,
        in_specs=placed,
        out_specs=(
            P(("wide", "narrow"), None, None),
            P(("wide", "narrow"), None, None),
            P("narrow", "wide"),
            P(),
            P(),
            P("narrow", "wide"),
            P(),
            P(),
            P(),
            P("narrow", "wide"),
            P(),
            P("narrow", "wide"),
            P(),
            P(),
            P(),
            P(),
            P(),
        ),
        check_vma=False,
    )
```

```python
import jax
import jax.numpy as jnp
from jax import lax
from jax.experimental import pallas as pl
from jax.experimental.pallas import tpu as pltpu
from jax.sharding import PartitionSpec as P

HEADS = 12
HEAD_DIM = 64


EXACT = lax.Precision.HIGHEST
MASKED = -1e30
EPSILON = 1e-05


def norm_forward(values, gain, shift):
    center = jnp.mean(values, -1, keepdims=True)
    centered = values - center
    inverse = lax.rsqrt(jnp.mean(centered * centered, -1, keepdims=True) + EPSILON)
    normed = centered * inverse
    return (normed * gain + shift, normed, inverse)


def norm_backward(grad, normed, inverse, gain):
    scaled = grad * gain
    first_mean = jnp.mean(scaled, -1, keepdims=True)
    second_mean = jnp.mean(scaled * normed, -1, keepdims=True)
    return (
        (scaled - first_mean - normed * second_mean) * inverse,
        jnp.sum(grad * normed, 0),
        jnp.sum(grad, 0),
    )


def normal_cdf(values):
    return 0.5 * (1.0 + lax.erf(values * 0.7071067811865476))


MESH_ID = pl.DeviceIdType.MESH


def axis_bits():
    names = []
    for axis in ("wide", "narrow"):
        count = lax.axis_size(axis).bit_length() - 1
        names += [(axis, bit) for bit in reversed(range(count))]
    return names


class Place:
    def __init__(self):
        self.index = {axis: lax.axis_index(axis) for axis in ("wide", "narrow")}
        self.names = axis_bits()
        self.bit = {name: (self.index[name[0]] // (1 << name[1])) % 2 for name in self.names}

    def across(self, name):
        axis, bit = name
        target = dict(self.index)
        target[axis] = target[axis] + (1 << bit) - (2 << bit) * self.bit[name]
        return target

    def greet(self):
        barrier = pltpu.get_barrier_semaphore()
        for name in self.names:
            pl.semaphore_signal(barrier, inc=1, device_id=self.across(name), device_id_type=MESH_ID)
        pl.semaphore_wait(barrier, len(self.names))


class Halving:
    def __init__(self, place, order, source, own, received, send_sems, recv_sems, first_sem):
        self.place, self.order = place, order
        self.source, self.own, self.received = source, own, received
        self.send_sems, self.recv_sems, self.first_sem = send_sems, recv_sems, first_sem

    def region(self, step, mine):
        index = []
        for name in self.place.names:
            if name in self.order[:step]:
                index.append(self.place.bit[name])
            elif name == self.order[step]:
                index.append(self.place.bit[name] if mine else 1 - self.place.bit[name])
            else:
                index.append(slice(None))
        return tuple(index)

    def copy(self, step):
        held = self.source if step == 0 else self.own
        return pltpu.make_async_remote_copy(
            src_ref=held.at[self.region(step, False)],
            dst_ref=self.received[step],
            send_sem=self.send_sems.at[self.first_sem + step],
            recv_sem=self.recv_sems.at[self.first_sem + step],
            device_id=self.place.across(self.order[step]),
            device_id_type=MESH_ID,
        )

    def send(self, step):
        self.copy(step).start()

    def add(self, step):
        self.copy(step).wait_recv()
        mine = self.region(step, True)
        if step + 1 < len(self.order):
            self.own[mine] = self.own[mine] + self.received[step][...]
            return None
        return self.own[mine].astype(jnp.float32) + self.received[step][...].astype(jnp.float32)

    def close(self):
        for step in range(len(self.order)):
            self.copy(step).wait_send()


def link_orders():
    wide = [("wide", bit) for bit in range(lax.axis_size("wide").bit_length() - 1)]
    narrow = [("narrow", bit) for bit in range(1, lax.axis_size("narrow").bit_length() - 1)]
    core = [("narrow", 0)]
    return {
        "y_x_z": core + narrow + wide,
        "x_y_z": core + wide[:1] + narrow + wide[1:],
        "x_z_y": core + wide + narrow,
        "y_z_x": core + narrow + wide[1:] + wide[:1],
    }


def attention_forward(qkv, key_bias, docs, length):
    width = qkv.shape[1] // 3
    pairs = width // 128

    def kernel(q_ref, k_ref, v_ref, bias_ref, mixed_ref, total_ref):
        lane = lax.broadcasted_iota(jnp.int32, (1, 128), 1)
        keys, values = k_ref[...], v_ref[...]
        queries = q_ref[...] * jnp.bfloat16(HEAD_DIM**-0.5)
        results = []
        for head in range(2):
            inside = (lane // HEAD_DIM) == head
            masked = jnp.where(inside, queries, jnp.zeros_like(queries))
            scores = dot_last(masked, keys) + bias_ref[0]
            highest = jnp.max(scores, -1, keepdims=True)
            powers = jnp.exp(scores - highest)
            summed = jnp.sum(powers, -1, keepdims=True)
            out = jnp.dot(powers.astype(jnp.bfloat16), values, preferred_element_type=jnp.float32)
            results.append((out / summed, highest + jnp.log(summed)))
        first = lane < HEAD_DIM
        mixed_ref[...] = jnp.where(first, results[0][0], results[1][0]).astype(jnp.bfloat16)
        total_ref[...] = jnp.where(first, results[0][1], results[1][1])

    def block(which):
        return pl.BlockSpec((length, 128), lambda doc, pair: (doc, which * pairs + pair))

    rows = docs * length
    return pl.pallas_call(
        kernel,
        grid=(docs, pairs),
        in_specs=[block(0), block(1), block(2), pl.BlockSpec((1, 1, length), lambda doc, pair: (doc, 0, 0))],
        out_specs=[block(0), block(0)],
        out_shape=[
            jax.ShapeDtypeStruct((rows, width), jnp.bfloat16),
            jax.ShapeDtypeStruct((rows, width), jnp.float32),
        ],
        compiler_params=pltpu.CompilerParams(vmem_limit_bytes=48 << 20),
        name="attention_forward",
    )(qkv, qkv, qkv, key_bias)


def dot_last(left, right):
    return lax.dot_general(left, right, (((1,), (1,)), ((), ())), preferred_element_type=jnp.float32)


def norm_back_rows(grad, normed, inverse, gain):
    scaled = grad * gain
    first = jnp.mean(scaled, -1, keepdims=True)
    second = jnp.mean(scaled * normed, -1, keepdims=True)
    return (scaled - first - normed * second) * inverse


def ffn_backward(grad_encoded, normed_two, inverse_two, second_gain, active, slope, hidden_low, down_weight, up_weight,
                 normed_one, inverse_one, first_gain):
    rows, width = hidden_low.shape
    ff = active.shape[1]
    names = axis_bits()
    steps = len(names)
    wide, narrow = lax.axis_size("wide"), lax.axis_size("narrow")
    wide_bits, narrow_bits = wide.bit_length() - 1, narrow.bit_length() - 1
    chunks = ff // narrow // 128
    third = chunks // 2
    d_rows, u_rows = width // wide, width // narrow
    row_block = 128
    row_steps = rows // row_block
    orders = link_orders()
    two = (2,)

    def chunk_of(step):
        step = jnp.clip(step, 0, chunks - 1)
        return step // 2 + third * (step % 2)

    def bits_of(number, count):
        return tuple((number >> bit) & 1 for bit in reversed(range(count)))

    def kernel(*refs):
        (ge, n2, q2, gain2, n1, q1, gain1, hidden) = refs[:8]
        act = refs[8 : 8 + narrow]
        slo = refs[8 + narrow : 8 + 2 * narrow]
        dws = refs[8 + 2 * narrow : 8 + 3 * narrow]
        uws = refs[8 + 3 * narrow : 8 + 4 * narrow]
        rest = list(refs[8 + 4 * narrow :])
        ga_out, up_out, down_out, sums_out, upb_out = rest[:5]
        rest = rest[5:]
        grad_hidden, lowered, lowered_t, hidden_t, upper, own = rest[:6]
        received = rest[6 : 6 + steps]
        send_sems, recv_sems = rest[6 + steps :]
        pid = pl.program_id(0)
        place = Place()
        pieces = []
        for number in range(chunks):
            order = orders["y_x_z"] if number % 2 == 0 else orders["x_y_z"]
            pieces.append(
                Halving(place, order, own.at[number], own.at[number], [r.at[number] for r in received],
                        send_sems, recv_sems, number * steps)
            )

        @pl.when(pid == 0)
        def _():
            place.greet()
            sums_out[...] = jnp.zeros_like(sums_out)

            def body(i, carry):
                at = pl.multiple_of(i * row_block, row_block)
                some = pl.ds(at, row_block)
                grad, normed = ge[some, :], n2[some, :].astype(jnp.float32)
                two = norm_back_rows(grad, normed, q2[some, :], gain2[...])
                low = two.astype(jnp.bfloat16)
                grad_hidden[some, :] = two
                lowered[some, :] = low
                lowered_t[:, some] = low.T
                hidden_t[:, some] = hidden[some, :].T
                sums_out[0:1, :] += jnp.sum(grad * normed, 0, keepdims=True)
                sums_out[1:2, :] += jnp.sum(grad, 0, keepdims=True)
                sums_out[2:3, :] += jnp.sum(low.astype(jnp.float32), 0, keepdims=True)
                return carry

            lax.fori_loop(0, row_steps, body, 0)

        @pl.when(pid < chunks)
        def _():
            actives = jnp.concatenate([ref[...] for ref in act], axis=1)
            result = jnp.dot(lowered_t[...], actives, preferred_element_type=jnp.float32).astype(jnp.bfloat16)
            for w in range(wide):
                for n in range(narrow):
                    own[(pid,) + bits_of(w, wide_bits) + bits_of(n, narrow_bits)] = result[
                        w * d_rows : (w + 1) * d_rows, n * 128 : (n + 1) * 128
                    ]

        @pl.when(pid >= chunks)
        def _():
            slopes = [ref[...] for ref in slo]
            downs = jnp.concatenate([ref[...] for ref in dws], axis=0)
            ups = jnp.concatenate([ref[...] for ref in uws], axis=1)
            block = 256
            total = jnp.zeros((1, narrow * 128), jnp.float32)
            for i in range(rows // block):
                some = slice(i * block, (i + 1) * block)
                grad_active = dot_last(lowered[some, :], downs)
                slope_rows = jnp.concatenate([s[some] for s in slopes], axis=1)
                grad_upper = (grad_active * slope_rows.astype(jnp.float32)).astype(jnp.bfloat16)
                total += jnp.sum(grad_upper.astype(jnp.float32), 0, keepdims=True)
                upper[some, :] = grad_upper
                grad_hidden[some, :] += dot_last(grad_upper, ups)
            upb_out[0] = total
            result = jnp.dot(hidden_t[...], upper[...], preferred_element_type=jnp.float32).astype(jnp.bfloat16)
            for n in range(narrow):
                for z in range(narrow):
                    high = bits_of(z, wide_bits - 1)
                    up_out[(0,) + high + (0,) + bits_of(n, narrow_bits)] = result[
                        n * u_rows : (n + 1) * u_rows, z * 128 : (z + 1) * 128
                    ]

        def advance(number, step):
            item = pieces[number]
            total = item.add(step)
            if total is None:
                item.send(step + 1)
            else:
                j = number // 2 + third * (number % 2)
                down_out[:, j * 128 : (j + 1) * 128] = total

        @pl.when(pid == 2 * chunks - 1)
        def _():
            def body(i, carry):
                at = pl.multiple_of(i * row_block, row_block)
                some = pl.ds(at, row_block)
                grad, normed = grad_hidden[some, :], n1[some, :].astype(jnp.float32)
                low = norm_back_rows(grad, normed, q1[some, :], gain1[...]).astype(jnp.bfloat16)
                ga_out[some, :] = low
                sums_out[3:4, :] += jnp.sum(grad * normed, 0, keepdims=True)
                sums_out[4:5, :] += jnp.sum(grad, 0, keepdims=True)
                sums_out[5:6, :] += jnp.sum(low.astype(jnp.float32), 0, keepdims=True)
                return carry

            lax.fori_loop(0, row_steps, body, 0)

        plan = {}
        for number in range(chunks):
            for step in range(steps):
                at = number + 1 if step == 0 else chunks + number // 2 + step
                plan.setdefault(min(at, 2 * chunks - 1), []).append((step, number))
        for at in range(2 * chunks):
            @pl.when(pid == at)
            def _():
                if at < chunks:
                    pieces[at].send(0)
                for step, number in sorted(plan.get(at, [])):
                    advance(number, step)
                if at == 2 * chunks - 1:
                    for item in pieces:
                        item.close()

    def whole(shape):
        return pl.BlockSpec(shape, lambda g: (0,) * len(shape), pipeline_mode=pl.Buffered(1))

    def slab_columns(shape, first):
        return [pl.BlockSpec(shape, lambda g, n=n: (0, n * chunks + chunk_of(g - first))) for n in range(narrow)]

    in_specs = [whole((rows, width)), whole((rows, width)), whole((rows, 1)), whole((1, width))]
    in_specs += [whole((rows, width)), whole((rows, 1)), whole((1, width)), whole((rows, width))]
    in_specs += slab_columns((rows, 128), 0) + slab_columns((rows, 128), chunks)
    in_specs += [pl.BlockSpec((128, width), lambda g, n=n: (n * chunks + chunk_of(g - chunks), 0)) for n in range(narrow)]
    in_specs += slab_columns((width, 128), chunks)
    high = two * (wide_bits - 1)
    low = two * narrow_bits
    up_shape = (third,) + high + (2,) + low + (u_rows, 128)
    zeros = (0,) * len(high)
    out_specs = [
        whole((rows, width)),
        pl.BlockSpec(
            (1,) + high + (1,) + low + (u_rows, 128),
            lambda g: (jnp.clip(g - chunks, 0, chunks - 1) // 2,) + zeros + (jnp.clip(g - chunks, 0, chunks - 1) % 2,)
            + (0,) * (narrow_bits + 2),
        ),
        whole((d_rows, chunks * 128)),
        whole((8, width)),
        pl.BlockSpec((1, 1, narrow * 128), lambda g: (chunk_of(g - chunks), 0, 0)),
    ]
    out_shape = [
        jax.ShapeDtypeStruct((rows, width), jnp.bfloat16),
        jax.ShapeDtypeStruct(up_shape, jnp.bfloat16),
        jax.ShapeDtypeStruct((d_rows, chunks * 128), jnp.float32),
        jax.ShapeDtypeStruct((8, width), jnp.float32),
        jax.ShapeDtypeStruct((chunks, 1, narrow * 128), jnp.float32),
    ]
    scratch = [
        pltpu.VMEM((rows, width), jnp.float32),
        pltpu.VMEM((rows, width), jnp.bfloat16),
        pltpu.VMEM((width, rows), jnp.bfloat16),
        pltpu.VMEM((width, rows), jnp.bfloat16),
        pltpu.VMEM((rows, narrow * 128), jnp.bfloat16),
        pltpu.VMEM((chunks,) + two * steps + (d_rows, 128), jnp.bfloat16),
    ]
    scratch += [pltpu.VMEM((chunks,) + two * (steps - 1 - s) + (d_rows, 128), jnp.bfloat16) for s in range(steps)]
    scratch += [pltpu.SemaphoreType.DMA((chunks * steps,)), pltpu.SemaphoreType.DMA((chunks * steps,))]
    return pl.pallas_call(
        kernel,
        grid=(2 * chunks,),
        in_specs=in_specs,
        out_specs=out_specs,
        out_shape=out_shape,
        scratch_shapes=scratch,
        compiler_params=pltpu.CompilerParams(collective_id=0, has_side_effects=True, vmem_limit_bytes=58 << 20),
        name="ffn_backward",
    )(grad_encoded, normed_two, inverse_two, second_gain, normed_one, inverse_one, first_gain, hidden_low,
      *([active] * narrow), *([slope] * narrow), *([down_weight] * narrow), *([up_weight] * narrow))


def attention_backward(grad_attended, mixed, out_weight, qkv, totals, key_bias, tokens, qkv_weight, up_grads, sums):
    rows, width = tokens.shape
    docs, _, length = key_bias.shape
    pairs = width // 128
    names = axis_bits()
    steps = len(names)
    wide, narrow = lax.axis_size("wide"), lax.axis_size("narrow")
    wide_bits, narrow_bits = wide.bit_length() - 1, narrow.bit_length() - 1
    half = narrow // 2
    half_bits = narrow_bits - 1
    lanes = width // half
    q_rows, o_rows = 3 * width // wide // 2, width // wide // 2
    q_parts = lanes // 128
    orders = link_orders()
    ups = up_grads.shape[0]
    u_rows = up_grads.shape[-2]
    attn_steps = docs * pairs
    token_block = 256
    token_steps = rows // token_block
    first_q = 1 + attn_steps
    first_t = first_q + q_parts
    grid = first_t + token_steps
    count = ups + 1 + q_parts
    small_rows = sums.shape[0]

    def bits_of(number, count):
        return tuple((number >> bit) & 1 for bit in reversed(range(count)))

    def kernel(*refs):
        (ga, mix, ow, q_ref, k_ref, v_ref, tot_ref, bias, tok, qw, up_hbm, small) = refs[:12]
        tokens_out, up_out, out_out, qkv_out, small_out, late_out = refs[12:18]
        rest = list(refs[18:])
        gm, mix_pair, gqkv_t, up_own, out_own, qkv_own = rest[:6]
        rest = rest[6:]
        up_received, out_received, qkv_received = rest[:steps], rest[steps : 2 * steps], rest[2 * steps : 3 * steps]
        small_sent, small_received, late_sent, late_received = rest[3 * steps : 3 * steps + 4]
        swap_out, swap_qkv, send_sems, recv_sems, local_sems = rest[3 * steps + 4 :]
        pid = pl.program_id(0)
        place = Place()
        core = place.bit["narrow", 0]
        pieces = []
        cycle = ["y_x_z", "x_y_z", "y_z_x", "x_z_y"]
        for number in range(ups):
            pieces.append(Halving(place, orders[cycle[number % 3]], up_hbm.at[number], up_own.at[number],
                                  [r.at[number] for r in up_received], send_sems, recv_sems, number * steps))
        pieces.append(Halving(place, orders["x_z_y"], out_own, out_own, out_received, send_sems, recv_sems, ups * steps))
        for number in range(q_parts):
            pieces.append(Halving(place, orders[cycle[(number + 1) % 3]], qkv_own.at[number], qkv_own.at[number],
                                  [r.at[number] for r in qkv_received], send_sems, recv_sems, (ups + 1 + number) * steps))
        base = count * steps

        def all_sum(sent, received, first):
            made = []
            for step in range(steps):
                made.append(pltpu.make_async_remote_copy(
                    src_ref=sent.at[step], dst_ref=received.at[step], send_sem=send_sems.at[first + step],
                    recv_sem=recv_sems.at[first + step], device_id=place.across(orders["x_y_z"][step]),
                    device_id_type=MESH_ID))
            return made

        small_copies = all_sum(small_sent, small_received, base)
        late_copies = all_sum(late_sent, late_received, base + steps)
        swap_refs = [swap_out.at[core]] + [swap_qkv.at[number, core] for number in range(q_parts)]
        swaps = [pltpu.make_async_remote_copy(
            src_ref=ref, dst_ref=ref, send_sem=send_sems.at[base + 2 * steps + slot],
            recv_sem=recv_sems.at[base + 2 * steps + slot], device_id=place.across(("narrow", 0)),
            device_id_type=MESH_ID) for slot, ref in enumerate(swap_refs)]
        local = []
        for number in range(ups):
            keep = pieces[number].region(0, True)
            local.append(pltpu.make_async_copy(up_hbm.at[number].at[keep], up_own.at[number].at[keep], local_sems.at[number]))

        def advance(number, step):
            item = pieces[number]
            if step == 0 and number < ups:
                local[number].wait()
            total = item.add(step)
            if total is None:
                item.send(step + 1)
            elif number < ups:
                up_out[:, number * 128 : (number + 1) * 128] = total
            else:
                if number == ups:
                    swap_out[core] = total
                else:
                    swap_qkv[number - ups - 1, core] = total
                swaps[number - ups].start()

        def advance_small(copies, sent, received, out, step):
            copies[step].wait_recv()
            total = sent[step] + received[step]
            if step + 1 < steps:
                sent[step + 1] = total
                copies[step + 1].start()
            else:
                out[...] = total

        @pl.when(pid == 0)
        def _():
            place.greet()
            for number in range(ups):
                pieces[number].send(0)
                local[number].start()
            small_sent[0] = small[...]
            small_copies[0].start()
            grads_t = ga[...].T
            result = jnp.dot(grads_t, mix[...], preferred_element_type=jnp.float32).astype(jnp.bfloat16)
            for w in range(wide):
                for h in range(2):
                    for y in range(half):
                        at = (w * 2 + h) * o_rows
                        out_own[bits_of(w, wide_bits) + bits_of(y, half_bits) + (h,)] = result[
                            at : at + o_rows, y * lanes : (y + 1) * lanes
                        ]
            pieces[ups].send(0)
            grad_mixed = dot_last(ga[...], ow[...]).astype(jnp.bfloat16)
            for pair in range(pairs):
                gm[pair] = grad_mixed[:, pair * 128 : (pair + 1) * 128]
                mix_pair[pair] = mix[:, pair * 128 : (pair + 1) * 128]

        @pl.when((pid >= 1) & (pid < first_q))
        def _():
            number = pid - 1
            pair, doc = number // docs, number % docs
            some = pl.ds(pl.multiple_of(doc * length, length), length)
            lane = lax.broadcasted_iota(jnp.int32, (1, 128), 1)
            scale = jnp.bfloat16(HEAD_DIM**-0.5)
            queries, keys, values = q_ref[...] * scale, k_ref[...], v_ref[...]
            grads = gm[pair, some, :]
            product = grads.astype(jnp.float32) * mix_pair[pair, some, :].astype(jnp.float32)
            queries_t, grads_t = queries.T, grads.T
            zero = jnp.zeros_like(queries)
            query_parts = []
            for head in range(2):
                inside = (lane // HEAD_DIM) == head
                at = head * HEAD_DIM
                scores = dot_last(jnp.where(inside, queries, zero), keys) + bias[0]
                attention = jnp.exp(scores - tot_ref[:, at : at + 1])
                chance = dot_last(jnp.where(inside, grads, zero), values)
                inner = jnp.sum(jnp.where(inside, product, 0.0), -1, keepdims=True)
                grad_scores = (attention * (chance - inner)).astype(jnp.bfloat16)
                query_parts.append(jnp.dot(grad_scores, keys, preferred_element_type=jnp.float32))
                key_t = jnp.dot(queries_t[at : at + HEAD_DIM], grad_scores, preferred_element_type=jnp.float32)
                value_t = jnp.dot(grads_t[at : at + HEAD_DIM], attention.astype(jnp.bfloat16),
                                  preferred_element_type=jnp.float32)
                row = pair * 128 + at
                gqkv_t[pl.ds(pl.multiple_of(width + row, HEAD_DIM), HEAD_DIM), some] = key_t.astype(jnp.bfloat16)
                gqkv_t[pl.ds(pl.multiple_of(2 * width + row, HEAD_DIM), HEAD_DIM), some] = value_t.astype(jnp.bfloat16)
            grad_query = jnp.where(lane < HEAD_DIM, query_parts[0], query_parts[1]) * HEAD_DIM**-0.5
            gqkv_t[pl.ds(pl.multiple_of(pair * 128, 128), 128), some] = grad_query.astype(jnp.bfloat16).T

        for part in range(q_parts):
            @pl.when(pid == first_q + part)
            def _():
                if part == 0:
                    ones = jnp.ones((8, rows), jnp.bfloat16)
                    late_sent[0] = jnp.concatenate(
                        [dot_last(ones, gqkv_t[:width, :]), dot_last(ones, gqkv_t[2 * width :, :])], axis=1
                    )
                    late_copies[0].start()
                columns = jnp.concatenate(
                    [tok[:, y * lanes + part * 128 : y * lanes + (part + 1) * 128] for y in range(half)], axis=1
                )
                result = jnp.dot(gqkv_t[...], columns, preferred_element_type=jnp.float32).astype(jnp.bfloat16)
                for w in range(wide):
                    for h in range(2):
                        for y in range(half):
                            at = (w * 2 + h) * q_rows
                            qkv_own[(part,) + bits_of(w, wide_bits) + bits_of(y, half_bits) + (h,)] = result[
                                at : at + q_rows, y * 128 : (y + 1) * 128
                            ]
                pieces[ups + 1 + part].send(0)

        @pl.when(pid >= first_t)
        def _():
            at = pl.multiple_of((pid - first_t) * token_block, token_block)
            some = pl.ds(at, token_block)
            grad_t = jnp.dot(qw[...], gqkv_t[:, some], preferred_element_type=jnp.float32)
            tokens_out[some, :] = (grad_t.T + ga[some, :].astype(jnp.float32)).astype(jnp.bfloat16)

        plan = {}
        for step, at in enumerate((2, 6, 8, 10, 11)):
            for number in range(ups):
                plan.setdefault(at, []).append((number, step))
        for step, at in enumerate((2, 7, 9, 11, 12)):
            plan.setdefault(at, []).append((ups, step))
        for step in range(steps):
            for part in range(q_parts):
                at = first_t + step if step < token_steps else grid - 1
                if step == 0:
                    at = min(first_q + part + 1, first_t)
                plan.setdefault(at, []).append((ups + 1 + part, step))
        for at in range(grid):
            @pl.when(pid == at)
            def _():
                if at % 2 == 1 and at // 2 < steps:
                    advance_small(small_copies, small_sent, small_received, small_out, at // 2)
                for number, step in sorted(plan.get(at, []), key=lambda entry: entry[1]):
                    advance(number, step)
                if at == grid - 1:
                    for step in range(steps):
                        advance_small(late_copies, late_sent, late_received, late_out, step)
                    for copy in swaps:
                        copy.wait()
                    out_out[...] = swap_out[...]
                    qkv_out[...] = swap_qkv[...]
                    for item in pieces:
                        item.close()
                    for copy in small_copies + late_copies:
                        copy.wait_send()

    def whole(shape):
        return pl.BlockSpec(shape, lambda g: (0,) * len(shape), pipeline_mode=pl.Buffered(1))

    def number_of(g):
        return jnp.clip(g - 1, 0, attn_steps - 1)

    def tile(which):
        return pl.BlockSpec((length, 128), lambda g: (number_of(g) % docs, which * pairs + number_of(g) // docs))

    two = (2,)
    any_space = pl.BlockSpec(memory_space=pl.ANY)
    in_specs = [whole((rows, width)), whole((rows, width)), whole((width, width)), tile(0), tile(1), tile(2), tile(0)]
    in_specs += [pl.BlockSpec((1, 1, length), lambda g: (number_of(g) % docs, 0, 0)), whole((rows, width))]
    in_specs += [whole((width, 3 * width)), any_space, whole((small_rows, width))]
    out_shape = [
        jax.ShapeDtypeStruct((rows, width), jnp.bfloat16),
        jax.ShapeDtypeStruct((u_rows, ups * 128), jnp.float32),
        jax.ShapeDtypeStruct((2, o_rows, lanes), jnp.float32),
        jax.ShapeDtypeStruct((q_parts, 2, q_rows, 128), jnp.float32),
        jax.ShapeDtypeStruct((small_rows, width), jnp.float32),
        jax.ShapeDtypeStruct((8, 2 * width), jnp.float32),
    ]
    wide_dims, half_dims = two * wide_bits, two * half_bits
    scratch = [
        pltpu.VMEM((pairs, rows, 128), jnp.bfloat16),
        pltpu.VMEM((pairs, rows, 128), jnp.bfloat16),
        pltpu.VMEM((3 * width, rows), jnp.bfloat16),
        pltpu.VMEM(up_grads.shape, jnp.bfloat16),
        pltpu.VMEM(wide_dims + half_dims + two + (o_rows, lanes), jnp.bfloat16),
        pltpu.VMEM((q_parts,) + wide_dims + half_dims + two + (q_rows, 128), jnp.bfloat16),
    ]
    scratch += [pltpu.VMEM((ups,) + two * (steps - 1 - s) + (u_rows, 128), jnp.bfloat16) for s in range(steps)]
    scratch += [pltpu.VMEM(two * (steps - 1 - s) + (o_rows, lanes), jnp.bfloat16) for s in range(steps)]
    scratch += [pltpu.VMEM((q_parts,) + two * (steps - 1 - s) + (q_rows, 128), jnp.bfloat16) for s in range(steps)]
    scratch += [pltpu.VMEM((steps, small_rows, width), jnp.float32)] * 2
    scratch += [pltpu.VMEM((steps, 8, 2 * width), jnp.float32)] * 2
    scratch += [pltpu.VMEM(out_shape[2].shape, jnp.float32), pltpu.VMEM(out_shape[3].shape, jnp.float32)]
    sems = count * steps + 2 * steps + 1 + q_parts
    scratch += [pltpu.SemaphoreType.DMA((sems,)), pltpu.SemaphoreType.DMA((sems,)), pltpu.SemaphoreType.DMA((ups,))]
    return pl.pallas_call(
        kernel,
        grid=(grid,),
        in_specs=in_specs,
        out_specs=[whole(item.shape) for item in out_shape],
        out_shape=out_shape,
        scratch_shapes=scratch,
        compiler_params=pltpu.CompilerParams(collective_id=1, has_side_effects=True, vmem_limit_bytes=60 << 20),
        name="attention_backward",
    )(grad_attended, mixed, out_weight, qkv, qkv, qkv, totals, key_bias, tokens, qkv_weight, up_grads, sums)


def on_device_fast(
    tokens,
    doc_lengths,
    qkv_weight,
    query_bias,
    value_bias,
    out_weight,
    out_bias,
    first_gain,
    first_shift,
    up_weight,
    up_bias,
    down_weight,
    down_bias,
    second_gain,
    second_shift,
    dir_weight,
    dir_bias,
    segment_rows,
    segment_slots,
    pair_rows,
    pair_labels,
    out_cotangent,
):
    doc_count, length, model_width = tokens.shape
    low = jnp.bfloat16
    token_rows = tokens.reshape(doc_count * length, model_width)
    allowed = lax.broadcasted_iota(jnp.int32, (doc_count, length), 1) < doc_lengths[:, None]
    key_bias = jnp.where(allowed, 0.0, MASKED).astype(jnp.float32).reshape(doc_count, 1, length)
    allowed_rows = allowed.reshape(-1, 1).astype(jnp.float32)
    bias_row = jnp.concatenate([query_bias, jnp.zeros_like(query_bias), value_bias]).astype(jnp.float32)
    qkv = (jnp.dot(token_rows, qkv_weight, preferred_element_type=jnp.float32) + bias_row).astype(low)
    mixed, totals = attention_forward(qkv, key_bias, doc_count, length)
    attended = jnp.dot(mixed, out_weight, preferred_element_type=jnp.float32) + out_bias.astype(jnp.float32)
    resid_one = token_rows.astype(jnp.float32) + attended
    hidden_one, normed_one, inverse_one = norm_forward(
        resid_one, first_gain.astype(jnp.float32), first_shift.astype(jnp.float32)
    )
    hidden_low = hidden_one.astype(low)
    upper_pre = jnp.dot(hidden_low, up_weight, preferred_element_type=jnp.float32) + up_bias.astype(jnp.float32)
    cumulative = normal_cdf(upper_pre)
    active = (upper_pre * cumulative).astype(low)
    density = jnp.exp(-0.5 * upper_pre * upper_pre) * 0.3989422804014327
    slope = (cumulative + upper_pre * density).astype(low)
    lowered = jnp.dot(active, down_weight, preferred_element_type=jnp.float32) + down_bias.astype(jnp.float32)
    resid_two = hidden_one + lowered
    second_float = second_gain.astype(jnp.float32)
    normed_out, normed_two, inverse_two = norm_forward(resid_two, second_float, second_shift.astype(jnp.float32))
    encoded_rows = (normed_out * allowed_rows).astype(low)
    doc_starts = lax.broadcasted_iota(jnp.int32, (doc_count, 1), 0) * length
    picked_rows = (segment_rows + doc_starts).reshape(-1)
    picked = encoded_rows[picked_rows]
    slots = segment_slots.reshape(-1)
    outgoing = jnp.zeros_like(picked).at[slots].set(picked)
    arrived = lax.all_to_all(outgoing, "wide", split_axis=0, concat_axis=0, tiled=True)
    pairs = pair_rows.reshape(-1, 2)
    labels = pair_labels.reshape(-1)
    first_rows = arrived[pairs[:, 0]]
    second_rows = arrived[pairs[:, 1]]
    logits = (
        jnp.dot(first_rows, dir_weight[:model_width], preferred_element_type=jnp.float32)
        + jnp.dot(second_rows, dir_weight[model_width:], preferred_element_type=jnp.float32)
        + dir_bias.astype(jnp.float32)
    )
    powers_head = jnp.exp(logits - jnp.max(logits, -1, keepdims=True))
    chance = powers_head / jnp.sum(powers_head, -1, keepdims=True)
    classes = lax.broadcasted_iota(jnp.int32, logits.shape, 1)
    delta = chance - (labels[:, None] == classes).astype(jnp.float32)
    first_float = first_rows.astype(jnp.float32)
    second_rows_float = second_rows.astype(jnp.float32)
    grad_dir_weight = jnp.concatenate(
        [
            jnp.dot(first_float.T, delta, precision=EXACT, preferred_element_type=jnp.float32),
            jnp.dot(
                second_rows_float.T, delta, precision=EXACT, preferred_element_type=jnp.float32
            ),
        ]
    )
    grad_dir_bias = jnp.sum(delta, 0)
    dir_float = dir_weight.astype(jnp.float32)
    grad_first = jnp.dot(
        delta, dir_float[:model_width].T, precision=EXACT, preferred_element_type=jnp.float32
    )
    grad_second = jnp.dot(
        delta, dir_float[model_width:].T, precision=EXACT, preferred_element_type=jnp.float32
    )
    grad_arrived = jnp.zeros((arrived.shape[0], model_width), jnp.float32)
    grad_arrived = grad_arrived.at[pairs[:, 0]].add(grad_first).at[pairs[:, 1]].add(grad_second)
    returned = lax.all_to_all(
        grad_arrived.astype(jnp.bfloat16), "wide", split_axis=0, concat_axis=0, tiled=True
    )
    grad_picked = returned[slots].astype(jnp.float32)
    grad_encoded = (
        out_cotangent.reshape(-1, model_width).astype(jnp.float32).at[picked_rows].add(grad_picked)
    )
    grad_encoded = grad_encoded * allowed_rows
    grad_attended, up_blocks, out_down, sums, up_sums = ffn_backward(
        grad_encoded, normed_two.astype(low), inverse_two, second_float[None], active, slope, hidden_low,
        down_weight, up_weight, normed_one.astype(low), inverse_one, first_gain.astype(jnp.float32)[None],
    )
    classes_count = dir_weight.shape[1]
    up_rows = up_sums.reshape(-1, up_sums.shape[-1] // 128, 128).transpose(1, 0, 2).reshape(-1, model_width)
    dir_rows = grad_dir_weight.reshape(2, model_width, classes_count).transpose(0, 2, 1).reshape(-1, model_width)
    dir_row = jnp.pad(grad_dir_bias, (0, model_width - classes_count))[None]
    sums = jnp.concatenate([sums[:6], up_rows, dir_rows, dir_row])
    sums = jnp.pad(sums, ((0, -sums.shape[0] % 8), (0, 0)))
    grad_tokens, out_up, out_out, out_qkv, sums, late = attention_backward(
        grad_attended, mixed, out_weight, qkv, totals, key_bias, token_rows, qkv_weight, up_blocks, sums
    )
    core = lax.axis_index("narrow") % 2
    width = model_width // lax.axis_size("narrow")
    out_qkv = out_qkv.transpose(1, 2, 0, 3).reshape(-1, 2 * width)
    out_out = out_out.reshape(-1, 2 * width)

    def own_lanes(rows):
        return lax.dynamic_slice_in_dim(rows, core * width, width, 1).T

    first_dir = 6 + up_rows.shape[0]
    last_dir = first_dir + 2 * classes_count
    dir_sum = sums[first_dir:last_dir].reshape(2, classes_count, model_width).transpose(0, 2, 1)
    return (
        encoded_rows.reshape(tokens.shape),
        grad_tokens.reshape(tokens.shape),
        own_lanes(out_qkv),
        late[0, :model_width],
        late[0, model_width:],
        own_lanes(out_out),
        sums[5],
        sums[3],
        sums[4],
        out_up,
        sums[6:first_dir].reshape(-1),
        out_down.T,
        sums[2],
        sums[0],
        sums[1],
        dir_sum.reshape(2 * model_width, classes_count),
        sums[last_dir, :classes_count],
    )


def on_device(
    tokens,
    doc_lengths,
    qkv_weight,
    query_bias,
    value_bias,
    out_weight,
    out_bias,
    first_gain,
    first_shift,
    up_weight,
    up_bias,
    down_weight,
    down_bias,
    second_gain,
    second_shift,
    dir_weight,
    dir_bias,
    segment_rows,
    segment_slots,
    pair_rows,
    pair_labels,
    out_cotangent,
):
    doc_count, length, model_width = tokens.shape
    score_scale = HEAD_DIM ** (-0.5)
    token_rows = tokens.reshape(doc_count * length, model_width)
    allowed = lax.broadcasted_iota(jnp.int32, (doc_count, length), 1) < doc_lengths[:, None]
    allowed_rows = allowed.reshape(-1, 1).astype(jnp.float32)
    bias_row = jnp.concatenate([query_bias, jnp.zeros_like(query_bias), value_bias]).astype(
        jnp.float32
    )
    qkv = (jnp.dot(token_rows, qkv_weight, preferred_element_type=jnp.float32) + bias_row).astype(
        jnp.bfloat16
    )

    def split_heads(doc_block, which):
        return doc_block[:, which * model_width : (which + 1) * model_width].reshape(
            length, HEADS, HEAD_DIM
        )

    def scores_of(queries, key_rows, doc_mask):
        scores = (
            jnp.einsum("qhd,khd->hqk", queries, key_rows, preferred_element_type=jnp.float32)
            * score_scale
        )
        return jnp.where(doc_mask[None, None, :], scores, MASKED)

    mixed_parts = []
    log_totals = []
    for doc_index in range(doc_count):
        doc_block = qkv[doc_index * length : (doc_index + 1) * length]
        queries = split_heads(doc_block, 0)
        key_rows = split_heads(doc_block, 1)
        value_rows = split_heads(doc_block, 2)
        scores = scores_of(queries, key_rows, allowed[doc_index])
        highest = jnp.max(scores, -1, keepdims=True)
        powers = jnp.exp(scores - highest)
        summed = jnp.sum(powers, -1, keepdims=True)
        attention = (powers / summed).astype(jnp.bfloat16)
        log_totals.append(highest + jnp.log(summed))
        mixed_parts.append(
            jnp.einsum(
                "hqk,khd->qhd", attention, value_rows, preferred_element_type=jnp.float32
            ).reshape(length, model_width)
        )
    mixed = jnp.concatenate(mixed_parts).astype(jnp.bfloat16)
    attended = jnp.dot(mixed, out_weight, preferred_element_type=jnp.float32) + out_bias.astype(
        jnp.float32
    )
    resid_one = token_rows.astype(jnp.float32) + attended
    hidden_one, normed_one, inverse_one = norm_forward(
        resid_one, first_gain.astype(jnp.float32), first_shift.astype(jnp.float32)
    )
    hidden_low = hidden_one.astype(jnp.bfloat16)
    upper_pre = jnp.dot(hidden_low, up_weight, preferred_element_type=jnp.float32) + up_bias.astype(
        jnp.float32
    )
    cumulative = normal_cdf(upper_pre)
    active = (upper_pre * cumulative).astype(jnp.bfloat16)
    lowered = jnp.dot(active, down_weight, preferred_element_type=jnp.float32) + down_bias.astype(
        jnp.float32
    )
    resid_two = hidden_one + lowered
    second_float = second_gain.astype(jnp.float32)
    normed_out, normed_two, inverse_two = norm_forward(
        resid_two, second_float, second_shift.astype(jnp.float32)
    )
    encoded_rows = (normed_out * allowed_rows).astype(jnp.bfloat16)
    doc_starts = lax.broadcasted_iota(jnp.int32, (doc_count, 1), 0) * length
    picked_rows = (segment_rows + doc_starts).reshape(-1)
    picked = encoded_rows[picked_rows]
    slots = segment_slots.reshape(-1)
    outgoing = jnp.zeros_like(picked).at[slots].set(picked)
    arrived = lax.all_to_all(outgoing, "wide", split_axis=0, concat_axis=0, tiled=True)
    pairs = pair_rows.reshape(-1, 2)
    labels = pair_labels.reshape(-1)
    first_rows = arrived[pairs[:, 0]]
    second_rows = arrived[pairs[:, 1]]
    logits = (
        jnp.dot(first_rows, dir_weight[:model_width], preferred_element_type=jnp.float32)
        + jnp.dot(second_rows, dir_weight[model_width:], preferred_element_type=jnp.float32)
        + dir_bias.astype(jnp.float32)
    )
    powers_head = jnp.exp(logits - jnp.max(logits, -1, keepdims=True))
    chance = powers_head / jnp.sum(powers_head, -1, keepdims=True)
    classes = lax.broadcasted_iota(jnp.int32, logits.shape, 1)
    delta = chance - (labels[:, None] == classes).astype(jnp.float32)
    first_float = first_rows.astype(jnp.float32)
    second_rows_float = second_rows.astype(jnp.float32)
    grad_dir_weight = jnp.concatenate(
        [
            jnp.dot(first_float.T, delta, precision=EXACT, preferred_element_type=jnp.float32),
            jnp.dot(
                second_rows_float.T, delta, precision=EXACT, preferred_element_type=jnp.float32
            ),
        ]
    )
    grad_dir_bias = jnp.sum(delta, 0)
    dir_float = dir_weight.astype(jnp.float32)
    grad_first = jnp.dot(
        delta, dir_float[:model_width].T, precision=EXACT, preferred_element_type=jnp.float32
    )
    grad_second = jnp.dot(
        delta, dir_float[model_width:].T, precision=EXACT, preferred_element_type=jnp.float32
    )
    grad_arrived = jnp.zeros((arrived.shape[0], model_width), jnp.float32)
    grad_arrived = grad_arrived.at[pairs[:, 0]].add(grad_first).at[pairs[:, 1]].add(grad_second)
    returned = lax.all_to_all(
        grad_arrived.astype(jnp.bfloat16), "wide", split_axis=0, concat_axis=0, tiled=True
    )
    grad_picked = returned[slots].astype(jnp.float32)
    grad_encoded = (
        out_cotangent.reshape(-1, model_width).astype(jnp.float32).at[picked_rows].add(grad_picked)
    )
    grad_encoded = grad_encoded * allowed_rows
    grad_two, grad_second_gain, grad_second_shift = norm_backward(
        grad_encoded, normed_two, inverse_two, second_float
    )
    grad_lowered = grad_two.astype(jnp.bfloat16)
    grad_down_weight = jnp.einsum(
        "rf,rd->fd", active, grad_lowered, preferred_element_type=jnp.float32
    )
    grad_down_bias = jnp.sum(grad_lowered.astype(jnp.float32), 0)
    grad_active = jnp.einsum(
        "rd,fd->rf", grad_lowered, down_weight, preferred_element_type=jnp.float32
    )
    density = jnp.exp(-0.5 * upper_pre * upper_pre) * 0.3989422804014327
    grad_upper = (grad_active * (cumulative + upper_pre * density)).astype(jnp.bfloat16)
    grad_up_weight = jnp.einsum(
        "rd,rf->df", hidden_low, grad_upper, preferred_element_type=jnp.float32
    )
    grad_up_bias = jnp.sum(grad_upper.astype(jnp.float32), 0)
    grad_hidden = grad_two + jnp.einsum(
        "rf,df->rd", grad_upper, up_weight, preferred_element_type=jnp.float32
    )
    grad_one, grad_first_gain, grad_first_shift = norm_backward(
        grad_hidden, normed_one, inverse_one, first_gain.astype(jnp.float32)
    )
    grad_attended = grad_one.astype(jnp.bfloat16)
    grad_out_weight = jnp.einsum(
        "rd,re->de", mixed, grad_attended, preferred_element_type=jnp.float32
    )
    grad_out_bias = jnp.sum(grad_attended.astype(jnp.float32), 0)
    grad_mixed = jnp.einsum(
        "re,de->rd", grad_attended, out_weight, preferred_element_type=jnp.float32
    ).astype(jnp.bfloat16)
    grad_parts = []
    for doc_index in range(doc_count):
        doc_block = qkv[doc_index * length : (doc_index + 1) * length]
        queries = split_heads(doc_block, 0)
        key_rows = split_heads(doc_block, 1)
        value_rows = split_heads(doc_block, 2)
        scores = scores_of(queries, key_rows, allowed[doc_index])
        attention = jnp.exp(scores - log_totals[doc_index])
        grad_doc = grad_mixed[doc_index * length : (doc_index + 1) * length].reshape(
            length, HEADS, HEAD_DIM
        )
        grad_chance = jnp.einsum(
            "qhd,khd->hqk", grad_doc, value_rows, preferred_element_type=jnp.float32
        )
        inner = jnp.sum(grad_chance * attention, -1, keepdims=True)
        grad_scores = (attention * (grad_chance - inner)).astype(jnp.bfloat16)
        grad_query = (
            jnp.einsum("hqk,khd->qhd", grad_scores, key_rows, preferred_element_type=jnp.float32)
            * score_scale
        )
        grad_key = (
            jnp.einsum("hqk,qhd->khd", grad_scores, queries, preferred_element_type=jnp.float32)
            * score_scale
        )
        grad_value = jnp.einsum(
            "hqk,qhd->khd",
            attention.astype(jnp.bfloat16),
            grad_doc,
            preferred_element_type=jnp.float32,
        )
        grad_parts.append(
            jnp.concatenate(
                [
                    grad_query.reshape(length, model_width),
                    grad_key.reshape(length, model_width),
                    grad_value.reshape(length, model_width),
                ],
                axis=1,
            )
        )
    grad_qkv = jnp.concatenate(grad_parts).astype(jnp.bfloat16)
    grad_qkv_float = grad_qkv.astype(jnp.float32)
    grad_query_bias = jnp.sum(grad_qkv_float[:, :model_width], 0)
    grad_value_bias = jnp.sum(grad_qkv_float[:, 2 * model_width :], 0)
    grad_qkv_weight = jnp.einsum(
        "rd,re->de", token_rows, grad_qkv, preferred_element_type=jnp.float32
    )
    grad_tokens = (
        jnp.einsum("re,de->rd", grad_qkv, qkv_weight, preferred_element_type=jnp.float32) + grad_one
    ).astype(jnp.bfloat16)
    matrices = (grad_qkv_weight, grad_out_weight, grad_up_weight, grad_down_weight)
    partial_sums = (
        lax.psum_scatter(
            matrices[0].astype(jnp.bfloat16), "wide", scatter_dimension=1, tiled=True
        ).astype(jnp.float32),
        lax.psum_scatter(
            matrices[1].astype(jnp.bfloat16), "wide", scatter_dimension=1, tiled=True
        ).astype(jnp.float32),
        lax.psum_scatter(
            matrices[2].astype(jnp.bfloat16), "wide", scatter_dimension=1, tiled=True
        ).astype(jnp.float32),
        lax.psum_scatter(
            matrices[3].astype(jnp.bfloat16), "wide", scatter_dimension=1, tiled=True
        ).astype(jnp.float32),
    )
    summed_mats = (
        lax.psum_scatter(
            partial_sums[0].astype(jnp.bfloat16), "narrow", scatter_dimension=0, tiled=True
        ).astype(jnp.float32),
        lax.psum_scatter(
            partial_sums[1].astype(jnp.bfloat16), "narrow", scatter_dimension=0, tiled=True
        ).astype(jnp.float32),
        lax.psum_scatter(
            partial_sums[2].astype(jnp.bfloat16), "narrow", scatter_dimension=0, tiled=True
        ).astype(jnp.float32),
        lax.psum_scatter(
            partial_sums[3].astype(jnp.bfloat16), "narrow", scatter_dimension=0, tiled=True
        ).astype(jnp.float32),
    )
    smalls = lax.psum(
        (
            grad_query_bias,
            grad_value_bias,
            grad_out_bias,
            grad_first_gain,
            grad_first_shift,
            grad_up_bias,
            grad_down_bias,
            grad_second_gain,
            grad_second_shift,
            grad_dir_weight,
            grad_dir_bias,
        ),
        ("wide", "narrow"),
    )
    return (
        encoded_rows.reshape(tokens.shape),
        grad_tokens.reshape(tokens.shape),
        summed_mats[0],
        smalls[0],
        smalls[1],
        summed_mats[1],
        smalls[2],
        smalls[3],
        smalls[4],
        summed_mats[2],
        smalls[5],
        summed_mats[3],
        smalls[6],
        smalls[7],
        smalls[8],
        smalls[9],
        smalls[10],
    )


def fits_blocks(mesh):
    wide, narrow = mesh.shape["wide"], mesh.shape["narrow"]
    width, ff = HEADS * HEAD_DIM, 4 * HEADS * HEAD_DIM
    if wide != 2 * narrow or narrow < 4 or narrow & (narrow - 1):
        return False
    lanes = (ff // narrow, ff // wide, 2 * width // narrow)
    rows = (width // wide, width // narrow, width // wide // 2, 3 * width // wide // 2)
    return all(size % 128 == 0 for size in lanes) and all(size % 16 == 0 for size in rows)


def solution(mesh):
    placed = (
        P(("wide", "narrow"), None, None),
        P(("wide", "narrow")),
        P(),
        P(),
        P(),
        P(),
        P(),
        P(),
        P(),
        P(),
        P(),
        P(),
        P(),
        P(),
        P(),
        P(),
        P(),
        P(("wide", "narrow"), None),
        P(("wide", "narrow"), None),
        P(("wide", "narrow"), None, None),
        P(("wide", "narrow"), None),
        P(("wide", "narrow"), None, None),
    )
    return jax.shard_map(
        on_device_fast if fits_blocks(mesh) else on_device,
        mesh=mesh,
        in_specs=placed,
        out_specs=(
            P(("wide", "narrow"), None, None),
            P(("wide", "narrow"), None, None),
            P("narrow", "wide"),
            P(),
            P(),
            P("narrow", "wide"),
            P(),
            P(),
            P(),
            P("narrow", "wide"),
            P(),
            P("narrow", "wide"),
            P(),
            P(),
            P(),
            P(),
            P(),
        ),
        check_vma=False,
    )
```

```python
import jax
import jax.numpy as jnp
from jax import lax
from jax.experimental import pallas as pl
from jax.experimental.pallas import tpu as pltpu
from jax.sharding import PartitionSpec as P

HEADS = 12
HEAD_DIM = 64


EXACT = lax.Precision.HIGHEST
MASKED = -1e30
EPSILON = 1e-05


def norm_forward(values, gain, shift):
    center = jnp.mean(values, -1, keepdims=True)
    centered = values - center
    inverse = lax.rsqrt(jnp.mean(centered * centered, -1, keepdims=True) + EPSILON)
    normed = centered * inverse
    return (normed * gain + shift, normed, inverse)


def norm_backward(grad, normed, inverse, gain):
    scaled = grad * gain
    first_mean = jnp.mean(scaled, -1, keepdims=True)
    second_mean = jnp.mean(scaled * normed, -1, keepdims=True)
    return (
        (scaled - first_mean - normed * second_mean) * inverse,
        jnp.sum(grad * normed, 0),
        jnp.sum(grad, 0),
    )


def normal_cdf(values):
    return 0.5 * (1.0 + lax.erf(values * 0.7071067811865476))


MESH_ID = pl.DeviceIdType.MESH


def axis_bits():
    names = []
    for axis in ("wide", "narrow"):
        count = lax.axis_size(axis).bit_length() - 1
        names += [(axis, bit) for bit in reversed(range(count))]
    return names


class Place:
    def __init__(self):
        self.index = {axis: lax.axis_index(axis) for axis in ("wide", "narrow")}
        self.names = axis_bits()
        self.bit = {name: (self.index[name[0]] // (1 << name[1])) % 2 for name in self.names}

    def across(self, name):
        axis, bit = name
        target = dict(self.index)
        target[axis] = target[axis] + (1 << bit) - (2 << bit) * self.bit[name]
        return target

    def ahead(self, offset):
        target = dict(self.index)
        target["wide"] = (target["wide"] + offset) % lax.axis_size("wide")
        return target

    def greet(self, all_wide=False):
        barrier = pltpu.get_barrier_semaphore()
        targets = [self.across(name) for name in self.names if not (all_wide and name[0] == "wide")]
        if all_wide:
            targets += [self.ahead(offset) for offset in range(1, lax.axis_size("wide"))]
        for target in targets:
            pl.semaphore_signal(barrier, inc=1, device_id=target, device_id_type=MESH_ID)
        pl.semaphore_wait(barrier, len(targets))


class Halving:
    def __init__(self, place, names, order, source, own, received, send_sems, recv_sems, first_sem):
        self.place, self.names, self.order = place, names, order
        self.source, self.own, self.received = source, own, received
        self.send_sems, self.recv_sems, self.first_sem = send_sems, recv_sems, first_sem

    def region(self, step, mine):
        index = []
        for name in self.names:
            if name in self.order[:step]:
                index.append(self.place.bit[name])
            elif name == self.order[step]:
                index.append(self.place.bit[name] if mine else 1 - self.place.bit[name])
            else:
                index.append(slice(None))
        return tuple(index)

    def copy(self, step):
        held = self.source if step == 0 else self.own
        return pltpu.make_async_remote_copy(
            src_ref=held.at[self.region(step, False)],
            dst_ref=self.received[step],
            send_sem=self.send_sems.at[self.first_sem + step],
            recv_sem=self.recv_sems.at[self.first_sem + step],
            device_id=self.place.across(self.order[step]),
            device_id_type=MESH_ID,
        )

    def send(self, step):
        self.copy(step).start()

    def add(self, step):
        self.copy(step).wait_recv()
        mine = self.region(step, True)
        if step + 1 < len(self.order):
            self.own[mine] = self.own[mine] + self.received[step][...]
            return None
        return self.own[mine].astype(jnp.float32) + self.received[step][...].astype(jnp.float32)

    def merge(self, step):
        self.copy(step).wait_recv()
        mine = self.region(step, True)
        self.own[mine] = self.own[mine] + self.received[step][...]

    def close(self):
        for step in range(len(self.order)):
            self.copy(step).wait_send()


def link_orders():
    wide = [("wide", bit) for bit in range(lax.axis_size("wide").bit_length() - 1)]
    narrow = [("narrow", bit) for bit in range(1, lax.axis_size("narrow").bit_length() - 1)]
    core, x, near, far = [("narrow", 0)], wide[:1], wide[1:-1], wide[-1:]
    return [core + narrow + x + near + far, core + x + near + narrow + far, core + near + narrow + x + far]


def attention_forward(qkv, key_bias, docs, length):
    width = qkv.shape[1] // 3
    pairs = width // 128

    def kernel(q_ref, k_ref, v_ref, bias_ref, mixed_ref, total_ref):
        lane = lax.broadcasted_iota(jnp.int32, (1, 128), 1)
        keys, values = k_ref[...], v_ref[...]
        queries = q_ref[...] * jnp.bfloat16(HEAD_DIM**-0.5)
        results = []
        for head in range(2):
            inside = (lane // HEAD_DIM) == head
            masked = jnp.where(inside, queries, jnp.zeros_like(queries))
            scores = dot_last(masked, keys) + bias_ref[0]
            highest = jnp.max(scores, -1, keepdims=True)
            powers = jnp.exp(scores - highest)
            summed = jnp.sum(powers, -1, keepdims=True)
            out = jnp.dot(powers.astype(jnp.bfloat16), values, preferred_element_type=jnp.float32)
            results.append((out / summed, highest + jnp.log(summed)))
        first = lane < HEAD_DIM
        mixed_ref[...] = jnp.where(first, results[0][0], results[1][0]).astype(jnp.bfloat16)
        total_ref[...] = jnp.where(first, results[0][1], results[1][1])

    def block(which):
        return pl.BlockSpec((length, 128), lambda doc, pair: (doc, which * pairs + pair))

    rows = docs * length
    return pl.pallas_call(
        kernel,
        grid=(docs, pairs),
        in_specs=[block(0), block(1), block(2), pl.BlockSpec((1, 1, length), lambda doc, pair: (doc, 0, 0))],
        out_specs=[block(0), block(0)],
        out_shape=[
            jax.ShapeDtypeStruct((rows, width), jnp.bfloat16),
            jax.ShapeDtypeStruct((rows, width), jnp.float32),
        ],
        compiler_params=pltpu.CompilerParams(vmem_limit_bytes=48 << 20),
        name="attention_forward",
    )(qkv, qkv, qkv, key_bias)


def dot_last(left, right):
    return lax.dot_general(left, right, (((1,), (1,)), ((), ())), preferred_element_type=jnp.float32)


def norm_back_rows(grad, normed, inverse, gain):
    scaled = grad * gain
    first = jnp.mean(scaled, -1, keepdims=True)
    second = jnp.mean(scaled * normed, -1, keepdims=True)
    return (scaled - first - normed * second) * inverse


def parts_of(values, count):
    terms = []
    for _ in range(count):
        term = values.astype(jnp.bfloat16).astype(jnp.float32)
        terms.append(term)
        values = values - term
    return jnp.concatenate(terms).astype(jnp.bfloat16)


def one_hot(row, count):
    lines = lax.broadcasted_iota(jnp.int32, (count, row.shape[1]), 0)
    return jnp.where(lines == row, 1.0, 0.0).astype(jnp.bfloat16)


def ffn_backward(lengths, numbers, encoded, cotangent, dir_rows, dir_bias, normed_two, inverse_two, second_gain, active, slope, hidden_low, down_weight, up_weight,
                 normed_one, inverse_one, first_gain):
    rows, width = hidden_low.shape
    ff = active.shape[1]
    segments, classes = numbers.shape[1], dir_bias.shape[0]
    length = rows // lengths.shape[0]
    names = axis_bits()
    steps = len(names)
    wide, narrow = lax.axis_size("wide"), lax.axis_size("narrow")
    wide_bits, narrow_bits = wide.bit_length() - 1, narrow.bit_length() - 1
    chunks = ff // narrow // 128
    third = chunks // 2
    d_rows, u_rows = width // wide, width // narrow
    row_block = 128
    row_steps = rows // row_block
    orders = link_orders()
    two = (2,)
    first_dir = 6 + narrow
    sum_rows = pl.cdiv(first_dir + 3 * classes, 8) * 8

    def chunk_of(step):
        step = jnp.clip(step, 0, chunks - 1)
        return step // 2 + third * (step % 2)

    def bits_of(number, count):
        return tuple((number >> bit) & 1 for bit in reversed(range(count)))

    def kernel(*refs):
        lens, nums, enc, cot, dir_w, dir_b = refs[:6]
        refs = refs[6:]
        (n2, q2, gain2, n1, q1, gain1, hidden) = refs[:7]
        refs = refs[7:]
        act = refs[:narrow]
        slo = refs[narrow : 2 * narrow]
        dws = refs[2 * narrow : 3 * narrow]
        uws = refs[3 * narrow : 4 * narrow]
        rest = list(refs[4 * narrow :])
        ga_out, up_out, down_out, sums_out = rest[:4]
        rest = rest[4:]
        grad_hidden, lowered, lowered_t, hidden_t, own, up_own, up_received = rest[:7]
        received = rest[7 : 7 + steps]
        select, leaving, arrived, leaving_grads, arrived_grads = rest[7 + steps : 12 + steps]
        send_sems, recv_sems, local_sems = rest[12 + steps :]
        pid = pl.program_id(0)
        place = Place()
        pieces = []
        for number in range(chunks):
            pieces.append(
                Halving(place, names, orders[number % 3], own.at[number], own.at[number],
                        [r.at[number] for r in received], send_sems, recv_sems, number * steps)
            )
        core = ("narrow", 0)
        up_names = [name for name in names if name != ("wide", 0)]
        up_pieces = [
            Halving(place, up_names, [core], up_own.at[number], up_own.at[number], [up_received.at[number]],
                    send_sems, recv_sems, chunks * steps + number)
            for number in range(chunks)
        ]

        def up_write(number):
            mine = up_pieces[number].region(0, True)
            return pltpu.make_async_copy(
                up_own.at[number].at[mine],
                up_out.at[(number // 2,) + (slice(None),) * (wide_bits - 1) + (number % 2,)],
                local_sems.at[number],
            )

        def exchange(source, landing, first):
            made = []
            for offset in range(1, wide):
                target = place.ahead(offset)
                made.append(pltpu.make_async_remote_copy(
                    src_ref=source.at[target["wide"]], dst_ref=landing.at[place.index["wide"]],
                    send_sem=send_sems.at[first + offset - 1], recv_sem=recv_sems.at[first + offset - 1],
                    device_id=target, device_id_type=MESH_ID))
            me = place.index["wide"]
            for copy in made:
                copy.start()
            landing[me] = source[me]
            for copy in made:
                copy.wait()
            return landing[...].reshape(segments, width)

        @pl.when(pid == 0)
        def _():
            place.greet(all_wide=True)
            sums_out[...] = jnp.zeros_like(sums_out)
            base = chunks * steps + chunks
            select[...] = dot_last(one_hot(nums[0:1, :], rows), one_hot(nums[1:2, :], segments)).astype(jnp.bfloat16)
            picked = jnp.dot(select[...].T, enc[...], preferred_element_type=jnp.float32).astype(jnp.bfloat16)
            leaving[...] = picked.reshape(leaving.shape)
            rows_in = exchange(leaving, arrived, base)
            pair_first, pair_second = one_hot(nums[2:3, :], segments), one_hot(nums[3:4, :], segments)
            scores = dot_last(dir_w[...], rows_in)

            def chosen(values, pairs):
                split = jnp.dot(parts_of(values, 3), pairs, preferred_element_type=jnp.float32)
                return split[:classes] + split[classes : 2 * classes] + split[2 * classes :]

            logits = chosen(scores[:classes], pair_first) + chosen(scores[classes:], pair_second) + dir_b[...]
            powers = jnp.exp(logits - jnp.max(logits, 0, keepdims=True))
            chance = powers / jnp.sum(powers, 0, keepdims=True)
            kinds = lax.broadcasted_iota(jnp.int32, logits.shape, 0)
            delta = chance - jnp.where(kinds == nums[4:5, :], 1.0, 0.0)
            sums_out[first_dir + 2 * classes : first_dir + 3 * classes, :] = jnp.broadcast_to(
                jnp.sum(delta, 1, keepdims=True), (classes, width)
            )
            split = parts_of(delta, 2)
            gathered = []
            for pairs in (pair_first, pair_second):
                both = dot_last(split, pairs)
                gathered.append(both[:classes] + both[classes:])
            per_row = parts_of(jnp.concatenate(gathered), 2)
            both = jnp.dot(per_row, rows_in, preferred_element_type=jnp.float32)
            sums_out[first_dir : first_dir + 2 * classes, :] = both[: 2 * classes] + both[2 * classes :]
            twice = jnp.concatenate([dir_w[...], dir_w[...]])
            grads = jnp.dot(per_row.T, twice, preferred_element_type=jnp.float32).astype(jnp.bfloat16)
            leaving_grads[...] = grads.reshape(leaving.shape)
            grads_in = exchange(leaving_grads, arrived_grads, base + wide - 1)

            def body(i, carry):
                at = pl.multiple_of(i * row_block, row_block)
                some = pl.ds(at, row_block)
                normed = n2[some, :].astype(jnp.float32)
                doc = at // length
                line = lax.broadcasted_iota(jnp.int32, (row_block, 1), 0) + (at - doc * length)
                grad = cot[some, :].astype(jnp.float32) + jnp.dot(
                    select[some, :], grads_in, preferred_element_type=jnp.float32
                )
                grad = jnp.where(line < lens[doc], grad, 0.0)
                two = norm_back_rows(grad, normed, q2[some, :], gain2[...])
                low = two.astype(jnp.bfloat16)
                grad_hidden[some, :] = two
                lowered[some, :] = low
                lowered_t[:, some] = low.T
                hidden_t[:, some] = hidden[some, :].T
                sums_out[0:1, :] += jnp.sum(grad * normed, 0, keepdims=True)
                sums_out[1:2, :] += jnp.sum(grad, 0, keepdims=True)
                sums_out[2:3, :] += jnp.sum(low.astype(jnp.float32), 0, keepdims=True)
                return carry

            lax.fori_loop(0, row_steps, body, 0)

        @pl.when(pid < chunks)
        def _():
            actives = jnp.concatenate([ref[...] for ref in act], axis=1)
            result = jnp.dot(lowered_t[...], actives, preferred_element_type=jnp.float32).astype(jnp.bfloat16)
            for w in range(wide):
                for n in range(narrow):
                    own[(pid,) + bits_of(w, wide_bits) + bits_of(n, narrow_bits)] = result[
                        w * d_rows : (w + 1) * d_rows, n * 128 : (n + 1) * 128
                    ]

        @pl.when(pid >= chunks)
        def _():
            slopes = jnp.concatenate([ref[...] for ref in slo], axis=1)
            downs = jnp.concatenate([ref[...] for ref in dws], axis=0)
            ups = jnp.concatenate([ref[...] for ref in uws], axis=1)
            grad_active = dot_last(lowered[...], downs)
            grad_upper = (grad_active * slopes.astype(jnp.float32)).astype(jnp.bfloat16)
            totals = jnp.sum(grad_upper.astype(jnp.float32), 0, keepdims=True)
            at = pl.ds(pl.multiple_of(chunk_of(pid - chunks) * 128, 128), 128)
            for n in range(narrow):
                sums_out[6 + n : 7 + n, at] = totals[:, n * 128 : (n + 1) * 128]
            result = jnp.dot(hidden_t[...], grad_upper, preferred_element_type=jnp.float32).astype(jnp.bfloat16)
            for n in range(narrow):
                for z in range(narrow):
                    high = bits_of(z, wide_bits - 1)
                    up_own[(pid - chunks,) + high + bits_of(n, narrow_bits)] = result[
                        n * u_rows : (n + 1) * u_rows, z * 128 : (z + 1) * 128
                    ]
            grad_hidden[...] += dot_last(grad_upper, ups)

        def advance(number, step):
            item = pieces[number]
            total = item.add(step)
            if total is None:
                item.send(step + 1)
            else:
                j = number // 2 + third * (number % 2)
                down_out[:, j * 128 : (j + 1) * 128] = total

        for number in range(chunks):
            @pl.when(pid == chunks + number)
            def _():
                up_pieces[number].send(0)

        @pl.when(pid == 2 * chunks - 1)
        def _():
            def body(i, carry):
                at = pl.multiple_of(i * row_block, row_block)
                some = pl.ds(at, row_block)
                grad, normed = grad_hidden[some, :], n1[some, :].astype(jnp.float32)
                low = norm_back_rows(grad, normed, q1[some, :], gain1[...]).astype(jnp.bfloat16)
                ga_out[some, :] = low
                sums_out[3:4, :] += jnp.sum(grad * normed, 0, keepdims=True)
                sums_out[4:5, :] += jnp.sum(grad, 0, keepdims=True)
                sums_out[5:6, :] += jnp.sum(low.astype(jnp.float32), 0, keepdims=True)
                return carry

            lax.fori_loop(0, row_steps, body, 0)

        plan = {}
        for number in range(chunks):
            for step in range(steps):
                at = number + 1 if step == 0 else chunks + number // 2 + step
                plan.setdefault(min(at, 2 * chunks - 1), []).append((step, number))
        for at in range(2 * chunks):
            @pl.when(pid == at)
            def _():
                if at < chunks:
                    pieces[at].send(0)
                if at > chunks:
                    up_pieces[at - chunks - 1].merge(0)
                    up_write(at - chunks - 1).start()
                for step, number in sorted(plan.get(at, [])):
                    advance(number, step)
                if at == 2 * chunks - 1:
                    up_pieces[chunks - 1].merge(0)
                    up_write(chunks - 1).start()
                    for number in range(chunks):
                        up_write(number).wait()
                    for item in pieces + up_pieces:
                        item.close()

    def whole(shape):
        return pl.BlockSpec(shape, lambda g: (0,) * len(shape), pipeline_mode=pl.Buffered(1))

    def slab_columns(shape, first):
        return [pl.BlockSpec(shape, lambda g, n=n: (0, n * chunks + chunk_of(g - first))) for n in range(narrow)]

    in_specs = [pl.BlockSpec(memory_space=pltpu.SMEM), whole(numbers.shape), whole((rows, width)), whole((rows, width))]
    in_specs += [whole(dir_rows.shape), whole(dir_bias.shape)]
    in_specs += [whole((rows, width)), whole((rows, 1)), whole((1, width))]
    in_specs += [whole((rows, width)), whole((rows, 1)), whole((1, width)), whole((rows, width))]
    in_specs += slab_columns((rows, 128), 0) + slab_columns((rows, 128), chunks)
    in_specs += [pl.BlockSpec((128, width), lambda g, n=n: (n * chunks + chunk_of(g - chunks), 0)) for n in range(narrow)]
    in_specs += slab_columns((width, 128), chunks)
    high = two * (wide_bits - 1)
    low = two * narrow_bits
    up_shape = (third,) + high + (2,) + low[1:] + (u_rows, 128)
    out_specs = [
        whole((rows, width)),
        pl.BlockSpec(memory_space=pl.ANY),
        whole((d_rows, chunks * 128)),
        whole((sum_rows, width)),
    ]
    out_shape = [
        jax.ShapeDtypeStruct((rows, width), jnp.bfloat16),
        jax.ShapeDtypeStruct(up_shape, jnp.bfloat16),
        jax.ShapeDtypeStruct((d_rows, chunks * 128), jnp.float32),
        jax.ShapeDtypeStruct((sum_rows, width), jnp.float32),
    ]
    scratch = [
        pltpu.VMEM((rows, width), jnp.float32),
        pltpu.VMEM((rows, width), jnp.bfloat16),
        pltpu.VMEM((width, rows), jnp.bfloat16),
        pltpu.VMEM((width, rows), jnp.bfloat16),
        pltpu.VMEM((chunks,) + two * steps + (d_rows, 128), jnp.bfloat16),
        pltpu.VMEM((chunks,) + high + low + (u_rows, 128), jnp.bfloat16),
        pltpu.VMEM((chunks,) + high + low[1:] + (u_rows, 128), jnp.bfloat16),
    ]
    scratch += [pltpu.VMEM((chunks,) + two * (steps - 1 - s) + (d_rows, 128), jnp.bfloat16) for s in range(steps)]
    scratch += [pltpu.VMEM((rows, segments), jnp.bfloat16)]
    scratch += [pltpu.VMEM((wide, segments // wide, width), jnp.bfloat16)] * 4
    sems = chunks * steps + chunks + 2 * (wide - 1)
    scratch += [pltpu.SemaphoreType.DMA((sems,)), pltpu.SemaphoreType.DMA((sems,)), pltpu.SemaphoreType.DMA((chunks,))]
    return pl.pallas_call(
        kernel,
        grid=(2 * chunks,),
        in_specs=in_specs,
        out_specs=out_specs,
        out_shape=out_shape,
        scratch_shapes=scratch,
        compiler_params=pltpu.CompilerParams(collective_id=0, has_side_effects=True, vmem_limit_bytes=58 << 20),
        name="ffn_backward",
    )(lengths, numbers, encoded, cotangent, dir_rows, dir_bias, normed_two, inverse_two, second_gain, normed_one, inverse_one, first_gain, hidden_low,
      *([active] * narrow), *([slope] * narrow), *([down_weight] * narrow), *([up_weight] * narrow))


def attention_backward(grad_attended, mixed, out_weight, qkv, totals, key_bias, tokens, qkv_weight, up_grads, sums):
    rows, width = tokens.shape
    docs, _, length = key_bias.shape
    pairs = width // 128
    names = axis_bits()
    steps = len(names)
    wide, narrow = lax.axis_size("wide"), lax.axis_size("narrow")
    wide_bits, narrow_bits = wide.bit_length() - 1, narrow.bit_length() - 1
    half = narrow // 2
    half_bits = narrow_bits - 1
    lanes = width // half
    q_rows, o_rows = 3 * width // wide // 2, width // wide // 2
    q_parts = lanes // 128
    orders = link_orders()
    ups = up_grads.shape[0]
    u_rows = up_grads.shape[-2]
    attn_steps = docs * pairs
    token_block = 256
    token_steps = rows // token_block
    first_q = 1 + attn_steps
    first_t = first_q + q_parts
    grid = first_t + token_steps
    count = ups + 1 + q_parts
    small_rows = sums.shape[0]

    def bits_of(number, count):
        return tuple((number >> bit) & 1 for bit in reversed(range(count)))

    def kernel(*refs):
        (ga, mix, ow, q_ref, k_ref, v_ref, tot_ref, bias, tok_hbm, qw_hbm, up_hbm, small) = refs[:12]
        tokens_out, up_out, out_out, qkv_out, small_out, late_out = refs[12:18]
        rest = list(refs[18:])
        gm, mix_pair, gqkv_t, up_own, out_own, qkv_own = rest[:6]
        rest = rest[6:]
        up_received, rest = rest[: steps - 1], rest[steps - 1 :]
        out_received, qkv_received, rest = rest[:steps], rest[steps : 2 * steps], rest[2 * steps :]
        small_sent, small_received, late_sent, late_received, swap_out, swap_qkv, tok, qw = rest[:8]
        send_sems, recv_sems, local_sems = rest[8:]
        pid = pl.program_id(0)
        place = Place()
        core = place.bit["narrow", 0]
        pieces = []
        for number in range(ups):
            pieces.append(Halving(place, names[:-1], orders[number % 3][1:], up_hbm.at[number], up_own.at[number],
                                  [r.at[number] for r in up_received], send_sems, recv_sems, number * steps))
        pieces.append(Halving(place, names, orders[1], out_own, out_own, out_received, send_sems, recv_sems, ups * steps))
        for number in range(q_parts):
            pieces.append(Halving(place, names, orders[number % 3], qkv_own.at[number], qkv_own.at[number],
                                  [r.at[number] for r in qkv_received], send_sems, recv_sems, (ups + 1 + number) * steps))
        base = count * steps

        def all_sum(sent, received, first):
            made = []
            for step in range(steps):
                made.append(pltpu.make_async_remote_copy(
                    src_ref=sent.at[step], dst_ref=received.at[step], send_sem=send_sems.at[first + step],
                    recv_sem=recv_sems.at[first + step], device_id=place.across(orders[0][step]),
                    device_id_type=MESH_ID))
            return made

        small_copies = all_sum(small_sent, small_received, base)
        late_copies = all_sum(late_sent, late_received, base + steps)
        swap_refs = [swap_out.at[core]] + [swap_qkv.at[number, core] for number in range(q_parts)]
        swaps = [pltpu.make_async_remote_copy(
            src_ref=ref, dst_ref=ref, send_sem=send_sems.at[base + 2 * steps + slot],
            recv_sem=recv_sems.at[base + 2 * steps + slot], device_id=place.across(("narrow", 0)),
            device_id_type=MESH_ID) for slot, ref in enumerate(swap_refs)]
        local = []
        for number in range(ups):
            keep = pieces[number].region(0, True)
            local.append(pltpu.make_async_copy(up_hbm.at[number].at[keep], up_own.at[number].at[keep], local_sems.at[number]))

        loads = [pltpu.make_async_copy(tok_hbm, tok, local_sems.at[ups]),
                 pltpu.make_async_copy(qw_hbm, qw, local_sems.at[ups + 1])]

        def advance(number, step):
            item = pieces[number]
            if step == 0 and number < ups:
                local[number].wait()
            total = item.add(step)
            if total is None:
                item.send(step + 1)
            elif number < ups:
                up_out[:, number * 128 : (number + 1) * 128] = total
            else:
                if number == ups:
                    swap_out[core] = total
                else:
                    swap_qkv[number - ups - 1, core] = total
                swaps[number - ups].start()

        def advance_small(copies, sent, received, out, step):
            copies[step].wait_recv()
            total = sent[step] + received[step]
            if step + 1 < steps:
                sent[step + 1] = total
                copies[step + 1].start()
            else:
                out[...] = total

        @pl.when(pid == 0)
        def _():
            place.greet()
            for number in range(ups):
                pieces[number].send(0)
                local[number].start()
            small_sent[0] = small[...]
            small_copies[0].start()
            for load in loads:
                load.start()
            grads_t = ga[...].T
            result = jnp.dot(grads_t, mix[...], preferred_element_type=jnp.float32).astype(jnp.bfloat16)
            for w in range(wide):
                for h in range(2):
                    for y in range(half):
                        at = (w * 2 + h) * o_rows
                        out_own[bits_of(w, wide_bits) + bits_of(y, half_bits) + (h,)] = result[
                            at : at + o_rows, y * lanes : (y + 1) * lanes
                        ]
            pieces[ups].send(0)
            grad_mixed = dot_last(ga[...], ow[...]).astype(jnp.bfloat16)
            for pair in range(pairs):
                gm[pair] = grad_mixed[:, pair * 128 : (pair + 1) * 128]
                mix_pair[pair] = mix[:, pair * 128 : (pair + 1) * 128]

        @pl.when((pid >= 1) & (pid < first_q))
        def _():
            number = pid - 1
            pair, doc = number // docs, number % docs
            some = pl.ds(pl.multiple_of(doc * length, length), length)
            lane = lax.broadcasted_iota(jnp.int32, (1, 128), 1)
            scale = jnp.bfloat16(HEAD_DIM**-0.5)
            queries, keys, values = q_ref[...] * scale, k_ref[...], v_ref[...]
            grads = gm[pair, some, :]
            product = grads.astype(jnp.float32) * mix_pair[pair, some, :].astype(jnp.float32)
            queries_t, grads_t = queries.T, grads.T
            zero = jnp.zeros_like(queries)
            query_parts = []
            for head in range(2):
                inside = (lane // HEAD_DIM) == head
                at = head * HEAD_DIM
                scores = dot_last(jnp.where(inside, queries, zero), keys) + bias[0]
                attention = jnp.exp(scores - tot_ref[:, at : at + 1])
                chance = dot_last(jnp.where(inside, grads, zero), values)
                inner = jnp.sum(jnp.where(inside, product, 0.0), -1, keepdims=True)
                grad_scores = (attention * (chance - inner)).astype(jnp.bfloat16)
                query_parts.append(jnp.dot(grad_scores, keys, preferred_element_type=jnp.float32))
                key_t = jnp.dot(queries_t[at : at + HEAD_DIM], grad_scores, preferred_element_type=jnp.float32)
                value_t = jnp.dot(grads_t[at : at + HEAD_DIM], attention.astype(jnp.bfloat16),
                                  preferred_element_type=jnp.float32)
                row = pair * 128 + at
                gqkv_t[pl.ds(pl.multiple_of(width + row, HEAD_DIM), HEAD_DIM), some] = key_t.astype(jnp.bfloat16)
                gqkv_t[pl.ds(pl.multiple_of(2 * width + row, HEAD_DIM), HEAD_DIM), some] = value_t.astype(jnp.bfloat16)
            grad_query = jnp.where(lane < HEAD_DIM, query_parts[0], query_parts[1]) * HEAD_DIM**-0.5
            gqkv_t[pl.ds(pl.multiple_of(pair * 128, 128), 128), some] = grad_query.astype(jnp.bfloat16).T

        for part in range(q_parts):
            @pl.when(pid == first_q + part)
            def _():
                if part == 0:
                    for load in loads:
                        load.wait()
                    ones = jnp.ones((8, rows), jnp.bfloat16)
                    late_sent[0] = jnp.concatenate(
                        [dot_last(ones, gqkv_t[:width, :]), dot_last(ones, gqkv_t[2 * width :, :])], axis=1
                    )
                    late_copies[0].start()
                columns = jnp.concatenate(
                    [tok[:, y * lanes + part * 128 : y * lanes + (part + 1) * 128] for y in range(half)], axis=1
                )
                result = jnp.dot(gqkv_t[...], columns, preferred_element_type=jnp.float32).astype(jnp.bfloat16)
                for w in range(wide):
                    for h in range(2):
                        for y in range(half):
                            at = (w * 2 + h) * q_rows
                            qkv_own[(part,) + bits_of(w, wide_bits) + bits_of(y, half_bits) + (h,)] = result[
                                at : at + q_rows, y * 128 : (y + 1) * 128
                            ]
                pieces[ups + 1 + part].send(0)

        @pl.when(pid >= first_t)
        def _():
            at = pl.multiple_of((pid - first_t) * token_block, token_block)
            some = pl.ds(at, token_block)
            grad_t = jnp.dot(qw[...], gqkv_t[:, some], preferred_element_type=jnp.float32)
            tokens_out[some, :] = (grad_t.T + ga[some, :].astype(jnp.float32)).astype(jnp.bfloat16)

        plan, small_plan, late_plan = {}, {}, {}
        for step, at in enumerate((4, 7, 8, 11)):
            for number in range(ups):
                plan.setdefault(at, []).append((number, step))
        for step, at in enumerate((1, 7, 9, 10, 12)):
            plan.setdefault(at, []).append((ups, step))
        for part in range(q_parts):
            for step in range(steps):
                plan.setdefault(first_q + part + 1 if step == 0 else grid - 1, []).append((ups + 1 + part, step))
        for step, at in enumerate((2, 3, 5, 7, 9)):
            small_plan[at] = step
        for step in range(steps):
            late_plan[first_q + 1 + step] = step
        for at in range(grid):
            @pl.when(pid == at)
            def _():
                if at in small_plan:
                    advance_small(small_copies, small_sent, small_received, small_out, small_plan[at])
                for number, step in sorted(plan.get(at, []), key=lambda entry: (entry[1], entry[0])):
                    advance(number, step)
                if at in late_plan:
                    advance_small(late_copies, late_sent, late_received, late_out, late_plan[at])
                if at == grid - 1:
                    for copy in swaps:
                        copy.wait()
                    out_out[...] = swap_out[...]
                    qkv_out[...] = swap_qkv[...]
                    for item in pieces:
                        item.close()
                    for copy in small_copies + late_copies:
                        copy.wait_send()

    def whole(shape):
        return pl.BlockSpec(shape, lambda g: (0,) * len(shape), pipeline_mode=pl.Buffered(1))

    def number_of(g):
        return jnp.clip(g - 1, 0, attn_steps - 1)

    def tile(which):
        return pl.BlockSpec((length, 128), lambda g: (number_of(g) % docs, which * pairs + number_of(g) // docs))

    two = (2,)
    any_space = pl.BlockSpec(memory_space=pl.ANY)
    in_specs = [whole((rows, width)), whole((rows, width)), whole((width, width)), tile(0), tile(1), tile(2), tile(0)]
    in_specs += [pl.BlockSpec((1, 1, length), lambda g: (number_of(g) % docs, 0, 0)), any_space]
    in_specs += [any_space, any_space, whole((small_rows, width))]
    out_shape = [
        jax.ShapeDtypeStruct((rows, width), jnp.bfloat16),
        jax.ShapeDtypeStruct((u_rows, ups * 128), jnp.float32),
        jax.ShapeDtypeStruct((2, o_rows, lanes), jnp.float32),
        jax.ShapeDtypeStruct((q_parts, 2, q_rows, 128), jnp.float32),
        jax.ShapeDtypeStruct((small_rows, width), jnp.float32),
        jax.ShapeDtypeStruct((8, 2 * width), jnp.float32),
    ]
    wide_dims, half_dims = two * wide_bits, two * half_bits
    scratch = [
        pltpu.VMEM((pairs, rows, 128), jnp.bfloat16),
        pltpu.VMEM((pairs, rows, 128), jnp.bfloat16),
        pltpu.VMEM((3 * width, rows), jnp.bfloat16),
        pltpu.VMEM(up_grads.shape, jnp.bfloat16),
        pltpu.VMEM(wide_dims + half_dims + two + (o_rows, lanes), jnp.bfloat16),
        pltpu.VMEM((q_parts,) + wide_dims + half_dims + two + (q_rows, 128), jnp.bfloat16),
    ]
    scratch += [pltpu.VMEM((ups,) + two * (steps - 2 - s) + (u_rows, 128), jnp.bfloat16) for s in range(steps - 1)]
    scratch += [pltpu.VMEM(two * (steps - 1 - s) + (o_rows, lanes), jnp.bfloat16) for s in range(steps)]
    scratch += [pltpu.VMEM((q_parts,) + two * (steps - 1 - s) + (q_rows, 128), jnp.bfloat16) for s in range(steps)]
    scratch += [pltpu.VMEM((steps, small_rows, width), jnp.float32)] * 2
    scratch += [pltpu.VMEM((steps, 8, 2 * width), jnp.float32)] * 2
    scratch += [pltpu.VMEM(out_shape[2].shape, jnp.float32), pltpu.VMEM(out_shape[3].shape, jnp.float32)]
    scratch += [pltpu.VMEM(tokens.shape, jnp.bfloat16), pltpu.VMEM(qkv_weight.shape, jnp.bfloat16)]
    sems = count * steps + 2 * steps + 1 + q_parts
    scratch += [pltpu.SemaphoreType.DMA((sems,)), pltpu.SemaphoreType.DMA((sems,)), pltpu.SemaphoreType.DMA((ups + 2,))]
    return pl.pallas_call(
        kernel,
        grid=(grid,),
        in_specs=in_specs,
        out_specs=[whole(item.shape) for item in out_shape],
        out_shape=out_shape,
        scratch_shapes=scratch,
        compiler_params=pltpu.CompilerParams(collective_id=1, has_side_effects=True, vmem_limit_bytes=60 << 20),
        name="attention_backward",
    )(grad_attended, mixed, out_weight, qkv, qkv, qkv, totals, key_bias, tokens, qkv_weight, up_grads, sums)


def on_device_fast(
    tokens,
    doc_lengths,
    qkv_weight,
    query_bias,
    value_bias,
    out_weight,
    out_bias,
    first_gain,
    first_shift,
    up_weight,
    up_bias,
    down_weight,
    down_bias,
    second_gain,
    second_shift,
    dir_weight,
    dir_bias,
    segment_rows,
    segment_slots,
    pair_rows,
    pair_labels,
    out_cotangent,
):
    doc_count, length, model_width = tokens.shape
    low = jnp.bfloat16
    token_rows = tokens.reshape(doc_count * length, model_width)
    allowed = lax.broadcasted_iota(jnp.int32, (doc_count, length), 1) < doc_lengths[:, None]
    key_bias = jnp.where(allowed, 0.0, MASKED).astype(jnp.float32).reshape(doc_count, 1, length)
    allowed_rows = allowed.reshape(-1, 1).astype(jnp.float32)
    bias_row = jnp.concatenate([query_bias, jnp.zeros_like(query_bias), value_bias]).astype(jnp.float32)
    qkv = (jnp.dot(token_rows, qkv_weight, preferred_element_type=jnp.float32) + bias_row).astype(low)
    mixed, totals = attention_forward(qkv, key_bias, doc_count, length)
    attended = jnp.dot(mixed, out_weight, preferred_element_type=jnp.float32) + out_bias.astype(jnp.float32)
    resid_one = token_rows.astype(jnp.float32) + attended
    hidden_one, normed_one, inverse_one = norm_forward(
        resid_one, first_gain.astype(jnp.float32), first_shift.astype(jnp.float32)
    )
    hidden_low = hidden_one.astype(low)
    upper_pre = jnp.dot(hidden_low, up_weight, preferred_element_type=jnp.float32) + up_bias.astype(jnp.float32)
    cumulative = normal_cdf(upper_pre)
    active = (upper_pre * cumulative).astype(low)
    density = jnp.exp(-0.5 * upper_pre * upper_pre) * 0.3989422804014327
    slope = (cumulative + upper_pre * density).astype(low)
    lowered = jnp.dot(active, down_weight, preferred_element_type=jnp.float32) + down_bias.astype(jnp.float32)
    resid_two = hidden_one + lowered
    second_float = second_gain.astype(jnp.float32)
    normed_out, normed_two, inverse_two = norm_forward(resid_two, second_float, second_shift.astype(jnp.float32))
    encoded_rows = (normed_out * allowed_rows).astype(low)
    classes_count = dir_weight.shape[1]
    doc_starts = lax.broadcasted_iota(jnp.int32, (doc_count, 1), 0) * length
    numbers = jnp.concatenate(
        [(segment_rows + doc_starts).reshape(1, -1), segment_slots, pair_rows[:, :, 0], pair_rows[:, :, 1], pair_labels]
    )
    numbers = jnp.pad(numbers, ((0, -numbers.shape[0] % 8), (0, 0)))
    dir_rows = dir_weight.reshape(2, model_width, classes_count).transpose(0, 2, 1).reshape(-1, model_width)
    grad_attended, up_blocks, out_down, sums = ffn_backward(
        doc_lengths, numbers, encoded_rows, out_cotangent.reshape(-1, model_width), dir_rows,
        dir_bias.astype(jnp.float32)[:, None], normed_two.astype(low), inverse_two, second_float[None], active, slope,
        hidden_low, down_weight, up_weight, normed_one.astype(low), inverse_one, first_gain.astype(jnp.float32)[None],
    )
    grad_tokens, out_up, out_out, out_qkv, sums, late = attention_backward(
        grad_attended, mixed, out_weight, qkv, totals, key_bias, token_rows, qkv_weight, up_blocks, sums
    )
    core = lax.axis_index("narrow") % 2
    width = model_width // lax.axis_size("narrow")
    out_qkv = out_qkv.transpose(1, 2, 0, 3).reshape(-1, 2 * width)
    out_out = out_out.reshape(-1, 2 * width)

    def own_lanes(rows):
        return lax.dynamic_slice_in_dim(rows, core * width, width, 1).T

    first_dir = 6 + lax.axis_size("narrow")
    last_dir = first_dir + 2 * classes_count
    dir_sum = sums[first_dir:last_dir].reshape(2, classes_count, model_width).transpose(0, 2, 1)
    return (
        encoded_rows.reshape(tokens.shape),
        grad_tokens.reshape(tokens.shape),
        own_lanes(out_qkv),
        late[0, :model_width],
        late[0, model_width:],
        own_lanes(out_out),
        sums[5],
        sums[3],
        sums[4],
        out_up,
        sums[6:first_dir].reshape(-1),
        out_down.T,
        sums[2],
        sums[0],
        sums[1],
        dir_sum.reshape(2 * model_width, classes_count),
        sums[last_dir : last_dir + classes_count, 0],
    )


def on_device(
    tokens,
    doc_lengths,
    qkv_weight,
    query_bias,
    value_bias,
    out_weight,
    out_bias,
    first_gain,
    first_shift,
    up_weight,
    up_bias,
    down_weight,
    down_bias,
    second_gain,
    second_shift,
    dir_weight,
    dir_bias,
    segment_rows,
    segment_slots,
    pair_rows,
    pair_labels,
    out_cotangent,
):
    doc_count, length, model_width = tokens.shape
    score_scale = HEAD_DIM ** (-0.5)
    token_rows = tokens.reshape(doc_count * length, model_width)
    allowed = lax.broadcasted_iota(jnp.int32, (doc_count, length), 1) < doc_lengths[:, None]
    allowed_rows = allowed.reshape(-1, 1).astype(jnp.float32)
    bias_row = jnp.concatenate([query_bias, jnp.zeros_like(query_bias), value_bias]).astype(
        jnp.float32
    )
    qkv = (jnp.dot(token_rows, qkv_weight, preferred_element_type=jnp.float32) + bias_row).astype(
        jnp.bfloat16
    )

    def split_heads(doc_block, which):
        return doc_block[:, which * model_width : (which + 1) * model_width].reshape(
            length, HEADS, HEAD_DIM
        )

    def scores_of(queries, key_rows, doc_mask):
        scores = (
            jnp.einsum("qhd,khd->hqk", queries, key_rows, preferred_element_type=jnp.float32)
            * score_scale
        )
        return jnp.where(doc_mask[None, None, :], scores, MASKED)

    mixed_parts = []
    log_totals = []
    for doc_index in range(doc_count):
        doc_block = qkv[doc_index * length : (doc_index + 1) * length]
        queries = split_heads(doc_block, 0)
        key_rows = split_heads(doc_block, 1)
        value_rows = split_heads(doc_block, 2)
        scores = scores_of(queries, key_rows, allowed[doc_index])
        highest = jnp.max(scores, -1, keepdims=True)
        powers = jnp.exp(scores - highest)
        summed = jnp.sum(powers, -1, keepdims=True)
        attention = (powers / summed).astype(jnp.bfloat16)
        log_totals.append(highest + jnp.log(summed))
        mixed_parts.append(
            jnp.einsum(
                "hqk,khd->qhd", attention, value_rows, preferred_element_type=jnp.float32
            ).reshape(length, model_width)
        )
    mixed = jnp.concatenate(mixed_parts).astype(jnp.bfloat16)
    attended = jnp.dot(mixed, out_weight, preferred_element_type=jnp.float32) + out_bias.astype(
        jnp.float32
    )
    resid_one = token_rows.astype(jnp.float32) + attended
    hidden_one, normed_one, inverse_one = norm_forward(
        resid_one, first_gain.astype(jnp.float32), first_shift.astype(jnp.float32)
    )
    hidden_low = hidden_one.astype(jnp.bfloat16)
    upper_pre = jnp.dot(hidden_low, up_weight, preferred_element_type=jnp.float32) + up_bias.astype(
        jnp.float32
    )
    cumulative = normal_cdf(upper_pre)
    active = (upper_pre * cumulative).astype(jnp.bfloat16)
    lowered = jnp.dot(active, down_weight, preferred_element_type=jnp.float32) + down_bias.astype(
        jnp.float32
    )
    resid_two = hidden_one + lowered
    second_float = second_gain.astype(jnp.float32)
    normed_out, normed_two, inverse_two = norm_forward(
        resid_two, second_float, second_shift.astype(jnp.float32)
    )
    encoded_rows = (normed_out * allowed_rows).astype(jnp.bfloat16)
    doc_starts = lax.broadcasted_iota(jnp.int32, (doc_count, 1), 0) * length
    picked_rows = (segment_rows + doc_starts).reshape(-1)
    picked = encoded_rows[picked_rows]
    slots = segment_slots.reshape(-1)
    outgoing = jnp.zeros_like(picked).at[slots].set(picked)
    arrived = lax.all_to_all(outgoing, "wide", split_axis=0, concat_axis=0, tiled=True)
    pairs = pair_rows.reshape(-1, 2)
    labels = pair_labels.reshape(-1)
    first_rows = arrived[pairs[:, 0]]
    second_rows = arrived[pairs[:, 1]]
    logits = (
        jnp.dot(first_rows, dir_weight[:model_width], preferred_element_type=jnp.float32)
        + jnp.dot(second_rows, dir_weight[model_width:], preferred_element_type=jnp.float32)
        + dir_bias.astype(jnp.float32)
    )
    powers_head = jnp.exp(logits - jnp.max(logits, -1, keepdims=True))
    chance = powers_head / jnp.sum(powers_head, -1, keepdims=True)
    classes = lax.broadcasted_iota(jnp.int32, logits.shape, 1)
    delta = chance - (labels[:, None] == classes).astype(jnp.float32)
    first_float = first_rows.astype(jnp.float32)
    second_rows_float = second_rows.astype(jnp.float32)
    grad_dir_weight = jnp.concatenate(
        [
            jnp.dot(first_float.T, delta, precision=EXACT, preferred_element_type=jnp.float32),
            jnp.dot(
                second_rows_float.T, delta, precision=EXACT, preferred_element_type=jnp.float32
            ),
        ]
    )
    grad_dir_bias = jnp.sum(delta, 0)
    dir_float = dir_weight.astype(jnp.float32)
    grad_first = jnp.dot(
        delta, dir_float[:model_width].T, precision=EXACT, preferred_element_type=jnp.float32
    )
    grad_second = jnp.dot(
        delta, dir_float[model_width:].T, precision=EXACT, preferred_element_type=jnp.float32
    )
    grad_arrived = jnp.zeros((arrived.shape[0], model_width), jnp.float32)
    grad_arrived = grad_arrived.at[pairs[:, 0]].add(grad_first).at[pairs[:, 1]].add(grad_second)
    returned = lax.all_to_all(
        grad_arrived.astype(jnp.bfloat16), "wide", split_axis=0, concat_axis=0, tiled=True
    )
    grad_picked = returned[slots].astype(jnp.float32)
    grad_encoded = (
        out_cotangent.reshape(-1, model_width).astype(jnp.float32).at[picked_rows].add(grad_picked)
    )
    grad_encoded = grad_encoded * allowed_rows
    grad_two, grad_second_gain, grad_second_shift = norm_backward(
        grad_encoded, normed_two, inverse_two, second_float
    )
    grad_lowered = grad_two.astype(jnp.bfloat16)
    grad_down_weight = jnp.einsum(
        "rf,rd->fd", active, grad_lowered, preferred_element_type=jnp.float32
    )
    grad_down_bias = jnp.sum(grad_lowered.astype(jnp.float32), 0)
    grad_active = jnp.einsum(
        "rd,fd->rf", grad_lowered, down_weight, preferred_element_type=jnp.float32
    )
    density = jnp.exp(-0.5 * upper_pre * upper_pre) * 0.3989422804014327
    grad_upper = (grad_active * (cumulative + upper_pre * density)).astype(jnp.bfloat16)
    grad_up_weight = jnp.einsum(
        "rd,rf->df", hidden_low, grad_upper, preferred_element_type=jnp.float32
    )
    grad_up_bias = jnp.sum(grad_upper.astype(jnp.float32), 0)
    grad_hidden = grad_two + jnp.einsum(
        "rf,df->rd", grad_upper, up_weight, preferred_element_type=jnp.float32
    )
    grad_one, grad_first_gain, grad_first_shift = norm_backward(
        grad_hidden, normed_one, inverse_one, first_gain.astype(jnp.float32)
    )
    grad_attended = grad_one.astype(jnp.bfloat16)
    grad_out_weight = jnp.einsum(
        "rd,re->de", mixed, grad_attended, preferred_element_type=jnp.float32
    )
    grad_out_bias = jnp.sum(grad_attended.astype(jnp.float32), 0)
    grad_mixed = jnp.einsum(
        "re,de->rd", grad_attended, out_weight, preferred_element_type=jnp.float32
    ).astype(jnp.bfloat16)
    grad_parts = []
    for doc_index in range(doc_count):
        doc_block = qkv[doc_index * length : (doc_index + 1) * length]
        queries = split_heads(doc_block, 0)
        key_rows = split_heads(doc_block, 1)
        value_rows = split_heads(doc_block, 2)
        scores = scores_of(queries, key_rows, allowed[doc_index])
        attention = jnp.exp(scores - log_totals[doc_index])
        grad_doc = grad_mixed[doc_index * length : (doc_index + 1) * length].reshape(
            length, HEADS, HEAD_DIM
        )
        grad_chance = jnp.einsum(
            "qhd,khd->hqk", grad_doc, value_rows, preferred_element_type=jnp.float32
        )
        inner = jnp.sum(grad_chance * attention, -1, keepdims=True)
        grad_scores = (attention * (grad_chance - inner)).astype(jnp.bfloat16)
        grad_query = (
            jnp.einsum("hqk,khd->qhd", grad_scores, key_rows, preferred_element_type=jnp.float32)
            * score_scale
        )
        grad_key = (
            jnp.einsum("hqk,qhd->khd", grad_scores, queries, preferred_element_type=jnp.float32)
            * score_scale
        )
        grad_value = jnp.einsum(
            "hqk,qhd->khd",
            attention.astype(jnp.bfloat16),
            grad_doc,
            preferred_element_type=jnp.float32,
        )
        grad_parts.append(
            jnp.concatenate(
                [
                    grad_query.reshape(length, model_width),
                    grad_key.reshape(length, model_width),
                    grad_value.reshape(length, model_width),
                ],
                axis=1,
            )
        )
    grad_qkv = jnp.concatenate(grad_parts).astype(jnp.bfloat16)
    grad_qkv_float = grad_qkv.astype(jnp.float32)
    grad_query_bias = jnp.sum(grad_qkv_float[:, :model_width], 0)
    grad_value_bias = jnp.sum(grad_qkv_float[:, 2 * model_width :], 0)
    grad_qkv_weight = jnp.einsum(
        "rd,re->de", token_rows, grad_qkv, preferred_element_type=jnp.float32
    )
    grad_tokens = (
        jnp.einsum("re,de->rd", grad_qkv, qkv_weight, preferred_element_type=jnp.float32) + grad_one
    ).astype(jnp.bfloat16)
    matrices = (grad_qkv_weight, grad_out_weight, grad_up_weight, grad_down_weight)
    partial_sums = (
        lax.psum_scatter(
            matrices[0].astype(jnp.bfloat16), "wide", scatter_dimension=1, tiled=True
        ).astype(jnp.float32),
        lax.psum_scatter(
            matrices[1].astype(jnp.bfloat16), "wide", scatter_dimension=1, tiled=True
        ).astype(jnp.float32),
        lax.psum_scatter(
            matrices[2].astype(jnp.bfloat16), "wide", scatter_dimension=1, tiled=True
        ).astype(jnp.float32),
        lax.psum_scatter(
            matrices[3].astype(jnp.bfloat16), "wide", scatter_dimension=1, tiled=True
        ).astype(jnp.float32),
    )
    summed_mats = (
        lax.psum_scatter(
            partial_sums[0].astype(jnp.bfloat16), "narrow", scatter_dimension=0, tiled=True
        ).astype(jnp.float32),
        lax.psum_scatter(
            partial_sums[1].astype(jnp.bfloat16), "narrow", scatter_dimension=0, tiled=True
        ).astype(jnp.float32),
        lax.psum_scatter(
            partial_sums[2].astype(jnp.bfloat16), "narrow", scatter_dimension=0, tiled=True
        ).astype(jnp.float32),
        lax.psum_scatter(
            partial_sums[3].astype(jnp.bfloat16), "narrow", scatter_dimension=0, tiled=True
        ).astype(jnp.float32),
    )
    smalls = lax.psum(
        (
            grad_query_bias,
            grad_value_bias,
            grad_out_bias,
            grad_first_gain,
            grad_first_shift,
            grad_up_bias,
            grad_down_bias,
            grad_second_gain,
            grad_second_shift,
            grad_dir_weight,
            grad_dir_bias,
        ),
        ("wide", "narrow"),
    )
    return (
        encoded_rows.reshape(tokens.shape),
        grad_tokens.reshape(tokens.shape),
        summed_mats[0],
        smalls[0],
        smalls[1],
        summed_mats[1],
        smalls[2],
        smalls[3],
        smalls[4],
        summed_mats[2],
        smalls[5],
        summed_mats[3],
        smalls[6],
        smalls[7],
        smalls[8],
        smalls[9],
        smalls[10],
    )


def fits_blocks(mesh):
    wide, narrow = mesh.shape["wide"], mesh.shape["narrow"]
    width, ff = HEADS * HEAD_DIM, 4 * HEADS * HEAD_DIM
    if wide != 2 * narrow or narrow < 4 or narrow & (narrow - 1):
        return False
    lanes = (ff // narrow, ff // wide, 2 * width // narrow)
    rows = (width // wide, width // narrow, width // wide // 2, 3 * width // wide // 2)
    return all(size % 128 == 0 for size in lanes) and all(size % 16 == 0 for size in rows)


def solution(mesh):
    placed = (
        P(("wide", "narrow"), None, None),
        P(("wide", "narrow")),
        P(),
        P(),
        P(),
        P(),
        P(),
        P(),
        P(),
        P(),
        P(),
        P(),
        P(),
        P(),
        P(),
        P(),
        P(),
        P(("wide", "narrow"), None),
        P(("wide", "narrow"), None),
        P(("wide", "narrow"), None, None),
        P(("wide", "narrow"), None),
        P(("wide", "narrow"), None, None),
    )
    return jax.shard_map(
        on_device_fast if fits_blocks(mesh) else on_device,
        mesh=mesh,
        in_specs=placed,
        out_specs=(
            P(("wide", "narrow"), None, None),
            P(("wide", "narrow"), None, None),
            P("narrow", "wide"),
            P(),
            P(),
            P("narrow", "wide"),
            P(),
            P(),
            P(),
            P("narrow", "wide"),
            P(),
            P("narrow", "wide"),
            P(),
            P(),
            P(),
            P(),
            P(),
        ),
        check_vma=False,
    )
```

```python
import jax
import jax.numpy as jnp
from jax import lax
from jax.experimental import pallas as pl
from jax.experimental.pallas import tpu as pltpu
from jax.sharding import PartitionSpec as P

HEADS = 12
HEAD_DIM = 64


EXACT = lax.Precision.HIGHEST
MASKED = -1e30
EPSILON = 1e-05


def norm_forward(values, gain, shift):
    center = jnp.mean(values, -1, keepdims=True)
    centered = values - center
    inverse = lax.rsqrt(jnp.mean(centered * centered, -1, keepdims=True) + EPSILON)
    normed = centered * inverse
    return (normed * gain + shift, normed, inverse)


def norm_backward(grad, normed, inverse, gain):
    scaled = grad * gain
    first_mean = jnp.mean(scaled, -1, keepdims=True)
    second_mean = jnp.mean(scaled * normed, -1, keepdims=True)
    return (
        (scaled - first_mean - normed * second_mean) * inverse,
        jnp.sum(grad * normed, 0),
        jnp.sum(grad, 0),
    )


def normal_cdf(values):
    return 0.5 * (1.0 + lax.erf(values * 0.7071067811865476))


MESH_ID = pl.DeviceIdType.MESH


def axis_bits():
    names = []
    for axis in ("wide", "narrow"):
        count = lax.axis_size(axis).bit_length() - 1
        names += [(axis, bit) for bit in reversed(range(count))]
    return names


class Place:
    def __init__(self):
        self.index = {axis: lax.axis_index(axis) for axis in ("wide", "narrow")}
        self.names = axis_bits()
        self.bit = {name: (self.index[name[0]] // (1 << name[1])) % 2 for name in self.names}

    def across(self, name):
        axis, bit = name
        target = dict(self.index)
        target[axis] = target[axis] + (1 << bit) - (2 << bit) * self.bit[name]
        return target

    def ahead(self, offset):
        target = dict(self.index)
        target["wide"] = (target["wide"] + offset) % lax.axis_size("wide")
        return target

    def greet(self, all_wide=False):
        barrier = pltpu.get_barrier_semaphore()
        targets = [self.across(name) for name in self.names if not (all_wide and name[0] == "wide")]
        if all_wide:
            targets += [self.ahead(offset) for offset in range(1, lax.axis_size("wide"))]
        for target in targets:
            pl.semaphore_signal(barrier, inc=1, device_id=target, device_id_type=MESH_ID)
        pl.semaphore_wait(barrier, len(targets))


class Halving:
    def __init__(self, place, names, order, source, own, received, send_sems, recv_sems, first_sem, tail=()):
        self.place, self.names, self.order = place, names, order
        self.source, self.own, self.received = source, own, received
        self.last = True
        self.send_sems, self.recv_sems, self.first_sem, self.tail = send_sems, recv_sems, first_sem, tail

    def region(self, step, mine):
        index = []
        for name in self.names:
            if name in self.order[:step]:
                index.append(self.place.bit[name])
            elif name == self.order[step]:
                index.append(self.place.bit[name] if mine else 1 - self.place.bit[name])
            else:
                index.append(slice(None))
        return tuple(index) + self.tail

    def copy(self, step):
        held = self.source if step == 0 else self.own
        return pltpu.make_async_remote_copy(
            src_ref=held.at[self.region(step, False)],
            dst_ref=self.received[step],
            send_sem=self.send_sems.at[self.first_sem + step],
            recv_sem=self.recv_sems.at[self.first_sem + step],
            device_id=self.place.across(self.order[step]),
            device_id_type=MESH_ID,
        )

    def send(self, step):
        self.copy(step).start()

    def add(self, step):
        self.copy(step).wait_recv()
        mine = self.region(step, True)
        if step + 1 < len(self.order) or not self.last:
            self.own[mine] = self.own[mine] + self.received[step][...]
            return None
        return self.own[mine].astype(jnp.float32) + self.received[step][...].astype(jnp.float32)

    def merge(self, step):
        self.last = False
        self.add(step)

    def close(self):
        for step in range(len(self.order)):
            self.copy(step).wait_send()


def link_orders():
    wide = [("wide", bit) for bit in range(lax.axis_size("wide").bit_length() - 1)]
    narrow = [("narrow", bit) for bit in range(1, lax.axis_size("narrow").bit_length() - 1)]
    core, x, near, far = [("narrow", 0)], wide[:1], wide[1:-1], wide[-1:]
    return [core + narrow + x + near + far, core + x + near + narrow + far, core + near + narrow + x + far]


def attention_forward(lengths, tokens, qkv_weight, vectors):
    rows, width = tokens.shape
    docs = lengths.shape[0]
    length = rows // docs
    pairs = width // 128

    def kernel(lens, tok, wq, wk, wv, vec, q_out, k_out, v_out, attention_out, mixed_out):
        weights = jnp.concatenate([wq[...], wk[...], wv[...]], axis=1)
        at = pl.ds(pl.multiple_of(pl.program_id(0) * 128, 128), 128)
        offsets = jnp.concatenate([vec[6:7, at], jnp.zeros((1, 128), jnp.float32), vec[7:8, at]], axis=1)
        qkv = (jnp.dot(tok[...], weights, preferred_element_type=jnp.float32) + offsets).astype(jnp.bfloat16)
        q_out[...] = qkv[:, :128]
        k_out[...] = qkv[:, 128:256]
        v_out[...] = qkv[:, 256:]
        first = lax.broadcasted_iota(jnp.int32, (1, 128), 1) < HEAD_DIM
        for doc in range(docs):
            some = slice(doc * length, (doc + 1) * length)
            queries = qkv[some, :128] * jnp.bfloat16(HEAD_DIM**-0.5)
            keys, values = qkv[some, 128:256], qkv[some, 256:]
            zero = jnp.zeros_like(queries)
            places = lax.broadcasted_iota(jnp.int32, (1, length), 1)
            bias = jnp.where(places < lens[doc], 0.0, MASKED)
            outs = []
            for head in range(2):
                masked = jnp.where(first, queries, zero) if head == 0 else jnp.where(first, zero, queries)
                scores = dot_last(masked, keys) + bias
                powers = jnp.exp(scores - jnp.max(scores, -1, keepdims=True))
                attention = (powers * (1.0 / jnp.sum(powers, -1, keepdims=True))).astype(jnp.bfloat16)
                attention_out[doc, head] = attention
                outs.append(jnp.dot(attention, values, preferred_element_type=jnp.float32))
            mixed_out[some, :] = jnp.where(first, outs[0], outs[1]).astype(jnp.bfloat16)

    def whole(shape):
        return pl.BlockSpec(shape, lambda pair: (0,) * len(shape), pipeline_mode=pl.Buffered(1))

    column = pl.BlockSpec((rows, 128), lambda pair: (0, pair))
    in_specs = [pl.BlockSpec(memory_space=pltpu.SMEM), whole((rows, width))]
    in_specs += [pl.BlockSpec((width, 128), lambda pair, n=n: (0, n * pairs + pair)) for n in range(3)]
    in_specs += [whole(vectors.shape)]
    low = jax.ShapeDtypeStruct((rows, width), jnp.bfloat16)
    return pl.pallas_call(
        kernel,
        grid=(pairs,),
        in_specs=in_specs,
        out_specs=[column] * 3
        + [pl.BlockSpec((docs, 2, length, length), lambda pair: (0, pair, 0, 0)), column],
        out_shape=[low] * 3 + [jax.ShapeDtypeStruct((docs, 2 * pairs, length, length), jnp.bfloat16), low],
        compiler_params=pltpu.CompilerParams(vmem_limit_bytes=56 << 20),
        name="attention_forward",
    )(lengths, tokens, qkv_weight, qkv_weight, qkv_weight, vectors)


def ffn_forward(lengths, mixed, tokens, out_weight, vectors, up_weight, down_weight):
    rows, width = tokens.shape
    ff = up_weight.shape[1]
    chunk = width
    chunks = ff // chunk
    length = rows // lengths.shape[0]
    row_block = 128

    def kernel(lens, mix, tok, ow, vec, up, down, hid_out, n1_out, q1_out, act_out, slope_out, n2_out, q2_out,
               enc_out, hidden, total):
        pid = pl.program_id(0)

        def each_block(body):
            def step(i, carry):
                body(pl.multiple_of(i * row_block, row_block))
                return carry

            lax.fori_loop(0, rows // row_block, step, 0)

        @pl.when(pid == 0)
        def _():
            total[...] = jnp.dot(mix[...], ow[...], preferred_element_type=jnp.float32)

            def body(at):
                some = pl.ds(at, row_block)
                summed = tok[some, :].astype(jnp.float32) + (total[some, :] + vec[0:1, :])
                out, normed, inverse = norm_forward(summed, vec[1:2, :], vec[2:3, :])
                hidden[some, :] = out
                hid_out[some, :] = out.astype(jnp.bfloat16)
                n1_out[some, :] = normed.astype(jnp.bfloat16)
                q1_out[some, :] = inverse
                total[some, :] = jnp.zeros_like(out)

            each_block(body)

        pre = jnp.dot(hid_out[...], up[...], preferred_element_type=jnp.float32) + vec[pl.ds(pid + 9, 1), :]
        cumulative = normal_cdf(pre)
        density = jnp.exp(-0.5 * pre * pre) * 0.3989422804014327
        active = (pre * cumulative).astype(jnp.bfloat16)
        act_out[...] = active
        slope_out[...] = (cumulative + pre * density).astype(jnp.bfloat16)
        total[...] += jnp.dot(active, down[...], preferred_element_type=jnp.float32)

        @pl.when(pid == chunks - 1)
        def _():
            def body(at):
                some = pl.ds(at, row_block)
                summed = hidden[some, :] + (total[some, :] + vec[3:4, :])
                out, normed, inverse = norm_forward(summed, vec[4:5, :], vec[5:6, :])
                n2_out[some, :] = normed.astype(jnp.bfloat16)
                q2_out[some, :] = inverse
                doc = at // length
                line = lax.broadcasted_iota(jnp.int32, (row_block, 1), 0) + (at - doc * length)
                enc_out[some, :] = jnp.where(line < lens[doc], out, 0.0).astype(jnp.bfloat16)

            each_block(body)

    def whole(shape):
        return pl.BlockSpec(shape, lambda f: (0,) * len(shape), pipeline_mode=pl.Buffered(1))

    wide_row, column = whole((rows, width)), pl.BlockSpec((rows, chunk), lambda f: (0, f))
    low = jax.ShapeDtypeStruct((rows, width), jnp.bfloat16)
    one = jax.ShapeDtypeStruct((rows, 1), jnp.float32)
    upper = jax.ShapeDtypeStruct((rows, ff), jnp.bfloat16)
    return pl.pallas_call(
        kernel,
        grid=(chunks,),
        in_specs=[
            pl.BlockSpec(memory_space=pltpu.SMEM), wide_row, wide_row, whole((width, width)), whole(vectors.shape),
            pl.BlockSpec((width, chunk), lambda f: (0, f)),
            pl.BlockSpec((chunk, width), lambda f: (f, 0)),
        ],
        out_specs=[wide_row, wide_row, whole((rows, 1)), column, column, wide_row, whole((rows, 1)), wide_row],
        out_shape=[low, low, one, upper, upper, low, one, low],
        scratch_shapes=[pltpu.VMEM((rows, width), jnp.float32), pltpu.VMEM((rows, width), jnp.float32)],
        compiler_params=pltpu.CompilerParams(vmem_limit_bytes=58 << 20),
        name="ffn_forward",
    )(lengths, mixed, tokens, out_weight, vectors, up_weight, down_weight)


def dot_last(left, right):
    return lax.dot_general(left, right, (((1,), (1,)), ((), ())), preferred_element_type=jnp.float32)


def norm_back_rows(grad, normed, inverse, gain):
    scaled = grad * gain
    first = jnp.mean(scaled, -1, keepdims=True)
    second = jnp.mean(scaled * normed, -1, keepdims=True)
    return (scaled - first - normed * second) * inverse


def parts_of(values, count):
    terms = []
    for _ in range(count):
        term = values.astype(jnp.bfloat16).astype(jnp.float32)
        terms.append(term)
        values = values - term
    return jnp.concatenate(terms).astype(jnp.bfloat16)


def one_hot(row, count):
    lines = lax.broadcasted_iota(jnp.int32, (count, row.shape[1]), 0)
    return jnp.where(lines == row, 1.0, 0.0).astype(jnp.bfloat16)


def ffn_backward(lengths, numbers, encoded, cotangent, dir_t, vectors, normed_two, inverse_two, active, slope, hidden_low, down_weight, up_weight,
                 normed_one, inverse_one):
    rows, width = hidden_low.shape
    ff = active.shape[1]
    segments, classes = numbers.shape[1], dir_t.shape[0]
    length = rows // lengths.shape[0]
    names = axis_bits()
    steps = len(names)
    wide, narrow = lax.axis_size("wide"), lax.axis_size("narrow")
    wide_bits, narrow_bits = wide.bit_length() - 1, narrow.bit_length() - 1
    chunks = ff // narrow // 128
    third = chunks // 2
    d_rows, u_rows = width // wide, width // narrow
    row_block = 128
    row_steps = rows // row_block
    orders = link_orders()
    two = (2,)
    early = 3
    first_dir = 6 + narrow
    sum_rows = pl.cdiv(first_dir + 3 * classes, 8) * 8

    def chunk_of(step):
        step = jnp.clip(step, 0, chunks - 1)
        return step // 2 + third * (step % 2)

    def bits_of(number, count):
        return tuple((number >> bit) & 1 for bit in reversed(range(count)))

    def kernel(*refs):
        lens, nums, enc, cot, dir_ref = refs[:5]
        refs = refs[5:]
        q2, q1, vec = refs[:3]
        far = refs[3:9]
        slo = refs[9 : 9 + narrow]
        rest = list(refs[9 + narrow :])
        ga_out, up_out, down_out, sums_out = rest[:4]
        rest = rest[4:]
        grad_hidden, lowered, lowered_t, hidden_t, own, up_own, up_received = rest[:7]
        received = rest[7 : 7 + early]
        rest = rest[7 + early :]
        select, picked, dir_w, leaving, arrived, leaving_grads, arrived_grads = rest[:7]
        near = rest[7:13]
        n2, hidden, act, dws, uws, n1 = near
        send_sems, recv_sems, local_sems = rest[13:]
        loads = [pltpu.make_async_copy(far[i], near[i], local_sems.at[2 * chunks + i]) for i in range(len(near))]
        pid = pl.program_id(0)
        place = Place()
        pieces = []
        for number in range(chunks):
            pieces.append(
                Halving(place, names, orders[number % 3][:early], own.at[number], own.at[number],
                        [r.at[number] for r in received], send_sems, recv_sems, number * early)
            )
        core = ("narrow", 0)
        up_names = [name for name in names if name != ("wide", 0)]
        up_pieces = [
            Halving(place, up_names, [core], up_own.at[number], up_own.at[number], [up_received.at[number]],
                    send_sems, recv_sems, chunks * early + number)
            for number in range(chunks)
        ]

        def up_write(number):
            mine = up_pieces[number].region(0, True)
            return pltpu.make_async_copy(
                up_own.at[number].at[mine],
                up_out.at[(number // 2,) + (slice(None),) * (wide_bits - 1) + (number % 2,)],
                local_sems.at[number],
            )

        def exchange(source, landing, first):
            made = []
            for offset in range(1, wide):
                target = place.ahead(offset)
                made.append(pltpu.make_async_remote_copy(
                    src_ref=source.at[target["wide"]], dst_ref=landing.at[place.index["wide"]],
                    send_sem=send_sems.at[first + offset - 1], recv_sem=recv_sems.at[first + offset - 1],
                    device_id=target, device_id_type=MESH_ID))
            me = place.index["wide"]
            for copy in made:
                copy.start()
            landing[me] = source[me]
            for copy in made:
                copy.wait()
            return landing[...].reshape(segments, 128)

        @pl.when(pid == 0)
        def _():
            for load in loads:
                load.start()
            place.greet(all_wide=True)
            sums_out[...] = jnp.zeros_like(sums_out)
            base = chunks * early + chunks
            select[...] = dot_last(one_hot(nums[0:1, :], rows), one_hot(nums[1:2, :], segments)).astype(jnp.bfloat16)
            picked[...] = jnp.dot(select[...].T, enc[...], preferred_element_type=jnp.float32).astype(jnp.bfloat16)
            halves = [dir_ref[:, n * width : (n + 1) * width].astype(jnp.float32) for n in range(2)]
            blank = jnp.zeros((128 - 2 * classes, width), jnp.float32)
            dir_w[...] = jnp.concatenate(halves + [blank]).astype(jnp.bfloat16)
            leaving[...] = dot_last(picked[...], dir_w[...]).reshape(leaving.shape)
            scores = exchange(leaving, arrived, base).T
            pair_first, pair_second = one_hot(nums[2:3, :], segments), one_hot(nums[3:4, :], segments)

            def chosen(values, pairs):
                split = jnp.dot(parts_of(values, 3), pairs, preferred_element_type=jnp.float32)
                return split[:classes] + split[classes : 2 * classes] + split[2 * classes :]

            logits = chosen(scores[:classes], pair_first) + chosen(scores[classes : 2 * classes], pair_second)
            logits = logits + jnp.broadcast_to(vec[8:9, :128], (128, 128)).T[:classes, 0:1]
            powers = jnp.exp(logits - jnp.max(logits, 0, keepdims=True))
            chance = powers / jnp.sum(powers, 0, keepdims=True)
            kinds = lax.broadcasted_iota(jnp.int32, logits.shape, 0)
            delta = chance - jnp.where(kinds == nums[4:5, :], 1.0, 0.0)
            split = parts_of(delta, 2)
            gathered = []
            for pairs in (pair_first, pair_second):
                both = dot_last(split, pairs)
                gathered.append(both[:classes] + both[classes:])
            gathered.append(jnp.zeros((128 - 2 * classes, segments), jnp.float32))
            leaving_grads[...] = jnp.concatenate(gathered).T.reshape(leaving.shape)
            sums_out[first_dir + 2 * classes : first_dir + 3 * classes, :] = jnp.broadcast_to(
                jnp.sum(delta, 1, keepdims=True), (classes, width)
            )
            back = exchange(leaving_grads, arrived_grads, base + wide - 1)
            coarse = back.astype(jnp.bfloat16)
            fine = (back - coarse.astype(jnp.float32)).astype(jnp.bfloat16)
            grads_in = (
                jnp.dot(coarse, dir_w[...], preferred_element_type=jnp.float32)
                + jnp.dot(fine, dir_w[...], preferred_element_type=jnp.float32)
            ).astype(jnp.bfloat16)
            back_t = back.T[: 2 * classes]
            both = jnp.dot(parts_of(back_t, 2), picked[...], preferred_element_type=jnp.float32)
            sums_out[first_dir : first_dir + 2 * classes, :] = both[: 2 * classes] + both[2 * classes :]
            loads[0].wait()
            loads[1].wait()

            def body(i, carry):
                at = pl.multiple_of(i * row_block, row_block)
                some = pl.ds(at, row_block)
                normed = n2[some, :].astype(jnp.float32)
                doc = at // length
                line = lax.broadcasted_iota(jnp.int32, (row_block, 1), 0) + (at - doc * length)
                grad = cot[some, :].astype(jnp.float32) + jnp.dot(
                    select[some, :], grads_in, preferred_element_type=jnp.float32
                )
                grad = jnp.where(line < lens[doc], grad, 0.0)
                two = norm_back_rows(grad, normed, q2[some, :], vec[4:5, :])
                low = two.astype(jnp.bfloat16)
                grad_hidden[some, :] = two
                lowered[some, :] = low
                lowered_t[:, some] = low.T
                hidden_t[:, some] = hidden[some, :].T
                sums_out[0:1, :] += jnp.sum(grad * normed, 0, keepdims=True)
                sums_out[1:2, :] += jnp.sum(grad, 0, keepdims=True)
                sums_out[2:3, :] += jnp.sum(low.astype(jnp.float32), 0, keepdims=True)
                return carry

            lax.fori_loop(0, row_steps, body, 0)

        def slab(n, step):
            return pl.ds(pl.multiple_of((n * chunks + chunk_of(step)) * 128, 128), 128)

        @pl.when(pid == 0)
        def _():
            loads[2].wait()

        @pl.when(pid < chunks)
        def _():
            actives = jnp.concatenate([act[:, slab(n, pid)] for n in range(narrow)], axis=1)
            result = jnp.dot(lowered_t[...], actives, preferred_element_type=jnp.float32).astype(jnp.bfloat16)
            for w in range(wide):
                for n in range(narrow):
                    own[(pid,) + bits_of(w, wide_bits) + bits_of(n, narrow_bits)] = result[
                        w * d_rows : (w + 1) * d_rows, n * 128 : (n + 1) * 128
                    ]

        @pl.when(pid == chunks)
        def _():
            for load in loads[3:]:
                load.wait()

        @pl.when(pid >= chunks)
        def _():
            slopes = jnp.concatenate([ref[...] for ref in slo], axis=1)
            downs = jnp.concatenate([dws[slab(n, pid - chunks), :] for n in range(narrow)], axis=0)
            ups = jnp.concatenate([uws[:, slab(n, pid - chunks)] for n in range(narrow)], axis=1)
            grad_active = dot_last(lowered[...], downs)
            grad_upper = (grad_active * slopes.astype(jnp.float32)).astype(jnp.bfloat16)
            totals = jnp.sum(grad_upper.astype(jnp.float32), 0, keepdims=True)
            at = pl.ds(pl.multiple_of(chunk_of(pid - chunks) * 128, 128), 128)
            for n in range(narrow):
                sums_out[6 + n : 7 + n, at] = totals[:, n * 128 : (n + 1) * 128]
            result = jnp.dot(hidden_t[...], grad_upper, preferred_element_type=jnp.float32).astype(jnp.bfloat16)
            for n in range(narrow):
                for z in range(narrow):
                    high = bits_of(z, wide_bits - 1)
                    up_own[(pid - chunks,) + high + bits_of(n, narrow_bits)] = result[
                        n * u_rows : (n + 1) * u_rows, z * 128 : (z + 1) * 128
                    ]
            grad_hidden[...] += dot_last(grad_upper, ups)

        def down_write(number):
            return pltpu.make_async_copy(
                own.at[number].at[pieces[number].region(early - 1, True)], down_out.at[number], local_sems.at[chunks + number]
            )

        def advance(number, step):
            pieces[number].merge(step)
            if step + 1 < early:
                pieces[number].send(step + 1)
            else:
                down_write(number).start()

        for number in range(chunks):
            @pl.when(pid == chunks + number)
            def _():
                up_pieces[number].send(0)

        @pl.when(pid == 2 * chunks - 1)
        def _():
            def body(i, carry):
                at = pl.multiple_of(i * row_block, row_block)
                some = pl.ds(at, row_block)
                grad, normed = grad_hidden[some, :], n1[some, :].astype(jnp.float32)
                low = norm_back_rows(grad, normed, q1[some, :], vec[1:2, :]).astype(jnp.bfloat16)
                ga_out[some, :] = low
                sums_out[3:4, :] += jnp.sum(grad * normed, 0, keepdims=True)
                sums_out[4:5, :] += jnp.sum(grad, 0, keepdims=True)
                sums_out[5:6, :] += jnp.sum(low.astype(jnp.float32), 0, keepdims=True)
                return carry

            lax.fori_loop(0, row_steps, body, 0)

        plan = {}
        for number in range(chunks):
            for step in range(early):
                at = (number + 1, chunks + 1 + 2 * (number // 3), chunks + 4 + number // 3)[step]
                plan.setdefault(min(at, 2 * chunks - 1), []).append((step, number))
        for at in range(2 * chunks):
            @pl.when(pid == at)
            def _():
                if at < chunks:
                    pieces[at].send(0)
                if at > chunks:
                    up_pieces[at - chunks - 1].merge(0)
                    up_write(at - chunks - 1).start()
                for step, number in sorted(plan.get(at, [])):
                    advance(number, step)
                if at == 2 * chunks - 1:
                    up_pieces[chunks - 1].merge(0)
                    up_write(chunks - 1).start()
                    for number in range(chunks):
                        up_write(number).wait()
                        down_write(number).wait()
                    for item in pieces + up_pieces:
                        item.close()

    def whole(shape):
        return pl.BlockSpec(shape, lambda g: (0,) * len(shape), pipeline_mode=pl.Buffered(1))

    def slab_columns(shape, first):
        return [pl.BlockSpec(shape, lambda g, n=n: (0, n * chunks + chunk_of(g - first))) for n in range(narrow)]

    in_specs = [pl.BlockSpec(memory_space=pltpu.SMEM), whole(numbers.shape), whole((rows, width)), whole((rows, width))]
    in_specs += [whole(dir_t.shape)]
    in_specs += [whole((rows, 1))] * 2 + [whole(vectors.shape)] + [pl.BlockSpec(memory_space=pl.ANY)] * 6
    in_specs += slab_columns((rows, 128), chunks)
    high = two * (wide_bits - 1)
    low = two * narrow_bits
    up_shape = (third,) + high + (2,) + low[1:] + (u_rows, 128)
    out_specs = [
        whole((rows, width)),
        pl.BlockSpec(memory_space=pl.ANY),
        pl.BlockSpec(memory_space=pl.ANY),
        whole((sum_rows, width)),
    ]
    out_shape = [
        jax.ShapeDtypeStruct((rows, width), jnp.bfloat16),
        jax.ShapeDtypeStruct(up_shape, jnp.bfloat16),
        jax.ShapeDtypeStruct((chunks,) + two * (steps - early) + (d_rows, 128), jnp.bfloat16),
        jax.ShapeDtypeStruct((sum_rows, width), jnp.float32),
    ]
    scratch = [
        pltpu.VMEM((rows, width), jnp.float32),
        pltpu.VMEM((rows, width), jnp.bfloat16),
        pltpu.VMEM((width, rows), jnp.bfloat16),
        pltpu.VMEM((width, rows), jnp.bfloat16),
        pltpu.VMEM((chunks,) + two * steps + (d_rows, 128), jnp.bfloat16),
        pltpu.VMEM((chunks,) + high + low + (u_rows, 128), jnp.bfloat16),
        pltpu.VMEM((chunks,) + high + low[1:] + (u_rows, 128), jnp.bfloat16),
    ]
    scratch += [pltpu.VMEM((chunks,) + two * (steps - 1 - s) + (d_rows, 128), jnp.bfloat16) for s in range(early)]
    scratch += [pltpu.VMEM((rows, segments), jnp.bfloat16), pltpu.VMEM((segments, width), jnp.bfloat16)]
    scratch += [pltpu.VMEM((128, width), jnp.bfloat16)]
    scratch += [pltpu.VMEM((wide, segments // wide, 128), jnp.float32)] * 4
    far = (normed_two, hidden_low, active, down_weight, up_weight, normed_one)
    scratch += [pltpu.VMEM(item.shape, item.dtype) for item in far]
    sems = chunks * early + chunks + 2 * (wide - 1)
    scratch += [pltpu.SemaphoreType.DMA((sems,)), pltpu.SemaphoreType.DMA((sems,)), pltpu.SemaphoreType.DMA((2 * chunks + len(far),))]
    return pl.pallas_call(
        kernel,
        grid=(2 * chunks,),
        in_specs=in_specs,
        out_specs=out_specs,
        out_shape=out_shape,
        scratch_shapes=scratch,
        compiler_params=pltpu.CompilerParams(collective_id=0, has_side_effects=True, vmem_limit_bytes=60 << 20),
        name="ffn_backward",
    )(lengths, numbers, encoded, cotangent, dir_t, inverse_two, inverse_one, vectors,
      *far, *([slope] * narrow))


def attention_backward(grad_attended, mixed, out_weight, queries, keys, values, attention, tokens, qkv_weight, up_grads,
                       down_grads, sums):
    rows, width = tokens.shape
    docs, _, length, _ = attention.shape
    pairs = width // 128
    names = axis_bits()
    steps = len(names)
    wide, narrow = lax.axis_size("wide"), lax.axis_size("narrow")
    wide_bits, narrow_bits = wide.bit_length() - 1, narrow.bit_length() - 1
    half = narrow // 2
    half_bits = narrow_bits - 1
    lanes = width // half
    q_rows, o_rows = 3 * width // wide // 2, width // wide // 2
    q_parts = lanes // 128
    orders = link_orders()
    ups = up_grads.shape[0]
    u_rows = up_grads.shape[-2]
    attn_steps = docs * pairs
    token_block = 256
    token_steps = rows // token_block
    first_q = 1 + attn_steps
    first_t = first_q + q_parts
    grid = first_t + token_steps
    downs, d_rows = down_grads.shape[0], down_grads.shape[-2]
    down_steps = len(down_grads.shape) - 3
    cuts = [(0, q_rows // 32 * 16), (q_rows // 32 * 16, q_rows)]
    u_cuts = [(0, u_rows // 2), (u_rows // 2, u_rows)]
    up_count, out_count = ups * len(u_cuts), q_parts
    first_part = up_count + out_count
    first_down = first_part + q_parts * len(cuts)
    count = first_down + downs
    small_rows = sums.shape[0]

    def bits_of(number, count):
        return tuple((number >> bit) & 1 for bit in reversed(range(count)))

    def kernel(*refs):
        (ga_hbm, mix_hbm, ow_hbm, q_ref, k_ref, v_ref, att_ref, tok_hbm, qw_hbm, up_hbm, down_hbm, small) = refs[:12]
        tokens_out, up_out, out_out, qkv_out, down_out, small_out, late_out = refs[12:19]
        rest = list(refs[19:])
        gm, mix_pair, gqkv_t, up_own, out_own, qkv_own = rest[:6]
        rest = rest[6:]
        up_received = [rest[i * (steps - 1) : (i + 1) * (steps - 1)] for i in range(len(u_cuts))]
        rest = rest[len(u_cuts) * (steps - 1) :]
        out_received, rest = rest[:steps], rest[steps:]
        qkv_received, rest = [rest[i * steps : (i + 1) * steps] for i in range(len(cuts))], rest[len(cuts) * steps :]
        down_own, down_received, rest = rest[0], rest[1 : 1 + down_steps], rest[1 + down_steps :]
        small_sent, small_received, late_sent, late_received, swap_out, swap_qkv, tok, qw, ga, mix, ow = rest[:11]
        send_sems, recv_sems, local_sems = rest[11:]
        pid = pl.program_id(0)
        place = Place()
        core = place.bit["narrow", 0]
        pieces = []
        for low, high in u_cuts:
            for part in range(ups):
                cut = len(pieces) // ups
                pieces.append(Halving(place, names[:-1], orders[part % 3][1:], up_hbm.at[part], up_own.at[part],
                                      [r.at[part] for r in up_received[cut]], send_sems, recv_sems, len(pieces) * steps,
                                      (slice(low, high), slice(None))))
        for part in range(out_count):
            pieces.append(Halving(place, names, orders[part % 3], out_own.at[part], out_own.at[part],
                                  [r.at[part] for r in out_received], send_sems, recv_sems, len(pieces) * steps))
        for part in range(q_parts):
            for cut, (low, high) in enumerate(cuts):
                pieces.append(Halving(place, names, orders[part % 3], qkv_own.at[part], qkv_own.at[part],
                                      [r.at[part] for r in qkv_received[cut]], send_sems, recv_sems, len(pieces) * steps,
                                      (slice(low, high), slice(None))))
        for number in range(downs):
            order = orders[number % 3][steps - down_steps :]
            pieces.append(Halving(place, [name for name in names if name in order], order, down_own.at[number],
                                  down_own.at[number], [r.at[number] for r in down_received], send_sems, recv_sems,
                                  len(pieces) * steps))
        base = count * steps

        def all_sum(sent, received, first):
            made = []
            for step in range(steps):
                made.append(pltpu.make_async_remote_copy(
                    src_ref=sent.at[step], dst_ref=received.at[step], send_sem=send_sems.at[first + step],
                    recv_sem=recv_sems.at[first + step], device_id=place.across(orders[0][step]),
                    device_id_type=MESH_ID))
            return made

        small_copies = all_sum(small_sent, small_received, base)
        late_copies = all_sum(late_sent, late_received, base + steps)
        swap_refs = [swap_out.at[part, core] for part in range(out_count)]
        swap_refs += [swap_qkv.at[part, core, low:high] for part in range(q_parts) for low, high in cuts]
        swaps = [pltpu.make_async_remote_copy(
            src_ref=ref, dst_ref=ref, send_sem=send_sems.at[base + 2 * steps + slot],
            recv_sem=recv_sems.at[base + 2 * steps + slot], device_id=place.across(("narrow", 0)),
            device_id_type=MESH_ID) for slot, ref in enumerate(swap_refs)]
        local = []
        for number in range(ups):
            keep = pieces[number].region(0, True)[: -2]
            local.append(pltpu.make_async_copy(up_hbm.at[number].at[keep], up_own.at[number].at[keep], local_sems.at[number]))

        loads = [pltpu.make_async_copy(tok_hbm, tok, local_sems.at[ups]),
                 pltpu.make_async_copy(qw_hbm, qw, local_sems.at[ups + 1])]
        first_loads = [pltpu.make_async_copy(source, target, local_sems.at[ups + 3 + i])
                       for i, (source, target) in enumerate(((ga_hbm, ga), (mix_hbm, mix), (ow_hbm, ow)))]
        down_load = pltpu.make_async_copy(down_hbm, down_own, local_sems.at[ups + 2])

        def advance(number, step):
            item = pieces[number]
            if step == 0 and number < ups:
                local[number].wait()
            total = item.add(step)
            if total is None:
                item.send(step + 1)
            elif number < up_count:
                cut, part = divmod(number, ups)
                up_out[u_cuts[cut][0] : u_cuts[cut][1], part * 128 : (part + 1) * 128] = total
            elif number >= first_down:
                number -= first_down
                j = number // 2 + downs // 2 * (number % 2)
                down_out[:, j * 128 : (j + 1) * 128] = total
            else:
                if number < first_part:
                    swap_out[number - up_count, core] = total
                else:
                    part, cut = divmod(number - first_part, len(cuts))
                    swap_qkv[part, core, cuts[cut][0] : cuts[cut][1]] = total
                swaps[number - up_count].start()

        def advance_small(copies, sent, received, out, step):
            copies[step].wait_recv()
            total = sent[step] + received[step]
            if step + 1 < steps:
                sent[step + 1] = total
                copies[step + 1].start()
            else:
                out[...] = total

        @pl.when(pid == 0)
        def _():
            place.greet()
            for number in range(up_count):
                pieces[number].send(0)
            for number in range(ups):
                local[number].start()
            for load in first_loads:
                load.start()
            small_sent[0] = small[...]
            small_copies[0].start()
            down_load.start()
            for load in loads:
                load.start()
            for load in first_loads:
                load.wait()
            grads_t = ga[...].T
            result = jnp.dot(grads_t, mix[...], preferred_element_type=jnp.float32).astype(jnp.bfloat16)
            for w in range(wide):
                for h in range(2):
                    for y in range(half):
                        at = (w * 2 + h) * o_rows
                        for part in range(out_count):
                            first = y * lanes + part * 128
                            out_own[(part,) + bits_of(w, wide_bits) + bits_of(y, half_bits) + (h,)] = result[
                                at : at + o_rows, first : first + 128
                            ]
            for part in range(out_count):
                pieces[up_count + part].send(0)
            grad_mixed = dot_last(ga[...], ow[...]).astype(jnp.bfloat16)
            for pair in range(pairs):
                gm[pair] = grad_mixed[:, pair * 128 : (pair + 1) * 128]
                mix_pair[pair] = mix[:, pair * 128 : (pair + 1) * 128]
            down_load.wait()
            for number in range(downs):
                pieces[first_down + number].send(0)

        @pl.when((pid >= 1) & (pid < first_q))
        def _():
            number = pid - 1
            pair, doc = number // docs, number % docs
            some = pl.ds(pl.multiple_of(doc * length, length), length)
            lane = lax.broadcasted_iota(jnp.int32, (1, 128), 1)
            scaled, keys, values = q_ref[...] * jnp.bfloat16(HEAD_DIM**-0.5), k_ref[...], v_ref[...]
            grads = gm[pair, some, :]
            product = grads.astype(jnp.float32) * mix_pair[pair, some, :].astype(jnp.float32)
            queries_t, grads_t = scaled.T, grads.T
            zero = jnp.zeros_like(grads)
            query_parts = []
            for head in range(2):
                inside = (lane // HEAD_DIM) == head
                at = head * HEAD_DIM
                attention = att_ref[0, head]
                chance = dot_last(jnp.where(inside, grads, zero), values)
                inner = jnp.sum(jnp.where(inside, product, 0.0), -1, keepdims=True)
                grad_scores = (attention.astype(jnp.float32) * (chance - inner)).astype(jnp.bfloat16)
                query_parts.append(jnp.dot(grad_scores, keys, preferred_element_type=jnp.float32))
                key_t = jnp.dot(queries_t[at : at + HEAD_DIM], grad_scores, preferred_element_type=jnp.float32)
                value_t = jnp.dot(grads_t[at : at + HEAD_DIM], attention, preferred_element_type=jnp.float32)
                row = pair * 128 + at
                gqkv_t[pl.ds(pl.multiple_of(width + row, HEAD_DIM), HEAD_DIM), some] = key_t.astype(jnp.bfloat16)
                gqkv_t[pl.ds(pl.multiple_of(2 * width + row, HEAD_DIM), HEAD_DIM), some] = value_t.astype(jnp.bfloat16)
            grad_query = jnp.where(lane < HEAD_DIM, query_parts[0], query_parts[1]) * HEAD_DIM**-0.5
            gqkv_t[pl.ds(pl.multiple_of(pair * 128, 128), 128), some] = grad_query.astype(jnp.bfloat16).T

        for part in range(q_parts):
            @pl.when(pid == first_q + part)
            def _():
                if part == 0:
                    for load in loads:
                        load.wait()
                    ones = jnp.ones((8, rows), jnp.bfloat16)
                    late_sent[0] = jnp.concatenate(
                        [dot_last(ones, gqkv_t[:width, :]), dot_last(ones, gqkv_t[2 * width :, :])], axis=1
                    )
                    late_copies[0].start()
                columns = jnp.concatenate(
                    [tok[:, y * lanes + part * 128 : y * lanes + (part + 1) * 128] for y in range(half)], axis=1
                )
                result = jnp.dot(gqkv_t[...], columns, preferred_element_type=jnp.float32).astype(jnp.bfloat16)
                for w in range(wide):
                    for h in range(2):
                        for y in range(half):
                            at = (w * 2 + h) * q_rows
                            qkv_own[(part,) + bits_of(w, wide_bits) + bits_of(y, half_bits) + (h,)] = result[
                                at : at + q_rows, y * 128 : (y + 1) * 128
                            ]
                for cut in range(len(cuts)):
                    pieces[first_part + part * len(cuts) + cut].send(0)

        @pl.when(pid >= first_t)
        def _():
            at = pl.multiple_of((pid - first_t) * token_block, token_block)
            some = pl.ds(at, token_block)
            grad_t = jnp.dot(qw[...], gqkv_t[:, some], preferred_element_type=jnp.float32)
            tokens_out[...] = (grad_t.T + ga[some, :].astype(jnp.float32)).astype(jnp.bfloat16)

        plan, small_plan, late_plan = {}, {}, {}
        for cut, times in enumerate(((4, 7, 9, 12), (6, 8, 10, 14))):
            for step, at in enumerate(times):
                for part in range(ups):
                    plan.setdefault(at, []).append((cut * ups + part, step))
        for step, at in enumerate((1, 8, 10, 12, 14)):
            for part in range(out_count):
                plan.setdefault(at, []).append((up_count + part, step))
        for step, at in enumerate((3, 6)):
            for number in range(downs):
                plan.setdefault(at, []).append((first_down + number, step))
        for number in range(first_part, first_down):
            for step in range(steps):
                at = first_q + (number - first_part) // len(cuts) + 1 if step == 0 else grid - 1
                plan.setdefault(at, []).append((number, step))
        for step, at in enumerate((3, 6, 8, 10, 12)):
            small_plan[at] = step
        late_plan[first_q + 2] = 0
        for at in range(grid):
            @pl.when(pid == at)
            def _():
                if at in small_plan:
                    advance_small(small_copies, small_sent, small_received, small_out, small_plan[at])
                for number, step in sorted(plan.get(at, []), key=lambda entry: (entry[1], entry[0])):
                    if at == grid - 1 and number == first_part:
                        advance_small(late_copies, late_sent, late_received, late_out, step)
                    advance(number, step)
                if at in late_plan:
                    advance_small(late_copies, late_sent, late_received, late_out, late_plan[at])
                if at == grid - 1:
                    for copy in swaps:
                        copy.wait()

                    def own_lanes(lanes):
                        size = lanes.shape[1] // 2
                        return jnp.where(core == 0, lanes[:, :size], lanes[:, size:])

                    out_out[...] = own_lanes(jnp.concatenate(
                        [swap_out[part].reshape(2 * o_rows, 128) for part in range(out_count)], axis=1))
                    qkv_out[...] = own_lanes(jnp.concatenate(
                        [swap_qkv[part].reshape(2 * q_rows, 128) for part in range(q_parts)], axis=1))
                    for item in pieces:
                        item.close()
                    for copy in small_copies + late_copies:
                        copy.wait_send()

    def whole(shape):
        return pl.BlockSpec(shape, lambda g: (0,) * len(shape), pipeline_mode=pl.Buffered(1))

    def number_of(g):
        return jnp.clip(g - 1, 0, attn_steps - 1)

    tile = pl.BlockSpec((length, 128), lambda g: (number_of(g) % docs, number_of(g) // docs))

    two = (2,)
    any_space = pl.BlockSpec(memory_space=pl.ANY)
    in_specs = [any_space, any_space, any_space, tile, tile, tile]
    in_specs += [pl.BlockSpec((1, 2, length, length), lambda g: (number_of(g) % docs, number_of(g) // docs, 0, 0))]
    in_specs += [any_space, any_space, any_space, any_space, whole((small_rows, width))]
    out_shape = [
        jax.ShapeDtypeStruct((rows, width), jnp.bfloat16),
        jax.ShapeDtypeStruct((u_rows, ups * 128), jnp.float32),
        jax.ShapeDtypeStruct((2 * o_rows, lanes // 2), jnp.float32),
        jax.ShapeDtypeStruct((2 * q_rows, lanes // 2), jnp.float32),
        jax.ShapeDtypeStruct((d_rows, downs * 128), jnp.float32),
        jax.ShapeDtypeStruct((small_rows, width), jnp.float32),
        jax.ShapeDtypeStruct((8, 2 * width), jnp.float32),
    ]
    wide_dims, half_dims = two * wide_bits, two * half_bits
    scratch = [
        pltpu.VMEM((pairs, rows, 128), jnp.bfloat16),
        pltpu.VMEM((pairs, rows, 128), jnp.bfloat16),
        pltpu.VMEM((3 * width, rows), jnp.bfloat16),
        pltpu.VMEM(up_grads.shape, jnp.bfloat16),
        pltpu.VMEM((out_count,) + wide_dims + half_dims + two + (o_rows, 128), jnp.bfloat16),
        pltpu.VMEM((q_parts,) + wide_dims + half_dims + two + (q_rows, 128), jnp.bfloat16),
    ]
    for low, high in u_cuts:
        scratch += [pltpu.VMEM((ups,) + two * (steps - 2 - s) + (high - low, 128), jnp.bfloat16) for s in range(steps - 1)]
    scratch += [pltpu.VMEM((out_count,) + two * (steps - 1 - s) + (o_rows, 128), jnp.bfloat16) for s in range(steps)]
    for low, high in cuts:
        scratch += [pltpu.VMEM((q_parts,) + two * (steps - 1 - s) + (high - low, 128), jnp.bfloat16) for s in range(steps)]
    scratch += [pltpu.VMEM(down_grads.shape, jnp.bfloat16)]
    scratch += [pltpu.VMEM((downs,) + two * (down_steps - 1 - s) + (d_rows, 128), jnp.bfloat16) for s in range(down_steps)]
    scratch += [pltpu.VMEM((steps, small_rows, width), jnp.float32)] * 2
    scratch += [pltpu.VMEM((steps, 8, 2 * width), jnp.float32)] * 2
    scratch += [pltpu.VMEM((out_count, 2, o_rows, 128), jnp.float32), pltpu.VMEM((q_parts, 2, q_rows, 128), jnp.float32)]
    scratch += [pltpu.VMEM(tokens.shape, jnp.bfloat16), pltpu.VMEM(qkv_weight.shape, jnp.bfloat16)]
    scratch += [pltpu.VMEM(item.shape, jnp.bfloat16) for item in (grad_attended, mixed, out_weight)]
    sems = count * steps + 2 * steps + out_count + q_parts * len(cuts)
    scratch += [pltpu.SemaphoreType.DMA((sems,)), pltpu.SemaphoreType.DMA((sems,)), pltpu.SemaphoreType.DMA((ups + 6,))]
    return pl.pallas_call(
        kernel,
        grid=(grid,),
        in_specs=in_specs,
        out_specs=[pl.BlockSpec((token_block, width), lambda g: (jnp.clip(g - first_t, 0, token_steps - 1), 0))]
        + [whole(item.shape) for item in out_shape[1:]],
        out_shape=out_shape,
        scratch_shapes=scratch,
        compiler_params=pltpu.CompilerParams(collective_id=1, has_side_effects=True, vmem_limit_bytes=60 << 20),
        name="attention_backward",
    )(grad_attended, mixed, out_weight, queries, keys, values, attention, tokens, qkv_weight, up_grads, down_grads, sums)


def on_device_fast(
    tokens,
    doc_lengths,
    qkv_weight,
    query_bias,
    value_bias,
    out_weight,
    out_bias,
    first_gain,
    first_shift,
    up_weight,
    up_bias,
    down_weight,
    down_bias,
    second_gain,
    second_shift,
    dir_weight,
    dir_bias,
    segment_rows,
    segment_slots,
    pair_rows,
    pair_labels,
    out_cotangent,
):
    doc_count, length, model_width = tokens.shape
    token_rows = tokens.reshape(doc_count * length, model_width)
    rows_in = (out_bias, first_gain, first_shift, down_bias, second_gain, second_shift, query_bias, value_bias)
    last = jnp.pad(dir_bias, (0, model_width - dir_bias.shape[0]))
    vectors = jnp.concatenate([item[None] for item in rows_in + (last,)] + [up_bias.reshape(-1, model_width)])
    vectors = vectors.astype(jnp.float32)
    queries, keys, values, attention, mixed = attention_forward(doc_lengths, token_rows, qkv_weight, vectors)
    hidden_low, normed_one, inverse_one, active, slope, normed_two, inverse_two, encoded_rows = ffn_forward(
        doc_lengths, mixed, token_rows, out_weight, vectors, up_weight, down_weight
    )
    classes_count = dir_weight.shape[1]
    doc_starts = lax.broadcasted_iota(jnp.int32, (doc_count, 1), 0) * length
    numbers = jnp.concatenate(
        [(segment_rows + doc_starts).reshape(1, -1), segment_slots, pair_rows[:, :, 0], pair_rows[:, :, 1], pair_labels]
        + [pair_labels] * 3
    )
    grad_attended, up_blocks, down_blocks, sums = ffn_backward(
        doc_lengths, numbers, encoded_rows, out_cotangent.reshape(-1, model_width), dir_weight.T, vectors,
        normed_two, inverse_two, active, slope,
        hidden_low, down_weight, up_weight, normed_one, inverse_one,
    )
    grad_tokens, out_up, out_out, out_qkv, out_down, sums, late = attention_backward(
        grad_attended, mixed, out_weight, queries, keys, values, attention, token_rows, qkv_weight, up_blocks,
        down_blocks, sums,
    )
    first_dir = 6 + lax.axis_size("narrow")
    last_dir = first_dir + 2 * classes_count
    dir_sum = sums[first_dir:last_dir].reshape(2, classes_count, model_width).transpose(0, 2, 1)
    return (
        encoded_rows.reshape(tokens.shape),
        grad_tokens.reshape(tokens.shape),
        out_qkv.T,
        late[0, :model_width],
        late[0, model_width:],
        out_out.T,
        sums[5],
        sums[3],
        sums[4],
        out_up,
        sums[6:first_dir].reshape(-1),
        out_down.T,
        sums[2],
        sums[0],
        sums[1],
        dir_sum.reshape(2 * model_width, classes_count),
        sums[last_dir : last_dir + classes_count, 0],
    )


def on_device(
    tokens,
    doc_lengths,
    qkv_weight,
    query_bias,
    value_bias,
    out_weight,
    out_bias,
    first_gain,
    first_shift,
    up_weight,
    up_bias,
    down_weight,
    down_bias,
    second_gain,
    second_shift,
    dir_weight,
    dir_bias,
    segment_rows,
    segment_slots,
    pair_rows,
    pair_labels,
    out_cotangent,
):
    doc_count, length, model_width = tokens.shape
    score_scale = HEAD_DIM ** (-0.5)
    token_rows = tokens.reshape(doc_count * length, model_width)
    allowed = lax.broadcasted_iota(jnp.int32, (doc_count, length), 1) < doc_lengths[:, None]
    allowed_rows = allowed.reshape(-1, 1).astype(jnp.float32)
    bias_row = jnp.concatenate([query_bias, jnp.zeros_like(query_bias), value_bias]).astype(
        jnp.float32
    )
    qkv = (jnp.dot(token_rows, qkv_weight, preferred_element_type=jnp.float32) + bias_row).astype(
        jnp.bfloat16
    )

    def split_heads(doc_block, which):
        return doc_block[:, which * model_width : (which + 1) * model_width].reshape(
            length, HEADS, HEAD_DIM
        )

    def scores_of(queries, key_rows, doc_mask):
        scores = (
            jnp.einsum("qhd,khd->hqk", queries, key_rows, preferred_element_type=jnp.float32)
            * score_scale
        )
        return jnp.where(doc_mask[None, None, :], scores, MASKED)

    mixed_parts = []
    log_totals = []
    for doc_index in range(doc_count):
        doc_block = qkv[doc_index * length : (doc_index + 1) * length]
        queries = split_heads(doc_block, 0)
        key_rows = split_heads(doc_block, 1)
        value_rows = split_heads(doc_block, 2)
        scores = scores_of(queries, key_rows, allowed[doc_index])
        highest = jnp.max(scores, -1, keepdims=True)
        powers = jnp.exp(scores - highest)
        summed = jnp.sum(powers, -1, keepdims=True)
        attention = (powers / summed).astype(jnp.bfloat16)
        log_totals.append(highest + jnp.log(summed))
        mixed_parts.append(
            jnp.einsum(
                "hqk,khd->qhd", attention, value_rows, preferred_element_type=jnp.float32
            ).reshape(length, model_width)
        )
    mixed = jnp.concatenate(mixed_parts).astype(jnp.bfloat16)
    attended = jnp.dot(mixed, out_weight, preferred_element_type=jnp.float32) + out_bias.astype(
        jnp.float32
    )
    resid_one = token_rows.astype(jnp.float32) + attended
    hidden_one, normed_one, inverse_one = norm_forward(
        resid_one, first_gain.astype(jnp.float32), first_shift.astype(jnp.float32)
    )
    hidden_low = hidden_one.astype(jnp.bfloat16)
    upper_pre = jnp.dot(hidden_low, up_weight, preferred_element_type=jnp.float32) + up_bias.astype(
        jnp.float32
    )
    cumulative = normal_cdf(upper_pre)
    active = (upper_pre * cumulative).astype(jnp.bfloat16)
    lowered = jnp.dot(active, down_weight, preferred_element_type=jnp.float32) + down_bias.astype(
        jnp.float32
    )
    resid_two = hidden_one + lowered
    second_float = second_gain.astype(jnp.float32)
    normed_out, normed_two, inverse_two = norm_forward(
        resid_two, second_float, second_shift.astype(jnp.float32)
    )
    encoded_rows = (normed_out * allowed_rows).astype(jnp.bfloat16)
    doc_starts = lax.broadcasted_iota(jnp.int32, (doc_count, 1), 0) * length
    picked_rows = (segment_rows + doc_starts).reshape(-1)
    picked = encoded_rows[picked_rows]
    slots = segment_slots.reshape(-1)
    outgoing = jnp.zeros_like(picked).at[slots].set(picked)
    arrived = lax.all_to_all(outgoing, "wide", split_axis=0, concat_axis=0, tiled=True)
    pairs = pair_rows.reshape(-1, 2)
    labels = pair_labels.reshape(-1)
    first_rows = arrived[pairs[:, 0]]
    second_rows = arrived[pairs[:, 1]]
    logits = (
        jnp.dot(first_rows, dir_weight[:model_width], preferred_element_type=jnp.float32)
        + jnp.dot(second_rows, dir_weight[model_width:], preferred_element_type=jnp.float32)
        + dir_bias.astype(jnp.float32)
    )
    powers_head = jnp.exp(logits - jnp.max(logits, -1, keepdims=True))
    chance = powers_head / jnp.sum(powers_head, -1, keepdims=True)
    classes = lax.broadcasted_iota(jnp.int32, logits.shape, 1)
    delta = chance - (labels[:, None] == classes).astype(jnp.float32)
    first_float = first_rows.astype(jnp.float32)
    second_rows_float = second_rows.astype(jnp.float32)
    grad_dir_weight = jnp.concatenate(
        [
            jnp.dot(first_float.T, delta, precision=EXACT, preferred_element_type=jnp.float32),
            jnp.dot(
                second_rows_float.T, delta, precision=EXACT, preferred_element_type=jnp.float32
            ),
        ]
    )
    grad_dir_bias = jnp.sum(delta, 0)
    dir_float = dir_weight.astype(jnp.float32)
    grad_first = jnp.dot(
        delta, dir_float[:model_width].T, precision=EXACT, preferred_element_type=jnp.float32
    )
    grad_second = jnp.dot(
        delta, dir_float[model_width:].T, precision=EXACT, preferred_element_type=jnp.float32
    )
    grad_arrived = jnp.zeros((arrived.shape[0], model_width), jnp.float32)
    grad_arrived = grad_arrived.at[pairs[:, 0]].add(grad_first).at[pairs[:, 1]].add(grad_second)
    returned = lax.all_to_all(
        grad_arrived.astype(jnp.bfloat16), "wide", split_axis=0, concat_axis=0, tiled=True
    )
    grad_picked = returned[slots].astype(jnp.float32)
    grad_encoded = (
        out_cotangent.reshape(-1, model_width).astype(jnp.float32).at[picked_rows].add(grad_picked)
    )
    grad_encoded = grad_encoded * allowed_rows
    grad_two, grad_second_gain, grad_second_shift = norm_backward(
        grad_encoded, normed_two, inverse_two, second_float
    )
    grad_lowered = grad_two.astype(jnp.bfloat16)
    grad_down_weight = jnp.einsum(
        "rf,rd->fd", active, grad_lowered, preferred_element_type=jnp.float32
    )
    grad_down_bias = jnp.sum(grad_lowered.astype(jnp.float32), 0)
    grad_active = jnp.einsum(
        "rd,fd->rf", grad_lowered, down_weight, preferred_element_type=jnp.float32
    )
    density = jnp.exp(-0.5 * upper_pre * upper_pre) * 0.3989422804014327
    grad_upper = (grad_active * (cumulative + upper_pre * density)).astype(jnp.bfloat16)
    grad_up_weight = jnp.einsum(
        "rd,rf->df", hidden_low, grad_upper, preferred_element_type=jnp.float32
    )
    grad_up_bias = jnp.sum(grad_upper.astype(jnp.float32), 0)
    grad_hidden = grad_two + jnp.einsum(
        "rf,df->rd", grad_upper, up_weight, preferred_element_type=jnp.float32
    )
    grad_one, grad_first_gain, grad_first_shift = norm_backward(
        grad_hidden, normed_one, inverse_one, first_gain.astype(jnp.float32)
    )
    grad_attended = grad_one.astype(jnp.bfloat16)
    grad_out_weight = jnp.einsum(
        "rd,re->de", mixed, grad_attended, preferred_element_type=jnp.float32
    )
    grad_out_bias = jnp.sum(grad_attended.astype(jnp.float32), 0)
    grad_mixed = jnp.einsum(
        "re,de->rd", grad_attended, out_weight, preferred_element_type=jnp.float32
    ).astype(jnp.bfloat16)
    grad_parts = []
    for doc_index in range(doc_count):
        doc_block = qkv[doc_index * length : (doc_index + 1) * length]
        queries = split_heads(doc_block, 0)
        key_rows = split_heads(doc_block, 1)
        value_rows = split_heads(doc_block, 2)
        scores = scores_of(queries, key_rows, allowed[doc_index])
        attention = jnp.exp(scores - log_totals[doc_index])
        grad_doc = grad_mixed[doc_index * length : (doc_index + 1) * length].reshape(
            length, HEADS, HEAD_DIM
        )
        grad_chance = jnp.einsum(
            "qhd,khd->hqk", grad_doc, value_rows, preferred_element_type=jnp.float32
        )
        inner = jnp.sum(grad_chance * attention, -1, keepdims=True)
        grad_scores = (attention * (grad_chance - inner)).astype(jnp.bfloat16)
        grad_query = (
            jnp.einsum("hqk,khd->qhd", grad_scores, key_rows, preferred_element_type=jnp.float32)
            * score_scale
        )
        grad_key = (
            jnp.einsum("hqk,qhd->khd", grad_scores, queries, preferred_element_type=jnp.float32)
            * score_scale
        )
        grad_value = jnp.einsum(
            "hqk,qhd->khd",
            attention.astype(jnp.bfloat16),
            grad_doc,
            preferred_element_type=jnp.float32,
        )
        grad_parts.append(
            jnp.concatenate(
                [
                    grad_query.reshape(length, model_width),
                    grad_key.reshape(length, model_width),
                    grad_value.reshape(length, model_width),
                ],
                axis=1,
            )
        )
    grad_qkv = jnp.concatenate(grad_parts).astype(jnp.bfloat16)
    grad_qkv_float = grad_qkv.astype(jnp.float32)
    grad_query_bias = jnp.sum(grad_qkv_float[:, :model_width], 0)
    grad_value_bias = jnp.sum(grad_qkv_float[:, 2 * model_width :], 0)
    grad_qkv_weight = jnp.einsum(
        "rd,re->de", token_rows, grad_qkv, preferred_element_type=jnp.float32
    )
    grad_tokens = (
        jnp.einsum("re,de->rd", grad_qkv, qkv_weight, preferred_element_type=jnp.float32) + grad_one
    ).astype(jnp.bfloat16)
    matrices = (grad_qkv_weight, grad_out_weight, grad_up_weight, grad_down_weight)
    partial_sums = (
        lax.psum_scatter(
            matrices[0].astype(jnp.bfloat16), "wide", scatter_dimension=1, tiled=True
        ).astype(jnp.float32),
        lax.psum_scatter(
            matrices[1].astype(jnp.bfloat16), "wide", scatter_dimension=1, tiled=True
        ).astype(jnp.float32),
        lax.psum_scatter(
            matrices[2].astype(jnp.bfloat16), "wide", scatter_dimension=1, tiled=True
        ).astype(jnp.float32),
        lax.psum_scatter(
            matrices[3].astype(jnp.bfloat16), "wide", scatter_dimension=1, tiled=True
        ).astype(jnp.float32),
    )
    summed_mats = (
        lax.psum_scatter(
            partial_sums[0].astype(jnp.bfloat16), "narrow", scatter_dimension=0, tiled=True
        ).astype(jnp.float32),
        lax.psum_scatter(
            partial_sums[1].astype(jnp.bfloat16), "narrow", scatter_dimension=0, tiled=True
        ).astype(jnp.float32),
        lax.psum_scatter(
            partial_sums[2].astype(jnp.bfloat16), "narrow", scatter_dimension=0, tiled=True
        ).astype(jnp.float32),
        lax.psum_scatter(
            partial_sums[3].astype(jnp.bfloat16), "narrow", scatter_dimension=0, tiled=True
        ).astype(jnp.float32),
    )
    smalls = lax.psum(
        (
            grad_query_bias,
            grad_value_bias,
            grad_out_bias,
            grad_first_gain,
            grad_first_shift,
            grad_up_bias,
            grad_down_bias,
            grad_second_gain,
            grad_second_shift,
            grad_dir_weight,
            grad_dir_bias,
        ),
        ("wide", "narrow"),
    )
    return (
        encoded_rows.reshape(tokens.shape),
        grad_tokens.reshape(tokens.shape),
        summed_mats[0],
        smalls[0],
        smalls[1],
        summed_mats[1],
        smalls[2],
        smalls[3],
        smalls[4],
        summed_mats[2],
        smalls[5],
        summed_mats[3],
        smalls[6],
        smalls[7],
        smalls[8],
        smalls[9],
        smalls[10],
    )


def fits_blocks(mesh):
    wide, narrow = mesh.shape["wide"], mesh.shape["narrow"]
    width, ff = HEADS * HEAD_DIM, 4 * HEADS * HEAD_DIM
    if wide != 2 * narrow or narrow < 4 or narrow & (narrow - 1):
        return False
    lanes = (ff // narrow, ff // wide, 2 * width // narrow)
    rows = (width // wide, width // narrow, width // wide // 2, 3 * width // wide // 2)
    return all(size % 128 == 0 for size in lanes) and all(size % 16 == 0 for size in rows)


def solution(mesh):
    placed = (
        P(("wide", "narrow"), None, None),
        P(("wide", "narrow")),
        P(),
        P(),
        P(),
        P(),
        P(),
        P(),
        P(),
        P(),
        P(),
        P(),
        P(),
        P(),
        P(),
        P(),
        P(),
        P(("wide", "narrow"), None),
        P(("wide", "narrow"), None),
        P(("wide", "narrow"), None, None),
        P(("wide", "narrow"), None),
        P(("wide", "narrow"), None, None),
    )
    return jax.shard_map(
        on_device_fast if fits_blocks(mesh) else on_device,
        mesh=mesh,
        in_specs=placed,
        out_specs=(
            P(("wide", "narrow"), None, None),
            P(("wide", "narrow"), None, None),
            P("narrow", "wide"),
            P(),
            P(),
            P("narrow", "wide"),
            P(),
            P(),
            P(),
            P("narrow", "wide"),
            P(),
            P("narrow", "wide"),
            P(),
            P(),
            P(),
            P(),
            P(),
        ),
        check_vma=False,
    )
```

```python
import jax
import jax.numpy as jnp
from jax import lax
from jax.experimental import pallas as pl
from jax.experimental.pallas import tpu as pltpu
from jax.sharding import PartitionSpec as P

HEADS = 12
HEAD_DIM = 64


EXACT = lax.Precision.HIGHEST
MASKED = -1e30
EPSILON = 1e-05


def norm_forward(values, gain, shift):
    center = jnp.mean(values, -1, keepdims=True)
    centered = values - center
    inverse = lax.rsqrt(jnp.mean(centered * centered, -1, keepdims=True) + EPSILON)
    normed = centered * inverse
    return (normed * gain + shift, normed, inverse)


def norm_backward(grad, normed, inverse, gain):
    scaled = grad * gain
    first_mean = jnp.mean(scaled, -1, keepdims=True)
    second_mean = jnp.mean(scaled * normed, -1, keepdims=True)
    return (
        (scaled - first_mean - normed * second_mean) * inverse,
        jnp.sum(grad * normed, 0),
        jnp.sum(grad, 0),
    )


def normal_cdf(values):
    return 0.5 * (1.0 + lax.erf(values * 0.7071067811865476))


MESH_ID = pl.DeviceIdType.MESH


def axis_bits():
    names = []
    for axis in ("wide", "narrow"):
        count = lax.axis_size(axis).bit_length() - 1
        names += [(axis, bit) for bit in reversed(range(count))]
    return names


class Place:
    def __init__(self):
        self.index = {axis: lax.axis_index(axis) for axis in ("wide", "narrow")}
        self.names = axis_bits()
        self.bit = {name: (self.index[name[0]] // (1 << name[1])) % 2 for name in self.names}

    def across(self, name):
        axis, bit = name
        target = dict(self.index)
        target[axis] = target[axis] + (1 << bit) - (2 << bit) * self.bit[name]
        return target

    def ahead(self, offset):
        target = dict(self.index)
        target["wide"] = (target["wide"] + offset) % lax.axis_size("wide")
        return target

    def greet(self, all_wide=False):
        barrier = pltpu.get_barrier_semaphore()
        targets = [self.across(name) for name in self.names if not (all_wide and name[0] == "wide")]
        if all_wide:
            targets += [self.ahead(offset) for offset in range(1, lax.axis_size("wide"))]
        for target in targets:
            pl.semaphore_signal(barrier, inc=1, device_id=target, device_id_type=MESH_ID)
        pl.semaphore_wait(barrier, len(targets))


class Halving:
    def __init__(self, place, names, order, source, own, received, send_sems, recv_sems, first_sem, tail=()):
        self.place, self.names, self.order = place, names, order
        self.source, self.own, self.received = source, own, received
        self.last = True
        self.send_sems, self.recv_sems, self.first_sem, self.tail = send_sems, recv_sems, first_sem, tail

    def region(self, step, mine):
        index = []
        for name in self.names:
            if name in self.order[:step]:
                index.append(self.place.bit[name])
            elif name == self.order[step]:
                index.append(self.place.bit[name] if mine else 1 - self.place.bit[name])
            else:
                index.append(slice(None))
        return tuple(index) + self.tail

    def copy(self, step):
        held = self.source if step == 0 else self.own
        return pltpu.make_async_remote_copy(
            src_ref=held.at[self.region(step, False)],
            dst_ref=self.received[step],
            send_sem=self.send_sems.at[self.first_sem + step],
            recv_sem=self.recv_sems.at[self.first_sem + step],
            device_id=self.place.across(self.order[step]),
            device_id_type=MESH_ID,
        )

    def send(self, step):
        self.copy(step).start()

    def add(self, step):
        self.copy(step).wait_recv()
        mine = self.region(step, True)
        if step + 1 < len(self.order) or not self.last:
            self.own[mine] = self.own[mine] + self.received[step][...]
            return None
        return self.own[mine].astype(jnp.float32) + self.received[step][...].astype(jnp.float32)

    def merge(self, step):
        self.last = False
        self.add(step)

    def close(self):
        for step in range(len(self.order)):
            self.copy(step).wait_send()


def link_orders():
    wide = [("wide", bit) for bit in range(lax.axis_size("wide").bit_length() - 1)]
    narrow = [("narrow", bit) for bit in range(1, lax.axis_size("narrow").bit_length() - 1)]
    core, x, near, far = [("narrow", 0)], wide[:1], wide[1:-1], wide[-1:]
    return [core + narrow + x + near + far, core + x + near + narrow + far, core + near + narrow + x + far]


def attention_forward(lengths, tokens, qkv_weight, singles):
    rows, width = tokens.shape
    docs = lengths.shape[0]
    length = rows // docs
    pairs = width // 128

    kinds = [item.shape[0] for item in singles]
    lines = sum(max(1, size // width) for size in kinds)

    def kernel(lens, tok, wq, wk, wv, *refs):
        singles, (vec, q_out, k_out, v_out, attention_out, mixed_out) = refs[: len(kinds)], refs[len(kinds) :]

        @pl.when(pl.program_id(0) == 0)
        def _():
            at = 0
            for single, size in zip(singles, kinds):
                values = single[...].astype(jnp.float32)
                for first in range(0, size, width):
                    some = min(size, width)
                    vec[at, :some] = values[first : first + some]
                    at += 1

        weights = jnp.concatenate([wq[...], wk[...], wv[...]], axis=1)
        at = pl.ds(pl.multiple_of(pl.program_id(0) * 128, 128), 128)
        offsets = jnp.concatenate([vec[6:7, at], jnp.zeros((1, 128), jnp.float32), vec[7:8, at]], axis=1)
        qkv = (jnp.dot(tok[...], weights, preferred_element_type=jnp.float32) + offsets).astype(jnp.bfloat16)
        q_out[...] = qkv[:, :128]
        k_out[...] = qkv[:, 128:256]
        v_out[...] = qkv[:, 256:]
        first = lax.broadcasted_iota(jnp.int32, (1, 128), 1) < HEAD_DIM
        for doc in range(docs):
            some = slice(doc * length, (doc + 1) * length)
            queries = qkv[some, :128] * jnp.bfloat16(HEAD_DIM**-0.5)
            keys, values = qkv[some, 128:256], qkv[some, 256:]
            zero = jnp.zeros_like(queries)
            places = lax.broadcasted_iota(jnp.int32, (1, length), 1)
            bias = jnp.where(places < lens[doc], 0.0, MASKED)
            outs = []
            for head in range(2):
                masked = jnp.where(first, queries, zero) if head == 0 else jnp.where(first, zero, queries)
                scores = dot_last(masked, keys) + bias
                powers = jnp.exp(scores - jnp.max(scores, -1, keepdims=True))
                attention = (powers * (1.0 / jnp.sum(powers, -1, keepdims=True))).astype(jnp.bfloat16)
                attention_out[doc, head] = attention
                outs.append(jnp.dot(attention, values, preferred_element_type=jnp.float32))
            mixed_out[some, :] = jnp.where(first, outs[0], outs[1]).astype(jnp.bfloat16)

    def whole(shape):
        return pl.BlockSpec(shape, lambda pair: (0,) * len(shape), pipeline_mode=pl.Buffered(1))

    column = pl.BlockSpec((rows, 128), lambda pair: (0, pair))
    in_specs = [pl.BlockSpec(memory_space=pltpu.SMEM), whole((rows, width))]
    in_specs += [pl.BlockSpec((width, 128), lambda pair, n=n: (0, n * pairs + pair)) for n in range(3)]
    in_specs += [whole(item.shape) for item in singles]
    low = jax.ShapeDtypeStruct((rows, width), jnp.bfloat16)
    return pl.pallas_call(
        kernel,
        grid=(pairs,),
        in_specs=in_specs,
        out_specs=[whole((lines, width))] + [column] * 3
        + [pl.BlockSpec((docs, 2, length, length), lambda pair: (0, pair, 0, 0)), column],
        out_shape=[jax.ShapeDtypeStruct((lines, width), jnp.float32)] + [low] * 3 + [jax.ShapeDtypeStruct((docs, 2 * pairs, length, length), jnp.bfloat16), low],
        compiler_params=pltpu.CompilerParams(vmem_limit_bytes=56 << 20),
        name="attention_forward",
    )(lengths, tokens, qkv_weight, qkv_weight, qkv_weight, *singles)


def ffn_forward(lengths, mixed, tokens, out_weight, vectors, up_weight, down_weight):
    rows, width = tokens.shape
    ff = up_weight.shape[1]
    chunk = width
    chunks = ff // chunk
    length = rows // lengths.shape[0]
    row_block = 256

    def kernel(lens, mix, tok, ow, vec, up, down, hid_out, n1_out, q1_out, act_out, slope_out, n2_out, q2_out,
               enc_out, hidden, total):
        pid = pl.program_id(0)

        def each_block(body):
            def step(i, carry):
                body(pl.multiple_of(i * row_block, row_block))
                return carry

            lax.fori_loop(0, rows // row_block, step, 0)

        @pl.when(pid == 0)
        def _():
            total[...] = jnp.dot(mix[...], ow[...], preferred_element_type=jnp.float32)

            def body(at):
                some = pl.ds(at, row_block)
                summed = tok[some, :].astype(jnp.float32) + (total[some, :] + vec[0:1, :])
                out, normed, inverse = norm_forward(summed, vec[1:2, :], vec[2:3, :])
                hidden[some, :] = out
                hid_out[some, :] = out.astype(jnp.bfloat16)
                n1_out[some, :] = normed.astype(jnp.bfloat16)
                q1_out[some, :] = inverse
                total[some, :] = jnp.zeros_like(out)

            each_block(body)

        pre = jnp.dot(hid_out[...], up[...], preferred_element_type=jnp.float32) + vec[pl.ds(pid + 9, 1), :]
        cumulative = normal_cdf(pre)
        density = jnp.exp(-0.5 * pre * pre) * 0.3989422804014327
        active = (pre * cumulative).astype(jnp.bfloat16)
        act_out[...] = active
        slope_out[...] = (cumulative + pre * density).astype(jnp.bfloat16)
        total[...] += jnp.dot(active, down[...], preferred_element_type=jnp.float32)

        @pl.when(pid == chunks - 1)
        def _():
            def body(at):
                some = pl.ds(at, row_block)
                summed = hidden[some, :] + (total[some, :] + vec[3:4, :])
                out, normed, inverse = norm_forward(summed, vec[4:5, :], vec[5:6, :])
                n2_out[some, :] = normed.astype(jnp.bfloat16)
                q2_out[some, :] = inverse
                doc = at // length
                line = lax.broadcasted_iota(jnp.int32, (row_block, 1), 0) + (at - doc * length)
                enc_out[some, :] = jnp.where(line < lens[doc], out, 0.0).astype(jnp.bfloat16)

            each_block(body)

    def whole(shape):
        return pl.BlockSpec(shape, lambda f: (0,) * len(shape), pipeline_mode=pl.Buffered(1))

    wide_row, column = whole((rows, width)), pl.BlockSpec((rows, chunk), lambda f: (0, f))
    low = jax.ShapeDtypeStruct((rows, width), jnp.bfloat16)
    one = jax.ShapeDtypeStruct((rows, 1), jnp.float32)
    upper = jax.ShapeDtypeStruct((rows, ff), jnp.bfloat16)
    return pl.pallas_call(
        kernel,
        grid=(chunks,),
        in_specs=[
            pl.BlockSpec(memory_space=pltpu.SMEM), wide_row, wide_row, whole((width, width)), whole(vectors.shape),
            pl.BlockSpec((width, chunk), lambda f: (0, f)),
            pl.BlockSpec((chunk, width), lambda f: (f, 0)),
        ],
        out_specs=[wide_row, wide_row, whole((rows, 1)), column, column, wide_row, whole((rows, 1)), wide_row],
        out_shape=[low, low, one, upper, upper, low, one, low],
        scratch_shapes=[pltpu.VMEM((rows, width), jnp.float32), pltpu.VMEM((rows, width), jnp.float32)],
        compiler_params=pltpu.CompilerParams(vmem_limit_bytes=58 << 20),
        name="ffn_forward",
    )(lengths, mixed, tokens, out_weight, vectors, up_weight, down_weight)


def dot_last(left, right):
    return lax.dot_general(left, right, (((1,), (1,)), ((), ())), preferred_element_type=jnp.float32)


def norm_back_rows(grad, normed, inverse, gain):
    scaled = grad * gain
    first = jnp.mean(scaled, -1, keepdims=True)
    second = jnp.mean(scaled * normed, -1, keepdims=True)
    return (scaled - first - normed * second) * inverse


def parts_of(values, count):
    terms = []
    for _ in range(count):
        term = values.astype(jnp.bfloat16).astype(jnp.float32)
        terms.append(term)
        values = values - term
    return jnp.concatenate(terms).astype(jnp.bfloat16)


def one_hot(row, count):
    lines = lax.broadcasted_iota(jnp.int32, (count, row.shape[1]), 0)
    return jnp.where(lines == row, 1.0, 0.0).astype(jnp.bfloat16)


def ffn_backward(lengths, segment_rows, segment_slots, pair_rows, pair_labels, encoded, cotangent, dir_t, vectors, normed_two, inverse_two, active, slope, hidden_low, down_weight, up_weight,
                 normed_one, inverse_one):
    rows, width = hidden_low.shape
    ff = active.shape[1]
    segments, classes = segment_slots.shape[1], dir_t.shape[0]
    numbers = (segment_rows, segment_slots, pair_rows, pair_labels)
    length = rows // lengths.shape[0]
    names = axis_bits()
    steps = len(names)
    wide, narrow = lax.axis_size("wide"), lax.axis_size("narrow")
    wide_bits, narrow_bits = wide.bit_length() - 1, narrow.bit_length() - 1
    chunks = ff // narrow // 128
    third = chunks // 2
    d_rows, u_rows = width // wide, width // narrow
    row_block = 256
    row_steps = rows // row_block
    orders = link_orders()
    two = (2,)
    early = 3
    first_dir = 6 + narrow
    sum_rows = pl.cdiv(first_dir + 3 * classes, 8) * 8

    def chunk_of(step):
        step = jnp.clip(step, 0, chunks - 1)
        return step // 2 + third * (step % 2)

    def bits_of(number, count):
        return tuple((number >> bit) & 1 for bit in reversed(range(count)))

    def kernel(*refs):
        lens, seg_rows, seg_slots, pair_nums, labels, enc, cot, dir_ref = refs[:8]
        refs = refs[8:]
        q2, q1, vec = refs[:3]
        far = refs[3:9]
        slo = refs[9 : 9 + narrow]
        rest = list(refs[9 + narrow :])
        ga_out, up_out, down_out, sums_out = rest[:4]
        rest = rest[4:]
        grad_hidden, lowered, lowered_t, hidden_t, own, up_own, up_received = rest[:7]
        received = rest[7 : 7 + early]
        rest = rest[7 + early :]
        select, picked, dir_w, leaving, arrived, leaving_grads, arrived_grads = rest[:7]
        near = rest[7:13]
        n2, hidden, act, dws, uws, n1 = near
        send_sems, recv_sems, local_sems = rest[13:]
        loads = [pltpu.make_async_copy(far[i], near[i], local_sems.at[2 * chunks + i]) for i in range(len(near))]
        pid = pl.program_id(0)
        place = Place()
        pieces = []
        for number in range(chunks):
            pieces.append(
                Halving(place, names, orders[number % 3][:early], own.at[number], own.at[number],
                        [r.at[number] for r in received], send_sems, recv_sems, number * early)
            )
        core = ("narrow", 0)
        up_names = [name for name in names if name != ("wide", 0)]
        up_pieces = [
            Halving(place, up_names, [core], up_own.at[number], up_own.at[number], [up_received.at[number]],
                    send_sems, recv_sems, chunks * early + number)
            for number in range(chunks)
        ]

        def up_write(number):
            mine = up_pieces[number].region(0, True)
            return pltpu.make_async_copy(
                up_own.at[number].at[mine],
                up_out.at[(number // 2,) + (slice(None),) * (wide_bits - 1) + (number % 2,)],
                local_sems.at[number],
            )

        def exchange(source, landing, first, meanwhile=None):
            made = []
            for offset in range(1, wide):
                target = place.ahead(offset)
                made.append(pltpu.make_async_remote_copy(
                    src_ref=source.at[target["wide"]], dst_ref=landing.at[place.index["wide"]],
                    send_sem=send_sems.at[first + offset - 1], recv_sem=recv_sems.at[first + offset - 1],
                    device_id=target, device_id_type=MESH_ID))
            me = place.index["wide"]
            for copy in made:
                copy.start()
            landing[me] = source[me]
            if meanwhile:
                meanwhile()
            for copy in made:
                copy.wait()
            return landing[...].reshape(segments, 128)

        def turn_hidden():
            def body(i, carry):
                some = pl.ds(pl.multiple_of(i * row_block, row_block), row_block)
                hidden_t[:, some] = hidden[some, :].T
                return carry

            loads[1].wait()
            lax.fori_loop(0, row_steps, body, 0)

        @pl.when(pid == 0)
        def _():
            for load in loads:
                load.start()
            place.greet(all_wide=True)
            sums_out[...] = jnp.zeros_like(sums_out)
            base = chunks * early + chunks
            docs = rows // length
            places = jnp.concatenate([seg_rows[doc : doc + 1, :] + doc * length for doc in range(docs)], axis=1)
            select[...] = dot_last(one_hot(places, rows), one_hot(seg_slots[...], segments)).astype(jnp.bfloat16)
            picked[...] = jnp.dot(select[...].T, enc[...], preferred_element_type=jnp.float32).astype(jnp.bfloat16)
            halves = [dir_ref[:, n * width : (n + 1) * width].astype(jnp.float32) for n in range(2)]
            blank = jnp.zeros((128 - 2 * classes, width), jnp.float32)
            dir_w[...] = jnp.concatenate(halves + [blank]).astype(jnp.bfloat16)
            leaving[...] = dot_last(picked[...], dir_w[...]).reshape(leaving.shape)
            scores = exchange(leaving, arrived, base, turn_hidden).T
            pair_first, pair_second = one_hot(pair_nums[0:1, :], segments), one_hot(pair_nums[1:2, :], segments)

            def chosen(values, pairs):
                split = jnp.dot(parts_of(values, 3), pairs, preferred_element_type=jnp.float32)
                return split[:classes] + split[classes : 2 * classes] + split[2 * classes :]

            logits = chosen(scores[:classes], pair_first) + chosen(scores[classes : 2 * classes], pair_second)
            logits = logits + jnp.broadcast_to(vec[8:9, :128], (128, 128)).T[:classes, 0:1]
            powers = jnp.exp(logits - jnp.max(logits, 0, keepdims=True))
            chance = powers / jnp.sum(powers, 0, keepdims=True)
            kinds = lax.broadcasted_iota(jnp.int32, logits.shape, 0)
            delta = chance - jnp.where(kinds == labels[...], 1.0, 0.0)
            split = parts_of(delta, 2)
            gathered = []
            for pairs in (pair_first, pair_second):
                both = dot_last(split, pairs)
                gathered.append(both[:classes] + both[classes:])
            gathered.append(jnp.zeros((128 - 2 * classes, segments), jnp.float32))
            leaving_grads[...] = jnp.concatenate(gathered).T.reshape(leaving.shape)
            sums_out[first_dir + 2 * classes : first_dir + 3 * classes, :] = jnp.broadcast_to(
                jnp.sum(delta, 1, keepdims=True), (classes, width)
            )
            back = exchange(leaving_grads, arrived_grads, base + wide - 1)
            coarse = back.astype(jnp.bfloat16)
            fine = (back - coarse.astype(jnp.float32)).astype(jnp.bfloat16)
            grads_in = (
                jnp.dot(coarse, dir_w[...], preferred_element_type=jnp.float32)
                + jnp.dot(fine, dir_w[...], preferred_element_type=jnp.float32)
            ).astype(jnp.bfloat16)
            back_t = back.T[: 2 * classes]
            both = jnp.dot(parts_of(back_t, 2), picked[...], preferred_element_type=jnp.float32)
            sums_out[first_dir : first_dir + 2 * classes, :] = both[: 2 * classes] + both[2 * classes :]
            loads[0].wait()

            def body(i, carry):
                at = pl.multiple_of(i * row_block, row_block)
                some = pl.ds(at, row_block)
                normed = n2[some, :].astype(jnp.float32)
                doc = at // length
                line = lax.broadcasted_iota(jnp.int32, (row_block, 1), 0) + (at - doc * length)
                grad = cot[some, :].astype(jnp.float32) + jnp.dot(
                    select[some, :], grads_in, preferred_element_type=jnp.float32
                )
                grad = jnp.where(line < lens[doc], grad, 0.0)
                two = norm_back_rows(grad, normed, q2[some, :], vec[4:5, :])
                low = two.astype(jnp.bfloat16)
                grad_hidden[some, :] = two
                lowered[some, :] = low
                lowered_t[:, some] = low.T
                sums_out[0:1, :] += jnp.sum(grad * normed, 0, keepdims=True)
                sums_out[1:2, :] += jnp.sum(grad, 0, keepdims=True)
                sums_out[2:3, :] += jnp.sum(low.astype(jnp.float32), 0, keepdims=True)
                return carry

            lax.fori_loop(0, row_steps, body, 0)

        def slab(n, step):
            return pl.ds(pl.multiple_of((n * chunks + chunk_of(step)) * 128, 128), 128)

        @pl.when(pid == 0)
        def _():
            loads[2].wait()

        @pl.when(pid < chunks)
        def _():
            actives = jnp.concatenate([act[:, slab(n, pid)] for n in range(narrow)], axis=1)
            result = jnp.dot(lowered_t[...], actives, preferred_element_type=jnp.float32).astype(jnp.bfloat16)
            for w in range(wide):
                for n in range(narrow):
                    own[(pid,) + bits_of(w, wide_bits) + bits_of(n, narrow_bits)] = result[
                        w * d_rows : (w + 1) * d_rows, n * 128 : (n + 1) * 128
                    ]

        @pl.when(pid == chunks)
        def _():
            for load in loads[3:]:
                load.wait()

        @pl.when(pid >= chunks)
        def _():
            slopes = jnp.concatenate([ref[...] for ref in slo], axis=1)
            downs = jnp.concatenate([dws[slab(n, pid - chunks), :] for n in range(narrow)], axis=0)
            ups = jnp.concatenate([uws[:, slab(n, pid - chunks)] for n in range(narrow)], axis=1)
            grad_active = dot_last(lowered[...], downs)
            grad_upper = (grad_active * slopes.astype(jnp.float32)).astype(jnp.bfloat16)
            totals = jnp.sum(grad_upper.astype(jnp.float32), 0, keepdims=True)
            at = pl.ds(pl.multiple_of(chunk_of(pid - chunks) * 128, 128), 128)
            for n in range(narrow):
                sums_out[6 + n : 7 + n, at] = totals[:, n * 128 : (n + 1) * 128]
            result = jnp.dot(hidden_t[...], grad_upper, preferred_element_type=jnp.float32).astype(jnp.bfloat16)
            for n in range(narrow):
                for z in range(narrow):
                    high = bits_of(z, wide_bits - 1)
                    up_own[(pid - chunks,) + high + bits_of(n, narrow_bits)] = result[
                        n * u_rows : (n + 1) * u_rows, z * 128 : (z + 1) * 128
                    ]
            grad_hidden[...] += dot_last(grad_upper, ups)

        def down_write(number):
            return pltpu.make_async_copy(
                own.at[number].at[pieces[number].region(early - 1, True)], down_out.at[number], local_sems.at[chunks + number]
            )

        def advance(number, step):
            pieces[number].merge(step)
            if step + 1 < early:
                pieces[number].send(step + 1)
            else:
                down_write(number).start()

        for number in range(chunks):
            @pl.when(pid == chunks + number)
            def _():
                up_pieces[number].send(0)

        @pl.when(pid == 2 * chunks - 1)
        def _():
            def body(i, carry):
                at = pl.multiple_of(i * row_block, row_block)
                some = pl.ds(at, row_block)
                grad, normed = grad_hidden[some, :], n1[some, :].astype(jnp.float32)
                low = norm_back_rows(grad, normed, q1[some, :], vec[1:2, :]).astype(jnp.bfloat16)
                ga_out[some, :] = low
                sums_out[3:4, :] += jnp.sum(grad * normed, 0, keepdims=True)
                sums_out[4:5, :] += jnp.sum(grad, 0, keepdims=True)
                sums_out[5:6, :] += jnp.sum(low.astype(jnp.float32), 0, keepdims=True)
                return carry

            lax.fori_loop(0, row_steps, body, 0)

        plan = {}
        for number in range(chunks):
            for step in range(early):
                at = (number + 1, chunks + 1 + 2 * (number // 3), chunks + 4 + number // 3)[step]
                plan.setdefault(min(at, 2 * chunks - 1), []).append((step, number))
        for at in range(2 * chunks):
            @pl.when(pid == at)
            def _():
                if at < chunks:
                    pieces[at].send(0)
                if at > chunks:
                    up_pieces[at - chunks - 1].merge(0)
                    up_write(at - chunks - 1).start()
                for step, number in sorted(plan.get(at, [])):
                    advance(number, step)
                if at == 2 * chunks - 1:
                    up_pieces[chunks - 1].merge(0)
                    up_write(chunks - 1).start()
                    for number in range(chunks):
                        up_write(number).wait()
                        down_write(number).wait()
                    for item in pieces + up_pieces:
                        item.close()

    def whole(shape):
        return pl.BlockSpec(shape, lambda g: (0,) * len(shape), pipeline_mode=pl.Buffered(1))

    def slab_columns(shape, first):
        return [pl.BlockSpec(shape, lambda g, n=n: (0, n * chunks + chunk_of(g - first))) for n in range(narrow)]

    in_specs = [pl.BlockSpec(memory_space=pltpu.SMEM), *[whole(item.shape) for item in numbers],
                whole((rows, width)), whole((rows, width))]
    in_specs += [whole(dir_t.shape)]
    in_specs += [whole((rows, 1))] * 2 + [whole(vectors.shape)] + [pl.BlockSpec(memory_space=pl.ANY)] * 6
    in_specs += slab_columns((rows, 128), chunks)
    high = two * (wide_bits - 1)
    low = two * narrow_bits
    up_shape = (third,) + high + (2,) + low[1:] + (u_rows, 128)
    out_specs = [
        whole((rows, width)),
        pl.BlockSpec(memory_space=pl.ANY),
        pl.BlockSpec(memory_space=pl.ANY),
        whole((sum_rows, width)),
    ]
    out_shape = [
        jax.ShapeDtypeStruct((rows, width), jnp.bfloat16),
        jax.ShapeDtypeStruct(up_shape, jnp.bfloat16),
        jax.ShapeDtypeStruct((chunks,) + two * (steps - early) + (d_rows, 128), jnp.bfloat16),
        jax.ShapeDtypeStruct((sum_rows, width), jnp.float32),
    ]
    scratch = [
        pltpu.VMEM((rows, width), jnp.float32),
        pltpu.VMEM((rows, width), jnp.bfloat16),
        pltpu.VMEM((width, rows), jnp.bfloat16),
        pltpu.VMEM((width, rows), jnp.bfloat16),
        pltpu.VMEM((chunks,) + two * steps + (d_rows, 128), jnp.bfloat16),
        pltpu.VMEM((chunks,) + high + low + (u_rows, 128), jnp.bfloat16),
        pltpu.VMEM((chunks,) + high + low[1:] + (u_rows, 128), jnp.bfloat16),
    ]
    scratch += [pltpu.VMEM((chunks,) + two * (steps - 1 - s) + (d_rows, 128), jnp.bfloat16) for s in range(early)]
    scratch += [pltpu.VMEM((rows, segments), jnp.bfloat16), pltpu.VMEM((segments, width), jnp.bfloat16)]
    scratch += [pltpu.VMEM((128, width), jnp.bfloat16)]
    scratch += [pltpu.VMEM((wide, segments // wide, 128), jnp.float32)] * 4
    far = (normed_two, hidden_low, active, down_weight, up_weight, normed_one)
    scratch += [pltpu.VMEM(item.shape, item.dtype) for item in far]
    sems = chunks * early + chunks + 2 * (wide - 1)
    scratch += [pltpu.SemaphoreType.DMA((sems,)), pltpu.SemaphoreType.DMA((sems,)), pltpu.SemaphoreType.DMA((2 * chunks + len(far),))]
    return pl.pallas_call(
        kernel,
        grid=(2 * chunks,),
        in_specs=in_specs,
        out_specs=out_specs,
        out_shape=out_shape,
        scratch_shapes=scratch,
        compiler_params=pltpu.CompilerParams(collective_id=0, has_side_effects=True, vmem_limit_bytes=60 << 20),
        name="ffn_backward",
    )(lengths, *numbers, encoded, cotangent, dir_t, inverse_two, inverse_one, vectors,
      *far, *([slope] * narrow))


def attention_backward(grad_attended, mixed, out_weight, queries, keys, values, attention, tokens, qkv_weight, up_grads,
                       down_grads, sums):
    rows, width = tokens.shape
    docs, _, length, _ = attention.shape
    pairs = width // 128
    names = axis_bits()
    steps = len(names)
    wide, narrow = lax.axis_size("wide"), lax.axis_size("narrow")
    wide_bits, narrow_bits = wide.bit_length() - 1, narrow.bit_length() - 1
    half = narrow // 2
    half_bits = narrow_bits - 1
    lanes = width // half
    q_rows, o_rows = 3 * width // wide // 2, width // wide // 2
    q_parts = lanes // 128
    orders = link_orders()
    ups = up_grads.shape[0]
    u_rows = up_grads.shape[-2]
    attn_steps = docs * pairs
    token_block = 256
    token_steps = rows // token_block
    first_q = 1 + attn_steps
    first_t = first_q + q_parts
    grid = first_t + token_steps
    downs, d_rows = down_grads.shape[0], down_grads.shape[-2]
    down_steps = len(down_grads.shape) - 3
    cuts = [(0, q_rows // 32 * 16), (q_rows // 32 * 16, q_rows)]
    u_cuts = [(0, u_rows // 2), (u_rows // 2, u_rows)]
    up_count, out_count = ups * len(u_cuts), q_parts
    first_part = up_count + out_count
    first_down = first_part + q_parts * len(cuts)
    count = first_down + downs
    small_rows = sums.shape[0]

    def bits_of(number, count):
        return tuple((number >> bit) & 1 for bit in reversed(range(count)))

    def kernel(*refs):
        (ga_hbm, mix_hbm, ow_hbm, q_ref, k_ref, v_ref, att_ref, tok_hbm, qw_hbm, up_hbm, down_hbm, small) = refs[:12]
        tokens_out, up_out, out_out, qkv_out, down_out, small_out, late_out = refs[12:19]
        rest = list(refs[19:])
        gm, mix_pair, gqkv_t, up_own, out_own, qkv_own = rest[:6]
        rest = rest[6:]
        up_received = [rest[i * (steps - 1) : (i + 1) * (steps - 1)] for i in range(len(u_cuts))]
        rest = rest[len(u_cuts) * (steps - 1) :]
        out_received, rest = rest[:steps], rest[steps:]
        qkv_received, rest = [rest[i * steps : (i + 1) * steps] for i in range(len(cuts))], rest[len(cuts) * steps :]
        down_own, down_received, rest = rest[0], rest[1 : 1 + down_steps], rest[1 + down_steps :]
        small_sent, small_received, late_sent, late_received, swap_out, swap_qkv, tok, qw, ga, mix, ow = rest[:11]
        send_sems, recv_sems, local_sems = rest[11:]
        pid = pl.program_id(0)
        place = Place()
        core = place.bit["narrow", 0]
        pieces = []
        for low, high in u_cuts:
            for part in range(ups):
                cut = len(pieces) // ups
                pieces.append(Halving(place, names[:-1], orders[part % 3][1:], up_hbm.at[part], up_own.at[part],
                                      [r.at[part] for r in up_received[cut]], send_sems, recv_sems, len(pieces) * steps,
                                      (slice(low, high), slice(None))))
        for part in range(out_count):
            pieces.append(Halving(place, names, orders[part % 3], out_own.at[part], out_own.at[part],
                                  [r.at[part] for r in out_received], send_sems, recv_sems, len(pieces) * steps))
        for part in range(q_parts):
            for cut, (low, high) in enumerate(cuts):
                pieces.append(Halving(place, names, orders[part % 3], qkv_own.at[part], qkv_own.at[part],
                                      [r.at[part] for r in qkv_received[cut]], send_sems, recv_sems, len(pieces) * steps,
                                      (slice(low, high), slice(None))))
        for number in range(downs):
            order = orders[number % 3][steps - down_steps :]
            pieces.append(Halving(place, [name for name in names if name in order], order, down_own.at[number],
                                  down_own.at[number], [r.at[number] for r in down_received], send_sems, recv_sems,
                                  len(pieces) * steps))
        base = count * steps

        def all_sum(sent, received, first):
            made = []
            for step in range(steps):
                made.append(pltpu.make_async_remote_copy(
                    src_ref=sent.at[step], dst_ref=received.at[step], send_sem=send_sems.at[first + step],
                    recv_sem=recv_sems.at[first + step], device_id=place.across(orders[0][step]),
                    device_id_type=MESH_ID))
            return made

        small_copies = all_sum(small_sent, small_received, base)
        late_copies = all_sum(late_sent, late_received, base + steps)
        swap_refs = [swap_out.at[part, core] for part in range(out_count)]
        swap_refs += [swap_qkv.at[part, core, low:high] for part in range(q_parts) for low, high in cuts]
        swaps = [pltpu.make_async_remote_copy(
            src_ref=ref, dst_ref=ref, send_sem=send_sems.at[base + 2 * steps + slot],
            recv_sem=recv_sems.at[base + 2 * steps + slot], device_id=place.across(("narrow", 0)),
            device_id_type=MESH_ID) for slot, ref in enumerate(swap_refs)]
        local = []
        for number in range(ups):
            keep = pieces[number].region(0, True)[: -2]
            local.append(pltpu.make_async_copy(up_hbm.at[number].at[keep], up_own.at[number].at[keep], local_sems.at[number]))

        loads = [pltpu.make_async_copy(tok_hbm, tok, local_sems.at[ups]),
                 pltpu.make_async_copy(qw_hbm, qw, local_sems.at[ups + 1])]
        first_loads = [pltpu.make_async_copy(source, target, local_sems.at[ups + 3 + i])
                       for i, (source, target) in enumerate(((ga_hbm, ga), (mix_hbm, mix), (ow_hbm, ow)))]
        down_load = pltpu.make_async_copy(down_hbm, down_own, local_sems.at[ups + 2])

        def advance(number, step):
            item = pieces[number]
            if step == 0 and number < ups:
                local[number].wait()
            total = item.add(step)
            if total is None:
                item.send(step + 1)
            elif number < up_count:
                cut, part = divmod(number, ups)
                up_out[u_cuts[cut][0] : u_cuts[cut][1], part * 128 : (part + 1) * 128] = total
            elif number >= first_down:
                number -= first_down
                j = number // 2 + downs // 2 * (number % 2)
                down_out[:, j * 128 : (j + 1) * 128] = total
            else:
                if number < first_part:
                    swap_out[number - up_count, core] = total
                else:
                    part, cut = divmod(number - first_part, len(cuts))
                    swap_qkv[part, core, cuts[cut][0] : cuts[cut][1]] = total
                swaps[number - up_count].start()

        def advance_small(copies, sent, received, out, step):
            copies[step].wait_recv()
            total = sent[step] + received[step]
            if step + 1 < steps:
                sent[step + 1] = total
                copies[step + 1].start()
            else:
                out[...] = total

        @pl.when(pid == 0)
        def _():
            place.greet()
            for number in range(up_count):
                pieces[number].send(0)
            for number in range(ups):
                local[number].start()
            for load in first_loads:
                load.start()
            small_sent[0] = small[...]
            small_copies[0].start()
            down_load.start()
            for load in loads:
                load.start()
            for load in first_loads:
                load.wait()
            grads_t = ga[...].T
            result = jnp.dot(grads_t, mix[...], preferred_element_type=jnp.float32).astype(jnp.bfloat16)
            for w in range(wide):
                for h in range(2):
                    for y in range(half):
                        at = (w * 2 + h) * o_rows
                        for part in range(out_count):
                            first = y * lanes + part * 128
                            out_own[(part,) + bits_of(w, wide_bits) + bits_of(y, half_bits) + (h,)] = result[
                                at : at + o_rows, first : first + 128
                            ]
            for part in range(out_count):
                pieces[up_count + part].send(0)
            grad_mixed = dot_last(ga[...], ow[...]).astype(jnp.bfloat16)
            for pair in range(pairs):
                gm[pair] = grad_mixed[:, pair * 128 : (pair + 1) * 128]
                mix_pair[pair] = mix[:, pair * 128 : (pair + 1) * 128]
            down_load.wait()
            for number in range(downs):
                pieces[first_down + number].send(0)

        @pl.when((pid >= 1) & (pid < first_q))
        def _():
            number = pid - 1
            pair, doc = number // docs, number % docs
            some = pl.ds(pl.multiple_of(doc * length, length), length)
            lane = lax.broadcasted_iota(jnp.int32, (1, 128), 1)
            scaled, keys, values = q_ref[...] * jnp.bfloat16(HEAD_DIM**-0.5), k_ref[...], v_ref[...]
            grads = gm[pair, some, :]
            product = grads.astype(jnp.float32) * mix_pair[pair, some, :].astype(jnp.float32)
            queries_t, grads_t = scaled.T, grads.T
            zero = jnp.zeros_like(grads)
            query_parts = []
            for head in range(2):
                inside = (lane // HEAD_DIM) == head
                at = head * HEAD_DIM
                attention = att_ref[0, head]
                chance = dot_last(jnp.where(inside, grads, zero), values)
                inner = jnp.sum(jnp.where(inside, product, 0.0), -1, keepdims=True)
                grad_scores = (attention.astype(jnp.float32) * (chance - inner)).astype(jnp.bfloat16)
                query_parts.append(jnp.dot(grad_scores, keys, preferred_element_type=jnp.float32))
                key_t = jnp.dot(queries_t[at : at + HEAD_DIM], grad_scores, preferred_element_type=jnp.float32)
                value_t = jnp.dot(grads_t[at : at + HEAD_DIM], attention, preferred_element_type=jnp.float32)
                row = pair * 128 + at
                gqkv_t[pl.ds(pl.multiple_of(width + row, HEAD_DIM), HEAD_DIM), some] = key_t.astype(jnp.bfloat16)
                gqkv_t[pl.ds(pl.multiple_of(2 * width + row, HEAD_DIM), HEAD_DIM), some] = value_t.astype(jnp.bfloat16)
            grad_query = jnp.where(lane < HEAD_DIM, query_parts[0], query_parts[1]) * HEAD_DIM**-0.5
            gqkv_t[pl.ds(pl.multiple_of(pair * 128, 128), 128), some] = grad_query.astype(jnp.bfloat16).T

        for part in range(q_parts):
            @pl.when(pid == first_q + part)
            def _():
                if part == 0:
                    for load in loads:
                        load.wait()
                    ones = jnp.ones((8, rows), jnp.bfloat16)
                    late_sent[0] = jnp.concatenate(
                        [dot_last(ones, gqkv_t[:width, :]), dot_last(ones, gqkv_t[2 * width :, :])], axis=1
                    )
                    late_copies[0].start()
                columns = jnp.concatenate(
                    [tok[:, y * lanes + part * 128 : y * lanes + (part + 1) * 128] for y in range(half)], axis=1
                )
                result = jnp.dot(gqkv_t[...], columns, preferred_element_type=jnp.float32).astype(jnp.bfloat16)
                for w in range(wide):
                    for h in range(2):
                        for y in range(half):
                            at = (w * 2 + h) * q_rows
                            qkv_own[(part,) + bits_of(w, wide_bits) + bits_of(y, half_bits) + (h,)] = result[
                                at : at + q_rows, y * 128 : (y + 1) * 128
                            ]
                for cut in range(len(cuts)):
                    pieces[first_part + part * len(cuts) + cut].send(0)

        @pl.when(pid >= first_t)
        def _():
            at = pl.multiple_of((pid - first_t) * token_block, token_block)
            some = pl.ds(at, token_block)
            grad_t = jnp.dot(qw[...], gqkv_t[:, some], preferred_element_type=jnp.float32)
            tokens_out[...] = (grad_t.T + ga[some, :].astype(jnp.float32)).astype(jnp.bfloat16)

        plan, small_plan, late_plan = {}, {}, {}
        for cut, times in enumerate(((4, 7, 9, 12), (6, 8, 10, 14))):
            for step, at in enumerate(times):
                for part in range(ups):
                    plan.setdefault(at, []).append((cut * ups + part, step))
        for step, at in enumerate((1, 8, 10, 12, 14)):
            for part in range(out_count):
                plan.setdefault(at, []).append((up_count + part, step))
        for step, at in enumerate((3, 6)):
            for number in range(downs):
                plan.setdefault(at, []).append((first_down + number, step))
        for number in range(first_part, first_down):
            for step in range(steps):
                at = first_q + (number - first_part) // len(cuts) + 1 if step == 0 else grid - 1
                plan.setdefault(at, []).append((number, step))
        for step, at in enumerate((3, 6, 8, 10, 12)):
            small_plan[at] = step
        late_plan[first_q + 2] = 0
        for at in range(grid):
            @pl.when(pid == at)
            def _():
                if at in small_plan:
                    advance_small(small_copies, small_sent, small_received, small_out, small_plan[at])
                for number, step in sorted(plan.get(at, []), key=lambda entry: (entry[1], entry[0])):
                    if at == grid - 1 and number == first_part:
                        advance_small(late_copies, late_sent, late_received, late_out, step)
                    advance(number, step)
                if at in late_plan:
                    advance_small(late_copies, late_sent, late_received, late_out, late_plan[at])
                if at == grid - 1:
                    for copy in swaps:
                        copy.wait()

                    def own_lanes(lanes):
                        size = lanes.shape[1] // 2
                        return jnp.where(core == 0, lanes[:, :size], lanes[:, size:])

                    out_out[...] = own_lanes(jnp.concatenate(
                        [swap_out[part].reshape(2 * o_rows, 128) for part in range(out_count)], axis=1))
                    qkv_out[...] = own_lanes(jnp.concatenate(
                        [swap_qkv[part].reshape(2 * q_rows, 128) for part in range(q_parts)], axis=1))
                    for item in pieces:
                        item.close()
                    for copy in small_copies + late_copies:
                        copy.wait_send()

    def whole(shape):
        return pl.BlockSpec(shape, lambda g: (0,) * len(shape), pipeline_mode=pl.Buffered(1))

    def number_of(g):
        return jnp.clip(g - 1, 0, attn_steps - 1)

    tile = pl.BlockSpec((length, 128), lambda g: (number_of(g) % docs, number_of(g) // docs))

    two = (2,)
    any_space = pl.BlockSpec(memory_space=pl.ANY)
    in_specs = [any_space, any_space, any_space, tile, tile, tile]
    in_specs += [pl.BlockSpec((1, 2, length, length), lambda g: (number_of(g) % docs, number_of(g) // docs, 0, 0))]
    in_specs += [any_space, any_space, any_space, any_space, whole((small_rows, width))]
    out_shape = [
        jax.ShapeDtypeStruct((rows, width), jnp.bfloat16),
        jax.ShapeDtypeStruct((u_rows, ups * 128), jnp.float32),
        jax.ShapeDtypeStruct((2 * o_rows, lanes // 2), jnp.float32),
        jax.ShapeDtypeStruct((2 * q_rows, lanes // 2), jnp.float32),
        jax.ShapeDtypeStruct((d_rows, downs * 128), jnp.float32),
        jax.ShapeDtypeStruct((small_rows, width), jnp.float32),
        jax.ShapeDtypeStruct((8, 2 * width), jnp.float32),
    ]
    wide_dims, half_dims = two * wide_bits, two * half_bits
    scratch = [
        pltpu.VMEM((pairs, rows, 128), jnp.bfloat16),
        pltpu.VMEM((pairs, rows, 128), jnp.bfloat16),
        pltpu.VMEM((3 * width, rows), jnp.bfloat16),
        pltpu.VMEM(up_grads.shape, jnp.bfloat16),
        pltpu.VMEM((out_count,) + wide_dims + half_dims + two + (o_rows, 128), jnp.bfloat16),
        pltpu.VMEM((q_parts,) + wide_dims + half_dims + two + (q_rows, 128), jnp.bfloat16),
    ]
    for low, high in u_cuts:
        scratch += [pltpu.VMEM((ups,) + two * (steps - 2 - s) + (high - low, 128), jnp.bfloat16) for s in range(steps - 1)]
    scratch += [pltpu.VMEM((out_count,) + two * (steps - 1 - s) + (o_rows, 128), jnp.bfloat16) for s in range(steps)]
    for low, high in cuts:
        scratch += [pltpu.VMEM((q_parts,) + two * (steps - 1 - s) + (high - low, 128), jnp.bfloat16) for s in range(steps)]
    scratch += [pltpu.VMEM(down_grads.shape, jnp.bfloat16)]
    scratch += [pltpu.VMEM((downs,) + two * (down_steps - 1 - s) + (d_rows, 128), jnp.bfloat16) for s in range(down_steps)]
    scratch += [pltpu.VMEM((steps, small_rows, width), jnp.float32)] * 2
    scratch += [pltpu.VMEM((steps, 8, 2 * width), jnp.float32)] * 2
    scratch += [pltpu.VMEM((out_count, 2, o_rows, 128), jnp.float32), pltpu.VMEM((q_parts, 2, q_rows, 128), jnp.float32)]
    scratch += [pltpu.VMEM(tokens.shape, jnp.bfloat16), pltpu.VMEM(qkv_weight.shape, jnp.bfloat16)]
    scratch += [pltpu.VMEM(item.shape, jnp.bfloat16) for item in (grad_attended, mixed, out_weight)]
    sems = count * steps + 2 * steps + out_count + q_parts * len(cuts)
    scratch += [pltpu.SemaphoreType.DMA((sems,)), pltpu.SemaphoreType.DMA((sems,)), pltpu.SemaphoreType.DMA((ups + 6,))]
    return pl.pallas_call(
        kernel,
        grid=(grid,),
        in_specs=in_specs,
        out_specs=[pl.BlockSpec((token_block, width), lambda g: (jnp.clip(g - first_t, 0, token_steps - 1), 0))]
        + [whole(item.shape) for item in out_shape[1:]],
        out_shape=out_shape,
        scratch_shapes=scratch,
        compiler_params=pltpu.CompilerParams(collective_id=1, has_side_effects=True, vmem_limit_bytes=60 << 20),
        name="attention_backward",
    )(grad_attended, mixed, out_weight, queries, keys, values, attention, tokens, qkv_weight, up_grads, down_grads, sums)


def hand_out(grad_tokens, sums, late, narrow, classes, turned, *blocks):
    rows, width = grad_tokens.shape
    steps = 4
    first_dir = 6 + narrow

    def kernel(tokens_ref, sums_ref, late_ref, *refs):
        ins, outs = refs[: len(blocks)], refs[len(blocks) :]
        outs[0][...] = tokens_ref[...]

        @pl.when(pl.program_id(0) == 0)
        def _():
            for source, target in zip(ins, outs[1:]):
                target[...] = source[...] if source.shape == target.shape else source[...].T
            singles = outs[1 + len(blocks) :]
            for number in range(6):
                singles[number][...] = sums_ref[number, :]
            for number in range(2):
                singles[6 + number][...] = late_ref[0, number * width : (number + 1) * width]
            for number in range(narrow):
                singles[8][number * width : (number + 1) * width] = sums_ref[6 + number, :]
            singles[9][...] = sums_ref[first_dir : first_dir + 2 * classes, :]
            square = (classes, 128)
            matching = lax.broadcasted_iota(jnp.int32, square, 0) == lax.broadcasted_iota(jnp.int32, square, 1)
            biases = sums_ref[first_dir + 2 * classes : first_dir + 3 * classes, :128]
            singles[10][...] = jnp.sum(jnp.where(matching, biases, 0.0), 0)[:classes]

    def whole(shape):
        return pl.BlockSpec(shape, lambda g: (0,) * len(shape))

    some = pl.BlockSpec((rows // steps, width), lambda g: (g, 0))
    small = [(width,)] * 8 + [(narrow * width,), (2 * classes, width), (classes,)]
    shapes = [block.shape[::-1] if number in turned else block.shape for number, block in enumerate(blocks)]
    out_shape = [jax.ShapeDtypeStruct((rows, width), jnp.bfloat16)]
    out_shape += [jax.ShapeDtypeStruct(shape, jnp.float32) for shape in shapes + small]
    return pl.pallas_call(
        kernel,
        grid=(steps,),
        in_specs=[some] + [whole(item.shape) for item in (sums, late) + blocks],
        out_specs=[some] + [whole(item.shape) for item in out_shape[1:]],
        out_shape=out_shape,
        name="hand_out",
    )(grad_tokens, sums, late, *blocks)


def on_device_fast(
    tokens,
    doc_lengths,
    qkv_weight,
    query_bias,
    value_bias,
    out_weight,
    out_bias,
    first_gain,
    first_shift,
    up_weight,
    up_bias,
    down_weight,
    down_bias,
    second_gain,
    second_shift,
    dir_weight,
    dir_bias,
    segment_rows,
    segment_slots,
    pair_rows,
    pair_labels,
    out_cotangent,
):
    doc_count, length, model_width = tokens.shape
    token_rows = tokens.reshape(doc_count * length, model_width)
    singles = (out_bias, first_gain, first_shift, down_bias, second_gain, second_shift, query_bias, value_bias)
    vectors, queries, keys, values, attention, mixed = attention_forward(
        doc_lengths, token_rows, qkv_weight, singles + (dir_bias, up_bias)
    )
    hidden_low, normed_one, inverse_one, active, slope, normed_two, inverse_two, encoded_rows = ffn_forward(
        doc_lengths, mixed, token_rows, out_weight, vectors, up_weight, down_weight
    )
    classes_count = dir_weight.shape[1]
    grad_attended, up_blocks, down_blocks, sums = ffn_backward(
        doc_lengths, segment_rows, segment_slots, pair_rows[0].T, pair_labels, encoded_rows, out_cotangent.reshape(-1, model_width), dir_weight.T, vectors,
        normed_two, inverse_two, active, slope,
        hidden_low, down_weight, up_weight, normed_one, inverse_one,
    )
    grad_tokens, out_up, out_out, out_qkv, out_down, sums, late = attention_backward(
        grad_attended, mixed, out_weight, queries, keys, values, attention, token_rows, qkv_weight, up_blocks,
        down_blocks, sums,
    )
    grad_tokens, out_up, out_out, out_qkv, out_down, *smalls = hand_out(
        grad_tokens, sums, late, lax.axis_size("narrow"), classes_count, (1, 2), out_up, out_out, out_qkv, out_down
    )
    return (
        encoded_rows.reshape(tokens.shape),
        grad_tokens.reshape(tokens.shape),
        out_qkv,
        smalls[6],
        smalls[7],
        out_out,
        smalls[5],
        smalls[3],
        smalls[4],
        out_up,
        smalls[8],
        out_down.T,
        smalls[2],
        smalls[0],
        smalls[1],
        smalls[9].reshape(2, classes_count, model_width).transpose(0, 2, 1).reshape(2 * model_width, classes_count),
        smalls[10],
    )


def on_device(
    tokens,
    doc_lengths,
    qkv_weight,
    query_bias,
    value_bias,
    out_weight,
    out_bias,
    first_gain,
    first_shift,
    up_weight,
    up_bias,
    down_weight,
    down_bias,
    second_gain,
    second_shift,
    dir_weight,
    dir_bias,
    segment_rows,
    segment_slots,
    pair_rows,
    pair_labels,
    out_cotangent,
):
    doc_count, length, model_width = tokens.shape
    score_scale = HEAD_DIM ** (-0.5)
    token_rows = tokens.reshape(doc_count * length, model_width)
    allowed = lax.broadcasted_iota(jnp.int32, (doc_count, length), 1) < doc_lengths[:, None]
    allowed_rows = allowed.reshape(-1, 1).astype(jnp.float32)
    bias_row = jnp.concatenate([query_bias, jnp.zeros_like(query_bias), value_bias]).astype(
        jnp.float32
    )
    qkv = (jnp.dot(token_rows, qkv_weight, preferred_element_type=jnp.float32) + bias_row).astype(
        jnp.bfloat16
    )

    def split_heads(doc_block, which):
        return doc_block[:, which * model_width : (which + 1) * model_width].reshape(
            length, HEADS, HEAD_DIM
        )

    def scores_of(queries, key_rows, doc_mask):
        scores = (
            jnp.einsum("qhd,khd->hqk", queries, key_rows, preferred_element_type=jnp.float32)
            * score_scale
        )
        return jnp.where(doc_mask[None, None, :], scores, MASKED)

    mixed_parts = []
    log_totals = []
    for doc_index in range(doc_count):
        doc_block = qkv[doc_index * length : (doc_index + 1) * length]
        queries = split_heads(doc_block, 0)
        key_rows = split_heads(doc_block, 1)
        value_rows = split_heads(doc_block, 2)
        scores = scores_of(queries, key_rows, allowed[doc_index])
        highest = jnp.max(scores, -1, keepdims=True)
        powers = jnp.exp(scores - highest)
        summed = jnp.sum(powers, -1, keepdims=True)
        attention = (powers / summed).astype(jnp.bfloat16)
        log_totals.append(highest + jnp.log(summed))
        mixed_parts.append(
            jnp.einsum(
                "hqk,khd->qhd", attention, value_rows, preferred_element_type=jnp.float32
            ).reshape(length, model_width)
        )
    mixed = jnp.concatenate(mixed_parts).astype(jnp.bfloat16)
    attended = jnp.dot(mixed, out_weight, preferred_element_type=jnp.float32) + out_bias.astype(
        jnp.float32
    )
    resid_one = token_rows.astype(jnp.float32) + attended
    hidden_one, normed_one, inverse_one = norm_forward(
        resid_one, first_gain.astype(jnp.float32), first_shift.astype(jnp.float32)
    )
    hidden_low = hidden_one.astype(jnp.bfloat16)
    upper_pre = jnp.dot(hidden_low, up_weight, preferred_element_type=jnp.float32) + up_bias.astype(
        jnp.float32
    )
    cumulative = normal_cdf(upper_pre)
    active = (upper_pre * cumulative).astype(jnp.bfloat16)
    lowered = jnp.dot(active, down_weight, preferred_element_type=jnp.float32) + down_bias.astype(
        jnp.float32
    )
    resid_two = hidden_one + lowered
    second_float = second_gain.astype(jnp.float32)
    normed_out, normed_two, inverse_two = norm_forward(
        resid_two, second_float, second_shift.astype(jnp.float32)
    )
    encoded_rows = (normed_out * allowed_rows).astype(jnp.bfloat16)
    doc_starts = lax.broadcasted_iota(jnp.int32, (doc_count, 1), 0) * length
    picked_rows = (segment_rows + doc_starts).reshape(-1)
    picked = encoded_rows[picked_rows]
    slots = segment_slots.reshape(-1)
    outgoing = jnp.zeros_like(picked).at[slots].set(picked)
    arrived = lax.all_to_all(outgoing, "wide", split_axis=0, concat_axis=0, tiled=True)
    pairs = pair_rows.reshape(-1, 2)
    labels = pair_labels.reshape(-1)
    first_rows = arrived[pairs[:, 0]]
    second_rows = arrived[pairs[:, 1]]
    logits = (
        jnp.dot(first_rows, dir_weight[:model_width], preferred_element_type=jnp.float32)
        + jnp.dot(second_rows, dir_weight[model_width:], preferred_element_type=jnp.float32)
        + dir_bias.astype(jnp.float32)
    )
    powers_head = jnp.exp(logits - jnp.max(logits, -1, keepdims=True))
    chance = powers_head / jnp.sum(powers_head, -1, keepdims=True)
    classes = lax.broadcasted_iota(jnp.int32, logits.shape, 1)
    delta = chance - (labels[:, None] == classes).astype(jnp.float32)
    first_float = first_rows.astype(jnp.float32)
    second_rows_float = second_rows.astype(jnp.float32)
    grad_dir_weight = jnp.concatenate(
        [
            jnp.dot(first_float.T, delta, precision=EXACT, preferred_element_type=jnp.float32),
            jnp.dot(
                second_rows_float.T, delta, precision=EXACT, preferred_element_type=jnp.float32
            ),
        ]
    )
    grad_dir_bias = jnp.sum(delta, 0)
    dir_float = dir_weight.astype(jnp.float32)
    grad_first = jnp.dot(
        delta, dir_float[:model_width].T, precision=EXACT, preferred_element_type=jnp.float32
    )
    grad_second = jnp.dot(
        delta, dir_float[model_width:].T, precision=EXACT, preferred_element_type=jnp.float32
    )
    grad_arrived = jnp.zeros((arrived.shape[0], model_width), jnp.float32)
    grad_arrived = grad_arrived.at[pairs[:, 0]].add(grad_first).at[pairs[:, 1]].add(grad_second)
    returned = lax.all_to_all(
        grad_arrived.astype(jnp.bfloat16), "wide", split_axis=0, concat_axis=0, tiled=True
    )
    grad_picked = returned[slots].astype(jnp.float32)
    grad_encoded = (
        out_cotangent.reshape(-1, model_width).astype(jnp.float32).at[picked_rows].add(grad_picked)
    )
    grad_encoded = grad_encoded * allowed_rows
    grad_two, grad_second_gain, grad_second_shift = norm_backward(
        grad_encoded, normed_two, inverse_two, second_float
    )
    grad_lowered = grad_two.astype(jnp.bfloat16)
    grad_down_weight = jnp.einsum(
        "rf,rd->fd", active, grad_lowered, preferred_element_type=jnp.float32
    )
    grad_down_bias = jnp.sum(grad_lowered.astype(jnp.float32), 0)
    grad_active = jnp.einsum(
        "rd,fd->rf", grad_lowered, down_weight, preferred_element_type=jnp.float32
    )
    density = jnp.exp(-0.5 * upper_pre * upper_pre) * 0.3989422804014327
    grad_upper = (grad_active * (cumulative + upper_pre * density)).astype(jnp.bfloat16)
    grad_up_weight = jnp.einsum(
        "rd,rf->df", hidden_low, grad_upper, preferred_element_type=jnp.float32
    )
    grad_up_bias = jnp.sum(grad_upper.astype(jnp.float32), 0)
    grad_hidden = grad_two + jnp.einsum(
        "rf,df->rd", grad_upper, up_weight, preferred_element_type=jnp.float32
    )
    grad_one, grad_first_gain, grad_first_shift = norm_backward(
        grad_hidden, normed_one, inverse_one, first_gain.astype(jnp.float32)
    )
    grad_attended = grad_one.astype(jnp.bfloat16)
    grad_out_weight = jnp.einsum(
        "rd,re->de", mixed, grad_attended, preferred_element_type=jnp.float32
    )
    grad_out_bias = jnp.sum(grad_attended.astype(jnp.float32), 0)
    grad_mixed = jnp.einsum(
        "re,de->rd", grad_attended, out_weight, preferred_element_type=jnp.float32
    ).astype(jnp.bfloat16)
    grad_parts = []
    for doc_index in range(doc_count):
        doc_block = qkv[doc_index * length : (doc_index + 1) * length]
        queries = split_heads(doc_block, 0)
        key_rows = split_heads(doc_block, 1)
        value_rows = split_heads(doc_block, 2)
        scores = scores_of(queries, key_rows, allowed[doc_index])
        attention = jnp.exp(scores - log_totals[doc_index])
        grad_doc = grad_mixed[doc_index * length : (doc_index + 1) * length].reshape(
            length, HEADS, HEAD_DIM
        )
        grad_chance = jnp.einsum(
            "qhd,khd->hqk", grad_doc, value_rows, preferred_element_type=jnp.float32
        )
        inner = jnp.sum(grad_chance * attention, -1, keepdims=True)
        grad_scores = (attention * (grad_chance - inner)).astype(jnp.bfloat16)
        grad_query = (
            jnp.einsum("hqk,khd->qhd", grad_scores, key_rows, preferred_element_type=jnp.float32)
            * score_scale
        )
        grad_key = (
            jnp.einsum("hqk,qhd->khd", grad_scores, queries, preferred_element_type=jnp.float32)
            * score_scale
        )
        grad_value = jnp.einsum(
            "hqk,qhd->khd",
            attention.astype(jnp.bfloat16),
            grad_doc,
            preferred_element_type=jnp.float32,
        )
        grad_parts.append(
            jnp.concatenate(
                [
                    grad_query.reshape(length, model_width),
                    grad_key.reshape(length, model_width),
                    grad_value.reshape(length, model_width),
                ],
                axis=1,
            )
        )
    grad_qkv = jnp.concatenate(grad_parts).astype(jnp.bfloat16)
    grad_qkv_float = grad_qkv.astype(jnp.float32)
    grad_query_bias = jnp.sum(grad_qkv_float[:, :model_width], 0)
    grad_value_bias = jnp.sum(grad_qkv_float[:, 2 * model_width :], 0)
    grad_qkv_weight = jnp.einsum(
        "rd,re->de", token_rows, grad_qkv, preferred_element_type=jnp.float32
    )
    grad_tokens = (
        jnp.einsum("re,de->rd", grad_qkv, qkv_weight, preferred_element_type=jnp.float32) + grad_one
    ).astype(jnp.bfloat16)
    matrices = (grad_qkv_weight, grad_out_weight, grad_up_weight, grad_down_weight)
    partial_sums = (
        lax.psum_scatter(
            matrices[0].astype(jnp.bfloat16), "wide", scatter_dimension=1, tiled=True
        ).astype(jnp.float32),
        lax.psum_scatter(
            matrices[1].astype(jnp.bfloat16), "wide", scatter_dimension=1, tiled=True
        ).astype(jnp.float32),
        lax.psum_scatter(
            matrices[2].astype(jnp.bfloat16), "wide", scatter_dimension=1, tiled=True
        ).astype(jnp.float32),
        lax.psum_scatter(
            matrices[3].astype(jnp.bfloat16), "wide", scatter_dimension=1, tiled=True
        ).astype(jnp.float32),
    )
    summed_mats = (
        lax.psum_scatter(
            partial_sums[0].astype(jnp.bfloat16), "narrow", scatter_dimension=0, tiled=True
        ).astype(jnp.float32),
        lax.psum_scatter(
            partial_sums[1].astype(jnp.bfloat16), "narrow", scatter_dimension=0, tiled=True
        ).astype(jnp.float32),
        lax.psum_scatter(
            partial_sums[2].astype(jnp.bfloat16), "narrow", scatter_dimension=0, tiled=True
        ).astype(jnp.float32),
        lax.psum_scatter(
            partial_sums[3].astype(jnp.bfloat16), "narrow", scatter_dimension=0, tiled=True
        ).astype(jnp.float32),
    )
    smalls = lax.psum(
        (
            grad_query_bias,
            grad_value_bias,
            grad_out_bias,
            grad_first_gain,
            grad_first_shift,
            grad_up_bias,
            grad_down_bias,
            grad_second_gain,
            grad_second_shift,
            grad_dir_weight,
            grad_dir_bias,
        ),
        ("wide", "narrow"),
    )
    return (
        encoded_rows.reshape(tokens.shape),
        grad_tokens.reshape(tokens.shape),
        summed_mats[0],
        smalls[0],
        smalls[1],
        summed_mats[1],
        smalls[2],
        smalls[3],
        smalls[4],
        summed_mats[2],
        smalls[5],
        summed_mats[3],
        smalls[6],
        smalls[7],
        smalls[8],
        smalls[9],
        smalls[10],
    )


def fits_blocks(mesh):
    wide, narrow = mesh.shape["wide"], mesh.shape["narrow"]
    width, ff = HEADS * HEAD_DIM, 4 * HEADS * HEAD_DIM
    if wide != 2 * narrow or narrow < 4 or narrow & (narrow - 1):
        return False
    lanes = (ff // narrow, ff // wide, 2 * width // narrow)
    rows = (width // wide, width // narrow, width // wide // 2, 3 * width // wide // 2)
    return all(size % 128 == 0 for size in lanes) and all(size % 16 == 0 for size in rows)


def solution(mesh):
    placed = (
        P(("wide", "narrow"), None, None),
        P(("wide", "narrow")),
        P(),
        P(),
        P(),
        P(),
        P(),
        P(),
        P(),
        P(),
        P(),
        P(),
        P(),
        P(),
        P(),
        P(),
        P(),
        P(("wide", "narrow"), None),
        P(("wide", "narrow"), None),
        P(("wide", "narrow"), None, None),
        P(("wide", "narrow"), None),
        P(("wide", "narrow"), None, None),
    )
    return jax.shard_map(
        on_device_fast if fits_blocks(mesh) else on_device,
        mesh=mesh,
        in_specs=placed,
        out_specs=(
            P(("wide", "narrow"), None, None),
            P(("wide", "narrow"), None, None),
            P("narrow", "wide"),
            P(),
            P(),
            P("narrow", "wide"),
            P(),
            P(),
            P(),
            P("narrow", "wide"),
            P(),
            P("narrow", "wide"),
            P(),
            P(),
            P(),
            P(),
            P(),
        ),
        check_vma=False,
    )
```

```python
import jax
import jax.numpy as jnp
from jax import lax
from jax.experimental import pallas as pl
from jax.experimental.pallas import tpu as pltpu
from jax.sharding import PartitionSpec as P

HEADS = 12
HEAD_DIM = 64


EXACT = lax.Precision.HIGHEST
MASKED = -1e30
EPSILON = 1e-05


def norm_forward(values, gain, shift):
    center = jnp.mean(values, -1, keepdims=True)
    centered = values - center
    inverse = lax.rsqrt(jnp.mean(centered * centered, -1, keepdims=True) + EPSILON)
    normed = centered * inverse
    return (normed * gain + shift, normed, inverse)


def norm_backward(grad, normed, inverse, gain):
    scaled = grad * gain
    first_mean = jnp.mean(scaled, -1, keepdims=True)
    second_mean = jnp.mean(scaled * normed, -1, keepdims=True)
    return (
        (scaled - first_mean - normed * second_mean) * inverse,
        jnp.sum(grad * normed, 0),
        jnp.sum(grad, 0),
    )


def normal_cdf(values):
    return 0.5 * (1.0 + lax.erf(values * 0.7071067811865476))


MESH_ID = pl.DeviceIdType.MESH


def axis_bits():
    names = []
    for axis in ("wide", "narrow"):
        count = lax.axis_size(axis).bit_length() - 1
        names += [(axis, bit) for bit in reversed(range(count))]
    return names


class Place:
    def __init__(self):
        self.index = {axis: lax.axis_index(axis) for axis in ("wide", "narrow")}
        self.names = axis_bits()
        self.bit = {name: (self.index[name[0]] // (1 << name[1])) % 2 for name in self.names}

    def across(self, name):
        axis, bit = name
        target = dict(self.index)
        target[axis] = target[axis] + (1 << bit) - (2 << bit) * self.bit[name]
        return target

    def ahead(self, offset):
        target = dict(self.index)
        target["wide"] = (target["wide"] + offset) % lax.axis_size("wide")
        return target

    def greet(self, all_wide=False):
        barrier = pltpu.get_barrier_semaphore()
        targets = [self.across(name) for name in self.names if not (all_wide and name[0] == "wide")]
        if all_wide:
            targets += [self.ahead(offset) for offset in range(1, lax.axis_size("wide"))]
        for target in targets:
            pl.semaphore_signal(barrier, inc=1, device_id=target, device_id_type=MESH_ID)
        pl.semaphore_wait(barrier, len(targets))


class Halving:
    def __init__(self, place, names, order, source, own, received, send_sems, recv_sems, first_sem, tail=()):
        self.place, self.names, self.order = place, names, order
        self.source, self.own, self.received = source, own, received
        self.last = True
        self.send_sems, self.recv_sems, self.first_sem, self.tail = send_sems, recv_sems, first_sem, tail

    def region(self, step, mine):
        index = []
        for name in self.names:
            if name in self.order[:step]:
                index.append(self.place.bit[name])
            elif name == self.order[step]:
                index.append(self.place.bit[name] if mine else 1 - self.place.bit[name])
            else:
                index.append(slice(None))
        return tuple(index) + self.tail

    def copy(self, step):
        held = self.source if step == 0 else self.own
        return pltpu.make_async_remote_copy(
            src_ref=held.at[self.region(step, False)],
            dst_ref=self.received[step],
            send_sem=self.send_sems.at[self.first_sem + step],
            recv_sem=self.recv_sems.at[self.first_sem + step],
            device_id=self.place.across(self.order[step]),
            device_id_type=MESH_ID,
        )

    def send(self, step):
        self.copy(step).start()

    def add(self, step):
        self.copy(step).wait_recv()
        mine = self.region(step, True)
        if step + 1 < len(self.order) or not self.last:
            self.own[mine] = self.own[mine] + self.received[step][...]
            return None
        return self.own[mine].astype(jnp.float32) + self.received[step][...].astype(jnp.float32)

    def merge(self, step):
        self.last = False
        self.add(step)

    def close(self):
        for step in range(len(self.order)):
            self.copy(step).wait_send()


def link_orders():
    wide = [("wide", bit) for bit in range(lax.axis_size("wide").bit_length() - 1)]
    narrow = [("narrow", bit) for bit in range(1, lax.axis_size("narrow").bit_length() - 1)]
    core, x, near, far = [("narrow", 0)], wide[:1], wide[1:-1], wide[-1:]
    return [core + narrow + x + near + far, core + x + near + narrow + far, core + near + narrow + x + far]


def attention_forward(lengths, tokens, qkv_weight, singles):
    rows, width = tokens.shape
    docs = lengths.shape[0]
    length = rows // docs
    pairs = width // 128

    kinds = [item.shape[0] for item in singles]
    lines = sum(max(1, size // width) for size in kinds)

    def kernel(lens, tok, wq, wk, wv, *refs):
        singles, (vec, q_out, k_out, v_out, attention_out, mixed_out) = refs[: len(kinds)], refs[len(kinds) :]

        @pl.when(pl.program_id(0) == 0)
        def _():
            at = 0
            for single, size in zip(singles, kinds):
                values = single[...].astype(jnp.float32)
                for first in range(0, size, width):
                    some = min(size, width)
                    vec[at, :some] = values[first : first + some]
                    at += 1

        weights = jnp.concatenate([wq[...], wk[...], wv[...]], axis=1)
        at = pl.ds(pl.multiple_of(pl.program_id(0) * 128, 128), 128)
        offsets = jnp.concatenate([vec[6:7, at], jnp.zeros((1, 128), jnp.float32), vec[7:8, at]], axis=1)
        qkv = (jnp.dot(tok[...], weights, preferred_element_type=jnp.float32) + offsets).astype(jnp.bfloat16)
        q_out[...] = qkv[:, :128]
        k_out[...] = qkv[:, 128:256]
        v_out[...] = qkv[:, 256:]
        first = lax.broadcasted_iota(jnp.int32, (1, 128), 1) < HEAD_DIM
        for doc in range(docs):
            some = slice(doc * length, (doc + 1) * length)
            queries = qkv[some, :128] * jnp.bfloat16(HEAD_DIM**-0.5)
            keys, values = qkv[some, 128:256], qkv[some, 256:]
            zero = jnp.zeros_like(queries)
            places = lax.broadcasted_iota(jnp.int32, (1, length), 1)
            bias = jnp.where(places < lens[doc], 0.0, MASKED)
            outs = []
            for head in range(2):
                masked = jnp.where(first, queries, zero) if head == 0 else jnp.where(first, zero, queries)
                scores = dot_last(masked, keys) + bias
                powers = jnp.exp(scores - jnp.max(scores, -1, keepdims=True))
                attention = (powers * (1.0 / jnp.sum(powers, -1, keepdims=True))).astype(jnp.bfloat16)
                attention_out[doc, head] = attention
                outs.append(jnp.dot(attention, values, preferred_element_type=jnp.float32))
            mixed_out[some, :] = jnp.where(first, outs[0], outs[1]).astype(jnp.bfloat16)

    def whole(shape):
        return pl.BlockSpec(shape, lambda pair: (0,) * len(shape), pipeline_mode=pl.Buffered(1))

    column = pl.BlockSpec((rows, 128), lambda pair: (0, pair))
    in_specs = [pl.BlockSpec(memory_space=pltpu.SMEM), whole((rows, width))]
    in_specs += [pl.BlockSpec((width, 128), lambda pair, n=n: (0, n * pairs + pair)) for n in range(3)]
    in_specs += [whole(item.shape) for item in singles]
    low = jax.ShapeDtypeStruct((rows, width), jnp.bfloat16)
    return pl.pallas_call(
        kernel,
        grid=(pairs,),
        in_specs=in_specs,
        out_specs=[whole((lines, width))] + [column] * 3
        + [pl.BlockSpec((docs, 2, length, length), lambda pair: (0, pair, 0, 0)), column],
        out_shape=[jax.ShapeDtypeStruct((lines, width), jnp.float32)] + [low] * 3 + [jax.ShapeDtypeStruct((docs, 2 * pairs, length, length), jnp.bfloat16), low],
        compiler_params=pltpu.CompilerParams(vmem_limit_bytes=56 << 20),
        name="attention_forward",
    )(lengths, tokens, qkv_weight, qkv_weight, qkv_weight, *singles)


def ffn_forward(lengths, mixed, tokens, out_weight, vectors, up_weight, down_weight):
    rows, width = tokens.shape
    ff = up_weight.shape[1]
    chunk = width
    chunks = ff // chunk
    length = rows // lengths.shape[0]
    row_block = 256

    def kernel(lens, mix, tok, ow, vec, up, down, hid_out, n1_out, q1_out, act_out, slope_out, n2_out, q2_out,
               enc_out, hidden, total):
        pid = pl.program_id(0)

        def each_block(body):
            def step(i, carry):
                body(pl.multiple_of(i * row_block, row_block))
                return carry

            lax.fori_loop(0, rows // row_block, step, 0)

        @pl.when(pid == 0)
        def _():
            total[...] = jnp.dot(mix[...], ow[...], preferred_element_type=jnp.float32)

            def body(at):
                some = pl.ds(at, row_block)
                summed = tok[some, :].astype(jnp.float32) + (total[some, :] + vec[0:1, :])
                out, normed, inverse = norm_forward(summed, vec[1:2, :], vec[2:3, :])
                hidden[some, :] = out
                hid_out[some, :] = out.astype(jnp.bfloat16)
                n1_out[some, :] = normed.astype(jnp.bfloat16)
                q1_out[some, :] = inverse
                total[some, :] = jnp.zeros_like(out)

            each_block(body)

        pre = jnp.dot(hid_out[...], up[...], preferred_element_type=jnp.float32) + vec[pl.ds(pid + 9, 1), :]
        cumulative = normal_cdf(pre)
        density = jnp.exp(-0.5 * pre * pre) * 0.3989422804014327
        active = (pre * cumulative).astype(jnp.bfloat16)
        act_out[...] = active
        slope_out[...] = (cumulative + pre * density).astype(jnp.bfloat16)
        total[...] += jnp.dot(active, down[...], preferred_element_type=jnp.float32)

        @pl.when(pid == chunks - 1)
        def _():
            def body(at):
                some = pl.ds(at, row_block)
                summed = hidden[some, :] + (total[some, :] + vec[3:4, :])
                out, normed, inverse = norm_forward(summed, vec[4:5, :], vec[5:6, :])
                n2_out[some, :] = normed.astype(jnp.bfloat16)
                q2_out[some, :] = inverse
                doc = at // length
                line = lax.broadcasted_iota(jnp.int32, (row_block, 1), 0) + (at - doc * length)
                enc_out[some, :] = jnp.where(line < lens[doc], out, 0.0).astype(jnp.bfloat16)

            each_block(body)

    def whole(shape):
        return pl.BlockSpec(shape, lambda f: (0,) * len(shape), pipeline_mode=pl.Buffered(1))

    wide_row, column = whole((rows, width)), pl.BlockSpec((rows, chunk), lambda f: (0, f))
    low = jax.ShapeDtypeStruct((rows, width), jnp.bfloat16)
    one = jax.ShapeDtypeStruct((rows, 1), jnp.float32)
    upper = jax.ShapeDtypeStruct((rows, ff), jnp.bfloat16)
    return pl.pallas_call(
        kernel,
        grid=(chunks,),
        in_specs=[
            pl.BlockSpec(memory_space=pltpu.SMEM), wide_row, wide_row, whole((width, width)), whole(vectors.shape),
            pl.BlockSpec((width, chunk), lambda f: (0, f)),
            pl.BlockSpec((chunk, width), lambda f: (f, 0)),
        ],
        out_specs=[wide_row, wide_row, whole((rows, 1)), column, column, wide_row, whole((rows, 1)), wide_row],
        out_shape=[low, low, one, upper, upper, low, one, low],
        scratch_shapes=[pltpu.VMEM((rows, width), jnp.float32), pltpu.VMEM((rows, width), jnp.float32)],
        compiler_params=pltpu.CompilerParams(vmem_limit_bytes=58 << 20),
        name="ffn_forward",
    )(lengths, mixed, tokens, out_weight, vectors, up_weight, down_weight)


def dot_last(left, right):
    return lax.dot_general(left, right, (((1,), (1,)), ((), ())), preferred_element_type=jnp.float32)


def norm_back_rows(grad, normed, inverse, gain):
    scaled = grad * gain
    first = jnp.mean(scaled, -1, keepdims=True)
    second = jnp.mean(scaled * normed, -1, keepdims=True)
    return (scaled - first - normed * second) * inverse


def parts_of(values, count):
    terms = []
    for _ in range(count):
        term = values.astype(jnp.bfloat16).astype(jnp.float32)
        terms.append(term)
        values = values - term
    return jnp.concatenate(terms).astype(jnp.bfloat16)


def one_hot(row, count):
    lines = lax.broadcasted_iota(jnp.int32, (count, row.shape[1]), 0)
    return jnp.where(lines == row, 1.0, 0.0).astype(jnp.bfloat16)


def ffn_backward(lengths, segment_rows, segment_slots, pair_rows, pair_labels, encoded, cotangent, dir_t, vectors, normed_two, inverse_two, active, slope, hidden_low, down_weight, up_weight,
                 normed_one, inverse_one):
    rows, width = hidden_low.shape
    ff = active.shape[1]
    segments, classes = segment_slots.shape[1], dir_t.shape[0]
    numbers = (segment_rows, segment_slots, pair_rows, pair_labels)
    length = rows // lengths.shape[0]
    names = axis_bits()
    steps = len(names)
    wide, narrow = lax.axis_size("wide"), lax.axis_size("narrow")
    wide_bits, narrow_bits = wide.bit_length() - 1, narrow.bit_length() - 1
    chunks = ff // narrow // 128
    third = chunks // 2
    d_rows, u_rows = width // wide, width // narrow
    row_block = 256
    row_steps = rows // row_block
    orders = link_orders()
    two = (2,)
    early = 3
    first_dir = 6 + narrow
    sum_rows = pl.cdiv(first_dir + 2 * classes + 1, 16) * 16

    def chunk_of(step):
        step = jnp.clip(step, 0, chunks - 1)
        return step // 2 + third * (step % 2)

    def bits_of(number, count):
        return tuple((number >> bit) & 1 for bit in reversed(range(count)))

    def kernel(*refs):
        lens, seg_rows, seg_slots, pair_nums, labels, enc, cot, dir_ref = refs[:8]
        refs = refs[8:]
        q2, q1, vec = refs[:3]
        far = refs[3:9]
        slo = refs[9 : 9 + narrow]
        rest = list(refs[9 + narrow :])
        ga_out, up_out, down_out, sums_out = rest[:4]
        rest = rest[4:]
        grad_hidden, lowered, lowered_t, hidden_t, own, up_own, up_received = rest[:7]
        received = rest[7 : 7 + early]
        rest = rest[7 + early :]
        select, picked, dir_w, leaving, arrived, leaving_grads, arrived_grads = rest[:7]
        near = rest[7:13]
        n2, hidden, act, dws, uws, n1 = near
        send_sems, recv_sems, local_sems = rest[13:]
        loads = [pltpu.make_async_copy(far[i], near[i], local_sems.at[2 * chunks + i]) for i in range(len(near))]
        pid = pl.program_id(0)
        place = Place()
        pieces = []
        for number in range(chunks):
            pieces.append(
                Halving(place, names, orders[number % 3][:early], own.at[number], own.at[number],
                        [r.at[number] for r in received], send_sems, recv_sems, number * early)
            )
        core = ("narrow", 0)
        up_names = [name for name in names if name != ("wide", 0)]
        up_pieces = [
            Halving(place, up_names, [core], up_own.at[number], up_own.at[number], [up_received.at[number]],
                    send_sems, recv_sems, chunks * early + number)
            for number in range(chunks)
        ]

        def up_write(number):
            mine = up_pieces[number].region(0, True)
            return pltpu.make_async_copy(
                up_own.at[number].at[mine],
                up_out.at[(number // 2,) + (slice(None),) * (wide_bits - 1) + (number % 2,)],
                local_sems.at[number],
            )

        def exchange(source, landing, first, meanwhile=None):
            made = []
            for offset in range(1, wide):
                target = place.ahead(offset)
                made.append(pltpu.make_async_remote_copy(
                    src_ref=source.at[target["wide"]], dst_ref=landing.at[place.index["wide"]],
                    send_sem=send_sems.at[first + offset - 1], recv_sem=recv_sems.at[first + offset - 1],
                    device_id=target, device_id_type=MESH_ID))
            me = place.index["wide"]
            for copy in made:
                copy.start()
            landing[me] = source[me]
            if meanwhile:
                meanwhile()
            for copy in made:
                copy.wait()
            return landing[...].reshape(segments, 128)

        def turn_hidden():
            def body(i, carry):
                some = pl.ds(pl.multiple_of(i * row_block, row_block), row_block)
                hidden_t[:, some] = hidden[some, :].T
                return carry

            loads[1].wait()
            lax.fori_loop(0, row_steps, body, 0)

        @pl.when(pid == 0)
        def _():
            for load in loads:
                load.start()
            place.greet(all_wide=True)
            sums_out[...] = jnp.zeros_like(sums_out)
            base = chunks * early + chunks
            docs = rows // length
            places = jnp.concatenate([seg_rows[doc : doc + 1, :] + doc * length for doc in range(docs)], axis=1)
            select[...] = dot_last(one_hot(places, rows), one_hot(seg_slots[...], segments)).astype(jnp.bfloat16)
            picked[...] = jnp.dot(select[...].T, enc[...], preferred_element_type=jnp.float32).astype(jnp.bfloat16)
            halves = [dir_ref[:, n * width : (n + 1) * width].astype(jnp.float32) for n in range(2)]
            blank = jnp.zeros((128 - 2 * classes, width), jnp.float32)
            dir_w[...] = jnp.concatenate(halves + [blank]).astype(jnp.bfloat16)
            leaving[...] = dot_last(picked[...], dir_w[...]).reshape(leaving.shape)
            scores = exchange(leaving, arrived, base, turn_hidden).T
            pair_first, pair_second = one_hot(pair_nums[0:1, :], segments), one_hot(pair_nums[1:2, :], segments)

            def chosen(values, pairs):
                split = jnp.dot(parts_of(values, 3), pairs, preferred_element_type=jnp.float32)
                return split[:classes] + split[classes : 2 * classes] + split[2 * classes :]

            logits = chosen(scores[:classes], pair_first) + chosen(scores[classes : 2 * classes], pair_second)
            logits = logits + jnp.broadcast_to(vec[8:9, :128], (128, 128)).T[:classes, 0:1]
            powers = jnp.exp(logits - jnp.max(logits, 0, keepdims=True))
            chance = powers / jnp.sum(powers, 0, keepdims=True)
            kinds = lax.broadcasted_iota(jnp.int32, logits.shape, 0)
            delta = chance - jnp.where(kinds == labels[...], 1.0, 0.0)
            split = parts_of(delta, 2)
            gathered = []
            for pairs in (pair_first, pair_second):
                both = dot_last(split, pairs)
                gathered.append(both[:classes] + both[classes:])
            gathered.append(jnp.zeros((128 - 2 * classes, segments), jnp.float32))
            leaving_grads[...] = jnp.concatenate(gathered).T.reshape(leaving.shape)
            square = (classes, 128)
            matching = lax.broadcasted_iota(jnp.int32, square, 0) == lax.broadcasted_iota(jnp.int32, square, 1)
            biases = jnp.where(matching, jnp.sum(delta, 1, keepdims=True), 0.0)
            sums_out[first_dir + 2 * classes : first_dir + 2 * classes + 1, :128] = jnp.sum(biases, 0, keepdims=True)
            back = exchange(leaving_grads, arrived_grads, base + wide - 1)
            coarse = back.astype(jnp.bfloat16)
            fine = (back - coarse.astype(jnp.float32)).astype(jnp.bfloat16)
            grads_in = (
                jnp.dot(coarse, dir_w[...], preferred_element_type=jnp.float32)
                + jnp.dot(fine, dir_w[...], preferred_element_type=jnp.float32)
            ).astype(jnp.bfloat16)
            back_t = back.T[: 2 * classes]
            both = jnp.dot(parts_of(back_t, 2), picked[...], preferred_element_type=jnp.float32)
            sums_out[first_dir : first_dir + 2 * classes, :] = both[: 2 * classes] + both[2 * classes :]
            loads[0].wait()

            def body(i, carry):
                at = pl.multiple_of(i * row_block, row_block)
                some = pl.ds(at, row_block)
                normed = n2[some, :].astype(jnp.float32)
                doc = at // length
                line = lax.broadcasted_iota(jnp.int32, (row_block, 1), 0) + (at - doc * length)
                grad = cot[some, :].astype(jnp.float32) + jnp.dot(
                    select[some, :], grads_in, preferred_element_type=jnp.float32
                )
                grad = jnp.where(line < lens[doc], grad, 0.0)
                two = norm_back_rows(grad, normed, q2[some, :], vec[4:5, :])
                low = two.astype(jnp.bfloat16)
                grad_hidden[some, :] = two
                lowered[some, :] = low
                lowered_t[:, some] = low.T
                sums_out[0:1, :] += jnp.sum(grad * normed, 0, keepdims=True)
                sums_out[1:2, :] += jnp.sum(grad, 0, keepdims=True)
                sums_out[2:3, :] += jnp.sum(low.astype(jnp.float32), 0, keepdims=True)
                return carry

            lax.fori_loop(0, row_steps, body, 0)

        def slab(n, step):
            return pl.ds(pl.multiple_of((n * chunks + chunk_of(step)) * 128, 128), 128)

        @pl.when(pid == 0)
        def _():
            loads[2].wait()

        @pl.when(pid < chunks)
        def _():
            actives = jnp.concatenate([act[:, slab(n, pid)] for n in range(narrow)], axis=1)
            result = jnp.dot(lowered_t[...], actives, preferred_element_type=jnp.float32).astype(jnp.bfloat16)
            for w in range(wide):
                for n in range(narrow):
                    own[(pid,) + bits_of(w, wide_bits) + bits_of(n, narrow_bits)] = result[
                        w * d_rows : (w + 1) * d_rows, n * 128 : (n + 1) * 128
                    ]

        @pl.when(pid == chunks)
        def _():
            for load in loads[3:]:
                load.wait()

        @pl.when(pid >= chunks)
        def _():
            slopes = jnp.concatenate([ref[...] for ref in slo], axis=1)
            downs = jnp.concatenate([dws[slab(n, pid - chunks), :] for n in range(narrow)], axis=0)
            ups = jnp.concatenate([uws[:, slab(n, pid - chunks)] for n in range(narrow)], axis=1)
            grad_active = dot_last(lowered[...], downs)
            grad_upper = (grad_active * slopes.astype(jnp.float32)).astype(jnp.bfloat16)
            totals = jnp.sum(grad_upper.astype(jnp.float32), 0, keepdims=True)
            at = pl.ds(pl.multiple_of(chunk_of(pid - chunks) * 128, 128), 128)
            for n in range(narrow):
                sums_out[6 + n : 7 + n, at] = totals[:, n * 128 : (n + 1) * 128]
            result = jnp.dot(hidden_t[...], grad_upper, preferred_element_type=jnp.float32).astype(jnp.bfloat16)
            for n in range(narrow):
                for z in range(narrow):
                    high = bits_of(z, wide_bits - 1)
                    up_own[(pid - chunks,) + high + bits_of(n, narrow_bits)] = result[
                        n * u_rows : (n + 1) * u_rows, z * 128 : (z + 1) * 128
                    ]
            grad_hidden[...] += dot_last(grad_upper, ups)

        def down_write(number):
            return pltpu.make_async_copy(
                own.at[number].at[pieces[number].region(early - 1, True)], down_out.at[number], local_sems.at[chunks + number]
            )

        def advance(number, step):
            pieces[number].merge(step)
            if step + 1 < early:
                pieces[number].send(step + 1)
            else:
                down_write(number).start()

        for number in range(chunks):
            @pl.when(pid == chunks + number)
            def _():
                up_pieces[number].send(0)

        @pl.when(pid == 2 * chunks - 1)
        def _():
            def body(i, carry):
                at = pl.multiple_of(i * row_block, row_block)
                some = pl.ds(at, row_block)
                grad, normed = grad_hidden[some, :], n1[some, :].astype(jnp.float32)
                low = norm_back_rows(grad, normed, q1[some, :], vec[1:2, :]).astype(jnp.bfloat16)
                ga_out[some, :] = low
                sums_out[3:4, :] += jnp.sum(grad * normed, 0, keepdims=True)
                sums_out[4:5, :] += jnp.sum(grad, 0, keepdims=True)
                sums_out[5:6, :] += jnp.sum(low.astype(jnp.float32), 0, keepdims=True)
                return carry

            lax.fori_loop(0, row_steps, body, 0)

        plan = {}
        for number in range(chunks):
            for step in range(early):
                at = (number + 1, chunks + 1 + 2 * (number // 3), chunks + 4 + number // 3)[step]
                plan.setdefault(min(at, 2 * chunks - 1), []).append((step, number))
        for at in range(2 * chunks):
            @pl.when(pid == at)
            def _():
                if at < chunks:
                    pieces[at].send(0)
                if at > chunks:
                    up_pieces[at - chunks - 1].merge(0)
                    up_write(at - chunks - 1).start()
                for step, number in sorted(plan.get(at, [])):
                    advance(number, step)
                if at == 2 * chunks - 1:
                    up_pieces[chunks - 1].merge(0)
                    up_write(chunks - 1).start()
                    for number in range(chunks):
                        up_write(number).wait()
                        down_write(number).wait()
                    for item in pieces + up_pieces:
                        item.close()

    def whole(shape):
        return pl.BlockSpec(shape, lambda g: (0,) * len(shape), pipeline_mode=pl.Buffered(1))

    def slab_columns(shape, first):
        return [pl.BlockSpec(shape, lambda g, n=n: (0, n * chunks + chunk_of(g - first))) for n in range(narrow)]

    in_specs = [pl.BlockSpec(memory_space=pltpu.SMEM), *[whole(item.shape) for item in numbers],
                whole((rows, width)), whole((rows, width))]
    in_specs += [whole(dir_t.shape)]
    in_specs += [whole((rows, 1))] * 2 + [whole(vectors.shape)] + [pl.BlockSpec(memory_space=pl.ANY)] * 6
    in_specs += slab_columns((rows, 128), chunks)
    high = two * (wide_bits - 1)
    low = two * narrow_bits
    up_shape = (third,) + high + (2,) + low[1:] + (u_rows, 128)
    out_specs = [
        whole((rows, width)),
        pl.BlockSpec(memory_space=pl.ANY),
        pl.BlockSpec(memory_space=pl.ANY),
        whole((sum_rows, width)),
    ]
    out_shape = [
        jax.ShapeDtypeStruct((rows, width), jnp.bfloat16),
        jax.ShapeDtypeStruct(up_shape, jnp.bfloat16),
        jax.ShapeDtypeStruct((chunks,) + two * (steps - early) + (d_rows, 128), jnp.bfloat16),
        jax.ShapeDtypeStruct((sum_rows, width), jnp.float32),
    ]
    scratch = [
        pltpu.VMEM((rows, width), jnp.float32),
        pltpu.VMEM((rows, width), jnp.bfloat16),
        pltpu.VMEM((width, rows), jnp.bfloat16),
        pltpu.VMEM((width, rows), jnp.bfloat16),
        pltpu.VMEM((chunks,) + two * steps + (d_rows, 128), jnp.bfloat16),
        pltpu.VMEM((chunks,) + high + low + (u_rows, 128), jnp.bfloat16),
        pltpu.VMEM((chunks,) + high + low[1:] + (u_rows, 128), jnp.bfloat16),
    ]
    scratch += [pltpu.VMEM((chunks,) + two * (steps - 1 - s) + (d_rows, 128), jnp.bfloat16) for s in range(early)]
    scratch += [pltpu.VMEM((rows, segments), jnp.bfloat16), pltpu.VMEM((segments, width), jnp.bfloat16)]
    scratch += [pltpu.VMEM((128, width), jnp.bfloat16)]
    scratch += [pltpu.VMEM((wide, segments // wide, 128), jnp.float32)] * 4
    far = (normed_two, hidden_low, active, down_weight, up_weight, normed_one)
    scratch += [pltpu.VMEM(item.shape, item.dtype) for item in far]
    sems = chunks * early + chunks + 2 * (wide - 1)
    scratch += [pltpu.SemaphoreType.DMA((sems,)), pltpu.SemaphoreType.DMA((sems,)), pltpu.SemaphoreType.DMA((2 * chunks + len(far),))]
    return pl.pallas_call(
        kernel,
        grid=(2 * chunks,),
        in_specs=in_specs,
        out_specs=out_specs,
        out_shape=out_shape,
        scratch_shapes=scratch,
        compiler_params=pltpu.CompilerParams(collective_id=0, has_side_effects=True, vmem_limit_bytes=60 << 20),
        name="ffn_backward",
    )(lengths, *numbers, encoded, cotangent, dir_t, inverse_two, inverse_one, vectors,
      *far, *([slope] * narrow))


def attention_backward(grad_attended, mixed, out_weight, queries, keys, values, attention, tokens, qkv_weight, up_grads,
                       down_grads, sums):
    rows, width = tokens.shape
    docs, _, length, _ = attention.shape
    pairs = width // 128
    names = axis_bits()
    steps = len(names)
    wide, narrow = lax.axis_size("wide"), lax.axis_size("narrow")
    wide_bits, narrow_bits = wide.bit_length() - 1, narrow.bit_length() - 1
    half = narrow // 2
    half_bits = narrow_bits - 1
    lanes = width // half
    q_rows, o_rows = 3 * width // wide // 2, width // wide // 2
    q_parts = lanes // 128
    orders = link_orders()
    ups = up_grads.shape[0]
    u_rows = up_grads.shape[-2]
    attn_steps = docs * pairs
    token_block = 256
    token_steps = rows // token_block
    first_q = 1 + attn_steps
    first_t = first_q + q_parts
    grid = first_t + token_steps
    downs, d_rows = down_grads.shape[0], down_grads.shape[-2]
    down_steps = len(down_grads.shape) - 3
    cuts = [(0, q_rows // 32 * 16), (q_rows // 32 * 16, q_rows)]
    u_cuts = [(0, u_rows // 2), (u_rows // 2, u_rows)]
    up_count, out_count = ups * len(u_cuts), q_parts
    first_part = up_count + out_count
    first_down = first_part + q_parts * len(cuts)
    count = first_down + downs
    small_rows = sums.shape[0]
    late_rows = pl.cdiv(2 * pairs, 8) * 8
    s_cuts = [(0, small_rows // 4), (small_rows // 4, small_rows // 2), (small_rows // 2, small_rows)]

    def bits_of(number, count):
        return tuple((number >> bit) & 1 for bit in reversed(range(count)))

    def kernel(*refs):
        (ga_hbm, mix_hbm, ow_hbm, q_ref, k_ref, v_ref, att_ref, tok_hbm, qw_hbm, up_hbm, down_hbm, small) = refs[:12]
        tokens_out, up_out, out_out, qkv_out, down_out, small_out, late_out = refs[12:19]
        rest = list(refs[19:])
        gm, mix_pair, gqkv_t, up_own, out_own, qkv_own = rest[:6]
        rest = rest[6:]
        up_received = [rest[i * (steps - 1) : (i + 1) * (steps - 1)] for i in range(len(u_cuts))]
        rest = rest[len(u_cuts) * (steps - 1) :]
        out_received, rest = rest[:steps], rest[steps:]
        qkv_received, rest = [rest[i * steps : (i + 1) * steps] for i in range(len(cuts))], rest[len(cuts) * steps :]
        down_own, down_received, rest = rest[0], rest[1 : 1 + down_steps], rest[1 + down_steps :]
        small_sent, small_received, late_sent, late_received, swap_out, swap_qkv, tok, qw, ga, mix, ow = rest[:11]
        send_sems, recv_sems, local_sems = rest[11:]
        pid = pl.program_id(0)
        place = Place()
        core = place.bit["narrow", 0]
        pieces = []
        for low, high in u_cuts:
            for part in range(ups):
                cut = len(pieces) // ups
                pieces.append(Halving(place, names[:-1], orders[part % 3][1:], up_hbm.at[part], up_own.at[part],
                                      [r.at[part] for r in up_received[cut]], send_sems, recv_sems, len(pieces) * steps,
                                      (slice(low, high), slice(None))))
        for part in range(out_count):
            pieces.append(Halving(place, names, orders[part % 3], out_own.at[part], out_own.at[part],
                                  [r.at[part] for r in out_received], send_sems, recv_sems, len(pieces) * steps))
        for part in range(q_parts):
            for cut, (low, high) in enumerate(cuts):
                pieces.append(Halving(place, names, orders[part % 3], qkv_own.at[part], qkv_own.at[part],
                                      [r.at[part] for r in qkv_received[cut]], send_sems, recv_sems, len(pieces) * steps,
                                      (slice(low, high), slice(None))))
        for number in range(downs):
            order = orders[number % 3][steps - down_steps :]
            pieces.append(Halving(place, [name for name in names if name in order], order, down_own.at[number],
                                  down_own.at[number], [r.at[number] for r in down_received], send_sems, recv_sems,
                                  len(pieces) * steps))
        base = count * steps

        def all_sum(sent, received, first, order=0, rows=slice(None)):
            made = []
            for step in range(steps):
                made.append(pltpu.make_async_remote_copy(
                    src_ref=sent.at[step, rows], dst_ref=received.at[step, rows], send_sem=send_sems.at[first + step],
                    recv_sem=recv_sems.at[first + step], device_id=place.across(orders[order][step]),
                    device_id_type=MESH_ID))
            return made

        small_copies = [
            all_sum(small_sent, small_received, base + (2 + q_parts * len(cuts) + i) * steps + out_count, i, slice(low, high))
            for i, (low, high) in enumerate(s_cuts)
        ]
        late_copies = [all_sum(late_sent, late_received, base + steps)]
        swap_refs = [swap_out.at[part, core] for part in range(out_count)]
        swap_refs += [swap_qkv.at[part, core, low:high] for part in range(q_parts) for low, high in cuts]
        swaps = [pltpu.make_async_remote_copy(
            src_ref=ref, dst_ref=ref, send_sem=send_sems.at[base + 2 * steps + slot],
            recv_sem=recv_sems.at[base + 2 * steps + slot], device_id=place.across(("narrow", 0)),
            device_id_type=MESH_ID) for slot, ref in enumerate(swap_refs)]
        local = []
        for number in range(ups):
            keep = pieces[number].region(0, True)[: -2]
            local.append(pltpu.make_async_copy(up_hbm.at[number].at[keep], up_own.at[number].at[keep], local_sems.at[number]))

        loads = [pltpu.make_async_copy(tok_hbm, tok, local_sems.at[ups]),
                 pltpu.make_async_copy(qw_hbm, qw, local_sems.at[ups + 1])]
        first_loads = [pltpu.make_async_copy(source, target, local_sems.at[ups + 3 + i])
                       for i, (source, target) in enumerate(((ga_hbm, ga), (mix_hbm, mix), (ow_hbm, ow)))]
        down_load = pltpu.make_async_copy(down_hbm, down_own, local_sems.at[ups + 2])

        def advance(number, step):
            item = pieces[number]
            if step == 0 and number < ups:
                local[number].wait()
            total = item.add(step)
            if total is None:
                item.send(step + 1)
            elif number < up_count:
                cut, part = divmod(number, ups)
                up_out[u_cuts[cut][0] : u_cuts[cut][1], part * 128 : (part + 1) * 128] = total
            elif number >= first_down:
                number -= first_down
                j = number // 2 + downs // 2 * (number % 2)
                down_out[:, j * 128 : (j + 1) * 128] = total
            else:
                if number < first_part:
                    swap_out[number - up_count, core] = total
                else:
                    part, cut = divmod(number - first_part, len(cuts))
                    swap_qkv[part, core, cuts[cut][0] : cuts[cut][1]] = total
                swaps[number - up_count].start()

        def advance_small(lanes, sent, received, out, step):
            for copies in lanes:
                copies[step].wait_recv()
            total = sent[step] + received[step]
            if step + 1 < steps:
                sent[step + 1] = total
                for copies in lanes:
                    copies[step + 1].start()
            else:
                out[...] = total

        @pl.when(pid == 0)
        def _():
            place.greet()
            for number in range(up_count):
                pieces[number].send(0)
            for number in range(ups):
                local[number].start()
            for load in first_loads:
                load.start()
            small_sent[0] = small[...]
            for copies in small_copies:
                copies[0].start()
            down_load.start()
            for load in loads:
                load.start()
            for load in first_loads:
                load.wait()
            grads_t = ga[...].T
            result = jnp.dot(grads_t, mix[...], preferred_element_type=jnp.float32).astype(jnp.bfloat16)
            for w in range(wide):
                for h in range(2):
                    for y in range(half):
                        at = (w * 2 + h) * o_rows
                        for part in range(out_count):
                            first = y * lanes + part * 128
                            out_own[(part,) + bits_of(w, wide_bits) + bits_of(y, half_bits) + (h,)] = result[
                                at : at + o_rows, first : first + 128
                            ]
            for part in range(out_count):
                pieces[up_count + part].send(0)
            grad_mixed = dot_last(ga[...], ow[...]).astype(jnp.bfloat16)
            for pair in range(pairs):
                gm[pair] = grad_mixed[:, pair * 128 : (pair + 1) * 128]
                mix_pair[pair] = mix[:, pair * 128 : (pair + 1) * 128]
            down_load.wait()
            for number in range(downs):
                pieces[first_down + number].send(0)

        @pl.when((pid >= 1) & (pid < first_q))
        def _():
            number = pid - 1
            pair, doc = number // docs, number % docs
            some = pl.ds(pl.multiple_of(doc * length, length), length)
            lane = lax.broadcasted_iota(jnp.int32, (1, 128), 1)
            scaled, keys, values = q_ref[...] * jnp.bfloat16(HEAD_DIM**-0.5), k_ref[...], v_ref[...]
            grads = gm[pair, some, :]
            product = grads.astype(jnp.float32) * mix_pair[pair, some, :].astype(jnp.float32)
            queries_t, grads_t = scaled.T, grads.T
            zero = jnp.zeros_like(grads)
            query_parts = []
            for head in range(2):
                inside = (lane // HEAD_DIM) == head
                at = head * HEAD_DIM
                attention = att_ref[0, head]
                chance = dot_last(jnp.where(inside, grads, zero), values)
                inner = jnp.sum(jnp.where(inside, product, 0.0), -1, keepdims=True)
                grad_scores = (attention.astype(jnp.float32) * (chance - inner)).astype(jnp.bfloat16)
                query_parts.append(jnp.dot(grad_scores, keys, preferred_element_type=jnp.float32))
                key_t = jnp.dot(queries_t[at : at + HEAD_DIM], grad_scores, preferred_element_type=jnp.float32)
                value_t = jnp.dot(grads_t[at : at + HEAD_DIM], attention, preferred_element_type=jnp.float32)
                row = pair * 128 + at
                gqkv_t[pl.ds(pl.multiple_of(width + row, HEAD_DIM), HEAD_DIM), some] = key_t.astype(jnp.bfloat16)
                gqkv_t[pl.ds(pl.multiple_of(2 * width + row, HEAD_DIM), HEAD_DIM), some] = value_t.astype(jnp.bfloat16)
            grad_query = jnp.where(lane < HEAD_DIM, query_parts[0], query_parts[1]) * HEAD_DIM**-0.5
            gqkv_t[pl.ds(pl.multiple_of(pair * 128, 128), 128), some] = grad_query.astype(jnp.bfloat16).T

        for part in range(q_parts):
            @pl.when(pid == first_q + part)
            def _():
                if part == 0:
                    for load in loads:
                        load.wait()
                    ones = jnp.ones((8, rows), jnp.bfloat16)
                    for which in range(2):
                        totals = dot_last(ones, gqkv_t[2 * which * width : (2 * which + 1) * width, :])
                        for j in range(pairs):
                            late_sent[0, which * pairs + j : which * pairs + j + 1, :] = totals[
                                :1, j * 128 : (j + 1) * 128
                            ]
                    late_sent[0, 2 * pairs :, :] = jnp.zeros((late_rows - 2 * pairs, 128), jnp.float32)
                    late_copies[0][0].start()
                columns = jnp.concatenate(
                    [tok[:, y * lanes + part * 128 : y * lanes + (part + 1) * 128] for y in range(half)], axis=1
                )
                result = jnp.dot(gqkv_t[...], columns, preferred_element_type=jnp.float32).astype(jnp.bfloat16)
                for w in range(wide):
                    for h in range(2):
                        for y in range(half):
                            at = (w * 2 + h) * q_rows
                            qkv_own[(part,) + bits_of(w, wide_bits) + bits_of(y, half_bits) + (h,)] = result[
                                at : at + q_rows, y * 128 : (y + 1) * 128
                            ]
                for cut in range(len(cuts)):
                    pieces[first_part + part * len(cuts) + cut].send(0)

        @pl.when(pid >= first_t)
        def _():
            at = pl.multiple_of((pid - first_t) * token_block, token_block)
            some = pl.ds(at, token_block)
            grad_t = jnp.dot(qw[...], gqkv_t[:, some], preferred_element_type=jnp.float32)
            tokens_out[...] = (grad_t.T + ga[some, :].astype(jnp.float32)).astype(jnp.bfloat16)

        plan, small_plan, late_plan = {}, {}, {}
        for cut, times in enumerate(((5, 9, 12, 14), (8, 10, 13, 15))):
            for step, at in enumerate(times):
                for part in range(ups):
                    plan.setdefault(at, []).append((cut * ups + part, step))
        for step, at in enumerate((1, 9, 12, 14, 15)):
            for part in range(out_count):
                plan.setdefault(at, []).append((up_count + part, step))
        for step, at in enumerate((4, 8)):
            for number in range(downs):
                plan.setdefault(at, []).append((first_down + number, step))
        for number in range(first_part, first_down):
            for step in range(steps):
                at = first_q + (number - first_part) // len(cuts) + 1 if step == 0 else grid - 1
                plan.setdefault(at, []).append((number, step))
        for step, at in enumerate((3, 7, 9, 11, 13)):
            small_plan[at] = step
        late_plan[first_q + 2] = 0
        for at in range(grid):
            @pl.when(pid == at)
            def _():
                if at in small_plan:
                    advance_small(small_copies, small_sent, small_received, small_out, small_plan[at])
                for number, step in sorted(plan.get(at, []), key=lambda entry: (entry[1], entry[0])):
                    if at == grid - 1 and number == first_part:
                        advance_small(late_copies, late_sent, late_received, late_out, step)
                    advance(number, step)
                if at in late_plan:
                    advance_small(late_copies, late_sent, late_received, late_out, late_plan[at])
                if at == grid - 1:
                    for copy in swaps:
                        copy.wait()

                    def own_lanes(lanes):
                        size = lanes.shape[1] // 2
                        return jnp.where(core == 0, lanes[:, :size], lanes[:, size:])

                    out_out[...] = own_lanes(jnp.concatenate(
                        [swap_out[part].reshape(2 * o_rows, 128) for part in range(out_count)], axis=1))
                    qkv_out[...] = own_lanes(jnp.concatenate(
                        [swap_qkv[part].reshape(2 * q_rows, 128) for part in range(q_parts)], axis=1))
                    for item in pieces:
                        item.close()
                    for copies in small_copies + late_copies:
                        for copy in copies:
                            copy.wait_send()

    def whole(shape):
        return pl.BlockSpec(shape, lambda g: (0,) * len(shape), pipeline_mode=pl.Buffered(1))

    def number_of(g):
        return jnp.clip(g - 1, 0, attn_steps - 1)

    tile = pl.BlockSpec((length, 128), lambda g: (number_of(g) % docs, number_of(g) // docs))

    two = (2,)
    any_space = pl.BlockSpec(memory_space=pl.ANY)
    in_specs = [any_space, any_space, any_space, tile, tile, tile]
    in_specs += [pl.BlockSpec((1, 2, length, length), lambda g: (number_of(g) % docs, number_of(g) // docs, 0, 0))]
    in_specs += [any_space, any_space, any_space, any_space, whole((small_rows, width))]
    out_shape = [
        jax.ShapeDtypeStruct((rows, width), jnp.bfloat16),
        jax.ShapeDtypeStruct((u_rows, ups * 128), jnp.float32),
        jax.ShapeDtypeStruct((2 * o_rows, lanes // 2), jnp.float32),
        jax.ShapeDtypeStruct((2 * q_rows, lanes // 2), jnp.float32),
        jax.ShapeDtypeStruct((d_rows, downs * 128), jnp.float32),
        jax.ShapeDtypeStruct((small_rows, width), jnp.float32),
        jax.ShapeDtypeStruct((late_rows, 128), jnp.float32),
    ]
    wide_dims, half_dims = two * wide_bits, two * half_bits
    scratch = [
        pltpu.VMEM((pairs, rows, 128), jnp.bfloat16),
        pltpu.VMEM((pairs, rows, 128), jnp.bfloat16),
        pltpu.VMEM((3 * width, rows), jnp.bfloat16),
        pltpu.VMEM(up_grads.shape, jnp.bfloat16),
        pltpu.VMEM((out_count,) + wide_dims + half_dims + two + (o_rows, 128), jnp.bfloat16),
        pltpu.VMEM((q_parts,) + wide_dims + half_dims + two + (q_rows, 128), jnp.bfloat16),
    ]
    for low, high in u_cuts:
        scratch += [pltpu.VMEM((ups,) + two * (steps - 2 - s) + (high - low, 128), jnp.bfloat16) for s in range(steps - 1)]
    scratch += [pltpu.VMEM((out_count,) + two * (steps - 1 - s) + (o_rows, 128), jnp.bfloat16) for s in range(steps)]
    for low, high in cuts:
        scratch += [pltpu.VMEM((q_parts,) + two * (steps - 1 - s) + (high - low, 128), jnp.bfloat16) for s in range(steps)]
    scratch += [pltpu.VMEM(down_grads.shape, jnp.bfloat16)]
    scratch += [pltpu.VMEM((downs,) + two * (down_steps - 1 - s) + (d_rows, 128), jnp.bfloat16) for s in range(down_steps)]
    scratch += [pltpu.VMEM((steps, small_rows, width), jnp.float32)] * 2
    scratch += [pltpu.VMEM((steps, late_rows, 128), jnp.float32)] * 2
    scratch += [pltpu.VMEM((out_count, 2, o_rows, 128), jnp.float32), pltpu.VMEM((q_parts, 2, q_rows, 128), jnp.float32)]
    scratch += [pltpu.VMEM(tokens.shape, jnp.bfloat16), pltpu.VMEM(qkv_weight.shape, jnp.bfloat16)]
    scratch += [pltpu.VMEM(item.shape, jnp.bfloat16) for item in (grad_attended, mixed, out_weight)]
    sems = count * steps + (2 + q_parts * len(cuts) + len(s_cuts)) * steps + out_count
    scratch += [pltpu.SemaphoreType.DMA((sems,)), pltpu.SemaphoreType.DMA((sems,)), pltpu.SemaphoreType.DMA((ups + 6,))]
    return pl.pallas_call(
        kernel,
        grid=(grid,),
        in_specs=in_specs,
        out_specs=[pl.BlockSpec((token_block, width), lambda g: (jnp.clip(g - first_t, 0, token_steps - 1), 0))]
        + [whole(item.shape) for item in out_shape[1:]],
        out_shape=out_shape,
        scratch_shapes=scratch,
        compiler_params=pltpu.CompilerParams(collective_id=1, has_side_effects=True, vmem_limit_bytes=60 << 20),
        name="attention_backward",
    )(grad_attended, mixed, out_weight, queries, keys, values, attention, tokens, qkv_weight, up_grads, down_grads, sums)


def hand_out(grad_tokens, sums, late, narrow, classes, turned, *blocks):
    rows, width = grad_tokens.shape
    steps = 4
    first_dir = 6 + narrow

    def kernel(tokens_ref, sums_ref, late_ref, *refs):
        ins, outs = refs[: len(blocks)], refs[len(blocks) :]
        outs[0][...] = tokens_ref[...]

        @pl.when(pl.program_id(0) == 0)
        def _():
            for source, target in zip(ins, outs[1:]):
                target[...] = source[...] if source.shape == target.shape else source[...].T
            singles = outs[1 + len(blocks) :]
            for number in range(6):
                singles[number][...] = sums_ref[number, :]
            for number in range(2):
                for j in range(width // 128):
                    singles[6 + number][j * 128 : (j + 1) * 128] = late_ref[number * (width // 128) + j, :]
            for number in range(narrow):
                singles[8][number * width : (number + 1) * width] = sums_ref[6 + number, :]
            singles[9][...] = sums_ref[first_dir : first_dir + 2 * classes, :]
            singles[10][...] = sums_ref[first_dir + 2 * classes, :classes]

    def whole(shape):
        return pl.BlockSpec(shape, lambda g: (0,) * len(shape))

    some = pl.BlockSpec((rows // steps, width), lambda g: (g, 0))
    small = [(width,)] * 8 + [(narrow * width,), (2 * classes, width), (classes,)]
    shapes = [block.shape[::-1] if number in turned else block.shape for number, block in enumerate(blocks)]
    out_shape = [jax.ShapeDtypeStruct((rows, width), jnp.bfloat16)]
    out_shape += [jax.ShapeDtypeStruct(shape, jnp.float32) for shape in shapes + small]
    return pl.pallas_call(
        kernel,
        grid=(steps,),
        in_specs=[some] + [whole(item.shape) for item in (sums, late) + blocks],
        out_specs=[some] + [whole(item.shape) for item in out_shape[1:]],
        out_shape=out_shape,
        name="hand_out",
    )(grad_tokens, sums, late, *blocks)


def on_device_fast(
    tokens,
    doc_lengths,
    qkv_weight,
    query_bias,
    value_bias,
    out_weight,
    out_bias,
    first_gain,
    first_shift,
    up_weight,
    up_bias,
    down_weight,
    down_bias,
    second_gain,
    second_shift,
    dir_weight,
    dir_bias,
    segment_rows,
    segment_slots,
    pair_rows,
    pair_labels,
    out_cotangent,
):
    doc_count, length, model_width = tokens.shape
    token_rows = tokens.reshape(doc_count * length, model_width)
    singles = (out_bias, first_gain, first_shift, down_bias, second_gain, second_shift, query_bias, value_bias)
    vectors, queries, keys, values, attention, mixed = attention_forward(
        doc_lengths, token_rows, qkv_weight, singles + (dir_bias, up_bias)
    )
    hidden_low, normed_one, inverse_one, active, slope, normed_two, inverse_two, encoded_rows = ffn_forward(
        doc_lengths, mixed, token_rows, out_weight, vectors, up_weight, down_weight
    )
    classes_count = dir_weight.shape[1]
    grad_attended, up_blocks, down_blocks, sums = ffn_backward(
        doc_lengths, segment_rows, segment_slots, pair_rows[0].T, pair_labels, encoded_rows, out_cotangent.reshape(-1, model_width), dir_weight.T, vectors,
        normed_two, inverse_two, active, slope,
        hidden_low, down_weight, up_weight, normed_one, inverse_one,
    )
    grad_tokens, out_up, out_out, out_qkv, out_down, sums, late = attention_backward(
        grad_attended, mixed, out_weight, queries, keys, values, attention, token_rows, qkv_weight, up_blocks,
        down_blocks, sums,
    )
    grad_tokens, out_up, out_out, out_qkv, out_down, *smalls = hand_out(
        grad_tokens, sums, late, lax.axis_size("narrow"), classes_count, (1, 2), out_up, out_out, out_qkv, out_down
    )
    return (
        encoded_rows.reshape(tokens.shape),
        grad_tokens.reshape(tokens.shape),
        out_qkv,
        smalls[6],
        smalls[7],
        out_out,
        smalls[5],
        smalls[3],
        smalls[4],
        out_up,
        smalls[8],
        out_down.T,
        smalls[2],
        smalls[0],
        smalls[1],
        smalls[9].reshape(2, classes_count, model_width).transpose(0, 2, 1).reshape(2 * model_width, classes_count),
        smalls[10],
    )


def on_device(
    tokens,
    doc_lengths,
    qkv_weight,
    query_bias,
    value_bias,
    out_weight,
    out_bias,
    first_gain,
    first_shift,
    up_weight,
    up_bias,
    down_weight,
    down_bias,
    second_gain,
    second_shift,
    dir_weight,
    dir_bias,
    segment_rows,
    segment_slots,
    pair_rows,
    pair_labels,
    out_cotangent,
):
    doc_count, length, model_width = tokens.shape
    score_scale = HEAD_DIM ** (-0.5)
    token_rows = tokens.reshape(doc_count * length, model_width)
    allowed = lax.broadcasted_iota(jnp.int32, (doc_count, length), 1) < doc_lengths[:, None]
    allowed_rows = allowed.reshape(-1, 1).astype(jnp.float32)
    bias_row = jnp.concatenate([query_bias, jnp.zeros_like(query_bias), value_bias]).astype(
        jnp.float32
    )
    qkv = (jnp.dot(token_rows, qkv_weight, preferred_element_type=jnp.float32) + bias_row).astype(
        jnp.bfloat16
    )

    def split_heads(doc_block, which):
        return doc_block[:, which * model_width : (which + 1) * model_width].reshape(
            length, HEADS, HEAD_DIM
        )

    def scores_of(queries, key_rows, doc_mask):
        scores = (
            jnp.einsum("qhd,khd->hqk", queries, key_rows, preferred_element_type=jnp.float32)
            * score_scale
        )
        return jnp.where(doc_mask[None, None, :], scores, MASKED)

    mixed_parts = []
    log_totals = []
    for doc_index in range(doc_count):
        doc_block = qkv[doc_index * length : (doc_index + 1) * length]
        queries = split_heads(doc_block, 0)
        key_rows = split_heads(doc_block, 1)
        value_rows = split_heads(doc_block, 2)
        scores = scores_of(queries, key_rows, allowed[doc_index])
        highest = jnp.max(scores, -1, keepdims=True)
        powers = jnp.exp(scores - highest)
        summed = jnp.sum(powers, -1, keepdims=True)
        attention = (powers / summed).astype(jnp.bfloat16)
        log_totals.append(highest + jnp.log(summed))
        mixed_parts.append(
            jnp.einsum(
                "hqk,khd->qhd", attention, value_rows, preferred_element_type=jnp.float32
            ).reshape(length, model_width)
        )
    mixed = jnp.concatenate(mixed_parts).astype(jnp.bfloat16)
    attended = jnp.dot(mixed, out_weight, preferred_element_type=jnp.float32) + out_bias.astype(
        jnp.float32
    )
    resid_one = token_rows.astype(jnp.float32) + attended
    hidden_one, normed_one, inverse_one = norm_forward(
        resid_one, first_gain.astype(jnp.float32), first_shift.astype(jnp.float32)
    )
    hidden_low = hidden_one.astype(jnp.bfloat16)
    upper_pre = jnp.dot(hidden_low, up_weight, preferred_element_type=jnp.float32) + up_bias.astype(
        jnp.float32
    )
    cumulative = normal_cdf(upper_pre)
    active = (upper_pre * cumulative).astype(jnp.bfloat16)
    lowered = jnp.dot(active, down_weight, preferred_element_type=jnp.float32) + down_bias.astype(
        jnp.float32
    )
    resid_two = hidden_one + lowered
    second_float = second_gain.astype(jnp.float32)
    normed_out, normed_two, inverse_two = norm_forward(
        resid_two, second_float, second_shift.astype(jnp.float32)
    )
    encoded_rows = (normed_out * allowed_rows).astype(jnp.bfloat16)
    doc_starts = lax.broadcasted_iota(jnp.int32, (doc_count, 1), 0) * length
    picked_rows = (segment_rows + doc_starts).reshape(-1)
    picked = encoded_rows[picked_rows]
    slots = segment_slots.reshape(-1)
    outgoing = jnp.zeros_like(picked).at[slots].set(picked)
    arrived = lax.all_to_all(outgoing, "wide", split_axis=0, concat_axis=0, tiled=True)
    pairs = pair_rows.reshape(-1, 2)
    labels = pair_labels.reshape(-1)
    first_rows = arrived[pairs[:, 0]]
    second_rows = arrived[pairs[:, 1]]
    logits = (
        jnp.dot(first_rows, dir_weight[:model_width], preferred_element_type=jnp.float32)
        + jnp.dot(second_rows, dir_weight[model_width:], preferred_element_type=jnp.float32)
        + dir_bias.astype(jnp.float32)
    )
    powers_head = jnp.exp(logits - jnp.max(logits, -1, keepdims=True))
    chance = powers_head / jnp.sum(powers_head, -1, keepdims=True)
    classes = lax.broadcasted_iota(jnp.int32, logits.shape, 1)
    delta = chance - (labels[:, None] == classes).astype(jnp.float32)
    first_float = first_rows.astype(jnp.float32)
    second_rows_float = second_rows.astype(jnp.float32)
    grad_dir_weight = jnp.concatenate(
        [
            jnp.dot(first_float.T, delta, precision=EXACT, preferred_element_type=jnp.float32),
            jnp.dot(
                second_rows_float.T, delta, precision=EXACT, preferred_element_type=jnp.float32
            ),
        ]
    )
    grad_dir_bias = jnp.sum(delta, 0)
    dir_float = dir_weight.astype(jnp.float32)
    grad_first = jnp.dot(
        delta, dir_float[:model_width].T, precision=EXACT, preferred_element_type=jnp.float32
    )
    grad_second = jnp.dot(
        delta, dir_float[model_width:].T, precision=EXACT, preferred_element_type=jnp.float32
    )
    grad_arrived = jnp.zeros((arrived.shape[0], model_width), jnp.float32)
    grad_arrived = grad_arrived.at[pairs[:, 0]].add(grad_first).at[pairs[:, 1]].add(grad_second)
    returned = lax.all_to_all(
        grad_arrived.astype(jnp.bfloat16), "wide", split_axis=0, concat_axis=0, tiled=True
    )
    grad_picked = returned[slots].astype(jnp.float32)
    grad_encoded = (
        out_cotangent.reshape(-1, model_width).astype(jnp.float32).at[picked_rows].add(grad_picked)
    )
    grad_encoded = grad_encoded * allowed_rows
    grad_two, grad_second_gain, grad_second_shift = norm_backward(
        grad_encoded, normed_two, inverse_two, second_float
    )
    grad_lowered = grad_two.astype(jnp.bfloat16)
    grad_down_weight = jnp.einsum(
        "rf,rd->fd", active, grad_lowered, preferred_element_type=jnp.float32
    )
    grad_down_bias = jnp.sum(grad_lowered.astype(jnp.float32), 0)
    grad_active = jnp.einsum(
        "rd,fd->rf", grad_lowered, down_weight, preferred_element_type=jnp.float32
    )
    density = jnp.exp(-0.5 * upper_pre * upper_pre) * 0.3989422804014327
    grad_upper = (grad_active * (cumulative + upper_pre * density)).astype(jnp.bfloat16)
    grad_up_weight = jnp.einsum(
        "rd,rf->df", hidden_low, grad_upper, preferred_element_type=jnp.float32
    )
    grad_up_bias = jnp.sum(grad_upper.astype(jnp.float32), 0)
    grad_hidden = grad_two + jnp.einsum(
        "rf,df->rd", grad_upper, up_weight, preferred_element_type=jnp.float32
    )
    grad_one, grad_first_gain, grad_first_shift = norm_backward(
        grad_hidden, normed_one, inverse_one, first_gain.astype(jnp.float32)
    )
    grad_attended = grad_one.astype(jnp.bfloat16)
    grad_out_weight = jnp.einsum(
        "rd,re->de", mixed, grad_attended, preferred_element_type=jnp.float32
    )
    grad_out_bias = jnp.sum(grad_attended.astype(jnp.float32), 0)
    grad_mixed = jnp.einsum(
        "re,de->rd", grad_attended, out_weight, preferred_element_type=jnp.float32
    ).astype(jnp.bfloat16)
    grad_parts = []
    for doc_index in range(doc_count):
        doc_block = qkv[doc_index * length : (doc_index + 1) * length]
        queries = split_heads(doc_block, 0)
        key_rows = split_heads(doc_block, 1)
        value_rows = split_heads(doc_block, 2)
        scores = scores_of(queries, key_rows, allowed[doc_index])
        attention = jnp.exp(scores - log_totals[doc_index])
        grad_doc = grad_mixed[doc_index * length : (doc_index + 1) * length].reshape(
            length, HEADS, HEAD_DIM
        )
        grad_chance = jnp.einsum(
            "qhd,khd->hqk", grad_doc, value_rows, preferred_element_type=jnp.float32
        )
        inner = jnp.sum(grad_chance * attention, -1, keepdims=True)
        grad_scores = (attention * (grad_chance - inner)).astype(jnp.bfloat16)
        grad_query = (
            jnp.einsum("hqk,khd->qhd", grad_scores, key_rows, preferred_element_type=jnp.float32)
            * score_scale
        )
        grad_key = (
            jnp.einsum("hqk,qhd->khd", grad_scores, queries, preferred_element_type=jnp.float32)
            * score_scale
        )
        grad_value = jnp.einsum(
            "hqk,qhd->khd",
            attention.astype(jnp.bfloat16),
            grad_doc,
            preferred_element_type=jnp.float32,
        )
        grad_parts.append(
            jnp.concatenate(
                [
                    grad_query.reshape(length, model_width),
                    grad_key.reshape(length, model_width),
                    grad_value.reshape(length, model_width),
                ],
                axis=1,
            )
        )
    grad_qkv = jnp.concatenate(grad_parts).astype(jnp.bfloat16)
    grad_qkv_float = grad_qkv.astype(jnp.float32)
    grad_query_bias = jnp.sum(grad_qkv_float[:, :model_width], 0)
    grad_value_bias = jnp.sum(grad_qkv_float[:, 2 * model_width :], 0)
    grad_qkv_weight = jnp.einsum(
        "rd,re->de", token_rows, grad_qkv, preferred_element_type=jnp.float32
    )
    grad_tokens = (
        jnp.einsum("re,de->rd", grad_qkv, qkv_weight, preferred_element_type=jnp.float32) + grad_one
    ).astype(jnp.bfloat16)
    matrices = (grad_qkv_weight, grad_out_weight, grad_up_weight, grad_down_weight)
    partial_sums = (
        lax.psum_scatter(
            matrices[0].astype(jnp.bfloat16), "wide", scatter_dimension=1, tiled=True
        ).astype(jnp.float32),
        lax.psum_scatter(
            matrices[1].astype(jnp.bfloat16), "wide", scatter_dimension=1, tiled=True
        ).astype(jnp.float32),
        lax.psum_scatter(
            matrices[2].astype(jnp.bfloat16), "wide", scatter_dimension=1, tiled=True
        ).astype(jnp.float32),
        lax.psum_scatter(
            matrices[3].astype(jnp.bfloat16), "wide", scatter_dimension=1, tiled=True
        ).astype(jnp.float32),
    )
    summed_mats = (
        lax.psum_scatter(
            partial_sums[0].astype(jnp.bfloat16), "narrow", scatter_dimension=0, tiled=True
        ).astype(jnp.float32),
        lax.psum_scatter(
            partial_sums[1].astype(jnp.bfloat16), "narrow", scatter_dimension=0, tiled=True
        ).astype(jnp.float32),
        lax.psum_scatter(
            partial_sums[2].astype(jnp.bfloat16), "narrow", scatter_dimension=0, tiled=True
        ).astype(jnp.float32),
        lax.psum_scatter(
            partial_sums[3].astype(jnp.bfloat16), "narrow", scatter_dimension=0, tiled=True
        ).astype(jnp.float32),
    )
    smalls = lax.psum(
        (
            grad_query_bias,
            grad_value_bias,
            grad_out_bias,
            grad_first_gain,
            grad_first_shift,
            grad_up_bias,
            grad_down_bias,
            grad_second_gain,
            grad_second_shift,
            grad_dir_weight,
            grad_dir_bias,
        ),
        ("wide", "narrow"),
    )
    return (
        encoded_rows.reshape(tokens.shape),
        grad_tokens.reshape(tokens.shape),
        summed_mats[0],
        smalls[0],
        smalls[1],
        summed_mats[1],
        smalls[2],
        smalls[3],
        smalls[4],
        summed_mats[2],
        smalls[5],
        summed_mats[3],
        smalls[6],
        smalls[7],
        smalls[8],
        smalls[9],
        smalls[10],
    )


def fits_blocks(mesh):
    wide, narrow = mesh.shape["wide"], mesh.shape["narrow"]
    width, ff = HEADS * HEAD_DIM, 4 * HEADS * HEAD_DIM
    if wide != 2 * narrow or narrow < 4 or narrow & (narrow - 1):
        return False
    lanes = (ff // narrow, ff // wide, 2 * width // narrow)
    rows = (width // wide, width // narrow, width // wide // 2, 3 * width // wide // 2)
    return all(size % 128 == 0 for size in lanes) and all(size % 16 == 0 for size in rows)


def solution(mesh):
    placed = (
        P(("wide", "narrow"), None, None),
        P(("wide", "narrow")),
        P(),
        P(),
        P(),
        P(),
        P(),
        P(),
        P(),
        P(),
        P(),
        P(),
        P(),
        P(),
        P(),
        P(),
        P(),
        P(("wide", "narrow"), None),
        P(("wide", "narrow"), None),
        P(("wide", "narrow"), None, None),
        P(("wide", "narrow"), None),
        P(("wide", "narrow"), None, None),
    )
    return jax.shard_map(
        on_device_fast if fits_blocks(mesh) else on_device,
        mesh=mesh,
        in_specs=placed,
        out_specs=(
            P(("wide", "narrow"), None, None),
            P(("wide", "narrow"), None, None),
            P("narrow", "wide"),
            P(),
            P(),
            P("narrow", "wide"),
            P(),
            P(),
            P(),
            P("narrow", "wide"),
            P(),
            P("narrow", "wide"),
            P(),
            P(),
            P(),
            P(),
            P(),
        ),
        check_vma=False,
    )
```

```python
import jax
import jax.numpy as jnp
from jax import lax
from jax.experimental import pallas as pl
from jax.experimental.pallas import tpu as pltpu
from jax.sharding import PartitionSpec as P

HEADS = 12
HEAD_DIM = 64


EXACT = lax.Precision.HIGHEST
MASKED = -1e30
EPSILON = 1e-05


def norm_forward(values, gain, shift):
    center = jnp.mean(values, -1, keepdims=True)
    centered = values - center
    inverse = lax.rsqrt(jnp.mean(centered * centered, -1, keepdims=True) + EPSILON)
    normed = centered * inverse
    return (normed * gain + shift, normed, inverse)


def norm_backward(grad, normed, inverse, gain):
    scaled = grad * gain
    first_mean = jnp.mean(scaled, -1, keepdims=True)
    second_mean = jnp.mean(scaled * normed, -1, keepdims=True)
    return (
        (scaled - first_mean - normed * second_mean) * inverse,
        jnp.sum(grad * normed, 0),
        jnp.sum(grad, 0),
    )


def normal_cdf(values):
    return 0.5 * (1.0 + lax.erf(values * 0.7071067811865476))


MESH_ID = pl.DeviceIdType.MESH


def axis_bits():
    names = []
    for axis in ("wide", "narrow"):
        count = lax.axis_size(axis).bit_length() - 1
        names += [(axis, bit) for bit in reversed(range(count))]
    return names


class Place:
    def __init__(self):
        self.index = {axis: lax.axis_index(axis) for axis in ("wide", "narrow")}
        self.names = axis_bits()
        self.bit = {name: (self.index[name[0]] // (1 << name[1])) % 2 for name in self.names}

    def across(self, name):
        axis, bit = name
        target = dict(self.index)
        target[axis] = target[axis] + (1 << bit) - (2 << bit) * self.bit[name]
        return target

    def ahead(self, offset):
        target = dict(self.index)
        target["wide"] = (target["wide"] + offset) % lax.axis_size("wide")
        return target

    def greet(self, all_wide=False):
        barrier = pltpu.get_barrier_semaphore()
        targets = [self.across(name) for name in self.names if not (all_wide and name[0] == "wide")]
        if all_wide:
            targets += [self.ahead(offset) for offset in range(1, lax.axis_size("wide"))]
        for target in targets:
            pl.semaphore_signal(barrier, inc=1, device_id=target, device_id_type=MESH_ID)
        pl.semaphore_wait(barrier, len(targets))


class Halving:
    def __init__(self, place, names, order, source, own, received, send_sems, recv_sems, first_sem, tail=()):
        self.place, self.names, self.order = place, names, order
        self.source, self.own, self.received = source, own, received
        self.last = True
        self.send_sems, self.recv_sems, self.first_sem, self.tail = send_sems, recv_sems, first_sem, tail

    def region(self, step, mine):
        index = []
        for name in self.names:
            if name in self.order[:step]:
                index.append(self.place.bit[name])
            elif name == self.order[step]:
                index.append(self.place.bit[name] if mine else 1 - self.place.bit[name])
            else:
                index.append(slice(None))
        return tuple(index) + self.tail

    def copy(self, step):
        held = self.source if step == 0 else self.own
        return pltpu.make_async_remote_copy(
            src_ref=held.at[self.region(step, False)],
            dst_ref=self.received[step],
            send_sem=self.send_sems.at[self.first_sem + step],
            recv_sem=self.recv_sems.at[self.first_sem + step],
            device_id=self.place.across(self.order[step]),
            device_id_type=MESH_ID,
        )

    def send(self, step):
        self.copy(step).start()

    def add(self, step):
        self.copy(step).wait_recv()
        mine = self.region(step, True)
        if step + 1 < len(self.order) or not self.last:
            self.own[mine] = self.own[mine] + self.received[step][...]
            return None
        return self.own[mine].astype(jnp.float32) + self.received[step][...].astype(jnp.float32)

    def merge(self, step):
        self.last = False
        self.add(step)

    def close(self):
        for step in range(len(self.order)):
            self.copy(step).wait_send()


def link_orders():
    wide = [("wide", bit) for bit in range(lax.axis_size("wide").bit_length() - 1)]
    narrow = [("narrow", bit) for bit in range(1, lax.axis_size("narrow").bit_length() - 1)]
    core, x, near, far = [("narrow", 0)], wide[:1], wide[1:-1], wide[-1:]
    return [core + narrow + x + near + far, core + x + near + narrow + far, core + near + narrow + x + far]


def layer_forward(lengths, tokens, qkv_weight, out_weight, up_weight, down_weight, singles):
    rows, width = tokens.shape
    ff = up_weight.shape[1]
    docs = lengths.shape[0]
    length = rows // docs
    pairs, chunks = width // 128, ff // width
    kinds = [item.shape[0] for item in singles]
    lines = sum(max(1, size // width) for size in kinds)
    row_block = 256

    def kernel(lens, tok, wq, wk, wv, ow, up, down, *refs):
        singles, refs = refs[: len(kinds)], refs[len(kinds) :]
        vec, q_out, k_out, v_out, attention_out, mixed_out = refs[:6]
        hid_out, n1_out, q1_out, act_out, slope_out, n2_out, q2_out, enc_out = refs[6:14]
        mixed, hidden, total = refs[14:]
        pid = pl.program_id(0)

        def each_block(body):
            def step(i, carry):
                body(pl.multiple_of(i * row_block, row_block))
                return carry

            lax.fori_loop(0, rows // row_block, step, 0)

        @pl.when(pid == 0)
        def _():
            at = 0
            for single, size in zip(singles, kinds):
                values = single[...].astype(jnp.float32)
                for first in range(0, size, width):
                    some = min(size, width)
                    vec[at, :some] = values[first : first + some]
                    at += 1

        @pl.when(pid < pairs)
        def _():
            weights = jnp.concatenate([wq[...], wk[...], wv[...]], axis=1)
            at = pl.ds(pl.multiple_of(pid * 128, 128), 128)
            offsets = jnp.concatenate([vec[6:7, at], jnp.zeros((1, 128), jnp.float32), vec[7:8, at]], axis=1)
            qkv = (jnp.dot(tok[...], weights, preferred_element_type=jnp.float32) + offsets).astype(jnp.bfloat16)
            q_out[...] = qkv[:, :128]
            k_out[...] = qkv[:, 128:256]
            v_out[...] = qkv[:, 256:]
            first = lax.broadcasted_iota(jnp.int32, (1, 128), 1) < HEAD_DIM
            for doc in range(docs):
                some = slice(doc * length, (doc + 1) * length)
                queries = qkv[some, :128] * jnp.bfloat16(HEAD_DIM**-0.5)
                keys, values = qkv[some, 128:256], qkv[some, 256:]
                zero = jnp.zeros_like(queries)
                places = lax.broadcasted_iota(jnp.int32, (1, length), 1)
                bias = jnp.where(places < lens[doc], 0.0, MASKED)
                outs = []
                for head in range(2):
                    masked = jnp.where(first, queries, zero) if head == 0 else jnp.where(first, zero, queries)
                    scores = dot_last(masked, keys) + bias
                    powers = jnp.exp(scores - jnp.max(scores, -1, keepdims=True))
                    attention = (powers * (1.0 / jnp.sum(powers, -1, keepdims=True))).astype(jnp.bfloat16)
                    attention_out[doc, head] = attention
                    outs.append(jnp.dot(attention, values, preferred_element_type=jnp.float32))
                both = jnp.where(first, outs[0], outs[1]).astype(jnp.bfloat16)
                mixed_out[some, :] = both
                mixed[some, at] = both

        @pl.when(pid == pairs)
        def _():
            total[...] = jnp.dot(mixed[...], ow[...], preferred_element_type=jnp.float32)

            def body(at):
                some = pl.ds(at, row_block)
                summed = tok[some, :].astype(jnp.float32) + (total[some, :] + vec[0:1, :])
                out, normed, inverse = norm_forward(summed, vec[1:2, :], vec[2:3, :])
                hidden[some, :] = out
                hid_out[some, :] = out.astype(jnp.bfloat16)
                n1_out[some, :] = normed.astype(jnp.bfloat16)
                q1_out[some, :] = inverse
                total[some, :] = jnp.zeros_like(out)

            each_block(body)

        @pl.when(pid >= pairs)
        def _():
            offset = vec[pl.ds(pid - pairs + 9, 1), :]
            pre = jnp.dot(hid_out[...], up[...], preferred_element_type=jnp.float32) + offset
            cumulative = normal_cdf(pre)
            density = jnp.exp(-0.5 * pre * pre) * 0.3989422804014327
            active = (pre * cumulative).astype(jnp.bfloat16)
            act_out[...] = active
            slope_out[...] = (cumulative + pre * density).astype(jnp.bfloat16)
            total[...] += jnp.dot(active, down[...], preferred_element_type=jnp.float32)

        @pl.when(pid == pairs + chunks - 1)
        def _():
            def body(at):
                some = pl.ds(at, row_block)
                summed = hidden[some, :] + (total[some, :] + vec[3:4, :])
                out, normed, inverse = norm_forward(summed, vec[4:5, :], vec[5:6, :])
                n2_out[some, :] = normed.astype(jnp.bfloat16)
                q2_out[some, :] = inverse
                doc = at // length
                line = lax.broadcasted_iota(jnp.int32, (row_block, 1), 0) + (at - doc * length)
                enc_out[some, :] = jnp.where(line < lens[doc], out, 0.0).astype(jnp.bfloat16)

            each_block(body)

    def whole(shape):
        return pl.BlockSpec(shape, lambda g: (0,) * len(shape), pipeline_mode=pl.Buffered(1))

    def pair_of(g):
        return jnp.minimum(g, pairs - 1)

    def chunk_of(g):
        return jnp.clip(g - pairs, 0, chunks - 1)

    column = pl.BlockSpec((rows, 128), lambda g: (0, pair_of(g)))
    upper = pl.BlockSpec((rows, width), lambda g: (0, chunk_of(g)))
    full, one = whole((rows, width)), whole((rows, 1))
    in_specs = [pl.BlockSpec(memory_space=pltpu.SMEM), full]
    in_specs += [pl.BlockSpec((width, 128), lambda g, n=n: (0, n * pairs + pair_of(g))) for n in range(3)]
    in_specs += [whole((width, width)), pl.BlockSpec((width, width), lambda g: (0, chunk_of(g)))]
    in_specs += [pl.BlockSpec((width, width), lambda g: (chunk_of(g), 0))]
    in_specs += [whole(item.shape) for item in singles]
    low = jax.ShapeDtypeStruct((rows, width), jnp.bfloat16)
    inverse = jax.ShapeDtypeStruct((rows, 1), jnp.float32)
    high = jax.ShapeDtypeStruct((rows, ff), jnp.bfloat16)
    return pl.pallas_call(
        kernel,
        grid=(pairs + chunks,),
        in_specs=in_specs,
        out_specs=[whole((lines, width))] + [column] * 3
        + [pl.BlockSpec((docs, 2, length, length), lambda g: (0, pair_of(g), 0, 0)), column]
        + [full, full, one, upper, upper, full, one, full],
        out_shape=[jax.ShapeDtypeStruct((lines, width), jnp.float32)] + [low] * 3
        + [jax.ShapeDtypeStruct((docs, 2 * pairs, length, length), jnp.bfloat16), low]
        + [low, low, inverse, high, high, low, inverse, low],
        scratch_shapes=[pltpu.VMEM((rows, width), jnp.bfloat16)] + [pltpu.VMEM((rows, width), jnp.float32)] * 2,
        compiler_params=pltpu.CompilerParams(vmem_limit_bytes=60 << 20),
        name="layer_forward",
    )(lengths, tokens, qkv_weight, qkv_weight, qkv_weight, out_weight, up_weight, down_weight, *singles)


def dot_last(left, right):
    return lax.dot_general(left, right, (((1,), (1,)), ((), ())), preferred_element_type=jnp.float32)


def norm_back_rows(grad, normed, inverse, gain):
    scaled = grad * gain
    first = jnp.mean(scaled, -1, keepdims=True)
    second = jnp.mean(scaled * normed, -1, keepdims=True)
    return (scaled - first - normed * second) * inverse


def parts_of(values, count):
    terms = []
    for _ in range(count):
        term = values.astype(jnp.bfloat16).astype(jnp.float32)
        terms.append(term)
        values = values - term
    return jnp.concatenate(terms).astype(jnp.bfloat16)


def one_hot(row, count):
    lines = lax.broadcasted_iota(jnp.int32, (count, row.shape[1]), 0)
    return jnp.where(lines == row, 1.0, 0.0).astype(jnp.bfloat16)


def ffn_backward(lengths, segment_rows, segment_slots, pair_rows, pair_labels, encoded, cotangent, dir_t, vectors, normed_two, inverse_two, active, slope, hidden_low, down_weight, up_weight,
                 normed_one, inverse_one):
    rows, width = hidden_low.shape
    ff = active.shape[1]
    segments, classes = segment_slots.shape[1], dir_t.shape[0]
    numbers = (segment_rows, segment_slots, pair_rows, pair_labels)
    length = rows // lengths.shape[0]
    names = axis_bits()
    steps = len(names)
    wide, narrow = lax.axis_size("wide"), lax.axis_size("narrow")
    wide_bits, narrow_bits = wide.bit_length() - 1, narrow.bit_length() - 1
    chunks = ff // narrow // 128
    third = chunks // 2
    d_rows, u_rows = width // wide, width // narrow
    row_block = 256
    row_steps = rows // row_block
    orders = link_orders()
    two = (2,)
    early = 3
    first_dir = 6 + narrow
    sum_rows = pl.cdiv(first_dir + 2 * classes + 1, 16) * 16

    def chunk_of(step):
        step = jnp.clip(step, 0, chunks - 1)
        return step // 2 + third * (step % 2)

    def bits_of(number, count):
        return tuple((number >> bit) & 1 for bit in reversed(range(count)))

    def kernel(*refs):
        lens, seg_rows, seg_slots, pair_nums, labels, enc, cot, dir_ref = refs[:8]
        refs = refs[8:]
        q2, q1, vec = refs[:3]
        far = refs[3:9]
        slo = refs[9 : 9 + narrow]
        rest = list(refs[9 + narrow :])
        ga_out, up_out, down_out, sums_out = rest[:4]
        rest = rest[4:]
        grad_hidden, lowered, lowered_t, hidden_t, own, up_own, up_received = rest[:7]
        received = rest[7 : 7 + early]
        rest = rest[7 + early :]
        select, picked, dir_w, leaving, arrived, leaving_grads, arrived_grads = rest[:7]
        near = rest[7:13]
        n2, hidden, act, dws, uws, n1 = near
        send_sems, recv_sems, local_sems = rest[13:]
        loads = [pltpu.make_async_copy(far[i], near[i], local_sems.at[2 * chunks + i]) for i in range(len(near))]
        pid = pl.program_id(0)
        place = Place()
        pieces = []
        for number in range(chunks):
            pieces.append(
                Halving(place, names, orders[number % 3][:early], own.at[number], own.at[number],
                        [r.at[number] for r in received], send_sems, recv_sems, number * early)
            )
        core = ("narrow", 0)
        up_names = [name for name in names if name != ("wide", 0)]
        up_pieces = [
            Halving(place, up_names, [core], up_own.at[number], up_own.at[number], [up_received.at[number]],
                    send_sems, recv_sems, chunks * early + number)
            for number in range(chunks)
        ]

        def up_write(number):
            mine = up_pieces[number].region(0, True)
            return pltpu.make_async_copy(
                up_own.at[number].at[mine],
                up_out.at[(number // 2,) + (slice(None),) * (wide_bits - 1) + (number % 2,)],
                local_sems.at[number],
            )

        def exchange(source, landing, first, meanwhile=None):
            made = []
            for offset in range(1, wide):
                target = place.ahead(offset)
                made.append(pltpu.make_async_remote_copy(
                    src_ref=source.at[target["wide"]], dst_ref=landing.at[place.index["wide"]],
                    send_sem=send_sems.at[first + offset - 1], recv_sem=recv_sems.at[first + offset - 1],
                    device_id=target, device_id_type=MESH_ID))
            me = place.index["wide"]
            for copy in made:
                copy.start()
            landing[me] = source[me]
            if meanwhile:
                meanwhile()
            for copy in made:
                copy.wait()
            return landing[...].reshape(segments, 128)

        def turn_hidden():
            def body(i, carry):
                some = pl.ds(pl.multiple_of(i * row_block, row_block), row_block)
                hidden_t[:, some] = hidden[some, :].T
                return carry

            loads[1].wait()
            lax.fori_loop(0, row_steps, body, 0)

        @pl.when(pid == 0)
        def _():
            for load in loads:
                load.start()
            place.greet(all_wide=True)
            sums_out[...] = jnp.zeros_like(sums_out)
            base = chunks * early + chunks
            docs = rows // length
            places = jnp.concatenate([seg_rows[doc : doc + 1, :] + doc * length for doc in range(docs)], axis=1)
            select[...] = dot_last(one_hot(places, rows), one_hot(seg_slots[...], segments)).astype(jnp.bfloat16)
            picked[...] = jnp.dot(select[...].T, enc[...], preferred_element_type=jnp.float32).astype(jnp.bfloat16)
            halves = [dir_ref[:, n * width : (n + 1) * width].astype(jnp.float32) for n in range(2)]
            blank = jnp.zeros((128 - 2 * classes, width), jnp.float32)
            dir_w[...] = jnp.concatenate(halves + [blank]).astype(jnp.bfloat16)
            leaving[...] = dot_last(picked[...], dir_w[...]).reshape(leaving.shape)
            scores = exchange(leaving, arrived, base, turn_hidden).T
            pair_first, pair_second = one_hot(pair_nums[0:1, :], segments), one_hot(pair_nums[1:2, :], segments)

            def chosen(values, pairs):
                split = jnp.dot(parts_of(values, 3), pairs, preferred_element_type=jnp.float32)
                return split[:classes] + split[classes : 2 * classes] + split[2 * classes :]

            logits = chosen(scores[:classes], pair_first) + chosen(scores[classes : 2 * classes], pair_second)
            logits = logits + jnp.broadcast_to(vec[8:9, :128], (128, 128)).T[:classes, 0:1]
            powers = jnp.exp(logits - jnp.max(logits, 0, keepdims=True))
            chance = powers / jnp.sum(powers, 0, keepdims=True)
            kinds = lax.broadcasted_iota(jnp.int32, logits.shape, 0)
            delta = chance - jnp.where(kinds == labels[...], 1.0, 0.0)
            split = parts_of(delta, 2)
            gathered = []
            for pairs in (pair_first, pair_second):
                both = dot_last(split, pairs)
                gathered.append(both[:classes] + both[classes:])
            gathered.append(jnp.zeros((128 - 2 * classes, segments), jnp.float32))
            leaving_grads[...] = jnp.concatenate(gathered).T.reshape(leaving.shape)
            square = (classes, 128)
            matching = lax.broadcasted_iota(jnp.int32, square, 0) == lax.broadcasted_iota(jnp.int32, square, 1)
            biases = jnp.where(matching, jnp.sum(delta, 1, keepdims=True), 0.0)
            sums_out[first_dir + 2 * classes : first_dir + 2 * classes + 1, :128] = jnp.sum(biases, 0, keepdims=True)
            back = exchange(leaving_grads, arrived_grads, base + wide - 1)
            coarse = back.astype(jnp.bfloat16)
            fine = (back - coarse.astype(jnp.float32)).astype(jnp.bfloat16)
            grads_in = (
                jnp.dot(coarse, dir_w[...], preferred_element_type=jnp.float32)
                + jnp.dot(fine, dir_w[...], preferred_element_type=jnp.float32)
            ).astype(jnp.bfloat16)
            back_t = back.T[: 2 * classes]
            both = jnp.dot(parts_of(back_t, 2), picked[...], preferred_element_type=jnp.float32)
            sums_out[first_dir : first_dir + 2 * classes, :] = both[: 2 * classes] + both[2 * classes :]
            loads[0].wait()

            def body(i, carry):
                at = pl.multiple_of(i * row_block, row_block)
                some = pl.ds(at, row_block)
                normed = n2[some, :].astype(jnp.float32)
                doc = at // length
                line = lax.broadcasted_iota(jnp.int32, (row_block, 1), 0) + (at - doc * length)
                grad = cot[some, :].astype(jnp.float32) + jnp.dot(
                    select[some, :], grads_in, preferred_element_type=jnp.float32
                )
                grad = jnp.where(line < lens[doc], grad, 0.0)
                two = norm_back_rows(grad, normed, q2[some, :], vec[4:5, :])
                low = two.astype(jnp.bfloat16)
                grad_hidden[some, :] = two
                lowered[some, :] = low
                lowered_t[:, some] = low.T
                sums_out[0:1, :] += jnp.sum(grad * normed, 0, keepdims=True)
                sums_out[1:2, :] += jnp.sum(grad, 0, keepdims=True)
                sums_out[2:3, :] += jnp.sum(low.astype(jnp.float32), 0, keepdims=True)
                return carry

            lax.fori_loop(0, row_steps, body, 0)

        def slab(n, step):
            return pl.ds(pl.multiple_of((n * chunks + chunk_of(step)) * 128, 128), 128)

        @pl.when(pid == 0)
        def _():
            loads[2].wait()

        @pl.when(pid < chunks)
        def _():
            actives = jnp.concatenate([act[:, slab(n, pid)] for n in range(narrow)], axis=1)
            result = jnp.dot(lowered_t[...], actives, preferred_element_type=jnp.float32).astype(jnp.bfloat16)
            for w in range(wide):
                for n in range(narrow):
                    own[(pid,) + bits_of(w, wide_bits) + bits_of(n, narrow_bits)] = result[
                        w * d_rows : (w + 1) * d_rows, n * 128 : (n + 1) * 128
                    ]

        @pl.when(pid == chunks)
        def _():
            for load in loads[3:]:
                load.wait()

        @pl.when(pid >= chunks)
        def _():
            slopes = jnp.concatenate([ref[...] for ref in slo], axis=1)
            downs = jnp.concatenate([dws[slab(n, pid - chunks), :] for n in range(narrow)], axis=0)
            ups = jnp.concatenate([uws[:, slab(n, pid - chunks)] for n in range(narrow)], axis=1)
            grad_active = dot_last(lowered[...], downs)
            grad_upper = (grad_active * slopes.astype(jnp.float32)).astype(jnp.bfloat16)
            totals = jnp.sum(grad_upper.astype(jnp.float32), 0, keepdims=True)
            at = pl.ds(pl.multiple_of(chunk_of(pid - chunks) * 128, 128), 128)
            for n in range(narrow):
                sums_out[6 + n : 7 + n, at] = totals[:, n * 128 : (n + 1) * 128]
            result = jnp.dot(hidden_t[...], grad_upper, preferred_element_type=jnp.float32).astype(jnp.bfloat16)
            for n in range(narrow):
                for z in range(narrow):
                    high = bits_of(z, wide_bits - 1)
                    up_own[(pid - chunks,) + high + bits_of(n, narrow_bits)] = result[
                        n * u_rows : (n + 1) * u_rows, z * 128 : (z + 1) * 128
                    ]
            grad_hidden[...] += dot_last(grad_upper, ups)

        def down_write(number):
            return pltpu.make_async_copy(
                own.at[number].at[pieces[number].region(early - 1, True)], down_out.at[number], local_sems.at[chunks + number]
            )

        def advance(number, step):
            pieces[number].merge(step)
            if step + 1 < early:
                pieces[number].send(step + 1)
            else:
                down_write(number).start()

        for number in range(chunks):
            @pl.when(pid == chunks + number)
            def _():
                up_pieces[number].send(0)

        @pl.when(pid == 2 * chunks - 1)
        def _():
            def body(i, carry):
                at = pl.multiple_of(i * row_block, row_block)
                some = pl.ds(at, row_block)
                grad, normed = grad_hidden[some, :], n1[some, :].astype(jnp.float32)
                low = norm_back_rows(grad, normed, q1[some, :], vec[1:2, :]).astype(jnp.bfloat16)
                ga_out[some, :] = low
                sums_out[3:4, :] += jnp.sum(grad * normed, 0, keepdims=True)
                sums_out[4:5, :] += jnp.sum(grad, 0, keepdims=True)
                sums_out[5:6, :] += jnp.sum(low.astype(jnp.float32), 0, keepdims=True)
                return carry

            lax.fori_loop(0, row_steps, body, 0)

        plan = {}
        for number in range(chunks):
            for step in range(early):
                at = (number + 2, chunks + 1 + 2 * (number // 3), chunks + 4 + number // 3)[step]
                plan.setdefault(min(at, 2 * chunks - 1), []).append((step, number))
        for at in range(2 * chunks):
            @pl.when(pid == at)
            def _():
                if at < chunks:
                    pieces[at].send(0)
                if at > chunks:
                    up_pieces[at - chunks - 1].merge(0)
                    up_write(at - chunks - 1).start()
                for step, number in sorted(plan.get(at, [])):
                    advance(number, step)
                if at == 2 * chunks - 1:
                    up_pieces[chunks - 1].merge(0)
                    up_write(chunks - 1).start()
                    for number in range(chunks):
                        up_write(number).wait()
                        down_write(number).wait()
                    for item in pieces + up_pieces:
                        item.close()

    def whole(shape):
        return pl.BlockSpec(shape, lambda g: (0,) * len(shape), pipeline_mode=pl.Buffered(1))

    def slab_columns(shape, first):
        return [pl.BlockSpec(shape, lambda g, n=n: (0, n * chunks + chunk_of(g - first))) for n in range(narrow)]

    in_specs = [pl.BlockSpec(memory_space=pltpu.SMEM), *[whole(item.shape) for item in numbers],
                whole((rows, width)), whole((rows, width))]
    in_specs += [whole(dir_t.shape)]
    in_specs += [whole((rows, 1))] * 2 + [whole(vectors.shape)] + [pl.BlockSpec(memory_space=pl.ANY)] * 6
    in_specs += slab_columns((rows, 128), chunks)
    high = two * (wide_bits - 1)
    low = two * narrow_bits
    up_shape = (third,) + high + (2,) + low[1:] + (u_rows, 128)
    out_specs = [
        whole((rows, width)),
        pl.BlockSpec(memory_space=pl.ANY),
        pl.BlockSpec(memory_space=pl.ANY),
        whole((sum_rows, width)),
    ]
    out_shape = [
        jax.ShapeDtypeStruct((rows, width), jnp.bfloat16),
        jax.ShapeDtypeStruct(up_shape, jnp.bfloat16),
        jax.ShapeDtypeStruct((chunks,) + two * (steps - early) + (d_rows, 128), jnp.bfloat16),
        jax.ShapeDtypeStruct((sum_rows, width), jnp.float32),
    ]
    scratch = [
        pltpu.VMEM((rows, width), jnp.float32),
        pltpu.VMEM((rows, width), jnp.bfloat16),
        pltpu.VMEM((width, rows), jnp.bfloat16),
        pltpu.VMEM((width, rows), jnp.bfloat16),
        pltpu.VMEM((chunks,) + two * steps + (d_rows, 128), jnp.bfloat16),
        pltpu.VMEM((chunks,) + high + low + (u_rows, 128), jnp.bfloat16),
        pltpu.VMEM((chunks,) + high + low[1:] + (u_rows, 128), jnp.bfloat16),
    ]
    scratch += [pltpu.VMEM((chunks,) + two * (steps - 1 - s) + (d_rows, 128), jnp.bfloat16) for s in range(early)]
    scratch += [pltpu.VMEM((rows, segments), jnp.bfloat16), pltpu.VMEM((segments, width), jnp.bfloat16)]
    scratch += [pltpu.VMEM((128, width), jnp.bfloat16)]
    scratch += [pltpu.VMEM((wide, segments // wide, 128), jnp.float32)] * 4
    far = (normed_two, hidden_low, active, down_weight, up_weight, normed_one)
    scratch += [pltpu.VMEM(item.shape, item.dtype) for item in far]
    sems = chunks * early + chunks + 2 * (wide - 1)
    scratch += [pltpu.SemaphoreType.DMA((sems,)), pltpu.SemaphoreType.DMA((sems,)), pltpu.SemaphoreType.DMA((2 * chunks + len(far),))]
    return pl.pallas_call(
        kernel,
        grid=(2 * chunks,),
        in_specs=in_specs,
        out_specs=out_specs,
        out_shape=out_shape,
        scratch_shapes=scratch,
        compiler_params=pltpu.CompilerParams(collective_id=0, has_side_effects=True, vmem_limit_bytes=60 << 20),
        name="ffn_backward",
    )(lengths, *numbers, encoded, cotangent, dir_t, inverse_two, inverse_one, vectors,
      *far, *([slope] * narrow))


def attention_backward(grad_attended, mixed, out_weight, queries, keys, values, attention, tokens, qkv_weight, up_grads,
                       down_grads, sums):
    rows, width = tokens.shape
    docs, _, length, _ = attention.shape
    pairs = width // 128
    names = axis_bits()
    steps = len(names)
    wide, narrow = lax.axis_size("wide"), lax.axis_size("narrow")
    wide_bits, narrow_bits = wide.bit_length() - 1, narrow.bit_length() - 1
    half = narrow // 2
    half_bits = narrow_bits - 1
    lanes = width // half
    q_rows, o_rows = 3 * width // wide // 2, width // wide // 2
    q_parts = lanes // 128
    orders = link_orders()
    ups = up_grads.shape[0]
    u_rows = up_grads.shape[-2]
    attn_steps = docs * pairs
    token_block = 256
    token_steps = rows // token_block
    first_q = 1 + attn_steps
    first_t = first_q + q_parts
    grid = first_t + token_steps
    downs, d_rows = down_grads.shape[0], down_grads.shape[-2]
    down_steps = len(down_grads.shape) - 3
    cuts = [(0, q_rows // 32 * 16), (q_rows // 32 * 16, q_rows)]
    u_cuts = [(0, u_rows // 2), (u_rows // 2, u_rows)]
    up_count, out_count = ups * len(u_cuts), q_parts
    first_part = up_count + out_count
    first_down = first_part + q_parts * len(cuts)
    count = first_down + downs
    small_rows = sums.shape[0]
    late_rows = pl.cdiv(2 * pairs, 8) * 8
    s_cuts = [(0, small_rows // 4), (small_rows // 4, small_rows // 2), (small_rows // 2, small_rows)]

    def bits_of(number, count):
        return tuple((number >> bit) & 1 for bit in reversed(range(count)))

    def kernel(*refs):
        (ga_hbm, mix_hbm, ow_hbm, q_ref, k_ref, v_ref, att_ref, tok_hbm, qw_hbm, up_hbm, down_hbm, small) = refs[:12]
        tokens_out, up_out, out_out, qkv_out, down_out, small_out, late_out = refs[12:19]
        rest = list(refs[19:])
        gm, mix_pair, gqkv_t, up_own, out_own, qkv_own = rest[:6]
        rest = rest[6:]
        up_received = [rest[i * (steps - 1) : (i + 1) * (steps - 1)] for i in range(len(u_cuts))]
        rest = rest[len(u_cuts) * (steps - 1) :]
        out_received, rest = rest[:steps], rest[steps:]
        qkv_received, rest = [rest[i * steps : (i + 1) * steps] for i in range(len(cuts))], rest[len(cuts) * steps :]
        down_own, down_received, rest = rest[0], rest[1 : 1 + down_steps], rest[1 + down_steps :]
        small_sent, small_received, late_sent, late_received, swap_out, swap_qkv, tok, qw, ga, mix, ow = rest[:11]
        send_sems, recv_sems, local_sems = rest[11:]
        pid = pl.program_id(0)
        place = Place()
        core = place.bit["narrow", 0]
        pieces = []
        for low, high in u_cuts:
            for part in range(ups):
                cut = len(pieces) // ups
                pieces.append(Halving(place, names[:-1], orders[part % 3][1:], up_hbm.at[part], up_own.at[part],
                                      [r.at[part] for r in up_received[cut]], send_sems, recv_sems, len(pieces) * steps,
                                      (slice(low, high), slice(None))))
        for part in range(out_count):
            pieces.append(Halving(place, names, orders[part % 3], out_own.at[part], out_own.at[part],
                                  [r.at[part] for r in out_received], send_sems, recv_sems, len(pieces) * steps))
        for part in range(q_parts):
            for cut, (low, high) in enumerate(cuts):
                pieces.append(Halving(place, names, orders[part % 3], qkv_own.at[part], qkv_own.at[part],
                                      [r.at[part] for r in qkv_received[cut]], send_sems, recv_sems, len(pieces) * steps,
                                      (slice(low, high), slice(None))))
        for number in range(downs):
            order = orders[number % 3][steps - down_steps :]
            pieces.append(Halving(place, [name for name in names if name in order], order, down_own.at[number],
                                  down_own.at[number], [r.at[number] for r in down_received], send_sems, recv_sems,
                                  len(pieces) * steps))
        base = count * steps

        def all_sum(sent, received, first, order=0, rows=slice(None)):
            made = []
            for step in range(steps):
                made.append(pltpu.make_async_remote_copy(
                    src_ref=sent.at[step, rows], dst_ref=received.at[step, rows], send_sem=send_sems.at[first + step],
                    recv_sem=recv_sems.at[first + step], device_id=place.across(orders[order][step]),
                    device_id_type=MESH_ID))
            return made

        small_copies = [
            all_sum(small_sent, small_received, base + (2 + q_parts * len(cuts) + i) * steps + out_count, i, slice(low, high))
            for i, (low, high) in enumerate(s_cuts)
        ]
        late_copies = [all_sum(late_sent, late_received, base + steps)]
        swap_refs = [swap_out.at[part, core] for part in range(out_count)]
        swap_refs += [swap_qkv.at[part, core, low:high] for part in range(q_parts) for low, high in cuts]
        swaps = [pltpu.make_async_remote_copy(
            src_ref=ref, dst_ref=ref, send_sem=send_sems.at[base + 2 * steps + slot],
            recv_sem=recv_sems.at[base + 2 * steps + slot], device_id=place.across(("narrow", 0)),
            device_id_type=MESH_ID) for slot, ref in enumerate(swap_refs)]
        local = []
        for number in range(ups):
            keep = pieces[number].region(0, True)[: -2]
            local.append(pltpu.make_async_copy(up_hbm.at[number].at[keep], up_own.at[number].at[keep], local_sems.at[number]))

        loads = [pltpu.make_async_copy(tok_hbm, tok, local_sems.at[ups]),
                 pltpu.make_async_copy(qw_hbm, qw, local_sems.at[ups + 1])]
        first_loads = [pltpu.make_async_copy(source, target, local_sems.at[ups + 3 + i])
                       for i, (source, target) in enumerate(((ga_hbm, ga), (mix_hbm, mix), (ow_hbm, ow)))]
        down_load = pltpu.make_async_copy(down_hbm, down_own, local_sems.at[ups + 2])

        def advance(number, step):
            item = pieces[number]
            if step == 0 and number < ups:
                local[number].wait()
            total = item.add(step)
            if total is None:
                item.send(step + 1)
            elif number < up_count:
                cut, part = divmod(number, ups)
                up_out[u_cuts[cut][0] : u_cuts[cut][1], part * 128 : (part + 1) * 128] = total
            elif number >= first_down:
                number -= first_down
                j = number // 2 + downs // 2 * (number % 2)
                down_out[:, j * 128 : (j + 1) * 128] = total
            else:
                if number < first_part:
                    swap_out[number - up_count, core] = total
                else:
                    part, cut = divmod(number - first_part, len(cuts))
                    swap_qkv[part, core, cuts[cut][0] : cuts[cut][1]] = total
                swaps[number - up_count].start()

        def advance_small(lanes, sent, received, out, step):
            for copies in lanes:
                copies[step].wait_recv()
            total = sent[step] + received[step]
            if step + 1 < steps:
                sent[step + 1] = total
                for copies in lanes:
                    copies[step + 1].start()
            else:
                out[...] = total

        @pl.when(pid == 0)
        def _():
            place.greet()
            for number in range(up_count):
                pieces[number].send(0)
            for number in range(ups):
                local[number].start()
            for load in first_loads:
                load.start()
            small_sent[0] = small[...]
            for copies in small_copies:
                copies[0].start()
            down_load.start()
            for load in loads:
                load.start()
            for load in first_loads:
                load.wait()
            grads_t = ga[...].T
            result = jnp.dot(grads_t, mix[...], preferred_element_type=jnp.float32).astype(jnp.bfloat16)
            for w in range(wide):
                for h in range(2):
                    for y in range(half):
                        at = (w * 2 + h) * o_rows
                        for part in range(out_count):
                            first = y * lanes + part * 128
                            out_own[(part,) + bits_of(w, wide_bits) + bits_of(y, half_bits) + (h,)] = result[
                                at : at + o_rows, first : first + 128
                            ]
            for part in range(out_count):
                pieces[up_count + part].send(0)
            grad_mixed = dot_last(ga[...], ow[...]).astype(jnp.bfloat16)
            for pair in range(pairs):
                gm[pair] = grad_mixed[:, pair * 128 : (pair + 1) * 128]
                mix_pair[pair] = mix[:, pair * 128 : (pair + 1) * 128]
            down_load.wait()
            for number in range(downs):
                pieces[first_down + number].send(0)

        @pl.when((pid >= 1) & (pid < first_q))
        def _():
            number = pid - 1
            pair, doc = number // docs, number % docs
            some = pl.ds(pl.multiple_of(doc * length, length), length)
            lane = lax.broadcasted_iota(jnp.int32, (1, 128), 1)
            scaled, keys, values = q_ref[...] * jnp.bfloat16(HEAD_DIM**-0.5), k_ref[...], v_ref[...]
            grads = gm[pair, some, :]
            product = grads.astype(jnp.float32) * mix_pair[pair, some, :].astype(jnp.float32)
            queries_t, grads_t = scaled.T, grads.T
            zero = jnp.zeros_like(grads)
            query_parts = []
            for head in range(2):
                inside = (lane // HEAD_DIM) == head
                at = head * HEAD_DIM
                attention = att_ref[0, head]
                chance = dot_last(jnp.where(inside, grads, zero), values)
                inner = jnp.sum(jnp.where(inside, product, 0.0), -1, keepdims=True)
                grad_scores = (attention.astype(jnp.float32) * (chance - inner)).astype(jnp.bfloat16)
                query_parts.append(jnp.dot(grad_scores, keys, preferred_element_type=jnp.float32))
                key_t = jnp.dot(queries_t[at : at + HEAD_DIM], grad_scores, preferred_element_type=jnp.float32)
                value_t = jnp.dot(grads_t[at : at + HEAD_DIM], attention, preferred_element_type=jnp.float32)
                row = pair * 128 + at
                gqkv_t[pl.ds(pl.multiple_of(width + row, HEAD_DIM), HEAD_DIM), some] = key_t.astype(jnp.bfloat16)
                gqkv_t[pl.ds(pl.multiple_of(2 * width + row, HEAD_DIM), HEAD_DIM), some] = value_t.astype(jnp.bfloat16)
            grad_query = jnp.where(lane < HEAD_DIM, query_parts[0], query_parts[1]) * HEAD_DIM**-0.5
            gqkv_t[pl.ds(pl.multiple_of(pair * 128, 128), 128), some] = grad_query.astype(jnp.bfloat16).T

        for part in range(q_parts):
            @pl.when(pid == first_q + part)
            def _():
                if part == 0:
                    for load in loads:
                        load.wait()
                    ones = jnp.ones((8, rows), jnp.bfloat16)
                    for which in range(2):
                        totals = dot_last(ones, gqkv_t[2 * which * width : (2 * which + 1) * width, :])
                        for j in range(pairs):
                            late_sent[0, which * pairs + j : which * pairs + j + 1, :] = totals[
                                :1, j * 128 : (j + 1) * 128
                            ]
                    late_sent[0, 2 * pairs :, :] = jnp.zeros((late_rows - 2 * pairs, 128), jnp.float32)
                    late_copies[0][0].start()
                columns = jnp.concatenate(
                    [tok[:, y * lanes + part * 128 : y * lanes + (part + 1) * 128] for y in range(half)], axis=1
                )
                result = jnp.dot(gqkv_t[...], columns, preferred_element_type=jnp.float32).astype(jnp.bfloat16)
                for w in range(wide):
                    for h in range(2):
                        for y in range(half):
                            at = (w * 2 + h) * q_rows
                            qkv_own[(part,) + bits_of(w, wide_bits) + bits_of(y, half_bits) + (h,)] = result[
                                at : at + q_rows, y * 128 : (y + 1) * 128
                            ]
                for cut in range(len(cuts)):
                    pieces[first_part + part * len(cuts) + cut].send(0)

        @pl.when(pid >= first_t)
        def _():
            at = pl.multiple_of((pid - first_t) * token_block, token_block)
            some = pl.ds(at, token_block)
            grad_t = jnp.dot(qw[...], gqkv_t[:, some], preferred_element_type=jnp.float32)
            tokens_out[...] = (grad_t.T + ga[some, :].astype(jnp.float32)).astype(jnp.bfloat16)

        plan, small_plan, late_plan = {}, {}, {}
        for cut, times in enumerate(((5, 9, 12, 14), (8, 10, 13, 15))):
            for step, at in enumerate(times):
                for part in range(ups):
                    plan.setdefault(at, []).append((cut * ups + part, step))
        for step, at in enumerate((1, 9, 12, 14, 15)):
            for part in range(out_count):
                plan.setdefault(at, []).append((up_count + part, step))
        for step, at in enumerate((4, 8)):
            for number in range(downs):
                plan.setdefault(at, []).append((first_down + number, step))
        for number in range(first_part, first_down):
            for step in range(steps):
                at = first_q + (number - first_part) // len(cuts) + 1 if step == 0 else grid - 1
                plan.setdefault(at, []).append((number, step))
        for step, at in enumerate((3, 7, 9, 11, 13)):
            small_plan[at] = step
        late_plan[first_q + 2] = 0
        for at in range(grid):
            @pl.when(pid == at)
            def _():
                if at in small_plan:
                    advance_small(small_copies, small_sent, small_received, small_out, small_plan[at])
                for number, step in sorted(plan.get(at, []), key=lambda entry: (entry[1], entry[0])):
                    if at == grid - 1 and number == first_part:
                        advance_small(late_copies, late_sent, late_received, late_out, step)
                    advance(number, step)
                if at in late_plan:
                    advance_small(late_copies, late_sent, late_received, late_out, late_plan[at])
                if at == grid - 1:
                    for copy in swaps:
                        copy.wait()

                    def own_lanes(lanes):
                        size = lanes.shape[1] // 2
                        return jnp.where(core == 0, lanes[:, :size], lanes[:, size:])

                    out_out[...] = own_lanes(jnp.concatenate(
                        [swap_out[part].reshape(2 * o_rows, 128) for part in range(out_count)], axis=1))
                    qkv_out[...] = own_lanes(jnp.concatenate(
                        [swap_qkv[part].reshape(2 * q_rows, 128) for part in range(q_parts)], axis=1))
                    for item in pieces:
                        item.close()
                    for copies in small_copies + late_copies:
                        for copy in copies:
                            copy.wait_send()

    def whole(shape):
        return pl.BlockSpec(shape, lambda g: (0,) * len(shape), pipeline_mode=pl.Buffered(1))

    def number_of(g):
        return jnp.clip(g - 1, 0, attn_steps - 1)

    tile = pl.BlockSpec((length, 128), lambda g: (number_of(g) % docs, number_of(g) // docs))

    two = (2,)
    any_space = pl.BlockSpec(memory_space=pl.ANY)
    in_specs = [any_space, any_space, any_space, tile, tile, tile]
    in_specs += [pl.BlockSpec((1, 2, length, length), lambda g: (number_of(g) % docs, number_of(g) // docs, 0, 0))]
    in_specs += [any_space, any_space, any_space, any_space, whole((small_rows, width))]
    out_shape = [
        jax.ShapeDtypeStruct((rows, width), jnp.bfloat16),
        jax.ShapeDtypeStruct((u_rows, ups * 128), jnp.float32),
        jax.ShapeDtypeStruct((2 * o_rows, lanes // 2), jnp.float32),
        jax.ShapeDtypeStruct((2 * q_rows, lanes // 2), jnp.float32),
        jax.ShapeDtypeStruct((d_rows, downs * 128), jnp.float32),
        jax.ShapeDtypeStruct((small_rows, width), jnp.float32),
        jax.ShapeDtypeStruct((late_rows, 128), jnp.float32),
    ]
    wide_dims, half_dims = two * wide_bits, two * half_bits
    scratch = [
        pltpu.VMEM((pairs, rows, 128), jnp.bfloat16),
        pltpu.VMEM((pairs, rows, 128), jnp.bfloat16),
        pltpu.VMEM((3 * width, rows), jnp.bfloat16),
        pltpu.VMEM(up_grads.shape, jnp.bfloat16),
        pltpu.VMEM((out_count,) + wide_dims + half_dims + two + (o_rows, 128), jnp.bfloat16),
        pltpu.VMEM((q_parts,) + wide_dims + half_dims + two + (q_rows, 128), jnp.bfloat16),
    ]
    for low, high in u_cuts:
        scratch += [pltpu.VMEM((ups,) + two * (steps - 2 - s) + (high - low, 128), jnp.bfloat16) for s in range(steps - 1)]
    scratch += [pltpu.VMEM((out_count,) + two * (steps - 1 - s) + (o_rows, 128), jnp.bfloat16) for s in range(steps)]
    for low, high in cuts:
        scratch += [pltpu.VMEM((q_parts,) + two * (steps - 1 - s) + (high - low, 128), jnp.bfloat16) for s in range(steps)]
    scratch += [pltpu.VMEM(down_grads.shape, jnp.bfloat16)]
    scratch += [pltpu.VMEM((downs,) + two * (down_steps - 1 - s) + (d_rows, 128), jnp.bfloat16) for s in range(down_steps)]
    scratch += [pltpu.VMEM((steps, small_rows, width), jnp.float32)] * 2
    scratch += [pltpu.VMEM((steps, late_rows, 128), jnp.float32)] * 2
    scratch += [pltpu.VMEM((out_count, 2, o_rows, 128), jnp.float32), pltpu.VMEM((q_parts, 2, q_rows, 128), jnp.float32)]
    scratch += [pltpu.VMEM(tokens.shape, jnp.bfloat16), pltpu.VMEM(qkv_weight.shape, jnp.bfloat16)]
    scratch += [pltpu.VMEM(item.shape, jnp.bfloat16) for item in (grad_attended, mixed, out_weight)]
    sems = count * steps + (2 + q_parts * len(cuts) + len(s_cuts)) * steps + out_count
    scratch += [pltpu.SemaphoreType.DMA((sems,)), pltpu.SemaphoreType.DMA((sems,)), pltpu.SemaphoreType.DMA((ups + 6,))]
    return pl.pallas_call(
        kernel,
        grid=(grid,),
        in_specs=in_specs,
        out_specs=[pl.BlockSpec((token_block, width), lambda g: (jnp.clip(g - first_t, 0, token_steps - 1), 0))]
        + [whole(item.shape) for item in out_shape[1:]],
        out_shape=out_shape,
        scratch_shapes=scratch,
        compiler_params=pltpu.CompilerParams(collective_id=1, has_side_effects=True, vmem_limit_bytes=60 << 20),
        name="attention_backward",
    )(grad_attended, mixed, out_weight, queries, keys, values, attention, tokens, qkv_weight, up_grads, down_grads, sums)


def hand_out(grad_tokens, sums, late, narrow, classes, turned, *blocks):
    rows, width = grad_tokens.shape
    steps = 4
    first_dir = 6 + narrow

    def kernel(tokens_ref, sums_ref, late_ref, *refs):
        ins, outs = refs[: len(blocks)], refs[len(blocks) :]
        outs[0][...] = tokens_ref[...]

        @pl.when(pl.program_id(0) == 0)
        def _():
            for source, target in zip(ins, outs[1:]):
                target[...] = source[...] if source.shape == target.shape else source[...].T
            singles = outs[1 + len(blocks) :]
            for number in range(6):
                singles[number][...] = sums_ref[number, :]
            for number in range(2):
                for j in range(width // 128):
                    singles[6 + number][j * 128 : (j + 1) * 128] = late_ref[number * (width // 128) + j, :]
            for number in range(narrow):
                singles[8][number * width : (number + 1) * width] = sums_ref[6 + number, :]
            singles[9][...] = sums_ref[first_dir : first_dir + 2 * classes, :]
            singles[10][...] = sums_ref[first_dir + 2 * classes, :classes]

    def whole(shape):
        return pl.BlockSpec(shape, lambda g: (0,) * len(shape))

    some = pl.BlockSpec((rows // steps, width), lambda g: (g, 0))
    small = [(width,)] * 8 + [(narrow * width,), (2 * classes, width), (classes,)]
    shapes = [block.shape[::-1] if number in turned else block.shape for number, block in enumerate(blocks)]
    out_shape = [jax.ShapeDtypeStruct((rows, width), jnp.bfloat16)]
    out_shape += [jax.ShapeDtypeStruct(shape, jnp.float32) for shape in shapes + small]
    return pl.pallas_call(
        kernel,
        grid=(steps,),
        in_specs=[some] + [whole(item.shape) for item in (sums, late) + blocks],
        out_specs=[some] + [whole(item.shape) for item in out_shape[1:]],
        out_shape=out_shape,
        name="hand_out",
    )(grad_tokens, sums, late, *blocks)


def on_device_fast(
    tokens,
    doc_lengths,
    qkv_weight,
    query_bias,
    value_bias,
    out_weight,
    out_bias,
    first_gain,
    first_shift,
    up_weight,
    up_bias,
    down_weight,
    down_bias,
    second_gain,
    second_shift,
    dir_weight,
    dir_bias,
    segment_rows,
    segment_slots,
    pair_rows,
    pair_labels,
    out_cotangent,
):
    doc_count, length, model_width = tokens.shape
    token_rows = tokens.reshape(doc_count * length, model_width)
    singles = (out_bias, first_gain, first_shift, down_bias, second_gain, second_shift, query_bias, value_bias)
    vectors, queries, keys, values, attention, mixed, *kept = layer_forward(
        doc_lengths, token_rows, qkv_weight, out_weight, up_weight, down_weight, singles + (dir_bias, up_bias)
    )
    hidden_low, normed_one, inverse_one, active, slope, normed_two, inverse_two, encoded_rows = kept
    classes_count = dir_weight.shape[1]
    grad_attended, up_blocks, down_blocks, sums = ffn_backward(
        doc_lengths, segment_rows, segment_slots, pair_rows[0].T, pair_labels, encoded_rows, out_cotangent.reshape(-1, model_width), dir_weight.T, vectors,
        normed_two, inverse_two, active, slope,
        hidden_low, down_weight, up_weight, normed_one, inverse_one,
    )
    grad_tokens, out_up, out_out, out_qkv, out_down, sums, late = attention_backward(
        grad_attended, mixed, out_weight, queries, keys, values, attention, token_rows, qkv_weight, up_blocks,
        down_blocks, sums,
    )
    grad_tokens, out_up, out_out, out_qkv, out_down, *smalls = hand_out(
        grad_tokens, sums, late, lax.axis_size("narrow"), classes_count, (1, 2), out_up, out_out, out_qkv, out_down
    )
    return (
        encoded_rows.reshape(tokens.shape),
        grad_tokens.reshape(tokens.shape),
        out_qkv,
        smalls[6],
        smalls[7],
        out_out,
        smalls[5],
        smalls[3],
        smalls[4],
        out_up,
        smalls[8],
        out_down.T,
        smalls[2],
        smalls[0],
        smalls[1],
        smalls[9].reshape(2, classes_count, model_width).transpose(0, 2, 1).reshape(2 * model_width, classes_count),
        smalls[10],
    )


def on_device(
    tokens,
    doc_lengths,
    qkv_weight,
    query_bias,
    value_bias,
    out_weight,
    out_bias,
    first_gain,
    first_shift,
    up_weight,
    up_bias,
    down_weight,
    down_bias,
    second_gain,
    second_shift,
    dir_weight,
    dir_bias,
    segment_rows,
    segment_slots,
    pair_rows,
    pair_labels,
    out_cotangent,
):
    doc_count, length, model_width = tokens.shape
    score_scale = HEAD_DIM ** (-0.5)
    token_rows = tokens.reshape(doc_count * length, model_width)
    allowed = lax.broadcasted_iota(jnp.int32, (doc_count, length), 1) < doc_lengths[:, None]
    allowed_rows = allowed.reshape(-1, 1).astype(jnp.float32)
    bias_row = jnp.concatenate([query_bias, jnp.zeros_like(query_bias), value_bias]).astype(
        jnp.float32
    )
    qkv = (jnp.dot(token_rows, qkv_weight, preferred_element_type=jnp.float32) + bias_row).astype(
        jnp.bfloat16
    )

    def split_heads(doc_block, which):
        return doc_block[:, which * model_width : (which + 1) * model_width].reshape(
            length, HEADS, HEAD_DIM
        )

    def scores_of(queries, key_rows, doc_mask):
        scores = (
            jnp.einsum("qhd,khd->hqk", queries, key_rows, preferred_element_type=jnp.float32)
            * score_scale
        )
        return jnp.where(doc_mask[None, None, :], scores, MASKED)

    mixed_parts = []
    log_totals = []
    for doc_index in range(doc_count):
        doc_block = qkv[doc_index * length : (doc_index + 1) * length]
        queries = split_heads(doc_block, 0)
        key_rows = split_heads(doc_block, 1)
        value_rows = split_heads(doc_block, 2)
        scores = scores_of(queries, key_rows, allowed[doc_index])
        highest = jnp.max(scores, -1, keepdims=True)
        powers = jnp.exp(scores - highest)
        summed = jnp.sum(powers, -1, keepdims=True)
        attention = (powers / summed).astype(jnp.bfloat16)
        log_totals.append(highest + jnp.log(summed))
        mixed_parts.append(
            jnp.einsum(
                "hqk,khd->qhd", attention, value_rows, preferred_element_type=jnp.float32
            ).reshape(length, model_width)
        )
    mixed = jnp.concatenate(mixed_parts).astype(jnp.bfloat16)
    attended = jnp.dot(mixed, out_weight, preferred_element_type=jnp.float32) + out_bias.astype(
        jnp.float32
    )
    resid_one = token_rows.astype(jnp.float32) + attended
    hidden_one, normed_one, inverse_one = norm_forward(
        resid_one, first_gain.astype(jnp.float32), first_shift.astype(jnp.float32)
    )
    hidden_low = hidden_one.astype(jnp.bfloat16)
    upper_pre = jnp.dot(hidden_low, up_weight, preferred_element_type=jnp.float32) + up_bias.astype(
        jnp.float32
    )
    cumulative = normal_cdf(upper_pre)
    active = (upper_pre * cumulative).astype(jnp.bfloat16)
    lowered = jnp.dot(active, down_weight, preferred_element_type=jnp.float32) + down_bias.astype(
        jnp.float32
    )
    resid_two = hidden_one + lowered
    second_float = second_gain.astype(jnp.float32)
    normed_out, normed_two, inverse_two = norm_forward(
        resid_two, second_float, second_shift.astype(jnp.float32)
    )
    encoded_rows = (normed_out * allowed_rows).astype(jnp.bfloat16)
    doc_starts = lax.broadcasted_iota(jnp.int32, (doc_count, 1), 0) * length
    picked_rows = (segment_rows + doc_starts).reshape(-1)
    picked = encoded_rows[picked_rows]
    slots = segment_slots.reshape(-1)
    outgoing = jnp.zeros_like(picked).at[slots].set(picked)
    arrived = lax.all_to_all(outgoing, "wide", split_axis=0, concat_axis=0, tiled=True)
    pairs = pair_rows.reshape(-1, 2)
    labels = pair_labels.reshape(-1)
    first_rows = arrived[pairs[:, 0]]
    second_rows = arrived[pairs[:, 1]]
    logits = (
        jnp.dot(first_rows, dir_weight[:model_width], preferred_element_type=jnp.float32)
        + jnp.dot(second_rows, dir_weight[model_width:], preferred_element_type=jnp.float32)
        + dir_bias.astype(jnp.float32)
    )
    powers_head = jnp.exp(logits - jnp.max(logits, -1, keepdims=True))
    chance = powers_head / jnp.sum(powers_head, -1, keepdims=True)
    classes = lax.broadcasted_iota(jnp.int32, logits.shape, 1)
    delta = chance - (labels[:, None] == classes).astype(jnp.float32)
    first_float = first_rows.astype(jnp.float32)
    second_rows_float = second_rows.astype(jnp.float32)
    grad_dir_weight = jnp.concatenate(
        [
            jnp.dot(first_float.T, delta, precision=EXACT, preferred_element_type=jnp.float32),
            jnp.dot(
                second_rows_float.T, delta, precision=EXACT, preferred_element_type=jnp.float32
            ),
        ]
    )
    grad_dir_bias = jnp.sum(delta, 0)
    dir_float = dir_weight.astype(jnp.float32)
    grad_first = jnp.dot(
        delta, dir_float[:model_width].T, precision=EXACT, preferred_element_type=jnp.float32
    )
    grad_second = jnp.dot(
        delta, dir_float[model_width:].T, precision=EXACT, preferred_element_type=jnp.float32
    )
    grad_arrived = jnp.zeros((arrived.shape[0], model_width), jnp.float32)
    grad_arrived = grad_arrived.at[pairs[:, 0]].add(grad_first).at[pairs[:, 1]].add(grad_second)
    returned = lax.all_to_all(
        grad_arrived.astype(jnp.bfloat16), "wide", split_axis=0, concat_axis=0, tiled=True
    )
    grad_picked = returned[slots].astype(jnp.float32)
    grad_encoded = (
        out_cotangent.reshape(-1, model_width).astype(jnp.float32).at[picked_rows].add(grad_picked)
    )
    grad_encoded = grad_encoded * allowed_rows
    grad_two, grad_second_gain, grad_second_shift = norm_backward(
        grad_encoded, normed_two, inverse_two, second_float
    )
    grad_lowered = grad_two.astype(jnp.bfloat16)
    grad_down_weight = jnp.einsum(
        "rf,rd->fd", active, grad_lowered, preferred_element_type=jnp.float32
    )
    grad_down_bias = jnp.sum(grad_lowered.astype(jnp.float32), 0)
    grad_active = jnp.einsum(
        "rd,fd->rf", grad_lowered, down_weight, preferred_element_type=jnp.float32
    )
    density = jnp.exp(-0.5 * upper_pre * upper_pre) * 0.3989422804014327
    grad_upper = (grad_active * (cumulative + upper_pre * density)).astype(jnp.bfloat16)
    grad_up_weight = jnp.einsum(
        "rd,rf->df", hidden_low, grad_upper, preferred_element_type=jnp.float32
    )
    grad_up_bias = jnp.sum(grad_upper.astype(jnp.float32), 0)
    grad_hidden = grad_two + jnp.einsum(
        "rf,df->rd", grad_upper, up_weight, preferred_element_type=jnp.float32
    )
    grad_one, grad_first_gain, grad_first_shift = norm_backward(
        grad_hidden, normed_one, inverse_one, first_gain.astype(jnp.float32)
    )
    grad_attended = grad_one.astype(jnp.bfloat16)
    grad_out_weight = jnp.einsum(
        "rd,re->de", mixed, grad_attended, preferred_element_type=jnp.float32
    )
    grad_out_bias = jnp.sum(grad_attended.astype(jnp.float32), 0)
    grad_mixed = jnp.einsum(
        "re,de->rd", grad_attended, out_weight, preferred_element_type=jnp.float32
    ).astype(jnp.bfloat16)
    grad_parts = []
    for doc_index in range(doc_count):
        doc_block = qkv[doc_index * length : (doc_index + 1) * length]
        queries = split_heads(doc_block, 0)
        key_rows = split_heads(doc_block, 1)
        value_rows = split_heads(doc_block, 2)
        scores = scores_of(queries, key_rows, allowed[doc_index])
        attention = jnp.exp(scores - log_totals[doc_index])
        grad_doc = grad_mixed[doc_index * length : (doc_index + 1) * length].reshape(
            length, HEADS, HEAD_DIM
        )
        grad_chance = jnp.einsum(
            "qhd,khd->hqk", grad_doc, value_rows, preferred_element_type=jnp.float32
        )
        inner = jnp.sum(grad_chance * attention, -1, keepdims=True)
        grad_scores = (attention * (grad_chance - inner)).astype(jnp.bfloat16)
        grad_query = (
            jnp.einsum("hqk,khd->qhd", grad_scores, key_rows, preferred_element_type=jnp.float32)
            * score_scale
        )
        grad_key = (
            jnp.einsum("hqk,qhd->khd", grad_scores, queries, preferred_element_type=jnp.float32)
            * score_scale
        )
        grad_value = jnp.einsum(
            "hqk,qhd->khd",
            attention.astype(jnp.bfloat16),
            grad_doc,
            preferred_element_type=jnp.float32,
        )
        grad_parts.append(
            jnp.concatenate(
                [
                    grad_query.reshape(length, model_width),
                    grad_key.reshape(length, model_width),
                    grad_value.reshape(length, model_width),
                ],
                axis=1,
            )
        )
    grad_qkv = jnp.concatenate(grad_parts).astype(jnp.bfloat16)
    grad_qkv_float = grad_qkv.astype(jnp.float32)
    grad_query_bias = jnp.sum(grad_qkv_float[:, :model_width], 0)
    grad_value_bias = jnp.sum(grad_qkv_float[:, 2 * model_width :], 0)
    grad_qkv_weight = jnp.einsum(
        "rd,re->de", token_rows, grad_qkv, preferred_element_type=jnp.float32
    )
    grad_tokens = (
        jnp.einsum("re,de->rd", grad_qkv, qkv_weight, preferred_element_type=jnp.float32) + grad_one
    ).astype(jnp.bfloat16)
    matrices = (grad_qkv_weight, grad_out_weight, grad_up_weight, grad_down_weight)
    partial_sums = (
        lax.psum_scatter(
            matrices[0].astype(jnp.bfloat16), "wide", scatter_dimension=1, tiled=True
        ).astype(jnp.float32),
        lax.psum_scatter(
            matrices[1].astype(jnp.bfloat16), "wide", scatter_dimension=1, tiled=True
        ).astype(jnp.float32),
        lax.psum_scatter(
            matrices[2].astype(jnp.bfloat16), "wide", scatter_dimension=1, tiled=True
        ).astype(jnp.float32),
        lax.psum_scatter(
            matrices[3].astype(jnp.bfloat16), "wide", scatter_dimension=1, tiled=True
        ).astype(jnp.float32),
    )
    summed_mats = (
        lax.psum_scatter(
            partial_sums[0].astype(jnp.bfloat16), "narrow", scatter_dimension=0, tiled=True
        ).astype(jnp.float32),
        lax.psum_scatter(
            partial_sums[1].astype(jnp.bfloat16), "narrow", scatter_dimension=0, tiled=True
        ).astype(jnp.float32),
        lax.psum_scatter(
            partial_sums[2].astype(jnp.bfloat16), "narrow", scatter_dimension=0, tiled=True
        ).astype(jnp.float32),
        lax.psum_scatter(
            partial_sums[3].astype(jnp.bfloat16), "narrow", scatter_dimension=0, tiled=True
        ).astype(jnp.float32),
    )
    smalls = lax.psum(
        (
            grad_query_bias,
            grad_value_bias,
            grad_out_bias,
            grad_first_gain,
            grad_first_shift,
            grad_up_bias,
            grad_down_bias,
            grad_second_gain,
            grad_second_shift,
            grad_dir_weight,
            grad_dir_bias,
        ),
        ("wide", "narrow"),
    )
    return (
        encoded_rows.reshape(tokens.shape),
        grad_tokens.reshape(tokens.shape),
        summed_mats[0],
        smalls[0],
        smalls[1],
        summed_mats[1],
        smalls[2],
        smalls[3],
        smalls[4],
        summed_mats[2],
        smalls[5],
        summed_mats[3],
        smalls[6],
        smalls[7],
        smalls[8],
        smalls[9],
        smalls[10],
    )


def fits_blocks(mesh):
    wide, narrow = mesh.shape["wide"], mesh.shape["narrow"]
    width, ff = HEADS * HEAD_DIM, 4 * HEADS * HEAD_DIM
    if wide != 2 * narrow or narrow < 4 or narrow & (narrow - 1):
        return False
    lanes = (ff // narrow, ff // wide, 2 * width // narrow)
    rows = (width // wide, width // narrow, width // wide // 2, 3 * width // wide // 2)
    return all(size % 128 == 0 for size in lanes) and all(size % 16 == 0 for size in rows)


def solution(mesh):
    placed = (
        P(("wide", "narrow"), None, None),
        P(("wide", "narrow")),
        P(),
        P(),
        P(),
        P(),
        P(),
        P(),
        P(),
        P(),
        P(),
        P(),
        P(),
        P(),
        P(),
        P(),
        P(),
        P(("wide", "narrow"), None),
        P(("wide", "narrow"), None),
        P(("wide", "narrow"), None, None),
        P(("wide", "narrow"), None),
        P(("wide", "narrow"), None, None),
    )
    return jax.shard_map(
        on_device_fast if fits_blocks(mesh) else on_device,
        mesh=mesh,
        in_specs=placed,
        out_specs=(
            P(("wide", "narrow"), None, None),
            P(("wide", "narrow"), None, None),
            P("narrow", "wide"),
            P(),
            P(),
            P("narrow", "wide"),
            P(),
            P(),
            P(),
            P("narrow", "wide"),
            P(),
            P("narrow", "wide"),
            P(),
            P(),
            P(),
            P(),
            P(),
        ),
        check_vma=False,
    )
```

```python
import jax
import jax.numpy as jnp
from jax import lax
from jax.experimental import pallas as pl
from jax.experimental.pallas import tpu as pltpu
from jax.sharding import PartitionSpec as P

HEADS = 12
HEAD_DIM = 64


EXACT = lax.Precision.HIGHEST
MASKED = -1e30
EPSILON = 1e-05


def norm_forward(values, gain, shift):
    center = jnp.mean(values, -1, keepdims=True)
    centered = values - center
    inverse = lax.rsqrt(jnp.mean(centered * centered, -1, keepdims=True) + EPSILON)
    normed = centered * inverse
    return (normed * gain + shift, normed, inverse)


def norm_backward(grad, normed, inverse, gain):
    scaled = grad * gain
    first_mean = jnp.mean(scaled, -1, keepdims=True)
    second_mean = jnp.mean(scaled * normed, -1, keepdims=True)
    return (
        (scaled - first_mean - normed * second_mean) * inverse,
        jnp.sum(grad * normed, 0),
        jnp.sum(grad, 0),
    )


def normal_cdf(values):
    return 0.5 * (1.0 + lax.erf(values * 0.7071067811865476))


MESH_ID = pl.DeviceIdType.MESH


def axis_bits():
    names = []
    for axis in ("wide", "narrow"):
        count = lax.axis_size(axis).bit_length() - 1
        names += [(axis, bit) for bit in reversed(range(count))]
    return names


class Place:
    def __init__(self):
        self.index = {axis: lax.axis_index(axis) for axis in ("wide", "narrow")}
        self.names = axis_bits()
        self.bit = {name: (self.index[name[0]] // (1 << name[1])) % 2 for name in self.names}

    def across(self, name):
        axis, bit = name
        target = dict(self.index)
        target[axis] = target[axis] + (1 << bit) - (2 << bit) * self.bit[name]
        return target

    def ahead(self, offset):
        target = dict(self.index)
        target["wide"] = (target["wide"] + offset) % lax.axis_size("wide")
        return target

    def greet(self, all_wide=False):
        barrier = pltpu.get_barrier_semaphore()
        targets = [self.across(name) for name in self.names if not (all_wide and name[0] == "wide")]
        if all_wide:
            targets += [self.ahead(offset) for offset in range(1, lax.axis_size("wide"))]
        for target in targets:
            pl.semaphore_signal(barrier, inc=1, device_id=target, device_id_type=MESH_ID)
        pl.semaphore_wait(barrier, len(targets))


class Halving:
    def __init__(self, place, names, order, source, own, received, send_sems, recv_sems, first_sem, tail=()):
        self.place, self.names, self.order = place, names, order
        self.source, self.own, self.received = source, own, received
        self.last = True
        self.send_sems, self.recv_sems, self.first_sem, self.tail = send_sems, recv_sems, first_sem, tail

    def region(self, step, mine):
        index = []
        for name in self.names:
            if name in self.order[:step]:
                index.append(self.place.bit[name])
            elif name == self.order[step]:
                index.append(self.place.bit[name] if mine else 1 - self.place.bit[name])
            else:
                index.append(slice(None))
        return tuple(index) + self.tail

    def copy(self, step):
        held = self.source if step == 0 else self.own
        return pltpu.make_async_remote_copy(
            src_ref=held.at[self.region(step, False)],
            dst_ref=self.received[step],
            send_sem=self.send_sems.at[self.first_sem + step],
            recv_sem=self.recv_sems.at[self.first_sem + step],
            device_id=self.place.across(self.order[step]),
            device_id_type=MESH_ID,
        )

    def send(self, step):
        self.copy(step).start()

    def add(self, step):
        self.copy(step).wait_recv()
        mine = self.region(step, True)
        if step + 1 < len(self.order) or not self.last:
            self.own[mine] = self.own[mine] + self.received[step][...]
            return None
        return self.own[mine].astype(jnp.float32) + self.received[step][...].astype(jnp.float32)

    def merge(self, step):
        self.last = False
        self.add(step)

    def close(self):
        for step in range(len(self.order)):
            self.copy(step).wait_send()


def link_orders():
    wide = [("wide", bit) for bit in range(lax.axis_size("wide").bit_length() - 1)]
    narrow = [("narrow", bit) for bit in range(1, lax.axis_size("narrow").bit_length() - 1)]
    core, x, near, far = [("narrow", 0)], wide[:1], wide[1:-1], wide[-1:]
    return [core + narrow + x + near + far, core + x + near + narrow + far, core + near + narrow + x + far]


def layer_forward(lengths, tokens, qkv_weight, out_weight, up_weight, down_weight, singles):
    rows, width = tokens.shape
    ff = up_weight.shape[1]
    docs = lengths.shape[0]
    length = rows // docs
    pairs, chunks = width // 128, ff // width
    kinds = [item.shape[0] for item in singles]
    lines = sum(max(1, size // width) for size in kinds)
    row_block = 256

    def kernel(lens, tok, wq, wk, wv, ow, up, down, *refs):
        singles, refs = refs[: len(kinds)], refs[len(kinds) :]
        vec, q_out, k_out, v_out, attention_out, mixed_out = refs[:6]
        hid_out, n1_out, q1_out, act_out, slope_out, n2_out, q2_out, enc_out = refs[6:14]
        mixed, hidden, total = refs[14:]
        pid = pl.program_id(0)

        def each_block(body):
            def step(i, carry):
                body(pl.multiple_of(i * row_block, row_block))
                return carry

            lax.fori_loop(0, rows // row_block, step, 0)

        @pl.when(pid == 0)
        def _():
            at = 0
            for single, size in zip(singles, kinds):
                values = single[...].astype(jnp.float32)
                for first in range(0, size, width):
                    some = min(size, width)
                    vec[at, :some] = values[first : first + some]
                    at += 1

        @pl.when(pid < pairs)
        def _():
            weights = jnp.concatenate([wq[...], wk[...], wv[...]], axis=1)
            at = pl.ds(pl.multiple_of(pid * 128, 128), 128)
            offsets = jnp.concatenate([vec[6:7, at], jnp.zeros((1, 128), jnp.float32), vec[7:8, at]], axis=1)
            qkv = (jnp.dot(tok[...], weights, preferred_element_type=jnp.float32) + offsets).astype(jnp.bfloat16)
            q_out[...] = qkv[:, :128]
            k_out[...] = qkv[:, 128:256]
            v_out[...] = qkv[:, 256:]
            first = lax.broadcasted_iota(jnp.int32, (1, 128), 1) < HEAD_DIM
            for doc in range(docs):
                some = slice(doc * length, (doc + 1) * length)
                queries = qkv[some, :128] * jnp.bfloat16(HEAD_DIM**-0.5)
                keys, values = qkv[some, 128:256], qkv[some, 256:]
                zero = jnp.zeros_like(queries)
                places = lax.broadcasted_iota(jnp.int32, (1, length), 1)
                bias = jnp.where(places < lens[doc], 0.0, MASKED)
                outs = []
                for head in range(2):
                    masked = jnp.where(first, queries, zero) if head == 0 else jnp.where(first, zero, queries)
                    scores = dot_last(masked, keys) + bias
                    powers = jnp.exp(scores - jnp.max(scores, -1, keepdims=True))
                    attention = (powers * (1.0 / jnp.sum(powers, -1, keepdims=True))).astype(jnp.bfloat16)
                    attention_out[doc, head] = attention
                    outs.append(jnp.dot(attention, values, preferred_element_type=jnp.float32))
                both = jnp.where(first, outs[0], outs[1]).astype(jnp.bfloat16)
                mixed_out[some, :] = both
                mixed[some, at] = both

        @pl.when(pid == pairs)
        def _():
            total[...] = jnp.dot(mixed[...], ow[...], preferred_element_type=jnp.float32)

            def body(at):
                some = pl.ds(at, row_block)
                summed = tok[some, :].astype(jnp.float32) + (total[some, :] + vec[0:1, :])
                out, normed, inverse = norm_forward(summed, vec[1:2, :], vec[2:3, :])
                hidden[some, :] = out
                hid_out[some, :] = out.astype(jnp.bfloat16)
                n1_out[some, :] = normed.astype(jnp.bfloat16)
                q1_out[some, :] = inverse
                total[some, :] = jnp.zeros_like(out)

            each_block(body)

        @pl.when(pid >= pairs)
        def _():
            offset = vec[pl.ds(pid - pairs + 9, 1), :]
            pre = jnp.dot(hid_out[...], up[...], preferred_element_type=jnp.float32) + offset
            cumulative = normal_cdf(pre)
            density = jnp.exp(-0.5 * pre * pre) * 0.3989422804014327
            active = (pre * cumulative).astype(jnp.bfloat16)
            act_out[...] = active
            slope_out[...] = (cumulative + pre * density).astype(jnp.bfloat16)
            total[...] += jnp.dot(active, down[...], preferred_element_type=jnp.float32)

        @pl.when(pid == pairs + chunks - 1)
        def _():
            def body(at):
                some = pl.ds(at, row_block)
                summed = hidden[some, :] + (total[some, :] + vec[3:4, :])
                out, normed, inverse = norm_forward(summed, vec[4:5, :], vec[5:6, :])
                n2_out[some, :] = normed.astype(jnp.bfloat16)
                q2_out[some, :] = inverse
                doc = at // length
                line = lax.broadcasted_iota(jnp.int32, (row_block, 1), 0) + (at - doc * length)
                enc_out[some, :] = jnp.where(line < lens[doc], out, 0.0).astype(jnp.bfloat16)

            each_block(body)

    def whole(shape):
        return pl.BlockSpec(shape, lambda g: (0,) * len(shape), pipeline_mode=pl.Buffered(1))

    def pair_of(g):
        return jnp.minimum(g, pairs - 1)

    def chunk_of(g):
        return jnp.clip(g - pairs, 0, chunks - 1)

    column = pl.BlockSpec((rows, 128), lambda g: (0, pair_of(g)))
    upper = pl.BlockSpec((rows, width), lambda g: (0, chunk_of(g)))
    full, one = whole((rows, width)), whole((rows, 1))
    in_specs = [pl.BlockSpec(memory_space=pltpu.SMEM), full]
    in_specs += [pl.BlockSpec((width, 128), lambda g, n=n: (0, n * pairs + pair_of(g))) for n in range(3)]
    in_specs += [whole((width, width)), pl.BlockSpec((width, width), lambda g: (0, chunk_of(g)))]
    in_specs += [pl.BlockSpec((width, width), lambda g: (chunk_of(g), 0))]
    in_specs += [whole(item.shape) for item in singles]
    low = jax.ShapeDtypeStruct((rows, width), jnp.bfloat16)
    inverse = jax.ShapeDtypeStruct((rows, 1), jnp.float32)
    high = jax.ShapeDtypeStruct((rows, ff), jnp.bfloat16)
    return pl.pallas_call(
        kernel,
        grid=(pairs + chunks,),
        in_specs=in_specs,
        out_specs=[whole((lines, width))] + [column] * 3
        + [pl.BlockSpec((docs, 2, length, length), lambda g: (0, pair_of(g), 0, 0)), column]
        + [full, full, one, upper, upper, full, one, full],
        out_shape=[jax.ShapeDtypeStruct((lines, width), jnp.float32)] + [low] * 3
        + [jax.ShapeDtypeStruct((docs, 2 * pairs, length, length), jnp.bfloat16), low]
        + [low, low, inverse, high, high, low, inverse, low],
        scratch_shapes=[pltpu.VMEM((rows, width), jnp.bfloat16)] + [pltpu.VMEM((rows, width), jnp.float32)] * 2,
        compiler_params=pltpu.CompilerParams(vmem_limit_bytes=60 << 20),
        name="layer_forward",
    )(lengths, tokens, qkv_weight, qkv_weight, qkv_weight, out_weight, up_weight, down_weight, *singles)


def dot_last(left, right):
    return lax.dot_general(left, right, (((1,), (1,)), ((), ())), preferred_element_type=jnp.float32)


def norm_back_rows(grad, normed, inverse, gain):
    scaled = grad * gain
    first = jnp.mean(scaled, -1, keepdims=True)
    second = jnp.mean(scaled * normed, -1, keepdims=True)
    return (scaled - first - normed * second) * inverse


def parts_of(values, count):
    terms = []
    for _ in range(count):
        term = values.astype(jnp.bfloat16).astype(jnp.float32)
        terms.append(term)
        values = values - term
    return jnp.concatenate(terms).astype(jnp.bfloat16)


def one_hot(row, count):
    lines = lax.broadcasted_iota(jnp.int32, (count, row.shape[1]), 0)
    return jnp.where(lines == row, 1.0, 0.0).astype(jnp.bfloat16)


def ffn_backward(lengths, segment_rows, segment_slots, pair_rows, pair_labels, encoded, cotangent, dir_t, vectors, normed_two, inverse_two, active, slope, hidden_low, down_weight, up_weight,
                 normed_one, inverse_one):
    rows, width = hidden_low.shape
    ff = active.shape[1]
    segments, classes = segment_slots.shape[1], dir_t.shape[0]
    numbers = (segment_rows, segment_slots, pair_rows, pair_labels)
    length = rows // lengths.shape[0]
    names = axis_bits()
    steps = len(names)
    wide, narrow = lax.axis_size("wide"), lax.axis_size("narrow")
    wide_bits, narrow_bits = wide.bit_length() - 1, narrow.bit_length() - 1
    chunks = ff // narrow // 128
    third = chunks // 2
    d_rows, u_rows = width // wide, width // narrow
    row_block = 256
    row_steps = rows // row_block
    orders = link_orders()
    two = (2,)
    early = 3
    first_dir = 6 + narrow
    sum_rows = pl.cdiv(first_dir + 2 * classes + 1, 16) * 16

    def chunk_of(step):
        step = jnp.clip(step, 0, chunks - 1)
        return step // 2 + third * (step % 2)

    def bits_of(number, count):
        return tuple((number >> bit) & 1 for bit in reversed(range(count)))

    def kernel(*refs):
        lens, seg_rows, seg_slots, pair_nums, labels, enc, cot, dir_ref = refs[:8]
        refs = refs[8:]
        q2, q1, vec = refs[:3]
        far = refs[3:9]
        slo = refs[9 : 9 + narrow]
        rest = list(refs[9 + narrow :])
        ga_out, up_out, down_out, sums_out = rest[:4]
        rest = rest[4:]
        grad_hidden, lowered, lowered_t, hidden_t, own, up_own, up_received = rest[:7]
        received = rest[7 : 7 + early]
        rest = rest[7 + early :]
        select, picked, dir_w, leaving, arrived, leaving_grads, arrived_grads = rest[:7]
        near = rest[7:13]
        n2, hidden, act, dws, uws, n1 = near
        send_sems, recv_sems, local_sems = rest[13:]
        loads = [pltpu.make_async_copy(far[i], near[i], local_sems.at[2 * chunks + i]) for i in range(len(near))]
        pid = pl.program_id(0)
        place = Place()
        pieces = []
        for number in range(chunks):
            pieces.append(
                Halving(place, names, orders[number % 3][:early], own.at[number], own.at[number],
                        [r.at[number] for r in received], send_sems, recv_sems, number * early)
            )
        core = ("narrow", 0)
        up_names = [name for name in names if name != ("wide", 0)]
        up_pieces = [
            Halving(place, up_names, [core], up_own.at[number], up_own.at[number], [up_received.at[number]],
                    send_sems, recv_sems, chunks * early + number)
            for number in range(chunks)
        ]

        def up_write(number):
            mine = up_pieces[number].region(0, True)
            return pltpu.make_async_copy(
                up_own.at[number].at[mine],
                up_out.at[(number // 2,) + (slice(None),) * (wide_bits - 1) + (number % 2,)],
                local_sems.at[number],
            )

        def exchange(source, landing, first, meanwhile=None):
            made = []
            for offset in range(1, wide):
                target = place.ahead(offset)
                made.append(pltpu.make_async_remote_copy(
                    src_ref=source.at[target["wide"]], dst_ref=landing.at[place.index["wide"]],
                    send_sem=send_sems.at[first + offset - 1], recv_sem=recv_sems.at[first + offset - 1],
                    device_id=target, device_id_type=MESH_ID))
            me = place.index["wide"]
            for copy in made:
                copy.start()
            landing[me] = source[me]
            if meanwhile:
                meanwhile()
            for copy in made:
                copy.wait()
            return landing[...].reshape(segments, 128)

        def turn_hidden():
            def body(i, carry):
                some = pl.ds(pl.multiple_of(i * row_block, row_block), row_block)
                hidden_t[:, some] = hidden[some, :].T
                return carry

            loads[1].wait()
            lax.fori_loop(0, row_steps, body, 0)

        @pl.when(pid == 0)
        def _():
            for load in loads:
                load.start()
            place.greet(all_wide=True)
            sums_out[...] = jnp.zeros_like(sums_out)
            base = chunks * early + chunks
            docs = rows // length
            places = jnp.concatenate([seg_rows[doc : doc + 1, :] + doc * length for doc in range(docs)], axis=1)
            select[...] = dot_last(one_hot(places, rows), one_hot(seg_slots[...], segments)).astype(jnp.bfloat16)
            picked[...] = jnp.dot(select[...].T, enc[...], preferred_element_type=jnp.float32).astype(jnp.bfloat16)
            halves = [dir_ref[:, n * width : (n + 1) * width].astype(jnp.float32) for n in range(2)]
            blank = jnp.zeros((128 - 2 * classes, width), jnp.float32)
            dir_w[...] = jnp.concatenate(halves + [blank]).astype(jnp.bfloat16)
            leaving[...] = dot_last(picked[...], dir_w[...]).reshape(leaving.shape)
            scores = exchange(leaving, arrived, base, turn_hidden).T
            pair_first, pair_second = one_hot(pair_nums[0:1, :], segments), one_hot(pair_nums[1:2, :], segments)

            def chosen(values, pairs):
                split = jnp.dot(parts_of(values, 3), pairs, preferred_element_type=jnp.float32)
                return split[:classes] + split[classes : 2 * classes] + split[2 * classes :]

            logits = chosen(scores[:classes], pair_first) + chosen(scores[classes : 2 * classes], pair_second)
            logits = logits + jnp.broadcast_to(vec[8:9, :128], (128, 128)).T[:classes, 0:1]
            powers = jnp.exp(logits - jnp.max(logits, 0, keepdims=True))
            chance = powers / jnp.sum(powers, 0, keepdims=True)
            kinds = lax.broadcasted_iota(jnp.int32, logits.shape, 0)
            delta = chance - jnp.where(kinds == labels[...], 1.0, 0.0)
            split = parts_of(delta, 2)
            gathered = []
            for pairs in (pair_first, pair_second):
                both = dot_last(split, pairs)
                gathered.append(both[:classes] + both[classes:])
            gathered.append(jnp.zeros((128 - 2 * classes, segments), jnp.float32))
            leaving_grads[...] = jnp.concatenate(gathered).T.reshape(leaving.shape)
            square = (classes, 128)
            matching = lax.broadcasted_iota(jnp.int32, square, 0) == lax.broadcasted_iota(jnp.int32, square, 1)
            biases = jnp.where(matching, jnp.sum(delta, 1, keepdims=True), 0.0)
            sums_out[first_dir + 2 * classes : first_dir + 2 * classes + 1, :128] = jnp.sum(biases, 0, keepdims=True)
            back = exchange(leaving_grads, arrived_grads, base + wide - 1)
            coarse = back.astype(jnp.bfloat16)
            fine = (back - coarse.astype(jnp.float32)).astype(jnp.bfloat16)
            grads_in = (
                jnp.dot(coarse, dir_w[...], preferred_element_type=jnp.float32)
                + jnp.dot(fine, dir_w[...], preferred_element_type=jnp.float32)
            ).astype(jnp.bfloat16)
            back_t = back.T[: 2 * classes]
            both = jnp.dot(parts_of(back_t, 2), picked[...], preferred_element_type=jnp.float32)
            sums_out[first_dir : first_dir + 2 * classes, :] = both[: 2 * classes] + both[2 * classes :]
            loads[0].wait()

            def body(i, carry):
                at = pl.multiple_of(i * row_block, row_block)
                some = pl.ds(at, row_block)
                normed = n2[some, :].astype(jnp.float32)
                doc = at // length
                line = lax.broadcasted_iota(jnp.int32, (row_block, 1), 0) + (at - doc * length)
                grad = cot[some, :].astype(jnp.float32) + jnp.dot(
                    select[some, :], grads_in, preferred_element_type=jnp.float32
                )
                grad = jnp.where(line < lens[doc], grad, 0.0)
                two = norm_back_rows(grad, normed, q2[some, :], vec[4:5, :])
                low = two.astype(jnp.bfloat16)
                grad_hidden[some, :] = two
                lowered[some, :] = low
                lowered_t[:, some] = low.T
                sums_out[0:1, :] += jnp.sum(grad * normed, 0, keepdims=True)
                sums_out[1:2, :] += jnp.sum(grad, 0, keepdims=True)
                sums_out[2:3, :] += jnp.sum(low.astype(jnp.float32), 0, keepdims=True)
                return carry

            lax.fori_loop(0, row_steps, body, 0)

        def slab(n, step):
            return pl.ds(pl.multiple_of((n * chunks + chunk_of(step)) * 128, 128), 128)

        @pl.when(pid == 0)
        def _():
            loads[2].wait()

        @pl.when(pid < chunks)
        def _():
            actives = jnp.concatenate([act[:, slab(n, pid)] for n in range(narrow)], axis=1)
            result = jnp.dot(lowered_t[...], actives, preferred_element_type=jnp.float32).astype(jnp.bfloat16)
            for w in range(wide):
                for n in range(narrow):
                    own[(pid,) + bits_of(w, wide_bits) + bits_of(n, narrow_bits)] = result[
                        w * d_rows : (w + 1) * d_rows, n * 128 : (n + 1) * 128
                    ]

        @pl.when(pid == chunks)
        def _():
            for load in loads[3:]:
                load.wait()

        @pl.when(pid >= chunks)
        def _():
            slopes = jnp.concatenate([ref[...] for ref in slo], axis=1)
            downs = jnp.concatenate([dws[slab(n, pid - chunks), :] for n in range(narrow)], axis=0)
            ups = jnp.concatenate([uws[:, slab(n, pid - chunks)] for n in range(narrow)], axis=1)
            grad_active = dot_last(lowered[...], downs)
            grad_upper = (grad_active * slopes.astype(jnp.float32)).astype(jnp.bfloat16)
            totals = jnp.sum(grad_upper.astype(jnp.float32), 0, keepdims=True)
            at = pl.ds(pl.multiple_of(chunk_of(pid - chunks) * 128, 128), 128)
            for n in range(narrow):
                sums_out[6 + n : 7 + n, at] = totals[:, n * 128 : (n + 1) * 128]
            result = jnp.dot(hidden_t[...], grad_upper, preferred_element_type=jnp.float32).astype(jnp.bfloat16)
            for n in range(narrow):
                for z in range(narrow):
                    high = bits_of(z, wide_bits - 1)
                    up_own[(pid - chunks,) + high + bits_of(n, narrow_bits)] = result[
                        n * u_rows : (n + 1) * u_rows, z * 128 : (z + 1) * 128
                    ]
            grad_hidden[...] += dot_last(grad_upper, ups)

        def down_write(number):
            return pltpu.make_async_copy(
                own.at[number].at[pieces[number].region(early - 1, True)], down_out.at[number], local_sems.at[chunks + number]
            )

        def advance(number, step):
            pieces[number].merge(step)
            if step + 1 < early:
                pieces[number].send(step + 1)
            else:
                down_write(number).start()

        for number in range(chunks):
            @pl.when(pid == chunks + number)
            def _():
                up_pieces[number].send(0)

        @pl.when(pid == 2 * chunks - 1)
        def _():
            def body(i, carry):
                at = pl.multiple_of(i * row_block, row_block)
                some = pl.ds(at, row_block)
                grad, normed = grad_hidden[some, :], n1[some, :].astype(jnp.float32)
                low = norm_back_rows(grad, normed, q1[some, :], vec[1:2, :]).astype(jnp.bfloat16)
                ga_out[some, :] = low
                sums_out[3:4, :] += jnp.sum(grad * normed, 0, keepdims=True)
                sums_out[4:5, :] += jnp.sum(grad, 0, keepdims=True)
                sums_out[5:6, :] += jnp.sum(low.astype(jnp.float32), 0, keepdims=True)
                return carry

            lax.fori_loop(0, row_steps, body, 0)

        plan = {}
        for number in range(chunks):
            for step in range(early):
                at = (number + 2, chunks + 1 + 2 * (number // 3), chunks + 4 + number // 3)[step]
                plan.setdefault(min(at, 2 * chunks - 1), []).append((step, number))
        for at in range(2 * chunks):
            @pl.when(pid == at)
            def _():
                if at < chunks:
                    pieces[at].send(0)
                if at > chunks:
                    up_pieces[at - chunks - 1].merge(0)
                    up_write(at - chunks - 1).start()
                for step, number in sorted(plan.get(at, [])):
                    advance(number, step)
                if at == 2 * chunks - 1:
                    up_pieces[chunks - 1].merge(0)
                    up_write(chunks - 1).start()
                    for number in range(chunks):
                        up_write(number).wait()
                        down_write(number).wait()
                    for item in pieces + up_pieces:
                        item.close()

    def whole(shape):
        return pl.BlockSpec(shape, lambda g: (0,) * len(shape), pipeline_mode=pl.Buffered(1))

    def slab_columns(shape, first):
        return [pl.BlockSpec(shape, lambda g, n=n: (0, n * chunks + chunk_of(g - first))) for n in range(narrow)]

    in_specs = [pl.BlockSpec(memory_space=pltpu.SMEM), *[whole(item.shape) for item in numbers],
                whole((rows, width)), whole((rows, width))]
    in_specs += [whole(dir_t.shape)]
    in_specs += [whole((rows, 1))] * 2 + [whole(vectors.shape)] + [pl.BlockSpec(memory_space=pl.ANY)] * 6
    in_specs += slab_columns((rows, 128), chunks)
    high = two * (wide_bits - 1)
    low = two * narrow_bits
    up_shape = (third,) + high + (2,) + low[1:] + (u_rows, 128)
    out_specs = [
        whole((rows, width)),
        pl.BlockSpec(memory_space=pl.ANY),
        pl.BlockSpec(memory_space=pl.ANY),
        whole((sum_rows, width)),
    ]
    out_shape = [
        jax.ShapeDtypeStruct((rows, width), jnp.bfloat16),
        jax.ShapeDtypeStruct(up_shape, jnp.bfloat16),
        jax.ShapeDtypeStruct((chunks,) + two * (steps - early) + (d_rows, 128), jnp.bfloat16),
        jax.ShapeDtypeStruct((sum_rows, width), jnp.float32),
    ]
    scratch = [
        pltpu.VMEM((rows, width), jnp.float32),
        pltpu.VMEM((rows, width), jnp.bfloat16),
        pltpu.VMEM((width, rows), jnp.bfloat16),
        pltpu.VMEM((width, rows), jnp.bfloat16),
        pltpu.VMEM((chunks,) + two * steps + (d_rows, 128), jnp.bfloat16),
        pltpu.VMEM((chunks,) + high + low + (u_rows, 128), jnp.bfloat16),
        pltpu.VMEM((chunks,) + high + low[1:] + (u_rows, 128), jnp.bfloat16),
    ]
    scratch += [pltpu.VMEM((chunks,) + two * (steps - 1 - s) + (d_rows, 128), jnp.bfloat16) for s in range(early)]
    scratch += [pltpu.VMEM((rows, segments), jnp.bfloat16), pltpu.VMEM((segments, width), jnp.bfloat16)]
    scratch += [pltpu.VMEM((128, width), jnp.bfloat16)]
    scratch += [pltpu.VMEM((wide, segments // wide, 128), jnp.float32)] * 4
    far = (normed_two, hidden_low, active, down_weight, up_weight, normed_one)
    scratch += [pltpu.VMEM(item.shape, item.dtype) for item in far]
    sems = chunks * early + chunks + 2 * (wide - 1)
    scratch += [pltpu.SemaphoreType.DMA((sems,)), pltpu.SemaphoreType.DMA((sems,)), pltpu.SemaphoreType.DMA((2 * chunks + len(far),))]
    return pl.pallas_call(
        kernel,
        grid=(2 * chunks,),
        in_specs=in_specs,
        out_specs=out_specs,
        out_shape=out_shape,
        scratch_shapes=scratch,
        compiler_params=pltpu.CompilerParams(collective_id=0, has_side_effects=True, vmem_limit_bytes=60 << 20),
        name="ffn_backward",
    )(lengths, *numbers, encoded, cotangent, dir_t, inverse_two, inverse_one, vectors,
      *far, *([slope] * narrow))


def attention_backward(grad_attended, mixed, out_weight, queries, keys, values, attention, tokens, qkv_weight, up_grads,
                       down_grads, sums):
    rows, width = tokens.shape
    docs, _, length, _ = attention.shape
    pairs = width // 128
    names = axis_bits()
    steps = len(names)
    wide, narrow = lax.axis_size("wide"), lax.axis_size("narrow")
    wide_bits, narrow_bits = wide.bit_length() - 1, narrow.bit_length() - 1
    half = narrow // 2
    half_bits = narrow_bits - 1
    lanes = width // half
    q_rows, o_rows = 3 * width // wide // 2, width // wide // 2
    q_parts = lanes // 128
    orders = link_orders()
    ups = up_grads.shape[0]
    u_rows = up_grads.shape[-2]
    attn_steps = docs * pairs
    token_block = 256
    token_steps = rows // token_block
    first_q = 1 + attn_steps
    first_t = first_q + q_parts
    grid = first_t + token_steps
    downs, d_rows = down_grads.shape[0], down_grads.shape[-2]
    down_steps = len(down_grads.shape) - 3
    cuts = [(0, q_rows // 32 * 16), (q_rows // 32 * 16, q_rows)]
    u_cuts = [(0, u_rows // 2), (u_rows // 2, u_rows)]
    up_count, out_count = ups * len(u_cuts), q_parts
    first_part = up_count + out_count
    first_down = first_part + q_parts * len(cuts)
    count = first_down + downs
    small_rows = sums.shape[0]
    late_rows = pl.cdiv(2 * pairs, 8) * 8
    s_cuts = [(0, small_rows // 4), (small_rows // 4, small_rows // 2), (small_rows // 2, small_rows)]

    def bits_of(number, count):
        return tuple((number >> bit) & 1 for bit in reversed(range(count)))

    def kernel(*refs):
        (ga_hbm, mix_hbm, ow_hbm, q_ref, k_ref, v_ref, att_ref, tok_hbm, qw_hbm, up_hbm, down_hbm, small) = refs[:12]
        tokens_out, up_out, out_out, qkv_out, down_out, small_out, late_out = refs[12:19]
        rest = list(refs[19:])
        gm, mix_pair, gqkv_t, up_own, out_own, qkv_own = rest[:6]
        rest = rest[6:]
        up_received = [rest[i * (steps - 1) : (i + 1) * (steps - 1)] for i in range(len(u_cuts))]
        rest = rest[len(u_cuts) * (steps - 1) :]
        out_received, rest = rest[:steps], rest[steps:]
        qkv_received, rest = [rest[i * steps : (i + 1) * steps] for i in range(len(cuts))], rest[len(cuts) * steps :]
        down_own, down_received, rest = rest[0], rest[1 : 1 + down_steps], rest[1 + down_steps :]
        small_sent, small_received, late_sent, late_received, swap_out, swap_qkv, tok, qw, ga, mix, ow = rest[:11]
        send_sems, recv_sems, local_sems = rest[11:]
        pid = pl.program_id(0)
        place = Place()
        core = place.bit["narrow", 0]
        pieces = []
        for low, high in u_cuts:
            for part in range(ups):
                cut = len(pieces) // ups
                pieces.append(Halving(place, names[:-1], orders[part % 3][1:], up_hbm.at[part], up_own.at[part],
                                      [r.at[part] for r in up_received[cut]], send_sems, recv_sems, len(pieces) * steps,
                                      (slice(low, high), slice(None))))
        for part in range(out_count):
            pieces.append(Halving(place, names, orders[part % 3], out_own.at[part], out_own.at[part],
                                  [r.at[part] for r in out_received], send_sems, recv_sems, len(pieces) * steps))
        for part in range(q_parts):
            for cut, (low, high) in enumerate(cuts):
                pieces.append(Halving(place, names, orders[part % 3], qkv_own.at[part], qkv_own.at[part],
                                      [r.at[part] for r in qkv_received[cut]], send_sems, recv_sems, len(pieces) * steps,
                                      (slice(low, high), slice(None))))
        for number in range(downs):
            order = orders[number % 3][steps - down_steps :]
            pieces.append(Halving(place, [name for name in names if name in order], order, down_own.at[number],
                                  down_own.at[number], [r.at[number] for r in down_received], send_sems, recv_sems,
                                  len(pieces) * steps))
        base = count * steps

        def all_sum(sent, received, first, order=0, rows=slice(None)):
            made = []
            for step in range(steps):
                made.append(pltpu.make_async_remote_copy(
                    src_ref=sent.at[step, rows], dst_ref=received.at[step, rows], send_sem=send_sems.at[first + step],
                    recv_sem=recv_sems.at[first + step], device_id=place.across(orders[order][step]),
                    device_id_type=MESH_ID))
            return made

        small_copies = [
            all_sum(small_sent, small_received, base + (2 + q_parts * len(cuts) + i) * steps + out_count, i, slice(low, high))
            for i, (low, high) in enumerate(s_cuts)
        ]
        late_copies = [all_sum(late_sent, late_received, base + steps)]
        swap_refs = [swap_out.at[part, core] for part in range(out_count)]
        swap_refs += [swap_qkv.at[part, core, low:high] for part in range(q_parts) for low, high in cuts]
        swaps = [pltpu.make_async_remote_copy(
            src_ref=ref, dst_ref=ref, send_sem=send_sems.at[base + 2 * steps + slot],
            recv_sem=recv_sems.at[base + 2 * steps + slot], device_id=place.across(("narrow", 0)),
            device_id_type=MESH_ID) for slot, ref in enumerate(swap_refs)]
        local = []
        for number in range(ups):
            keep = pieces[number].region(0, True)[: -2]
            local.append(pltpu.make_async_copy(up_hbm.at[number].at[keep], up_own.at[number].at[keep], local_sems.at[number]))

        loads = [pltpu.make_async_copy(tok_hbm, tok, local_sems.at[ups]),
                 pltpu.make_async_copy(qw_hbm, qw, local_sems.at[ups + 1])]
        first_loads = [pltpu.make_async_copy(source, target, local_sems.at[ups + 3 + i])
                       for i, (source, target) in enumerate(((ga_hbm, ga), (mix_hbm, mix), (ow_hbm, ow)))]
        down_load = pltpu.make_async_copy(down_hbm, down_own, local_sems.at[ups + 2])

        def advance(number, step):
            item = pieces[number]
            if step == 0 and number < ups:
                local[number].wait()
            total = item.add(step)
            if total is None:
                item.send(step + 1)
            elif number < up_count:
                cut, part = divmod(number, ups)
                up_out[u_cuts[cut][0] : u_cuts[cut][1], part * 128 : (part + 1) * 128] = total
            elif number >= first_down:
                number -= first_down
                j = number // 2 + downs // 2 * (number % 2)
                down_out[:, j * 128 : (j + 1) * 128] = total
            else:
                if number < first_part:
                    swap_out[number - up_count, core] = total
                else:
                    part, cut = divmod(number - first_part, len(cuts))
                    swap_qkv[part, core, cuts[cut][0] : cuts[cut][1]] = total
                swaps[number - up_count].start()

        def advance_small(lanes, sent, received, out, step):
            for copies in lanes:
                copies[step].wait_recv()
            total = sent[step] + received[step]
            if step + 1 < steps:
                sent[step + 1] = total
                for copies in lanes:
                    copies[step + 1].start()
            else:
                out[...] = total

        @pl.when(pid == 0)
        def _():
            place.greet()
            for number in range(up_count):
                pieces[number].send(0)
            for number in range(ups):
                local[number].start()
            for load in first_loads:
                load.start()
            small_sent[0] = small[...]
            for copies in small_copies:
                copies[0].start()
            down_load.start()
            for load in loads:
                load.start()
            for load in first_loads:
                load.wait()
            grads_t = ga[...].T
            result = jnp.dot(grads_t, mix[...], preferred_element_type=jnp.float32).astype(jnp.bfloat16)
            for w in range(wide):
                for h in range(2):
                    for y in range(half):
                        at = (w * 2 + h) * o_rows
                        for part in range(out_count):
                            first = y * lanes + part * 128
                            out_own[(part,) + bits_of(w, wide_bits) + bits_of(y, half_bits) + (h,)] = result[
                                at : at + o_rows, first : first + 128
                            ]
            for part in range(out_count):
                pieces[up_count + part].send(0)
            grad_mixed = dot_last(ga[...], ow[...]).astype(jnp.bfloat16)
            for pair in range(pairs):
                gm[pair] = grad_mixed[:, pair * 128 : (pair + 1) * 128]
                mix_pair[pair] = mix[:, pair * 128 : (pair + 1) * 128]
            down_load.wait()
            for number in range(downs):
                pieces[first_down + number].send(0)

        @pl.when((pid >= 1) & (pid < first_q))
        def _():
            number = pid - 1
            pair, doc = number // docs, number % docs
            some = pl.ds(pl.multiple_of(doc * length, length), length)
            lane = lax.broadcasted_iota(jnp.int32, (1, 128), 1)
            scaled, keys, values = q_ref[...] * jnp.bfloat16(HEAD_DIM**-0.5), k_ref[...], v_ref[...]
            grads = gm[pair, some, :]
            product = grads.astype(jnp.float32) * mix_pair[pair, some, :].astype(jnp.float32)
            queries_t, grads_t = scaled.T, grads.T
            zero = jnp.zeros_like(grads)
            query_parts = []
            for head in range(2):
                inside = (lane // HEAD_DIM) == head
                at = head * HEAD_DIM
                attention = att_ref[0, head]
                chance = dot_last(jnp.where(inside, grads, zero), values)
                inner = jnp.sum(jnp.where(inside, product, 0.0), -1, keepdims=True)
                grad_scores = (attention.astype(jnp.float32) * (chance - inner)).astype(jnp.bfloat16)
                query_parts.append(jnp.dot(grad_scores, keys, preferred_element_type=jnp.float32))
                key_t = jnp.dot(queries_t[at : at + HEAD_DIM], grad_scores, preferred_element_type=jnp.float32)
                value_t = jnp.dot(grads_t[at : at + HEAD_DIM], attention, preferred_element_type=jnp.float32)
                row = pair * 128 + at
                gqkv_t[pl.ds(pl.multiple_of(width + row, HEAD_DIM), HEAD_DIM), some] = key_t.astype(jnp.bfloat16)
                gqkv_t[pl.ds(pl.multiple_of(2 * width + row, HEAD_DIM), HEAD_DIM), some] = value_t.astype(jnp.bfloat16)
            grad_query = jnp.where(lane < HEAD_DIM, query_parts[0], query_parts[1]) * HEAD_DIM**-0.5
            gqkv_t[pl.ds(pl.multiple_of(pair * 128, 128), 128), some] = grad_query.astype(jnp.bfloat16).T

        for part in range(q_parts):
            @pl.when(pid == first_q + part)
            def _():
                if part == 0:
                    for load in loads:
                        load.wait()
                    ones = jnp.ones((8, rows), jnp.bfloat16)
                    for which in range(2):
                        totals = dot_last(ones, gqkv_t[2 * which * width : (2 * which + 1) * width, :])
                        for j in range(pairs):
                            late_sent[0, which * pairs + j : which * pairs + j + 1, :] = totals[
                                :1, j * 128 : (j + 1) * 128
                            ]
                    late_sent[0, 2 * pairs :, :] = jnp.zeros((late_rows - 2 * pairs, 128), jnp.float32)
                    late_copies[0][0].start()
                columns = jnp.concatenate(
                    [tok[:, y * lanes + part * 128 : y * lanes + (part + 1) * 128] for y in range(half)], axis=1
                )
                result = jnp.dot(gqkv_t[...], columns, preferred_element_type=jnp.float32).astype(jnp.bfloat16)
                for w in range(wide):
                    for h in range(2):
                        for y in range(half):
                            at = (w * 2 + h) * q_rows
                            qkv_own[(part,) + bits_of(w, wide_bits) + bits_of(y, half_bits) + (h,)] = result[
                                at : at + q_rows, y * 128 : (y + 1) * 128
                            ]
                for cut in range(len(cuts)):
                    pieces[first_part + part * len(cuts) + cut].send(0)

        @pl.when(pid >= first_t)
        def _():
            at = pl.multiple_of((pid - first_t) * token_block, token_block)
            some = pl.ds(at, token_block)
            grad_t = jnp.dot(qw[...], gqkv_t[:, some], preferred_element_type=jnp.float32)
            tokens_out[...] = (grad_t.T + ga[some, :].astype(jnp.float32)).astype(jnp.bfloat16)

        plan, small_plan, late_plan = {}, {}, {}
        for cut, times in enumerate(((5, 9, 12, 14), (8, 10, 13, 15))):
            for step, at in enumerate(times):
                for part in range(ups):
                    plan.setdefault(at, []).append((cut * ups + part, step))
        for step, at in enumerate((1, 9, 12, 14, 15)):
            for part in range(out_count):
                plan.setdefault(at, []).append((up_count + part, step))
        for step, at in enumerate((4, 8)):
            for number in range(downs):
                plan.setdefault(at, []).append((first_down + number, step))
        for number in range(first_part, first_down):
            for step in range(steps):
                at = first_q + (number - first_part) // len(cuts) + 1 if step == 0 else grid - 1
                plan.setdefault(at, []).append((number, step))
        for step, at in enumerate((3, 7, 9, 11, 13)):
            small_plan[at] = step
        late_plan[first_q + 2] = 0
        for at in range(grid):
            @pl.when(pid == at)
            def _():
                if at in small_plan:
                    advance_small(small_copies, small_sent, small_received, small_out, small_plan[at])
                for number, step in sorted(plan.get(at, []), key=lambda entry: (entry[1], entry[0])):
                    if at == grid - 1 and number == first_part:
                        advance_small(late_copies, late_sent, late_received, late_out, step)
                    advance(number, step)
                if at in late_plan:
                    advance_small(late_copies, late_sent, late_received, late_out, late_plan[at])
                if at == grid - 1:
                    for copy in swaps:
                        copy.wait()

                    def own_lanes(lanes):
                        size = lanes.shape[1] // 2
                        return jnp.where(core == 0, lanes[:, :size], lanes[:, size:])

                    out_out[...] = own_lanes(jnp.concatenate(
                        [swap_out[part].reshape(2 * o_rows, 128) for part in range(out_count)], axis=1))
                    qkv_out[...] = own_lanes(jnp.concatenate(
                        [swap_qkv[part].reshape(2 * q_rows, 128) for part in range(q_parts)], axis=1))
                    for item in pieces:
                        item.close()
                    for copies in small_copies + late_copies:
                        for copy in copies:
                            copy.wait_send()

    def whole(shape):
        return pl.BlockSpec(shape, lambda g: (0,) * len(shape), pipeline_mode=pl.Buffered(1))

    def number_of(g):
        return jnp.clip(g - 1, 0, attn_steps - 1)

    tile = pl.BlockSpec((length, 128), lambda g: (number_of(g) % docs, number_of(g) // docs))

    two = (2,)
    any_space = pl.BlockSpec(memory_space=pl.ANY)
    in_specs = [any_space, any_space, any_space, tile, tile, tile]
    in_specs += [pl.BlockSpec((1, 2, length, length), lambda g: (number_of(g) % docs, number_of(g) // docs, 0, 0))]
    in_specs += [any_space, any_space, any_space, any_space, whole((small_rows, width))]
    out_shape = [
        jax.ShapeDtypeStruct((rows, width), jnp.bfloat16),
        jax.ShapeDtypeStruct((u_rows, ups * 128), jnp.float32),
        jax.ShapeDtypeStruct((2 * o_rows, lanes // 2), jnp.float32),
        jax.ShapeDtypeStruct((2 * q_rows, lanes // 2), jnp.float32),
        jax.ShapeDtypeStruct((d_rows, downs * 128), jnp.float32),
        jax.ShapeDtypeStruct((small_rows, width), jnp.float32),
        jax.ShapeDtypeStruct((late_rows, 128), jnp.float32),
    ]
    wide_dims, half_dims = two * wide_bits, two * half_bits
    scratch = [
        pltpu.VMEM((pairs, rows, 128), jnp.bfloat16),
        pltpu.VMEM((pairs, rows, 128), jnp.bfloat16),
        pltpu.VMEM((3 * width, rows), jnp.bfloat16),
        pltpu.VMEM(up_grads.shape, jnp.bfloat16),
        pltpu.VMEM((out_count,) + wide_dims + half_dims + two + (o_rows, 128), jnp.bfloat16),
        pltpu.VMEM((q_parts,) + wide_dims + half_dims + two + (q_rows, 128), jnp.bfloat16),
    ]
    for low, high in u_cuts:
        scratch += [pltpu.VMEM((ups,) + two * (steps - 2 - s) + (high - low, 128), jnp.bfloat16) for s in range(steps - 1)]
    scratch += [pltpu.VMEM((out_count,) + two * (steps - 1 - s) + (o_rows, 128), jnp.bfloat16) for s in range(steps)]
    for low, high in cuts:
        scratch += [pltpu.VMEM((q_parts,) + two * (steps - 1 - s) + (high - low, 128), jnp.bfloat16) for s in range(steps)]
    scratch += [pltpu.VMEM(down_grads.shape, jnp.bfloat16)]
    scratch += [pltpu.VMEM((downs,) + two * (down_steps - 1 - s) + (d_rows, 128), jnp.bfloat16) for s in range(down_steps)]
    scratch += [pltpu.VMEM((steps, small_rows, width), jnp.float32)] * 2
    scratch += [pltpu.VMEM((steps, late_rows, 128), jnp.float32)] * 2
    scratch += [pltpu.VMEM((out_count, 2, o_rows, 128), jnp.float32), pltpu.VMEM((q_parts, 2, q_rows, 128), jnp.float32)]
    scratch += [pltpu.VMEM(tokens.shape, jnp.bfloat16), pltpu.VMEM(qkv_weight.shape, jnp.bfloat16)]
    scratch += [pltpu.VMEM(item.shape, jnp.bfloat16) for item in (grad_attended, mixed, out_weight)]
    sems = count * steps + (2 + q_parts * len(cuts) + len(s_cuts)) * steps + out_count
    scratch += [pltpu.SemaphoreType.DMA((sems,)), pltpu.SemaphoreType.DMA((sems,)), pltpu.SemaphoreType.DMA((ups + 6,))]
    return pl.pallas_call(
        kernel,
        grid=(grid,),
        in_specs=in_specs,
        out_specs=[pl.BlockSpec((token_block, width), lambda g: (jnp.clip(g - first_t, 0, token_steps - 1), 0))]
        + [whole(item.shape) for item in out_shape[1:]],
        out_shape=out_shape,
        scratch_shapes=scratch,
        compiler_params=pltpu.CompilerParams(collective_id=1, has_side_effects=True, vmem_limit_bytes=60 << 20),
        name="attention_backward",
    )(grad_attended, mixed, out_weight, queries, keys, values, attention, tokens, qkv_weight, up_grads, down_grads, sums)


def hand_out(grad_tokens, sums, late, narrow, classes, turned, *blocks):
    rows, width = grad_tokens.shape
    steps = 2
    first_dir = 6 + narrow

    def kernel(tokens_ref, sums_ref, late_ref, *refs):
        ins, outs = refs[: len(blocks)], refs[len(blocks) :]
        outs[0][...] = tokens_ref[...]

        @pl.when(pl.program_id(0) == 0)
        def _():
            for source, target in zip(ins, outs[1:]):
                target[...] = source[...] if source.shape == target.shape else source[...].T
            singles = outs[1 + len(blocks) :]
            for number in range(6):
                singles[number][...] = sums_ref[number, :]
            for number in range(2):
                for j in range(width // 128):
                    singles[6 + number][j * 128 : (j + 1) * 128] = late_ref[number * (width // 128) + j, :]
            for number in range(narrow):
                singles[8][number * width : (number + 1) * width] = sums_ref[6 + number, :]
            singles[9][...] = sums_ref[first_dir : first_dir + 2 * classes, :]
            singles[10][...] = sums_ref[first_dir + 2 * classes, :classes]

    def whole(shape):
        return pl.BlockSpec(shape, lambda g: (0,) * len(shape))

    some = pl.BlockSpec((rows // steps, width), lambda g: (g, 0))
    small = [(width,)] * 8 + [(narrow * width,), (2 * classes, width), (classes,)]
    shapes = [block.shape[::-1] if number in turned else block.shape for number, block in enumerate(blocks)]
    out_shape = [jax.ShapeDtypeStruct((rows, width), jnp.bfloat16)]
    out_shape += [jax.ShapeDtypeStruct(shape, jnp.float32) for shape in shapes + small]
    return pl.pallas_call(
        kernel,
        grid=(steps,),
        in_specs=[some] + [whole(item.shape) for item in (sums, late) + blocks],
        out_specs=[some] + [whole(item.shape) for item in out_shape[1:]],
        out_shape=out_shape,
        name="hand_out",
    )(grad_tokens, sums, late, *blocks)


def on_device_fast(
    tokens,
    doc_lengths,
    qkv_weight,
    query_bias,
    value_bias,
    out_weight,
    out_bias,
    first_gain,
    first_shift,
    up_weight,
    up_bias,
    down_weight,
    down_bias,
    second_gain,
    second_shift,
    dir_weight,
    dir_bias,
    segment_rows,
    segment_slots,
    pair_rows,
    pair_labels,
    out_cotangent,
):
    doc_count, length, model_width = tokens.shape
    token_rows = tokens.reshape(doc_count * length, model_width)
    singles = (out_bias, first_gain, first_shift, down_bias, second_gain, second_shift, query_bias, value_bias)
    vectors, queries, keys, values, attention, mixed, *kept = layer_forward(
        doc_lengths, token_rows, qkv_weight, out_weight, up_weight, down_weight, singles + (dir_bias, up_bias)
    )
    hidden_low, normed_one, inverse_one, active, slope, normed_two, inverse_two, encoded_rows = kept
    classes_count = dir_weight.shape[1]
    grad_attended, up_blocks, down_blocks, sums = ffn_backward(
        doc_lengths, segment_rows, segment_slots, pair_rows[0].T, pair_labels, encoded_rows, out_cotangent.reshape(-1, model_width), dir_weight.T, vectors,
        normed_two, inverse_two, active, slope,
        hidden_low, down_weight, up_weight, normed_one, inverse_one,
    )
    grad_tokens, out_up, out_out, out_qkv, out_down, sums, late = attention_backward(
        grad_attended, mixed, out_weight, queries, keys, values, attention, token_rows, qkv_weight, up_blocks,
        down_blocks, sums,
    )
    grad_tokens, out_up, out_out, out_qkv, out_down, *smalls = hand_out(
        grad_tokens, sums, late, lax.axis_size("narrow"), classes_count, (1, 2), out_up, out_out, out_qkv, out_down
    )
    return (
        encoded_rows.reshape(tokens.shape),
        grad_tokens.reshape(tokens.shape),
        out_qkv,
        smalls[6],
        smalls[7],
        out_out,
        smalls[5],
        smalls[3],
        smalls[4],
        out_up,
        smalls[8],
        out_down.T,
        smalls[2],
        smalls[0],
        smalls[1],
        smalls[9].reshape(2, classes_count, model_width).transpose(0, 2, 1).reshape(2 * model_width, classes_count),
        smalls[10],
    )


def on_device(
    tokens,
    doc_lengths,
    qkv_weight,
    query_bias,
    value_bias,
    out_weight,
    out_bias,
    first_gain,
    first_shift,
    up_weight,
    up_bias,
    down_weight,
    down_bias,
    second_gain,
    second_shift,
    dir_weight,
    dir_bias,
    segment_rows,
    segment_slots,
    pair_rows,
    pair_labels,
    out_cotangent,
):
    doc_count, length, model_width = tokens.shape
    score_scale = HEAD_DIM ** (-0.5)
    token_rows = tokens.reshape(doc_count * length, model_width)
    allowed = lax.broadcasted_iota(jnp.int32, (doc_count, length), 1) < doc_lengths[:, None]
    allowed_rows = allowed.reshape(-1, 1).astype(jnp.float32)
    bias_row = jnp.concatenate([query_bias, jnp.zeros_like(query_bias), value_bias]).astype(
        jnp.float32
    )
    qkv = (jnp.dot(token_rows, qkv_weight, preferred_element_type=jnp.float32) + bias_row).astype(
        jnp.bfloat16
    )

    def split_heads(doc_block, which):
        return doc_block[:, which * model_width : (which + 1) * model_width].reshape(
            length, HEADS, HEAD_DIM
        )

    def scores_of(queries, key_rows, doc_mask):
        scores = (
            jnp.einsum("qhd,khd->hqk", queries, key_rows, preferred_element_type=jnp.float32)
            * score_scale
        )
        return jnp.where(doc_mask[None, None, :], scores, MASKED)

    mixed_parts = []
    log_totals = []
    for doc_index in range(doc_count):
        doc_block = qkv[doc_index * length : (doc_index + 1) * length]
        queries = split_heads(doc_block, 0)
        key_rows = split_heads(doc_block, 1)
        value_rows = split_heads(doc_block, 2)
        scores = scores_of(queries, key_rows, allowed[doc_index])
        highest = jnp.max(scores, -1, keepdims=True)
        powers = jnp.exp(scores - highest)
        summed = jnp.sum(powers, -1, keepdims=True)
        attention = (powers / summed).astype(jnp.bfloat16)
        log_totals.append(highest + jnp.log(summed))
        mixed_parts.append(
            jnp.einsum(
                "hqk,khd->qhd", attention, value_rows, preferred_element_type=jnp.float32
            ).reshape(length, model_width)
        )
    mixed = jnp.concatenate(mixed_parts).astype(jnp.bfloat16)
    attended = jnp.dot(mixed, out_weight, preferred_element_type=jnp.float32) + out_bias.astype(
        jnp.float32
    )
    resid_one = token_rows.astype(jnp.float32) + attended
    hidden_one, normed_one, inverse_one = norm_forward(
        resid_one, first_gain.astype(jnp.float32), first_shift.astype(jnp.float32)
    )
    hidden_low = hidden_one.astype(jnp.bfloat16)
    upper_pre = jnp.dot(hidden_low, up_weight, preferred_element_type=jnp.float32) + up_bias.astype(
        jnp.float32
    )
    cumulative = normal_cdf(upper_pre)
    active = (upper_pre * cumulative).astype(jnp.bfloat16)
    lowered = jnp.dot(active, down_weight, preferred_element_type=jnp.float32) + down_bias.astype(
        jnp.float32
    )
    resid_two = hidden_one + lowered
    second_float = second_gain.astype(jnp.float32)
    normed_out, normed_two, inverse_two = norm_forward(
        resid_two, second_float, second_shift.astype(jnp.float32)
    )
    encoded_rows = (normed_out * allowed_rows).astype(jnp.bfloat16)
    doc_starts = lax.broadcasted_iota(jnp.int32, (doc_count, 1), 0) * length
    picked_rows = (segment_rows + doc_starts).reshape(-1)
    picked = encoded_rows[picked_rows]
    slots = segment_slots.reshape(-1)
    outgoing = jnp.zeros_like(picked).at[slots].set(picked)
    arrived = lax.all_to_all(outgoing, "wide", split_axis=0, concat_axis=0, tiled=True)
    pairs = pair_rows.reshape(-1, 2)
    labels = pair_labels.reshape(-1)
    first_rows = arrived[pairs[:, 0]]
    second_rows = arrived[pairs[:, 1]]
    logits = (
        jnp.dot(first_rows, dir_weight[:model_width], preferred_element_type=jnp.float32)
        + jnp.dot(second_rows, dir_weight[model_width:], preferred_element_type=jnp.float32)
        + dir_bias.astype(jnp.float32)
    )
    powers_head = jnp.exp(logits - jnp.max(logits, -1, keepdims=True))
    chance = powers_head / jnp.sum(powers_head, -1, keepdims=True)
    classes = lax.broadcasted_iota(jnp.int32, logits.shape, 1)
    delta = chance - (labels[:, None] == classes).astype(jnp.float32)
    first_float = first_rows.astype(jnp.float32)
    second_rows_float = second_rows.astype(jnp.float32)
    grad_dir_weight = jnp.concatenate(
        [
            jnp.dot(first_float.T, delta, precision=EXACT, preferred_element_type=jnp.float32),
            jnp.dot(
                second_rows_float.T, delta, precision=EXACT, preferred_element_type=jnp.float32
            ),
        ]
    )
    grad_dir_bias = jnp.sum(delta, 0)
    dir_float = dir_weight.astype(jnp.float32)
    grad_first = jnp.dot(
        delta, dir_float[:model_width].T, precision=EXACT, preferred_element_type=jnp.float32
    )
    grad_second = jnp.dot(
        delta, dir_float[model_width:].T, precision=EXACT, preferred_element_type=jnp.float32
    )
    grad_arrived = jnp.zeros((arrived.shape[0], model_width), jnp.float32)
    grad_arrived = grad_arrived.at[pairs[:, 0]].add(grad_first).at[pairs[:, 1]].add(grad_second)
    returned = lax.all_to_all(
        grad_arrived.astype(jnp.bfloat16), "wide", split_axis=0, concat_axis=0, tiled=True
    )
    grad_picked = returned[slots].astype(jnp.float32)
    grad_encoded = (
        out_cotangent.reshape(-1, model_width).astype(jnp.float32).at[picked_rows].add(grad_picked)
    )
    grad_encoded = grad_encoded * allowed_rows
    grad_two, grad_second_gain, grad_second_shift = norm_backward(
        grad_encoded, normed_two, inverse_two, second_float
    )
    grad_lowered = grad_two.astype(jnp.bfloat16)
    grad_down_weight = jnp.einsum(
        "rf,rd->fd", active, grad_lowered, preferred_element_type=jnp.float32
    )
    grad_down_bias = jnp.sum(grad_lowered.astype(jnp.float32), 0)
    grad_active = jnp.einsum(
        "rd,fd->rf", grad_lowered, down_weight, preferred_element_type=jnp.float32
    )
    density = jnp.exp(-0.5 * upper_pre * upper_pre) * 0.3989422804014327
    grad_upper = (grad_active * (cumulative + upper_pre * density)).astype(jnp.bfloat16)
    grad_up_weight = jnp.einsum(
        "rd,rf->df", hidden_low, grad_upper, preferred_element_type=jnp.float32
    )
    grad_up_bias = jnp.sum(grad_upper.astype(jnp.float32), 0)
    grad_hidden = grad_two + jnp.einsum(
        "rf,df->rd", grad_upper, up_weight, preferred_element_type=jnp.float32
    )
    grad_one, grad_first_gain, grad_first_shift = norm_backward(
        grad_hidden, normed_one, inverse_one, first_gain.astype(jnp.float32)
    )
    grad_attended = grad_one.astype(jnp.bfloat16)
    grad_out_weight = jnp.einsum(
        "rd,re->de", mixed, grad_attended, preferred_element_type=jnp.float32
    )
    grad_out_bias = jnp.sum(grad_attended.astype(jnp.float32), 0)
    grad_mixed = jnp.einsum(
        "re,de->rd", grad_attended, out_weight, preferred_element_type=jnp.float32
    ).astype(jnp.bfloat16)
    grad_parts = []
    for doc_index in range(doc_count):
        doc_block = qkv[doc_index * length : (doc_index + 1) * length]
        queries = split_heads(doc_block, 0)
        key_rows = split_heads(doc_block, 1)
        value_rows = split_heads(doc_block, 2)
        scores = scores_of(queries, key_rows, allowed[doc_index])
        attention = jnp.exp(scores - log_totals[doc_index])
        grad_doc = grad_mixed[doc_index * length : (doc_index + 1) * length].reshape(
            length, HEADS, HEAD_DIM
        )
        grad_chance = jnp.einsum(
            "qhd,khd->hqk", grad_doc, value_rows, preferred_element_type=jnp.float32
        )
        inner = jnp.sum(grad_chance * attention, -1, keepdims=True)
        grad_scores = (attention * (grad_chance - inner)).astype(jnp.bfloat16)
        grad_query = (
            jnp.einsum("hqk,khd->qhd", grad_scores, key_rows, preferred_element_type=jnp.float32)
            * score_scale
        )
        grad_key = (
            jnp.einsum("hqk,qhd->khd", grad_scores, queries, preferred_element_type=jnp.float32)
            * score_scale
        )
        grad_value = jnp.einsum(
            "hqk,qhd->khd",
            attention.astype(jnp.bfloat16),
            grad_doc,
            preferred_element_type=jnp.float32,
        )
        grad_parts.append(
            jnp.concatenate(
                [
                    grad_query.reshape(length, model_width),
                    grad_key.reshape(length, model_width),
                    grad_value.reshape(length, model_width),
                ],
                axis=1,
            )
        )
    grad_qkv = jnp.concatenate(grad_parts).astype(jnp.bfloat16)
    grad_qkv_float = grad_qkv.astype(jnp.float32)
    grad_query_bias = jnp.sum(grad_qkv_float[:, :model_width], 0)
    grad_value_bias = jnp.sum(grad_qkv_float[:, 2 * model_width :], 0)
    grad_qkv_weight = jnp.einsum(
        "rd,re->de", token_rows, grad_qkv, preferred_element_type=jnp.float32
    )
    grad_tokens = (
        jnp.einsum("re,de->rd", grad_qkv, qkv_weight, preferred_element_type=jnp.float32) + grad_one
    ).astype(jnp.bfloat16)
    matrices = (grad_qkv_weight, grad_out_weight, grad_up_weight, grad_down_weight)
    partial_sums = (
        lax.psum_scatter(
            matrices[0].astype(jnp.bfloat16), "wide", scatter_dimension=1, tiled=True
        ).astype(jnp.float32),
        lax.psum_scatter(
            matrices[1].astype(jnp.bfloat16), "wide", scatter_dimension=1, tiled=True
        ).astype(jnp.float32),
        lax.psum_scatter(
            matrices[2].astype(jnp.bfloat16), "wide", scatter_dimension=1, tiled=True
        ).astype(jnp.float32),
        lax.psum_scatter(
            matrices[3].astype(jnp.bfloat16), "wide", scatter_dimension=1, tiled=True
        ).astype(jnp.float32),
    )
    summed_mats = (
        lax.psum_scatter(
            partial_sums[0].astype(jnp.bfloat16), "narrow", scatter_dimension=0, tiled=True
        ).astype(jnp.float32),
        lax.psum_scatter(
            partial_sums[1].astype(jnp.bfloat16), "narrow", scatter_dimension=0, tiled=True
        ).astype(jnp.float32),
        lax.psum_scatter(
            partial_sums[2].astype(jnp.bfloat16), "narrow", scatter_dimension=0, tiled=True
        ).astype(jnp.float32),
        lax.psum_scatter(
            partial_sums[3].astype(jnp.bfloat16), "narrow", scatter_dimension=0, tiled=True
        ).astype(jnp.float32),
    )
    smalls = lax.psum(
        (
            grad_query_bias,
            grad_value_bias,
            grad_out_bias,
            grad_first_gain,
            grad_first_shift,
            grad_up_bias,
            grad_down_bias,
            grad_second_gain,
            grad_second_shift,
            grad_dir_weight,
            grad_dir_bias,
        ),
        ("wide", "narrow"),
    )
    return (
        encoded_rows.reshape(tokens.shape),
        grad_tokens.reshape(tokens.shape),
        summed_mats[0],
        smalls[0],
        smalls[1],
        summed_mats[1],
        smalls[2],
        smalls[3],
        smalls[4],
        summed_mats[2],
        smalls[5],
        summed_mats[3],
        smalls[6],
        smalls[7],
        smalls[8],
        smalls[9],
        smalls[10],
    )


def fits_blocks(mesh):
    wide, narrow = mesh.shape["wide"], mesh.shape["narrow"]
    width, ff = HEADS * HEAD_DIM, 4 * HEADS * HEAD_DIM
    if wide != 2 * narrow or narrow < 4 or narrow & (narrow - 1):
        return False
    lanes = (ff // narrow, ff // wide, 2 * width // narrow)
    rows = (width // wide, width // narrow, width // wide // 2, 3 * width // wide // 2)
    return all(size % 128 == 0 for size in lanes) and all(size % 16 == 0 for size in rows)


def solution(mesh):
    placed = (
        P(("wide", "narrow"), None, None),
        P(("wide", "narrow")),
        P(),
        P(),
        P(),
        P(),
        P(),
        P(),
        P(),
        P(),
        P(),
        P(),
        P(),
        P(),
        P(),
        P(),
        P(),
        P(("wide", "narrow"), None),
        P(("wide", "narrow"), None),
        P(("wide", "narrow"), None, None),
        P(("wide", "narrow"), None),
        P(("wide", "narrow"), None, None),
    )
    return jax.shard_map(
        on_device_fast if fits_blocks(mesh) else on_device,
        mesh=mesh,
        in_specs=placed,
        out_specs=(
            P(("wide", "narrow"), None, None),
            P(("wide", "narrow"), None, None),
            P("narrow", "wide"),
            P(),
            P(),
            P("narrow", "wide"),
            P(),
            P(),
            P(),
            P("narrow", "wide"),
            P(),
            P("narrow", "wide"),
            P(),
            P(),
            P(),
            P(),
            P(),
        ),
        check_vma=False,
    )
```

```python
import jax
import jax.numpy as jnp
from jax import lax
from jax.experimental import pallas as pl
from jax.experimental.pallas import tpu as pltpu
from jax.sharding import PartitionSpec as P

HEADS = 12
HEAD_DIM = 64


EXACT = lax.Precision.HIGHEST
MASKED = -1e30
EPSILON = 1e-05


def norm_forward(values, gain, shift):
    center = jnp.mean(values, -1, keepdims=True)
    centered = values - center
    inverse = lax.rsqrt(jnp.mean(centered * centered, -1, keepdims=True) + EPSILON)
    normed = centered * inverse
    return (normed * gain + shift, normed, inverse)


def norm_backward(grad, normed, inverse, gain):
    scaled = grad * gain
    first_mean = jnp.mean(scaled, -1, keepdims=True)
    second_mean = jnp.mean(scaled * normed, -1, keepdims=True)
    return (
        (scaled - first_mean - normed * second_mean) * inverse,
        jnp.sum(grad * normed, 0),
        jnp.sum(grad, 0),
    )


def normal_cdf(values):
    return 0.5 * (1.0 + lax.erf(values * 0.7071067811865476))


MESH_ID = pl.DeviceIdType.MESH


def axis_bits():
    names = []
    for axis in ("wide", "narrow"):
        count = lax.axis_size(axis).bit_length() - 1
        names += [(axis, bit) for bit in reversed(range(count))]
    return names


class Place:
    def __init__(self):
        self.index = {axis: lax.axis_index(axis) for axis in ("wide", "narrow")}
        self.names = axis_bits()
        self.bit = {name: (self.index[name[0]] // (1 << name[1])) % 2 for name in self.names}

    def across(self, name):
        axis, bit = name
        target = dict(self.index)
        target[axis] = target[axis] + (1 << bit) - (2 << bit) * self.bit[name]
        return target

    def ahead(self, offset):
        target = dict(self.index)
        target["wide"] = (target["wide"] + offset) % lax.axis_size("wide")
        return target

    def greet(self, all_wide=False):
        barrier = pltpu.get_barrier_semaphore()
        targets = [self.across(name) for name in self.names if not (all_wide and name[0] == "wide")]
        if all_wide:
            targets += [self.ahead(offset) for offset in range(1, lax.axis_size("wide"))]
        for target in targets:
            pl.semaphore_signal(barrier, inc=1, device_id=target, device_id_type=MESH_ID)
        pl.semaphore_wait(barrier, len(targets))


class Halving:
    def __init__(self, place, names, order, source, own, received, send_sems, recv_sems, first_sem, tail=()):
        self.place, self.names, self.order = place, names, order
        self.source, self.own, self.received = source, own, received
        self.last = True
        self.send_sems, self.recv_sems, self.first_sem, self.tail = send_sems, recv_sems, first_sem, tail

    def region(self, step, mine):
        index = []
        for name in self.names:
            if name in self.order[:step]:
                index.append(self.place.bit[name])
            elif name == self.order[step]:
                index.append(self.place.bit[name] if mine else 1 - self.place.bit[name])
            else:
                index.append(slice(None))
        return tuple(index) + self.tail

    def copy(self, step):
        held = self.source if step == 0 else self.own
        return pltpu.make_async_remote_copy(
            src_ref=held.at[self.region(step, False)],
            dst_ref=self.received[step],
            send_sem=self.send_sems.at[self.first_sem + step],
            recv_sem=self.recv_sems.at[self.first_sem + step],
            device_id=self.place.across(self.order[step]),
            device_id_type=MESH_ID,
        )

    def send(self, step):
        self.copy(step).start()

    def add(self, step):
        self.copy(step).wait_recv()
        mine = self.region(step, True)
        if step + 1 < len(self.order) or not self.last:
            self.own[mine] = self.own[mine] + self.received[step][...]
            return None
        return self.own[mine].astype(jnp.float32) + self.received[step][...].astype(jnp.float32)

    def merge(self, step):
        self.last = False
        self.add(step)

    def close(self):
        for step in range(len(self.order)):
            self.copy(step).wait_send()


def link_orders():
    wide = [("wide", bit) for bit in range(lax.axis_size("wide").bit_length() - 1)]
    narrow = [("narrow", bit) for bit in range(1, lax.axis_size("narrow").bit_length() - 1)]
    core, x, near, far = [("narrow", 0)], wide[:1], wide[1:-1], wide[-1:]
    return [core + narrow + x + near + far, core + x + near + narrow + far, core + near + narrow + x + far]


def layer_forward(lengths, tokens, qkv_weight, out_weight, up_weight, down_weight, singles):
    rows, width = tokens.shape
    ff = up_weight.shape[1]
    docs = lengths.shape[0]
    length = rows // docs
    pairs, chunks = width // 128, ff // width
    kinds = [item.shape[0] for item in singles]
    lines = sum(max(1, size // width) for size in kinds)
    row_block = 512

    def kernel(lens, tok, wq, wk, wv, ow, up, down, *refs):
        singles, refs = refs[: len(kinds)], refs[len(kinds) :]
        vec, q_out, k_out, v_out, attention_out, mixed_out = refs[:6]
        hid_out, n1_out, q1_out, act_out, slope_out, n2_out, q2_out, enc_out = refs[6:14]
        mixed, hidden, total = refs[14:]
        pid = pl.program_id(0)

        def each_block(body):
            def step(i, carry):
                body(pl.multiple_of(i * row_block, row_block))
                return carry

            lax.fori_loop(0, rows // row_block, step, 0)

        @pl.when(pid == 0)
        def _():
            at = 0
            for single, size in zip(singles, kinds):
                values = single[...].astype(jnp.float32)
                for first in range(0, size, width):
                    some = min(size, width)
                    vec[at, :some] = values[first : first + some]
                    at += 1

        @pl.when(pid < pairs)
        def _():
            weights = jnp.concatenate([wq[...], wk[...], wv[...]], axis=1)
            at = pl.ds(pl.multiple_of(pid * 128, 128), 128)
            offsets = jnp.concatenate([vec[6:7, at], jnp.zeros((1, 128), jnp.float32), vec[7:8, at]], axis=1)
            qkv = (jnp.dot(tok[...], weights, preferred_element_type=jnp.float32) + offsets).astype(jnp.bfloat16)
            q_out[...] = qkv[:, :128]
            k_out[...] = qkv[:, 128:256]
            v_out[...] = qkv[:, 256:]
            first = lax.broadcasted_iota(jnp.int32, (1, 128), 1) < HEAD_DIM
            for doc in range(docs):
                some = slice(doc * length, (doc + 1) * length)
                queries = qkv[some, :128] * jnp.bfloat16(HEAD_DIM**-0.5)
                keys, values = qkv[some, 128:256], qkv[some, 256:]
                zero = jnp.zeros_like(queries)
                places = lax.broadcasted_iota(jnp.int32, (1, length), 1)
                bias = jnp.where(places < lens[doc], 0.0, MASKED)
                outs = []
                for head in range(2):
                    masked = jnp.where(first, queries, zero) if head == 0 else jnp.where(first, zero, queries)
                    scores = dot_last(masked, keys) + bias
                    powers = jnp.exp(scores - jnp.max(scores, -1, keepdims=True))
                    attention = (powers * (1.0 / jnp.sum(powers, -1, keepdims=True))).astype(jnp.bfloat16)
                    attention_out[doc, head] = attention
                    outs.append(jnp.dot(attention, values, preferred_element_type=jnp.float32))
                both = jnp.where(first, outs[0], outs[1]).astype(jnp.bfloat16)
                mixed_out[some, :] = both
                mixed[some, at] = both

        @pl.when(pid == pairs)
        def _():
            total[...] = jnp.dot(mixed[...], ow[...], preferred_element_type=jnp.float32)

            def body(at):
                some = pl.ds(at, row_block)
                summed = tok[some, :].astype(jnp.float32) + (total[some, :] + vec[0:1, :])
                out, normed, inverse = norm_forward(summed, vec[1:2, :], vec[2:3, :])
                hidden[some, :] = out
                hid_out[some, :] = out.astype(jnp.bfloat16)
                n1_out[some, :] = normed.astype(jnp.bfloat16)
                q1_out[some, :] = inverse
                total[some, :] = jnp.zeros_like(out)

            each_block(body)

        @pl.when(pid >= pairs)
        def _():
            offset = vec[pl.ds(pid - pairs + 9, 1), :]
            pre = jnp.dot(hid_out[...], up[...], preferred_element_type=jnp.float32) + offset
            cumulative = normal_cdf(pre)
            density = jnp.exp(-0.5 * pre * pre) * 0.3989422804014327
            active = (pre * cumulative).astype(jnp.bfloat16)
            act_out[...] = active
            slope_out[...] = (cumulative + pre * density).astype(jnp.bfloat16)
            total[...] += jnp.dot(active, down[...], preferred_element_type=jnp.float32)

        @pl.when(pid == pairs + chunks - 1)
        def _():
            def body(at):
                some = pl.ds(at, row_block)
                summed = hidden[some, :] + (total[some, :] + vec[3:4, :])
                out, normed, inverse = norm_forward(summed, vec[4:5, :], vec[5:6, :])
                n2_out[some, :] = normed.astype(jnp.bfloat16)
                q2_out[some, :] = inverse
                doc = at // length
                line = lax.broadcasted_iota(jnp.int32, (row_block, 1), 0) + (at - doc * length)
                enc_out[some, :] = jnp.where(line < lens[doc], out, 0.0).astype(jnp.bfloat16)

            each_block(body)

    def whole(shape):
        return pl.BlockSpec(shape, lambda g: (0,) * len(shape), pipeline_mode=pl.Buffered(1))

    def pair_of(g):
        return jnp.minimum(g, pairs - 1)

    def chunk_of(g):
        return jnp.clip(g - pairs, 0, chunks - 1)

    column = pl.BlockSpec((rows, 128), lambda g: (0, pair_of(g)))
    upper = pl.BlockSpec((rows, width), lambda g: (0, chunk_of(g)))
    full, one = whole((rows, width)), whole((rows, 1))
    in_specs = [pl.BlockSpec(memory_space=pltpu.SMEM), full]
    in_specs += [pl.BlockSpec((width, 128), lambda g, n=n: (0, n * pairs + pair_of(g))) for n in range(3)]
    in_specs += [whole((width, width)), pl.BlockSpec((width, width), lambda g: (0, chunk_of(g)))]
    in_specs += [pl.BlockSpec((width, width), lambda g: (chunk_of(g), 0))]
    in_specs += [whole(item.shape) for item in singles]
    low = jax.ShapeDtypeStruct((rows, width), jnp.bfloat16)
    inverse = jax.ShapeDtypeStruct((rows, 1), jnp.float32)
    high = jax.ShapeDtypeStruct((rows, ff), jnp.bfloat16)
    return pl.pallas_call(
        kernel,
        grid=(pairs + chunks,),
        in_specs=in_specs,
        out_specs=[whole((lines, width))] + [column] * 3
        + [pl.BlockSpec((docs, 2, length, length), lambda g: (0, pair_of(g), 0, 0)), column]
        + [full, full, one, upper, upper, full, one, full],
        out_shape=[jax.ShapeDtypeStruct((lines, width), jnp.float32)] + [low] * 3
        + [jax.ShapeDtypeStruct((docs, 2 * pairs, length, length), jnp.bfloat16), low]
        + [low, low, inverse, high, high, low, inverse, low],
        scratch_shapes=[pltpu.VMEM((rows, width), jnp.bfloat16)] + [pltpu.VMEM((rows, width), jnp.float32)] * 2,
        compiler_params=pltpu.CompilerParams(vmem_limit_bytes=60 << 20),
        name="layer_forward",
    )(lengths, tokens, qkv_weight, qkv_weight, qkv_weight, out_weight, up_weight, down_weight, *singles)


def dot_last(left, right):
    return lax.dot_general(left, right, (((1,), (1,)), ((), ())), preferred_element_type=jnp.float32)


def norm_back_rows(grad, normed, inverse, gain):
    scaled = grad * gain
    first = jnp.mean(scaled, -1, keepdims=True)
    second = jnp.mean(scaled * normed, -1, keepdims=True)
    return (scaled - first - normed * second) * inverse


def parts_of(values, count):
    terms = []
    for _ in range(count):
        term = values.astype(jnp.bfloat16).astype(jnp.float32)
        terms.append(term)
        values = values - term
    return jnp.concatenate(terms).astype(jnp.bfloat16)


def one_hot(row, count):
    lines = lax.broadcasted_iota(jnp.int32, (count, row.shape[1]), 0)
    return jnp.where(lines == row, 1.0, 0.0).astype(jnp.bfloat16)


def ffn_backward(lengths, segment_rows, segment_slots, pair_rows, pair_labels, encoded, cotangent, dir_t, vectors, normed_two, inverse_two, active, slope, hidden_low, down_weight, up_weight,
                 normed_one, inverse_one):
    rows, width = hidden_low.shape
    ff = active.shape[1]
    segments, classes = segment_slots.shape[1], dir_t.shape[0]
    numbers = (segment_rows, segment_slots, pair_rows, pair_labels)
    length = rows // lengths.shape[0]
    names = axis_bits()
    steps = len(names)
    wide, narrow = lax.axis_size("wide"), lax.axis_size("narrow")
    wide_bits, narrow_bits = wide.bit_length() - 1, narrow.bit_length() - 1
    chunks = ff // narrow // 128
    third = chunks // 2
    d_rows, u_rows = width // wide, width // narrow
    row_block = 512
    row_steps = rows // row_block
    orders = link_orders()
    two = (2,)
    early = 3
    first_dir = 6 + narrow
    sum_rows = pl.cdiv(first_dir + 2 * classes + 1, 16) * 16

    def chunk_of(step):
        step = jnp.clip(step, 0, chunks - 1)
        return step // 2 + third * (step % 2)

    def bits_of(number, count):
        return tuple((number >> bit) & 1 for bit in reversed(range(count)))

    def kernel(*refs):
        lens, seg_rows, seg_slots, pair_nums, labels, enc, cot, dir_ref = refs[:8]
        refs = refs[8:]
        q2, q1, vec = refs[:3]
        far = refs[3:9]
        slo = refs[9 : 9 + narrow]
        rest = list(refs[9 + narrow :])
        ga_out, up_out, down_out, sums_out = rest[:4]
        rest = rest[4:]
        grad_hidden, lowered, lowered_t, hidden_t, own, up_own, up_received = rest[:7]
        received = rest[7 : 7 + early]
        rest = rest[7 + early :]
        select, picked, dir_w, leaving, arrived, leaving_grads, arrived_grads = rest[:7]
        near = rest[7:13]
        n2, hidden, act, dws, uws, n1 = near
        send_sems, recv_sems, local_sems = rest[13:]
        loads = [pltpu.make_async_copy(far[i], near[i], local_sems.at[2 * chunks + i]) for i in range(len(near))]
        pid = pl.program_id(0)
        place = Place()
        pieces = []
        for number in range(chunks):
            pieces.append(
                Halving(place, names, orders[number % 3][:early], own.at[number], own.at[number],
                        [r.at[number] for r in received], send_sems, recv_sems, number * early)
            )
        core = ("narrow", 0)
        up_names = [name for name in names if name != ("wide", 0)]
        up_pieces = [
            Halving(place, up_names, [core], up_own.at[number], up_own.at[number], [up_received.at[number]],
                    send_sems, recv_sems, chunks * early + number)
            for number in range(chunks)
        ]

        def up_write(number):
            mine = up_pieces[number].region(0, True)
            return pltpu.make_async_copy(
                up_own.at[number].at[mine],
                up_out.at[(number // 2,) + (slice(None),) * (wide_bits - 1) + (number % 2,)],
                local_sems.at[number],
            )

        def exchange(source, landing, first, meanwhile=None):
            made = []
            for offset in range(1, wide):
                target = place.ahead(offset)
                made.append(pltpu.make_async_remote_copy(
                    src_ref=source.at[target["wide"]], dst_ref=landing.at[place.index["wide"]],
                    send_sem=send_sems.at[first + offset - 1], recv_sem=recv_sems.at[first + offset - 1],
                    device_id=target, device_id_type=MESH_ID))
            me = place.index["wide"]
            for copy in made:
                copy.start()
            landing[me] = source[me]
            if meanwhile:
                meanwhile()
            for copy in made:
                copy.wait()
            return landing[...].reshape(segments, 128)

        def turn_hidden():
            def body(i, carry):
                some = pl.ds(pl.multiple_of(i * row_block, row_block), row_block)
                hidden_t[:, some] = hidden[some, :].T
                return carry

            loads[1].wait()
            lax.fori_loop(0, row_steps, body, 0)

        @pl.when(pid == 0)
        def _():
            for load in loads:
                load.start()
            place.greet(all_wide=True)
            sums_out[...] = jnp.zeros_like(sums_out)
            base = chunks * early + chunks
            docs = rows // length
            places = jnp.concatenate([seg_rows[doc : doc + 1, :] + doc * length for doc in range(docs)], axis=1)
            select[...] = dot_last(one_hot(places, rows), one_hot(seg_slots[...], segments)).astype(jnp.bfloat16)
            picked[...] = jnp.dot(select[...].T, enc[...], preferred_element_type=jnp.float32).astype(jnp.bfloat16)
            halves = [dir_ref[:, n * width : (n + 1) * width].astype(jnp.float32) for n in range(2)]
            blank = jnp.zeros((128 - 2 * classes, width), jnp.float32)
            dir_w[...] = jnp.concatenate(halves + [blank]).astype(jnp.bfloat16)
            leaving[...] = dot_last(picked[...], dir_w[...]).reshape(leaving.shape)
            scores = exchange(leaving, arrived, base, turn_hidden).T
            pair_first, pair_second = one_hot(pair_nums[0:1, :], segments), one_hot(pair_nums[1:2, :], segments)

            def chosen(values, pairs):
                split = jnp.dot(parts_of(values, 3), pairs, preferred_element_type=jnp.float32)
                return split[:classes] + split[classes : 2 * classes] + split[2 * classes :]

            logits = chosen(scores[:classes], pair_first) + chosen(scores[classes : 2 * classes], pair_second)
            logits = logits + jnp.broadcast_to(vec[8:9, :128], (128, 128)).T[:classes, 0:1]
            powers = jnp.exp(logits - jnp.max(logits, 0, keepdims=True))
            chance = powers / jnp.sum(powers, 0, keepdims=True)
            kinds = lax.broadcasted_iota(jnp.int32, logits.shape, 0)
            delta = chance - jnp.where(kinds == labels[...], 1.0, 0.0)
            split = parts_of(delta, 2)
            gathered = []
            for pairs in (pair_first, pair_second):
                both = dot_last(split, pairs)
                gathered.append(both[:classes] + both[classes:])
            gathered.append(jnp.zeros((128 - 2 * classes, segments), jnp.float32))
            leaving_grads[...] = jnp.concatenate(gathered).T.reshape(leaving.shape)
            square = (classes, 128)
            matching = lax.broadcasted_iota(jnp.int32, square, 0) == lax.broadcasted_iota(jnp.int32, square, 1)
            biases = jnp.where(matching, jnp.sum(delta, 1, keepdims=True), 0.0)
            sums_out[first_dir + 2 * classes : first_dir + 2 * classes + 1, :128] = jnp.sum(biases, 0, keepdims=True)
            back = exchange(leaving_grads, arrived_grads, base + wide - 1)
            coarse = back.astype(jnp.bfloat16)
            fine = (back - coarse.astype(jnp.float32)).astype(jnp.bfloat16)
            grads_in = (
                jnp.dot(coarse, dir_w[...], preferred_element_type=jnp.float32)
                + jnp.dot(fine, dir_w[...], preferred_element_type=jnp.float32)
            ).astype(jnp.bfloat16)
            back_t = back.T[: 2 * classes]
            both = jnp.dot(parts_of(back_t, 2), picked[...], preferred_element_type=jnp.float32)
            sums_out[first_dir : first_dir + 2 * classes, :] = both[: 2 * classes] + both[2 * classes :]
            loads[0].wait()

            def body(i, carry):
                at = pl.multiple_of(i * row_block, row_block)
                some = pl.ds(at, row_block)
                normed = n2[some, :].astype(jnp.float32)
                doc = at // length
                line = lax.broadcasted_iota(jnp.int32, (row_block, 1), 0) + (at - doc * length)
                grad = cot[some, :].astype(jnp.float32) + jnp.dot(
                    select[some, :], grads_in, preferred_element_type=jnp.float32
                )
                grad = jnp.where(line < lens[doc], grad, 0.0)
                two = norm_back_rows(grad, normed, q2[some, :], vec[4:5, :])
                low = two.astype(jnp.bfloat16)
                grad_hidden[some, :] = two
                lowered[some, :] = low
                lowered_t[:, some] = low.T
                sums_out[0:1, :] += jnp.sum(grad * normed, 0, keepdims=True)
                sums_out[1:2, :] += jnp.sum(grad, 0, keepdims=True)
                sums_out[2:3, :] += jnp.sum(low.astype(jnp.float32), 0, keepdims=True)
                return carry

            lax.fori_loop(0, row_steps, body, 0)

        def slab(n, step):
            return pl.ds(pl.multiple_of((n * chunks + chunk_of(step)) * 128, 128), 128)

        @pl.when(pid == 0)
        def _():
            loads[2].wait()

        @pl.when(pid < chunks)
        def _():
            actives = jnp.concatenate([act[:, slab(n, pid)] for n in range(narrow)], axis=1)
            result = jnp.dot(lowered_t[...], actives, preferred_element_type=jnp.float32).astype(jnp.bfloat16)
            for w in range(wide):
                for n in range(narrow):
                    own[(pid,) + bits_of(w, wide_bits) + bits_of(n, narrow_bits)] = result[
                        w * d_rows : (w + 1) * d_rows, n * 128 : (n + 1) * 128
                    ]

        @pl.when(pid == chunks)
        def _():
            for load in loads[3:]:
                load.wait()

        @pl.when(pid >= chunks)
        def _():
            slopes = jnp.concatenate([ref[...] for ref in slo], axis=1)
            downs = jnp.concatenate([dws[slab(n, pid - chunks), :] for n in range(narrow)], axis=0)
            ups = jnp.concatenate([uws[:, slab(n, pid - chunks)] for n in range(narrow)], axis=1)
            grad_active = dot_last(lowered[...], downs)
            grad_upper = (grad_active * slopes.astype(jnp.float32)).astype(jnp.bfloat16)
            totals = jnp.sum(grad_upper.astype(jnp.float32), 0, keepdims=True)
            at = pl.ds(pl.multiple_of(chunk_of(pid - chunks) * 128, 128), 128)
            for n in range(narrow):
                sums_out[6 + n : 7 + n, at] = totals[:, n * 128 : (n + 1) * 128]
            result = jnp.dot(hidden_t[...], grad_upper, preferred_element_type=jnp.float32).astype(jnp.bfloat16)
            for n in range(narrow):
                for z in range(narrow):
                    high = bits_of(z, wide_bits - 1)
                    up_own[(pid - chunks,) + high + bits_of(n, narrow_bits)] = result[
                        n * u_rows : (n + 1) * u_rows, z * 128 : (z + 1) * 128
                    ]
            grad_hidden[...] += dot_last(grad_upper, ups)

        def down_write(number):
            return pltpu.make_async_copy(
                own.at[number].at[pieces[number].region(early - 1, True)], down_out.at[number], local_sems.at[chunks + number]
            )

        def advance(number, step):
            pieces[number].merge(step)
            if step + 1 < early:
                pieces[number].send(step + 1)
            else:
                down_write(number).start()

        for number in range(chunks):
            @pl.when(pid == chunks + number)
            def _():
                up_pieces[number].send(0)

        @pl.when(pid == 2 * chunks - 1)
        def _():
            def body(i, carry):
                at = pl.multiple_of(i * row_block, row_block)
                some = pl.ds(at, row_block)
                grad, normed = grad_hidden[some, :], n1[some, :].astype(jnp.float32)
                low = norm_back_rows(grad, normed, q1[some, :], vec[1:2, :]).astype(jnp.bfloat16)
                ga_out[some, :] = low
                sums_out[3:4, :] += jnp.sum(grad * normed, 0, keepdims=True)
                sums_out[4:5, :] += jnp.sum(grad, 0, keepdims=True)
                sums_out[5:6, :] += jnp.sum(low.astype(jnp.float32), 0, keepdims=True)
                return carry

            lax.fori_loop(0, row_steps, body, 0)

        plan = {}
        for number in range(chunks):
            for step in range(early):
                at = (number + 2, chunks + 1 + 2 * (number // 3), chunks + 4 + number // 3)[step]
                plan.setdefault(min(at, 2 * chunks - 1), []).append((step, number))
        for at in range(2 * chunks):
            @pl.when(pid == at)
            def _():
                if at < chunks:
                    pieces[at].send(0)
                if at > chunks:
                    up_pieces[at - chunks - 1].merge(0)
                    up_write(at - chunks - 1).start()
                for step, number in sorted(plan.get(at, [])):
                    advance(number, step)
                if at == 2 * chunks - 1:
                    up_pieces[chunks - 1].merge(0)
                    up_write(chunks - 1).start()
                    for number in range(chunks):
                        up_write(number).wait()
                        down_write(number).wait()
                    for item in pieces + up_pieces:
                        item.close()

    def whole(shape):
        return pl.BlockSpec(shape, lambda g: (0,) * len(shape), pipeline_mode=pl.Buffered(1))

    def slab_columns(shape, first):
        return [pl.BlockSpec(shape, lambda g, n=n: (0, n * chunks + chunk_of(g - first))) for n in range(narrow)]

    in_specs = [pl.BlockSpec(memory_space=pltpu.SMEM), *[whole(item.shape) for item in numbers],
                whole((rows, width)), whole((rows, width))]
    in_specs += [whole(dir_t.shape)]
    in_specs += [whole((rows, 1))] * 2 + [whole(vectors.shape)] + [pl.BlockSpec(memory_space=pl.ANY)] * 6
    in_specs += slab_columns((rows, 128), chunks)
    high = two * (wide_bits - 1)
    low = two * narrow_bits
    up_shape = (third,) + high + (2,) + low[1:] + (u_rows, 128)
    out_specs = [
        whole((rows, width)),
        pl.BlockSpec(memory_space=pl.ANY),
        pl.BlockSpec(memory_space=pl.ANY),
        whole((sum_rows, width)),
    ]
    out_shape = [
        jax.ShapeDtypeStruct((rows, width), jnp.bfloat16),
        jax.ShapeDtypeStruct(up_shape, jnp.bfloat16),
        jax.ShapeDtypeStruct((chunks,) + two * (steps - early) + (d_rows, 128), jnp.bfloat16),
        jax.ShapeDtypeStruct((sum_rows, width), jnp.float32),
    ]
    scratch = [
        pltpu.VMEM((rows, width), jnp.float32),
        pltpu.VMEM((rows, width), jnp.bfloat16),
        pltpu.VMEM((width, rows), jnp.bfloat16),
        pltpu.VMEM((width, rows), jnp.bfloat16),
        pltpu.VMEM((chunks,) + two * steps + (d_rows, 128), jnp.bfloat16),
        pltpu.VMEM((chunks,) + high + low + (u_rows, 128), jnp.bfloat16),
        pltpu.VMEM((chunks,) + high + low[1:] + (u_rows, 128), jnp.bfloat16),
    ]
    scratch += [pltpu.VMEM((chunks,) + two * (steps - 1 - s) + (d_rows, 128), jnp.bfloat16) for s in range(early)]
    scratch += [pltpu.VMEM((rows, segments), jnp.bfloat16), pltpu.VMEM((segments, width), jnp.bfloat16)]
    scratch += [pltpu.VMEM((128, width), jnp.bfloat16)]
    scratch += [pltpu.VMEM((wide, segments // wide, 128), jnp.float32)] * 4
    far = (normed_two, hidden_low, active, down_weight, up_weight, normed_one)
    scratch += [pltpu.VMEM(item.shape, item.dtype) for item in far]
    sems = chunks * early + chunks + 2 * (wide - 1)
    scratch += [pltpu.SemaphoreType.DMA((sems,)), pltpu.SemaphoreType.DMA((sems,)), pltpu.SemaphoreType.DMA((2 * chunks + len(far),))]
    return pl.pallas_call(
        kernel,
        grid=(2 * chunks,),
        in_specs=in_specs,
        out_specs=out_specs,
        out_shape=out_shape,
        scratch_shapes=scratch,
        compiler_params=pltpu.CompilerParams(collective_id=0, has_side_effects=True, vmem_limit_bytes=60 << 20),
        name="ffn_backward",
    )(lengths, *numbers, encoded, cotangent, dir_t, inverse_two, inverse_one, vectors,
      *far, *([slope] * narrow))


def attention_backward(grad_attended, mixed, out_weight, queries, keys, values, attention, tokens, qkv_weight, up_grads,
                       down_grads, sums):
    rows, width = tokens.shape
    docs, _, length, _ = attention.shape
    pairs = width // 128
    names = axis_bits()
    steps = len(names)
    wide, narrow = lax.axis_size("wide"), lax.axis_size("narrow")
    wide_bits, narrow_bits = wide.bit_length() - 1, narrow.bit_length() - 1
    half = narrow // 2
    half_bits = narrow_bits - 1
    lanes = width // half
    q_rows, o_rows = 3 * width // wide // 2, width // wide // 2
    q_parts = lanes // 128
    orders = link_orders()
    ups = up_grads.shape[0]
    u_rows = up_grads.shape[-2]
    attn_steps = docs * pairs
    token_block = 256
    token_steps = rows // token_block
    first_q = 1 + attn_steps
    first_t = first_q + q_parts
    grid = first_t + token_steps
    downs, d_rows = down_grads.shape[0], down_grads.shape[-2]
    down_steps = len(down_grads.shape) - 3
    cuts = [(0, q_rows // 24 * 16), (q_rows // 24 * 16, q_rows)]
    u_cuts = [(0, u_rows // 2), (u_rows // 2, u_rows)]
    up_count, out_count = ups * len(u_cuts), q_parts
    first_part = up_count + out_count
    first_down = first_part + q_parts * len(cuts)
    count = first_down + downs
    small_rows = sums.shape[0]
    late_rows = pl.cdiv(2 * pairs, 8) * 8
    s_cuts = [(0, small_rows // 4), (small_rows // 4, small_rows // 2), (small_rows // 2, small_rows)]

    def bits_of(number, count):
        return tuple((number >> bit) & 1 for bit in reversed(range(count)))

    def kernel(*refs):
        (ga_hbm, mix_hbm, ow_hbm, q_ref, k_ref, v_ref, att_ref, tok_hbm, qw_hbm, up_hbm, down_hbm, small) = refs[:12]
        tokens_out, up_out, out_out, qkv_out, down_out, small_out, late_out = refs[12:19]
        rest = list(refs[19:])
        gm, mix_pair, gqkv_t, up_own, out_own, qkv_own = rest[:6]
        rest = rest[6:]
        up_received = [rest[i * (steps - 1) : (i + 1) * (steps - 1)] for i in range(len(u_cuts))]
        rest = rest[len(u_cuts) * (steps - 1) :]
        out_received, rest = rest[:steps], rest[steps:]
        qkv_received, rest = [rest[i * steps : (i + 1) * steps] for i in range(len(cuts))], rest[len(cuts) * steps :]
        down_own, down_received, rest = rest[0], rest[1 : 1 + down_steps], rest[1 + down_steps :]
        small_sent, small_received, late_sent, late_received, swap_out, swap_qkv, tok, qw, ga, mix, ow = rest[:11]
        send_sems, recv_sems, local_sems = rest[11:]
        pid = pl.program_id(0)
        place = Place()
        core = place.bit["narrow", 0]
        pieces = []
        for low, high in u_cuts:
            for part in range(ups):
                cut = len(pieces) // ups
                pieces.append(Halving(place, names[:-1], orders[part % 3][1:], up_hbm.at[part], up_own.at[part],
                                      [r.at[part] for r in up_received[cut]], send_sems, recv_sems, len(pieces) * steps,
                                      (slice(low, high), slice(None))))
        for part in range(out_count):
            pieces.append(Halving(place, names, orders[part % 3], out_own.at[part], out_own.at[part],
                                  [r.at[part] for r in out_received], send_sems, recv_sems, len(pieces) * steps))
        for part in range(q_parts):
            for cut, (low, high) in enumerate(cuts):
                pieces.append(Halving(place, names, orders[part % 3], qkv_own.at[part], qkv_own.at[part],
                                      [r.at[part] for r in qkv_received[cut]], send_sems, recv_sems, len(pieces) * steps,
                                      (slice(low, high), slice(None))))
        for number in range(downs):
            order = orders[number % 3][steps - down_steps :]
            pieces.append(Halving(place, [name for name in names if name in order], order, down_own.at[number],
                                  down_own.at[number], [r.at[number] for r in down_received], send_sems, recv_sems,
                                  len(pieces) * steps))
        base = count * steps

        def all_sum(sent, received, first, order=0, rows=slice(None)):
            made = []
            for step in range(steps):
                made.append(pltpu.make_async_remote_copy(
                    src_ref=sent.at[step, rows], dst_ref=received.at[step, rows], send_sem=send_sems.at[first + step],
                    recv_sem=recv_sems.at[first + step], device_id=place.across(orders[order][step]),
                    device_id_type=MESH_ID))
            return made

        small_copies = [
            all_sum(small_sent, small_received, base + (2 + q_parts * len(cuts) + i) * steps + out_count, i, slice(low, high))
            for i, (low, high) in enumerate(s_cuts)
        ]
        late_copies = [all_sum(late_sent, late_received, base + steps)]
        swap_refs = [swap_out.at[part, core] for part in range(out_count)]
        swap_refs += [swap_qkv.at[part, core, low:high] for part in range(q_parts) for low, high in cuts]
        swaps = [pltpu.make_async_remote_copy(
            src_ref=ref, dst_ref=ref, send_sem=send_sems.at[base + 2 * steps + slot],
            recv_sem=recv_sems.at[base + 2 * steps + slot], device_id=place.across(("narrow", 0)),
            device_id_type=MESH_ID) for slot, ref in enumerate(swap_refs)]
        local = []
        for number in range(ups):
            keep = pieces[number].region(0, True)[: -2]
            local.append(pltpu.make_async_copy(up_hbm.at[number].at[keep], up_own.at[number].at[keep], local_sems.at[number]))

        loads = [pltpu.make_async_copy(tok_hbm, tok, local_sems.at[ups]),
                 pltpu.make_async_copy(qw_hbm, qw, local_sems.at[ups + 1])]
        first_loads = [pltpu.make_async_copy(source, target, local_sems.at[ups + 3 + i])
                       for i, (source, target) in enumerate(((ga_hbm, ga), (mix_hbm, mix), (ow_hbm, ow)))]
        down_load = pltpu.make_async_copy(down_hbm, down_own, local_sems.at[ups + 2])

        def advance(number, step):
            item = pieces[number]
            if step == 0 and number < ups:
                local[number].wait()
            total = item.add(step)
            if total is None:
                item.send(step + 1)
            elif number < up_count:
                cut, part = divmod(number, ups)
                up_out[u_cuts[cut][0] : u_cuts[cut][1], part * 128 : (part + 1) * 128] = total
            elif number >= first_down:
                number -= first_down
                j = number // 2 + downs // 2 * (number % 2)
                down_out[:, j * 128 : (j + 1) * 128] = total
            else:
                if number < first_part:
                    swap_out[number - up_count, core] = total
                else:
                    part, cut = divmod(number - first_part, len(cuts))
                    swap_qkv[part, core, cuts[cut][0] : cuts[cut][1]] = total
                swaps[number - up_count].start()

        def advance_small(lanes, sent, received, out, step):
            for copies in lanes:
                copies[step].wait_recv()
            total = sent[step] + received[step]
            if step + 1 < steps:
                sent[step + 1] = total
                for copies in lanes:
                    copies[step + 1].start()
            else:
                out[...] = total

        @pl.when(pid == 0)
        def _():
            place.greet()
            for number in range(up_count):
                pieces[number].send(0)
            for number in range(ups):
                local[number].start()
            for load in first_loads:
                load.start()
            small_sent[0] = small[...]
            for copies in small_copies:
                copies[0].start()
            down_load.start()
            for load in loads:
                load.start()
            for load in first_loads:
                load.wait()
            grads_t = ga[...].T
            result = jnp.dot(grads_t, mix[...], preferred_element_type=jnp.float32).astype(jnp.bfloat16)
            for w in range(wide):
                for h in range(2):
                    for y in range(half):
                        at = (w * 2 + h) * o_rows
                        for part in range(out_count):
                            first = y * lanes + part * 128
                            out_own[(part,) + bits_of(w, wide_bits) + bits_of(y, half_bits) + (h,)] = result[
                                at : at + o_rows, first : first + 128
                            ]
            for part in range(out_count):
                pieces[up_count + part].send(0)
            grad_mixed = dot_last(ga[...], ow[...]).astype(jnp.bfloat16)
            for pair in range(pairs):
                gm[pair] = grad_mixed[:, pair * 128 : (pair + 1) * 128]
                mix_pair[pair] = mix[:, pair * 128 : (pair + 1) * 128]
            down_load.wait()
            for number in range(downs):
                pieces[first_down + number].send(0)

        @pl.when((pid >= 1) & (pid < first_q))
        def _():
            number = pid - 1
            pair, doc = number // docs, number % docs
            some = pl.ds(pl.multiple_of(doc * length, length), length)
            lane = lax.broadcasted_iota(jnp.int32, (1, 128), 1)
            scaled, keys, values = q_ref[...] * jnp.bfloat16(HEAD_DIM**-0.5), k_ref[...], v_ref[...]
            grads = gm[pair, some, :]
            product = grads.astype(jnp.float32) * mix_pair[pair, some, :].astype(jnp.float32)
            queries_t, grads_t = scaled.T, grads.T
            zero = jnp.zeros_like(grads)
            query_parts = []
            for head in range(2):
                inside = (lane // HEAD_DIM) == head
                at = head * HEAD_DIM
                attention = att_ref[0, head]
                chance = dot_last(jnp.where(inside, grads, zero), values)
                inner = jnp.sum(jnp.where(inside, product, 0.0), -1, keepdims=True)
                grad_scores = (attention.astype(jnp.float32) * (chance - inner)).astype(jnp.bfloat16)
                query_parts.append(jnp.dot(grad_scores, keys, preferred_element_type=jnp.float32))
                key_t = jnp.dot(queries_t[at : at + HEAD_DIM], grad_scores, preferred_element_type=jnp.float32)
                value_t = jnp.dot(grads_t[at : at + HEAD_DIM], attention, preferred_element_type=jnp.float32)
                row = pair * 128 + at
                gqkv_t[pl.ds(pl.multiple_of(width + row, HEAD_DIM), HEAD_DIM), some] = key_t.astype(jnp.bfloat16)
                gqkv_t[pl.ds(pl.multiple_of(2 * width + row, HEAD_DIM), HEAD_DIM), some] = value_t.astype(jnp.bfloat16)
            grad_query = jnp.where(lane < HEAD_DIM, query_parts[0], query_parts[1]) * HEAD_DIM**-0.5
            gqkv_t[pl.ds(pl.multiple_of(pair * 128, 128), 128), some] = grad_query.astype(jnp.bfloat16).T

        for part in range(q_parts):
            @pl.when(pid == first_q + part)
            def _():
                if part == 0:
                    for load in loads:
                        load.wait()
                    ones = jnp.ones((8, rows), jnp.bfloat16)
                    for which in range(2):
                        totals = dot_last(ones, gqkv_t[2 * which * width : (2 * which + 1) * width, :])
                        for j in range(pairs):
                            late_sent[0, which * pairs + j : which * pairs + j + 1, :] = totals[
                                :1, j * 128 : (j + 1) * 128
                            ]
                    late_sent[0, 2 * pairs :, :] = jnp.zeros((late_rows - 2 * pairs, 128), jnp.float32)
                    late_copies[0][0].start()
                columns = jnp.concatenate(
                    [tok[:, y * lanes + part * 128 : y * lanes + (part + 1) * 128] for y in range(half)], axis=1
                )
                result = jnp.dot(gqkv_t[...], columns, preferred_element_type=jnp.float32).astype(jnp.bfloat16)
                for w in range(wide):
                    for h in range(2):
                        for y in range(half):
                            at = (w * 2 + h) * q_rows
                            qkv_own[(part,) + bits_of(w, wide_bits) + bits_of(y, half_bits) + (h,)] = result[
                                at : at + q_rows, y * 128 : (y + 1) * 128
                            ]
                for cut in range(len(cuts)):
                    pieces[first_part + part * len(cuts) + cut].send(0)

        @pl.when(pid >= first_t)
        def _():
            at = pl.multiple_of((pid - first_t) * token_block, token_block)
            some = pl.ds(at, token_block)
            grad_t = jnp.dot(qw[...], gqkv_t[:, some], preferred_element_type=jnp.float32)
            tokens_out[...] = (grad_t.T + ga[some, :].astype(jnp.float32)).astype(jnp.bfloat16)

        plan, small_plan, late_plan = {}, {}, {}
        for cut, times in enumerate(((5, 9, 12, 14), (8, 10, 13, 15))):
            for step, at in enumerate(times):
                for part in range(ups):
                    plan.setdefault(at, []).append((cut * ups + part, step))
        for step, at in enumerate((1, 9, 12, 14, 15)):
            for part in range(out_count):
                plan.setdefault(at, []).append((up_count + part, step))
        for step, at in enumerate((4, 8)):
            for number in range(downs):
                plan.setdefault(at, []).append((first_down + number, step))
        for number in range(first_part, first_down):
            for step in range(steps):
                at = first_q + (number - first_part) // len(cuts) + 1 if step == 0 else grid - 1
                plan.setdefault(at, []).append((number, step))
        for step, at in enumerate((3, 7, 9, 11, 13)):
            small_plan[at] = step
        late_plan[first_q + 2] = 0
        def turn(at, number, step):
            cut = (number - first_part) % len(cuts) if first_part <= number < first_down and at == grid - 1 else 0
            return step + cut, step, number

        for at in range(grid):
            @pl.when(pid == at)
            def _():
                if at in small_plan:
                    advance_small(small_copies, small_sent, small_received, small_out, small_plan[at])
                for number, step in sorted(plan.get(at, []), key=lambda entry: turn(at, *entry)):
                    if at == grid - 1 and number == first_part:
                        advance_small(late_copies, late_sent, late_received, late_out, step)
                    advance(number, step)
                if at in late_plan:
                    advance_small(late_copies, late_sent, late_received, late_out, late_plan[at])
                if at == grid - 1:
                    for copy in swaps:
                        copy.wait()

                    def own_lanes(lanes):
                        size = lanes.shape[1] // 2
                        return jnp.where(core == 0, lanes[:, :size], lanes[:, size:])

                    out_out[...] = own_lanes(jnp.concatenate(
                        [swap_out[part].reshape(2 * o_rows, 128) for part in range(out_count)], axis=1))
                    qkv_out[...] = own_lanes(jnp.concatenate(
                        [swap_qkv[part].reshape(2 * q_rows, 128) for part in range(q_parts)], axis=1))
                    for item in pieces:
                        item.close()
                    for copies in small_copies + late_copies:
                        for copy in copies:
                            copy.wait_send()

    def whole(shape):
        return pl.BlockSpec(shape, lambda g: (0,) * len(shape), pipeline_mode=pl.Buffered(1))

    def number_of(g):
        return jnp.clip(g - 1, 0, attn_steps - 1)

    tile = pl.BlockSpec((length, 128), lambda g: (number_of(g) % docs, number_of(g) // docs))

    two = (2,)
    any_space = pl.BlockSpec(memory_space=pl.ANY)
    in_specs = [any_space, any_space, any_space, tile, tile, tile]
    in_specs += [pl.BlockSpec((1, 2, length, length), lambda g: (number_of(g) % docs, number_of(g) // docs, 0, 0))]
    in_specs += [any_space, any_space, any_space, any_space, whole((small_rows, width))]
    out_shape = [
        jax.ShapeDtypeStruct((rows, width), jnp.bfloat16),
        jax.ShapeDtypeStruct((u_rows, ups * 128), jnp.float32),
        jax.ShapeDtypeStruct((2 * o_rows, lanes // 2), jnp.float32),
        jax.ShapeDtypeStruct((2 * q_rows, lanes // 2), jnp.float32),
        jax.ShapeDtypeStruct((d_rows, downs * 128), jnp.float32),
        jax.ShapeDtypeStruct((small_rows, width), jnp.float32),
        jax.ShapeDtypeStruct((late_rows, 128), jnp.float32),
    ]
    wide_dims, half_dims = two * wide_bits, two * half_bits
    scratch = [
        pltpu.VMEM((pairs, rows, 128), jnp.bfloat16),
        pltpu.VMEM((pairs, rows, 128), jnp.bfloat16),
        pltpu.VMEM((3 * width, rows), jnp.bfloat16),
        pltpu.VMEM(up_grads.shape, jnp.bfloat16),
        pltpu.VMEM((out_count,) + wide_dims + half_dims + two + (o_rows, 128), jnp.bfloat16),
        pltpu.VMEM((q_parts,) + wide_dims + half_dims + two + (q_rows, 128), jnp.bfloat16),
    ]
    for low, high in u_cuts:
        scratch += [pltpu.VMEM((ups,) + two * (steps - 2 - s) + (high - low, 128), jnp.bfloat16) for s in range(steps - 1)]
    scratch += [pltpu.VMEM((out_count,) + two * (steps - 1 - s) + (o_rows, 128), jnp.bfloat16) for s in range(steps)]
    for low, high in cuts:
        scratch += [pltpu.VMEM((q_parts,) + two * (steps - 1 - s) + (high - low, 128), jnp.bfloat16) for s in range(steps)]
    scratch += [pltpu.VMEM(down_grads.shape, jnp.bfloat16)]
    scratch += [pltpu.VMEM((downs,) + two * (down_steps - 1 - s) + (d_rows, 128), jnp.bfloat16) for s in range(down_steps)]
    scratch += [pltpu.VMEM((steps, small_rows, width), jnp.float32)] * 2
    scratch += [pltpu.VMEM((steps, late_rows, 128), jnp.float32)] * 2
    scratch += [pltpu.VMEM((out_count, 2, o_rows, 128), jnp.float32), pltpu.VMEM((q_parts, 2, q_rows, 128), jnp.float32)]
    scratch += [pltpu.VMEM(tokens.shape, jnp.bfloat16), pltpu.VMEM(qkv_weight.shape, jnp.bfloat16)]
    scratch += [pltpu.VMEM(item.shape, jnp.bfloat16) for item in (grad_attended, mixed, out_weight)]
    sems = count * steps + (2 + q_parts * len(cuts) + len(s_cuts)) * steps + out_count
    scratch += [pltpu.SemaphoreType.DMA((sems,)), pltpu.SemaphoreType.DMA((sems,)), pltpu.SemaphoreType.DMA((ups + 6,))]
    return pl.pallas_call(
        kernel,
        grid=(grid,),
        in_specs=in_specs,
        out_specs=[pl.BlockSpec((token_block, width), lambda g: (jnp.clip(g - first_t, 0, token_steps - 1), 0))]
        + [whole(item.shape) for item in out_shape[1:]],
        out_shape=out_shape,
        scratch_shapes=scratch,
        compiler_params=pltpu.CompilerParams(collective_id=1, has_side_effects=True, vmem_limit_bytes=60 << 20),
        name="attention_backward",
    )(grad_attended, mixed, out_weight, queries, keys, values, attention, tokens, qkv_weight, up_grads, down_grads, sums)


def hand_out(grad_tokens, sums, late, narrow, classes, turned, *blocks):
    rows, width = grad_tokens.shape
    steps = 2
    first_dir = 6 + narrow

    def kernel(tokens_ref, sums_ref, late_ref, *refs):
        ins, outs = refs[: len(blocks)], refs[len(blocks) :]
        outs[0][...] = tokens_ref[...]

        @pl.when(pl.program_id(0) == 0)
        def _():
            for source, target in zip(ins, outs[1:]):
                target[...] = source[...] if source.shape == target.shape else source[...].T
            singles = outs[1 + len(blocks) :]
            for number in range(6):
                singles[number][...] = sums_ref[number, :]
            for number in range(2):
                for j in range(width // 128):
                    singles[6 + number][j * 128 : (j + 1) * 128] = late_ref[number * (width // 128) + j, :]
            for number in range(narrow):
                singles[8][number * width : (number + 1) * width] = sums_ref[6 + number, :]
            singles[9][...] = sums_ref[first_dir : first_dir + 2 * classes, :]
            singles[10][...] = sums_ref[first_dir + 2 * classes, :classes]

    def whole(shape):
        return pl.BlockSpec(shape, lambda g: (0,) * len(shape))

    some = pl.BlockSpec((rows // steps, width), lambda g: (g, 0))
    small = [(width,)] * 8 + [(narrow * width,), (2 * classes, width), (classes,)]
    shapes = [block.shape[::-1] if number in turned else block.shape for number, block in enumerate(blocks)]
    out_shape = [jax.ShapeDtypeStruct((rows, width), jnp.bfloat16)]
    out_shape += [jax.ShapeDtypeStruct(shape, jnp.float32) for shape in shapes + small]
    return pl.pallas_call(
        kernel,
        grid=(steps,),
        in_specs=[some] + [whole(item.shape) for item in (sums, late) + blocks],
        out_specs=[some] + [whole(item.shape) for item in out_shape[1:]],
        out_shape=out_shape,
        name="hand_out",
    )(grad_tokens, sums, late, *blocks)


def on_device_fast(
    tokens,
    doc_lengths,
    qkv_weight,
    query_bias,
    value_bias,
    out_weight,
    out_bias,
    first_gain,
    first_shift,
    up_weight,
    up_bias,
    down_weight,
    down_bias,
    second_gain,
    second_shift,
    dir_weight,
    dir_bias,
    segment_rows,
    segment_slots,
    pair_rows,
    pair_labels,
    out_cotangent,
):
    doc_count, length, model_width = tokens.shape
    token_rows = tokens.reshape(doc_count * length, model_width)
    singles = (out_bias, first_gain, first_shift, down_bias, second_gain, second_shift, query_bias, value_bias)
    vectors, queries, keys, values, attention, mixed, *kept = layer_forward(
        doc_lengths, token_rows, qkv_weight, out_weight, up_weight, down_weight, singles + (dir_bias, up_bias)
    )
    hidden_low, normed_one, inverse_one, active, slope, normed_two, inverse_two, encoded_rows = kept
    classes_count = dir_weight.shape[1]
    grad_attended, up_blocks, down_blocks, sums = ffn_backward(
        doc_lengths, segment_rows, segment_slots, pair_rows[0].T, pair_labels, encoded_rows, out_cotangent.reshape(-1, model_width), dir_weight.T, vectors,
        normed_two, inverse_two, active, slope,
        hidden_low, down_weight, up_weight, normed_one, inverse_one,
    )
    grad_tokens, out_up, out_out, out_qkv, out_down, sums, late = attention_backward(
        grad_attended, mixed, out_weight, queries, keys, values, attention, token_rows, qkv_weight, up_blocks,
        down_blocks, sums,
    )
    grad_tokens, out_up, out_out, out_qkv, out_down, *smalls = hand_out(
        grad_tokens, sums, late, lax.axis_size("narrow"), classes_count, (1, 2), out_up, out_out, out_qkv, out_down
    )
    return (
        encoded_rows.reshape(tokens.shape),
        grad_tokens.reshape(tokens.shape),
        out_qkv,
        smalls[6],
        smalls[7],
        out_out,
        smalls[5],
        smalls[3],
        smalls[4],
        out_up,
        smalls[8],
        out_down.T,
        smalls[2],
        smalls[0],
        smalls[1],
        smalls[9].reshape(2, classes_count, model_width).transpose(0, 2, 1).reshape(2 * model_width, classes_count),
        smalls[10],
    )


def on_device(
    tokens,
    doc_lengths,
    qkv_weight,
    query_bias,
    value_bias,
    out_weight,
    out_bias,
    first_gain,
    first_shift,
    up_weight,
    up_bias,
    down_weight,
    down_bias,
    second_gain,
    second_shift,
    dir_weight,
    dir_bias,
    segment_rows,
    segment_slots,
    pair_rows,
    pair_labels,
    out_cotangent,
):
    doc_count, length, model_width = tokens.shape
    score_scale = HEAD_DIM ** (-0.5)
    token_rows = tokens.reshape(doc_count * length, model_width)
    allowed = lax.broadcasted_iota(jnp.int32, (doc_count, length), 1) < doc_lengths[:, None]
    allowed_rows = allowed.reshape(-1, 1).astype(jnp.float32)
    bias_row = jnp.concatenate([query_bias, jnp.zeros_like(query_bias), value_bias]).astype(
        jnp.float32
    )
    qkv = (jnp.dot(token_rows, qkv_weight, preferred_element_type=jnp.float32) + bias_row).astype(
        jnp.bfloat16
    )

    def split_heads(doc_block, which):
        return doc_block[:, which * model_width : (which + 1) * model_width].reshape(
            length, HEADS, HEAD_DIM
        )

    def scores_of(queries, key_rows, doc_mask):
        scores = (
            jnp.einsum("qhd,khd->hqk", queries, key_rows, preferred_element_type=jnp.float32)
            * score_scale
        )
        return jnp.where(doc_mask[None, None, :], scores, MASKED)

    mixed_parts = []
    log_totals = []
    for doc_index in range(doc_count):
        doc_block = qkv[doc_index * length : (doc_index + 1) * length]
        queries = split_heads(doc_block, 0)
        key_rows = split_heads(doc_block, 1)
        value_rows = split_heads(doc_block, 2)
        scores = scores_of(queries, key_rows, allowed[doc_index])
        highest = jnp.max(scores, -1, keepdims=True)
        powers = jnp.exp(scores - highest)
        summed = jnp.sum(powers, -1, keepdims=True)
        attention = (powers / summed).astype(jnp.bfloat16)
        log_totals.append(highest + jnp.log(summed))
        mixed_parts.append(
            jnp.einsum(
                "hqk,khd->qhd", attention, value_rows, preferred_element_type=jnp.float32
            ).reshape(length, model_width)
        )
    mixed = jnp.concatenate(mixed_parts).astype(jnp.bfloat16)
    attended = jnp.dot(mixed, out_weight, preferred_element_type=jnp.float32) + out_bias.astype(
        jnp.float32
    )
    resid_one = token_rows.astype(jnp.float32) + attended
    hidden_one, normed_one, inverse_one = norm_forward(
        resid_one, first_gain.astype(jnp.float32), first_shift.astype(jnp.float32)
    )
    hidden_low = hidden_one.astype(jnp.bfloat16)
    upper_pre = jnp.dot(hidden_low, up_weight, preferred_element_type=jnp.float32) + up_bias.astype(
        jnp.float32
    )
    cumulative = normal_cdf(upper_pre)
    active = (upper_pre * cumulative).astype(jnp.bfloat16)
    lowered = jnp.dot(active, down_weight, preferred_element_type=jnp.float32) + down_bias.astype(
        jnp.float32
    )
    resid_two = hidden_one + lowered
    second_float = second_gain.astype(jnp.float32)
    normed_out, normed_two, inverse_two = norm_forward(
        resid_two, second_float, second_shift.astype(jnp.float32)
    )
    encoded_rows = (normed_out * allowed_rows).astype(jnp.bfloat16)
    doc_starts = lax.broadcasted_iota(jnp.int32, (doc_count, 1), 0) * length
    picked_rows = (segment_rows + doc_starts).reshape(-1)
    picked = encoded_rows[picked_rows]
    slots = segment_slots.reshape(-1)
    outgoing = jnp.zeros_like(picked).at[slots].set(picked)
    arrived = lax.all_to_all(outgoing, "wide", split_axis=0, concat_axis=0, tiled=True)
    pairs = pair_rows.reshape(-1, 2)
    labels = pair_labels.reshape(-1)
    first_rows = arrived[pairs[:, 0]]
    second_rows = arrived[pairs[:, 1]]
    logits = (
        jnp.dot(first_rows, dir_weight[:model_width], preferred_element_type=jnp.float32)
        + jnp.dot(second_rows, dir_weight[model_width:], preferred_element_type=jnp.float32)
        + dir_bias.astype(jnp.float32)
    )
    powers_head = jnp.exp(logits - jnp.max(logits, -1, keepdims=True))
    chance = powers_head / jnp.sum(powers_head, -1, keepdims=True)
    classes = lax.broadcasted_iota(jnp.int32, logits.shape, 1)
    delta = chance - (labels[:, None] == classes).astype(jnp.float32)
    first_float = first_rows.astype(jnp.float32)
    second_rows_float = second_rows.astype(jnp.float32)
    grad_dir_weight = jnp.concatenate(
        [
            jnp.dot(first_float.T, delta, precision=EXACT, preferred_element_type=jnp.float32),
            jnp.dot(
                second_rows_float.T, delta, precision=EXACT, preferred_element_type=jnp.float32
            ),
        ]
    )
    grad_dir_bias = jnp.sum(delta, 0)
    dir_float = dir_weight.astype(jnp.float32)
    grad_first = jnp.dot(
        delta, dir_float[:model_width].T, precision=EXACT, preferred_element_type=jnp.float32
    )
    grad_second = jnp.dot(
        delta, dir_float[model_width:].T, precision=EXACT, preferred_element_type=jnp.float32
    )
    grad_arrived = jnp.zeros((arrived.shape[0], model_width), jnp.float32)
    grad_arrived = grad_arrived.at[pairs[:, 0]].add(grad_first).at[pairs[:, 1]].add(grad_second)
    returned = lax.all_to_all(
        grad_arrived.astype(jnp.bfloat16), "wide", split_axis=0, concat_axis=0, tiled=True
    )
    grad_picked = returned[slots].astype(jnp.float32)
    grad_encoded = (
        out_cotangent.reshape(-1, model_width).astype(jnp.float32).at[picked_rows].add(grad_picked)
    )
    grad_encoded = grad_encoded * allowed_rows
    grad_two, grad_second_gain, grad_second_shift = norm_backward(
        grad_encoded, normed_two, inverse_two, second_float
    )
    grad_lowered = grad_two.astype(jnp.bfloat16)
    grad_down_weight = jnp.einsum(
        "rf,rd->fd", active, grad_lowered, preferred_element_type=jnp.float32
    )
    grad_down_bias = jnp.sum(grad_lowered.astype(jnp.float32), 0)
    grad_active = jnp.einsum(
        "rd,fd->rf", grad_lowered, down_weight, preferred_element_type=jnp.float32
    )
    density = jnp.exp(-0.5 * upper_pre * upper_pre) * 0.3989422804014327
    grad_upper = (grad_active * (cumulative + upper_pre * density)).astype(jnp.bfloat16)
    grad_up_weight = jnp.einsum(
        "rd,rf->df", hidden_low, grad_upper, preferred_element_type=jnp.float32
    )
    grad_up_bias = jnp.sum(grad_upper.astype(jnp.float32), 0)
    grad_hidden = grad_two + jnp.einsum(
        "rf,df->rd", grad_upper, up_weight, preferred_element_type=jnp.float32
    )
    grad_one, grad_first_gain, grad_first_shift = norm_backward(
        grad_hidden, normed_one, inverse_one, first_gain.astype(jnp.float32)
    )
    grad_attended = grad_one.astype(jnp.bfloat16)
    grad_out_weight = jnp.einsum(
        "rd,re->de", mixed, grad_attended, preferred_element_type=jnp.float32
    )
    grad_out_bias = jnp.sum(grad_attended.astype(jnp.float32), 0)
    grad_mixed = jnp.einsum(
        "re,de->rd", grad_attended, out_weight, preferred_element_type=jnp.float32
    ).astype(jnp.bfloat16)
    grad_parts = []
    for doc_index in range(doc_count):
        doc_block = qkv[doc_index * length : (doc_index + 1) * length]
        queries = split_heads(doc_block, 0)
        key_rows = split_heads(doc_block, 1)
        value_rows = split_heads(doc_block, 2)
        scores = scores_of(queries, key_rows, allowed[doc_index])
        attention = jnp.exp(scores - log_totals[doc_index])
        grad_doc = grad_mixed[doc_index * length : (doc_index + 1) * length].reshape(
            length, HEADS, HEAD_DIM
        )
        grad_chance = jnp.einsum(
            "qhd,khd->hqk", grad_doc, value_rows, preferred_element_type=jnp.float32
        )
        inner = jnp.sum(grad_chance * attention, -1, keepdims=True)
        grad_scores = (attention * (grad_chance - inner)).astype(jnp.bfloat16)
        grad_query = (
            jnp.einsum("hqk,khd->qhd", grad_scores, key_rows, preferred_element_type=jnp.float32)
            * score_scale
        )
        grad_key = (
            jnp.einsum("hqk,qhd->khd", grad_scores, queries, preferred_element_type=jnp.float32)
            * score_scale
        )
        grad_value = jnp.einsum(
            "hqk,qhd->khd",
            attention.astype(jnp.bfloat16),
            grad_doc,
            preferred_element_type=jnp.float32,
        )
        grad_parts.append(
            jnp.concatenate(
                [
                    grad_query.reshape(length, model_width),
                    grad_key.reshape(length, model_width),
                    grad_value.reshape(length, model_width),
                ],
                axis=1,
            )
        )
    grad_qkv = jnp.concatenate(grad_parts).astype(jnp.bfloat16)
    grad_qkv_float = grad_qkv.astype(jnp.float32)
    grad_query_bias = jnp.sum(grad_qkv_float[:, :model_width], 0)
    grad_value_bias = jnp.sum(grad_qkv_float[:, 2 * model_width :], 0)
    grad_qkv_weight = jnp.einsum(
        "rd,re->de", token_rows, grad_qkv, preferred_element_type=jnp.float32
    )
    grad_tokens = (
        jnp.einsum("re,de->rd", grad_qkv, qkv_weight, preferred_element_type=jnp.float32) + grad_one
    ).astype(jnp.bfloat16)
    matrices = (grad_qkv_weight, grad_out_weight, grad_up_weight, grad_down_weight)
    partial_sums = (
        lax.psum_scatter(
            matrices[0].astype(jnp.bfloat16), "wide", scatter_dimension=1, tiled=True
        ).astype(jnp.float32),
        lax.psum_scatter(
            matrices[1].astype(jnp.bfloat16), "wide", scatter_dimension=1, tiled=True
        ).astype(jnp.float32),
        lax.psum_scatter(
            matrices[2].astype(jnp.bfloat16), "wide", scatter_dimension=1, tiled=True
        ).astype(jnp.float32),
        lax.psum_scatter(
            matrices[3].astype(jnp.bfloat16), "wide", scatter_dimension=1, tiled=True
        ).astype(jnp.float32),
    )
    summed_mats = (
        lax.psum_scatter(
            partial_sums[0].astype(jnp.bfloat16), "narrow", scatter_dimension=0, tiled=True
        ).astype(jnp.float32),
        lax.psum_scatter(
            partial_sums[1].astype(jnp.bfloat16), "narrow", scatter_dimension=0, tiled=True
        ).astype(jnp.float32),
        lax.psum_scatter(
            partial_sums[2].astype(jnp.bfloat16), "narrow", scatter_dimension=0, tiled=True
        ).astype(jnp.float32),
        lax.psum_scatter(
            partial_sums[3].astype(jnp.bfloat16), "narrow", scatter_dimension=0, tiled=True
        ).astype(jnp.float32),
    )
    smalls = lax.psum(
        (
            grad_query_bias,
            grad_value_bias,
            grad_out_bias,
            grad_first_gain,
            grad_first_shift,
            grad_up_bias,
            grad_down_bias,
            grad_second_gain,
            grad_second_shift,
            grad_dir_weight,
            grad_dir_bias,
        ),
        ("wide", "narrow"),
    )
    return (
        encoded_rows.reshape(tokens.shape),
        grad_tokens.reshape(tokens.shape),
        summed_mats[0],
        smalls[0],
        smalls[1],
        summed_mats[1],
        smalls[2],
        smalls[3],
        smalls[4],
        summed_mats[2],
        smalls[5],
        summed_mats[3],
        smalls[6],
        smalls[7],
        smalls[8],
        smalls[9],
        smalls[10],
    )


def fits_blocks(mesh):
    wide, narrow = mesh.shape["wide"], mesh.shape["narrow"]
    width, ff = HEADS * HEAD_DIM, 4 * HEADS * HEAD_DIM
    if wide != 2 * narrow or narrow < 4 or narrow & (narrow - 1):
        return False
    lanes = (ff // narrow, ff // wide, 2 * width // narrow)
    rows = (width // wide, width // narrow, width // wide // 2, 3 * width // wide // 2)
    return all(size % 128 == 0 for size in lanes) and all(size % 16 == 0 for size in rows)


def solution(mesh):
    placed = (
        P(("wide", "narrow"), None, None),
        P(("wide", "narrow")),
        P(),
        P(),
        P(),
        P(),
        P(),
        P(),
        P(),
        P(),
        P(),
        P(),
        P(),
        P(),
        P(),
        P(),
        P(),
        P(("wide", "narrow"), None),
        P(("wide", "narrow"), None),
        P(("wide", "narrow"), None, None),
        P(("wide", "narrow"), None),
        P(("wide", "narrow"), None, None),
    )
    return jax.shard_map(
        on_device_fast if fits_blocks(mesh) else on_device,
        mesh=mesh,
        in_specs=placed,
        out_specs=(
            P(("wide", "narrow"), None, None),
            P(("wide", "narrow"), None, None),
            P("narrow", "wide"),
            P(),
            P(),
            P("narrow", "wide"),
            P(),
            P(),
            P(),
            P("narrow", "wide"),
            P(),
            P("narrow", "wide"),
            P(),
            P(),
            P(),
            P(),
            P(),
        ),
        check_vma=False,
    )
```
